32 devices in a mesh: seq: 4 (over y, core), fsdp: 8 (over z, x).
Axes of the slice: x: 2, y: 2, z: 4, core: 2. Of those that a mesh axis runs over, the one named last changes fastest.
Arguments:
- tokens: bfloat16 [16384, 1024], P(('seq', 'fsdp')), may hold values from -6 to 6
- norm_gain: float32 [1024], replicated, may hold values from 0.5 to 1.5
- w_query: bfloat16 [1024, 1024], P('fsdp'), may hold values from -0.1875 to 0.1875
- w_key: bfloat16 [1024, 1024], P('fsdp'), may hold values from -0.1875 to 0.1875
- w_value: bfloat16 [1024, 1024], P('fsdp'), may hold values from -0.1875 to 0.1875
- w_beta: bfloat16 [1024, 8], P('fsdp'), may hold values from -0.1875 to 0.1875
- conv_taps: float32 [3, 4, 1024], replicated, may hold values from -3 to 3
- head_gain: float32 [128], replicated, may hold values from 0.5 to 1.5
- w_out: bfloat16 [1024, 1024], P('fsdp'), may hold values from -0.1875 to 0.1875
- ffn_gain: float32 [1024], replicated, may hold values from 0.5 to 1.5
- w_gate: bfloat16 [1024, 2816], P('fsdp'), may hold values from -0.1875 to 0.1875
- w_up: bfloat16 [1024, 2816], P('fsdp'), may hold values from -0.1875 to 0.1875
- w_down: bfloat16 [2816, 1024], P('fsdp'), may hold values from -0.109375 to 0.109375
- cotangent: bfloat16 [16384, 1024], P(('seq', 'fsdp')), may hold values from -6 to 6
- token_order: int32 [8, 2048], P('fsdp'), may hold values from 0 to 2047, each once within a row
- seq_lengths: int32 [8, 4], P('fsdp'), may hold values from 64 to 1024, as said below
Outputs:
- result: bfloat16 [16384, 1024], P(('seq', 'fsdp'))
- grad_tokens: float32 [16384, 1024], P(('seq', 'fsdp'))
- grad_norm_gain: float32 [1024], replicated
- grad_w_query: float32 [1024, 1024], P('fsdp')
- grad_w_key: float32 [1024, 1024], P('fsdp')
- grad_w_value: float32 [1024, 1024], P('fsdp')
- grad_w_beta: float32 [1024, 8], P('fsdp')
- grad_conv_taps: float32 [3, 4, 1024], replicated
- grad_head_gain: float32 [128], replicated
- grad_w_out: float32 [1024, 1024], P('fsdp')
- grad_ffn_gain: float32 [1024], replicated
- grad_w_gate: float32 [1024, 2816], P('fsdp')
- grad_w_up: float32 [1024, 2816], P('fsdp')
- grad_w_down: float32 [2816, 1024], P('fsdp')
The draws below stay inside these ranges and needn't reach their ends.
Inputs may be any that keep to these rules, and one draw needn't show every extreme that they name: `seq_lengths`: each row gives the lengths of a group's 4 sequences in packed order: multiples of 64 that sum to 2048, the longest exactly half of 2048. `token_order`: each row is a permutation of the arrival indices of one group.
All inputs are finite; a program needn't handle non-finite values.
Results may differ from the reference program's by a relative error of at most 0.02.
Values may be sent and summed in bfloat16 or wider, within the bound.
A program may use at most 256 MiB of HBM per device.

```python
import jax
import jax.numpy as jnp
from jax import lax

D = 1024
H = 8
DK = 128
FF = 2816
CONV = 4
CH = 64
GROUP = 2048
ROWS = 512
TOKENS = 16384
N_SEQ = 4
N_FSDP = 8


def draw_seq_lengths(key, part):
    half_spans = GROUP // (2 * CH)

    def one_group(group_key):
        key_first, key_second, key_place = jax.random.split(group_key, 3)
        first_len = jax.random.randint(key_first, (), 1, half_spans - 1)
        second_len = jax.random.randint(key_second, (), 1, half_spans - first_len)
        third_len = half_spans - first_len - second_len
        counts = jnp.stack([jnp.int32(half_spans), first_len, second_len, third_len]).astype(jnp.int32)
        place = jax.random.randint(key_place, (), 0, 4)
        return jnp.roll(counts, place) * CH
    return jax.vmap(one_group)(jax.random.split(key, N_FSDP)).astype(jnp.int32)


def level_of(own_key, extent, cuts, low, high):
    def one(axis_at, blocks):
        steps = jax.random.uniform(jax.random.fold_in(jax.random.fold_in(own_key, 6), axis_at), (blocks,), jnp.float32, low / len(cuts), high / len(cuts))
        return jnp.repeat(jnp.exp(steps), extent[axis_at] // blocks).reshape((-1,) + (1,) * (len(extent) - axis_at - 1))

    level = one(*cuts[0])
    for cut in cuts[1:]:
        level = level * one(*cut)
    return level


def noise(own_key, extent, scale, most, shards=(), kind=jnp.bfloat16):
    entries = scale * jax.random.normal(own_key, extent, jnp.float32)
    if shards:
        entries = entries * level_of(own_key, extent, shards, -0.22, 0.18)
    return jnp.clip(entries, -most, most).astype(kind)


def setup_inputs(seed: int = 0) -> dict:
    streams_of = jax.random.split(jax.random.key(seed), 17)
    return {
        "tokens": noise(streams_of[0], (TOKENS, D), 1.0, 6.0, ((0, 32),)),
        "norm_gain": jnp.clip(1.0 + 0.1 * jax.random.normal(streams_of[1], (D,), jnp.float32), 0.5, 1.5),
        "w_query": noise(streams_of[2], (D, D), D ** -0.5, 0.1875, ((0, 8),)),
        "w_key": noise(streams_of[3], (D, D), D ** -0.5, 0.1875, ((0, 8),)),
        "w_value": noise(streams_of[4], (D, D), D ** -0.5, 0.1875, ((0, 8),)),
        "w_beta": noise(streams_of[5], (D, H), D ** -0.5, 0.1875, ((0, 8),)),
        "conv_taps": noise(streams_of[6], (3, CONV, D), CONV ** -0.5, 3.0, (), jnp.float32),
        "head_gain": jnp.clip(1.0 + 0.1 * jax.random.normal(streams_of[7], (DK,), jnp.float32), 0.5, 1.5),
        "w_out": noise(streams_of[8], (D, D), D ** -0.5, 0.1875, ((0, 8),)),
        "ffn_gain": jnp.clip(1.0 + 0.1 * jax.random.normal(streams_of[9], (D,), jnp.float32), 0.5, 1.5),
        "w_gate": noise(streams_of[10], (D, FF), D ** -0.5, 0.1875, ((0, 8),)),
        "w_up": noise(streams_of[11], (D, FF), D ** -0.5, 0.1875, ((0, 8),)),
        "w_down": noise(streams_of[12], (FF, D), FF ** -0.5, 0.109375, ((0, 8),)),
        "cotangent": noise(streams_of[13], (TOKENS, D), 1.0, 6.0, ((0, 32),)),
        "token_order": jax.vmap(lambda own: jax.random.permutation(own, GROUP))(jax.random.split(streams_of[14], N_FSDP)).reshape((N_FSDP, GROUP)).astype(jnp.int32),
        "seq_lengths": draw_seq_lengths(jax.random.fold_in(streams_of[16], 71), 0),
    }


EPS_NORM = 1e-06
PRECISION_LEVEL = lax.Precision.HIGHEST

@jax.custom_vjp
def low(v):
    return lax.optimization_barrier(v.astype(jnp.bfloat16)).astype(jnp.float32)

@jax.custom_vjp
def low_back(v):
    return v

def low_keep(v):
    return (low(v), None)

def low_pass(kept, grad):
    return (grad,)

def back_keep(v):
    return (v, None)

def back_low(kept, grad):
    return (low(grad),)
low.defvjp(low_keep, low_pass)
low_back.defvjp(back_keep, back_low)

def matmul(first_op, second_op):
    return jnp.dot(first_op, second_op, precision=PRECISION_LEVEL, preferred_element_type=jnp.float32)

def rms_norm(values, gain):
    return values * lax.rsqrt(lax.optimization_barrier(jnp.mean(values * values, axis=-1, keepdims=True)) + EPS_NORM) * gain

def layout_masks(lengths, group_rows):
    starts = jnp.cumsum(lengths) - lengths
    places = jnp.arange(group_rows, dtype=jnp.int32)
    valid_taps = [jnp.ones((group_rows,), jnp.float32)]
    for offset in range(1, CONV):
        inside = (starts[None, :] > places[:, None] - offset) & (starts[None, :] <= places[:, None])
        valid_taps.append(1.0 - jnp.any(inside, axis=1).astype(jnp.float32))
    span_first = jnp.arange(group_rows // CH, dtype=jnp.int32) * CH
    retain = 1.0 - jnp.any(starts[None, :] == span_first[:, None], axis=1).astype(jnp.float32)
    return (valid_taps, retain)

def short_conv(signal, tap_weights, valid_taps):
    summed = signal * tap_weights[0]
    for offset in range(1, CONV):
        shifted = jnp.concatenate([jnp.zeros((offset, signal.shape[1]), jnp.float32), signal[:-offset]], axis=0)
        summed = summed + shifted * valid_taps[offset][:, None] * tap_weights[offset]
    return summed

def span_step(carried_state, inputs):
    query_block, input_keys, values, strength, retain = inputs
    carried_state = carried_state * retain
    identity = jnp.eye(CH, dtype=jnp.float32)
    lower_mask = jnp.tril(jnp.ones((CH, CH), jnp.float32), -1)
    incl_mask = jnp.tril(jnp.ones((CH, CH), jnp.float32))
    key_inner = jnp.einsum('hik,hjk->hij', input_keys, input_keys, precision=PRECISION_LEVEL)
    strict = strength[:, :, None] * key_inner * lower_mask
    inverse_t = identity - strict
    power_a = strict
    for level_idx in range(1, CH.bit_length() - 1):
        power_a = jnp.einsum('hij,hjk->hik', power_a, power_a, precision=PRECISION_LEVEL)
        inverse_t = jnp.einsum('hij,hjk->hik', inverse_t, identity + power_a, precision=PRECISION_LEVEL)
    weighted_keys = jnp.einsum('hij,hjk->hik', inverse_t, strength[:, :, None] * input_keys, precision=PRECISION_LEVEL)
    weighted_values = jnp.einsum('hij,hjk->hik', inverse_t, strength[:, :, None] * values, precision=PRECISION_LEVEL)
    fresh_update = weighted_values - jnp.einsum('jto,joa->jta', weighted_keys, carried_state, precision=PRECISION_LEVEL)
    scores = jnp.einsum('hik,hjk->hij', query_block, input_keys, precision=PRECISION_LEVEL) * incl_mask
    block_output = jnp.einsum('jto,joa->jta', query_block, carried_state, precision=PRECISION_LEVEL)
    block_output = block_output + jnp.einsum('hij,hjv->hiv', scores, fresh_update, precision=PRECISION_LEVEL)
    carried_state = carried_state + jnp.einsum('zgb,zga->zba', input_keys, fresh_update, precision=PRECISION_LEVEL)
    return (carried_state, block_output)

def delta_rule(query_h, key_h, value_h, strength, retain):
    group_rows, head_count = (query_h.shape[0], query_h.shape[1])
    blocks = group_rows // CH

    def to_blocks(array):
        return array.reshape(blocks, CH, head_count, -1).transpose(0, 2, 1, 3)
    strength_b = strength.reshape(blocks, CH, head_count).transpose(0, 2, 1)
    initial = jnp.zeros((head_count, DK, DK), jnp.float32)
    last_state, block_outs = lax.scan(jax.checkpoint(span_step), initial, (to_blocks(query_h), to_blocks(key_h), to_blocks(value_h), strength_b, retain))
    return block_outs.transpose(0, 2, 1, 3).reshape(group_rows, head_count, DK)

def mixer(query_in, key_in, value_in, beta_in, conv_in, gain_in, lengths):
    group_rows, head_count = (beta_in.shape[0], beta_in.shape[1])
    valid_taps, retain = layout_masks(lengths, group_rows)

    def activate(signal, tap_weights):
        return jax.nn.silu(short_conv(signal, tap_weights, valid_taps)).reshape(group_rows, head_count, DK)
    query_h = activate(query_in, conv_in[0])
    key_h = activate(key_in, conv_in[1])
    value_h = activate(value_in, conv_in[2])
    query_h = low(query_h * lax.rsqrt(lax.optimization_barrier(jnp.sum(query_h * query_h, axis=-1, keepdims=True)) + EPS_NORM) * DK ** (-0.5))
    key_h = low(key_h * lax.rsqrt(lax.optimization_barrier(jnp.sum(key_h * key_h, axis=-1, keepdims=True)) + EPS_NORM))
    strength = jax.nn.sigmoid(beta_in)
    block_output = delta_rule(query_h, key_h, value_h, strength, retain)
    block_output = block_output * lax.rsqrt(lax.optimization_barrier(jnp.mean(block_output * block_output, axis=-1, keepdims=True)) + EPS_NORM) * gain_in
    return block_output.reshape(group_rows, head_count * DK)

def residual_block(inputs, norm_gain, w_query, w_key, w_value, w_beta, conv_taps, head_gain, w_out, ffn_gain, w_gate, w_up, w_down, packing, lengths):
    group_rows = inputs.shape[0]
    inverse = jnp.zeros((group_rows,), jnp.int32).at[packing].set(jnp.arange(group_rows, dtype=jnp.int32))
    normed = low(rms_norm(inputs, norm_gain))
    proj_q = low(low_back(matmul(normed, w_query)))
    proj_k = low(low_back(matmul(normed, w_key)))
    proj_v = low(low_back(matmul(normed, w_value)))
    proj_b = low(low_back(matmul(normed, w_beta)))
    mixed_out = mixer(proj_q[packing], proj_k[packing], proj_v[packing], proj_b[packing], conv_taps, head_gain, lengths)[inverse]
    mixed_out = low(low_back(mixed_out))
    hidden = inputs + low_back(matmul(mixed_out, w_out))
    second = low(rms_norm(hidden, ffn_gain))
    gate_lin = low_back(matmul(second, w_gate))
    up_lin = low_back(matmul(second, w_up))
    active = low(jax.nn.silu(gate_lin) * up_lin)
    return hidden + matmul(active, w_down)

def reference(tokens, norm_gain, w_query, w_key, w_value, w_beta, conv_taps, head_gain, w_out, ffn_gain, w_gate, w_up, w_down, cotangent, token_order, seq_lengths):
    weights = (norm_gain.astype(jnp.float32), w_query.astype(jnp.float32), w_key.astype(jnp.float32), w_value.astype(jnp.float32), w_beta.astype(jnp.float32), conv_taps.astype(jnp.float32), head_gain.astype(jnp.float32), w_out.astype(jnp.float32), ffn_gain.astype(jnp.float32), w_gate.astype(jnp.float32), w_up.astype(jnp.float32), w_down.astype(jnp.float32))

    def regroup(array):
        return array.reshape(N_SEQ, N_FSDP, ROWS, D).transpose(1, 0, 2, 3).reshape(N_FSDP, GROUP, D)

    def ungroup(array):
        return array.reshape(N_FSDP, N_SEQ, ROWS, D).transpose(1, 0, 2, 3).reshape(TOKENS, D)
    group_inputs = regroup(tokens.astype(jnp.float32))
    group_cots = regroup(cotangent.astype(jnp.float32))

    def group_step(totals, inputs):
        x_group, cot_group, packing, lengths = inputs

        def forward(x_value, *params):
            return residual_block(x_value, *params, packing, lengths)
        out_value, pullback = jax.vjp(forward, x_group, *weights)
        gradients = pullback(cot_group)
        totals = tuple((total_one + grad_one for total_one, grad_one in zip(totals, gradients[1:])))
        return (totals, (out_value, gradients[0]))
    zero_grads = tuple((jnp.zeros_like(weight_one) for weight_one in weights))
    totals, (outputs, grad_inputs) = lax.scan(group_step, zero_grads, (group_inputs, group_cots, token_order, seq_lengths))
    return (ungroup(outputs).astype(jnp.bfloat16), ungroup(grad_inputs), totals[0], totals[1], totals[2], totals[3], totals[4], totals[5], totals[6], totals[7], totals[8], totals[9], totals[10], totals[11])
```

```python
import functools

import jax
import jax.numpy as jnp
from jax import lax
from jax.experimental import pallas as pl
from jax.experimental.pallas import tpu as pltpu
from jax.sharding import PartitionSpec as P

DK = 128
CONV = 4
CH = 64
BT = 128
HALO = 16
PB = 256
EPS_NORM = 1e-06

NN = (((1,), (0,)), ((), ()))
NT = (((1,), (1,)), ((), ()))
TN = (((0,), (0,)), ((), ()))


def bdot(first, second, dims=NN):
    return lax.dot_general(
        first.astype(jnp.bfloat16),
        second.astype(jnp.bfloat16),
        dims,
        preferred_element_type=jnp.float32,
    )


def iota(shape, axis):
    return lax.broadcasted_iota(jnp.int32, shape, axis)


def sigmoid(values):
    return 1.0 / (1.0 + jnp.exp(-values))


def fill_masks(mask_ref):
    rows, cols = iota((BT, BT), 0), iota((BT, BT), 1)
    size, level = 1, 0
    while size < BT:
        inside = (rows // (2 * size) == cols // (2 * size)) & (rows // size > cols // size)
        mask_ref[level] = jnp.where(inside, 1.0, 0.0)
        size, level = 2 * size, level + 1


def unit_lower_inverses(stricts, mask_ref):
    rows, cols = iota((BT, BT), 0), iota((BT, BT), 1)
    eye = jnp.where(rows == cols, 1.0, 0.0)
    inverses = [eye - strict * mask_ref[0] for strict in stricts]
    for level in range(1, 7):
        lows = [inverse.astype(jnp.bfloat16) for inverse in inverses]
        inner = [bdot(strict * mask_ref[level], low) for strict, low in zip(stricts, lows)]
        inverses = [
            inverse - bdot(low, mid) for inverse, low, mid in zip(inverses, lows, inner)
        ]
    return inverses


def tap_masks(first, second, third, count):
    rows = iota((count, 1), 0)
    flag = jnp.where(rows < CH, first, jnp.where(rows < BT, second, third))
    return [None] + [jnp.where(rows % CH < back, flag, 1.0) for back in range(1, CONV)]


def conv_of(halo_rows, taps, masks):
    total = halo_rows[HALO:] * taps[0]
    for back in range(1, CONV):
        total = total + pltpu.roll(halo_rows, back, 0)[HALO:] * (taps[back] * masks[back])
    return total


def block_flags(first, second):
    upper = iota((BT, 1), 0) < CH
    seen = jnp.where(upper, first, first * second)
    kept = jnp.where(upper, second, 1.0)
    return seen, kept


def pair_mask(second):
    rows, cols = iota((BT, BT), 0), iota((BT, BT), 1)
    cross = (rows >= CH) & (cols < CH)
    return rows, cols, jnp.where(cross, second, 1.0)


def permute_rows(column, source, width):
    hot = jnp.where(column == iota((column.shape[0], width), 1), 1.0, 0.0).astype(jnp.bfloat16)
    return lax.dot_general(hot, source, NN, preferred_element_type=jnp.float32)


def unpermute_rows(row, base, source, width):
    hot = jnp.where(row == iota((PB, width), 0) + base, 1.0, 0.0).astype(jnp.bfloat16)
    return lax.dot_general(hot, source, NN, preferred_element_type=jnp.float32)


def mixer_forward_kernel(
    heads,
    retain_ref,
    column_ref,
    row_ref,
    proj_ref,
    taps_ref,
    gain_ref,
    mixed_ref,
    packed_ref,
    delta_ref,
    inverse_ref,
    big_ref,
    update_ref,
    state_ref,
    mask_ref,
    fresh_ref,
    own_ref,
    add_ref,
    normed_ref,
):
    tokens = proj_ref.shape[0]
    blocks = tokens // BT
    fill_masks(mask_ref)
    packed_ref[0:HALO, :] = jnp.zeros((HALO, packed_ref.shape[1]), jnp.bfloat16)

    def permute(step, carry):
        base = pl.multiple_of(step * PB, PB)
        picked = permute_rows(column_ref[pl.ds(base, PB), :], proj_ref[...], tokens)
        packed_ref[pl.ds(HALO + base, PB), :] = picked.astype(jnp.bfloat16)
        return carry

    lax.fori_loop(0, tokens // PB, permute, 0)

    unroll = 2

    def prepare(step, carry):
        places, stricts, kept_values = [], [], []
        for sub in range(unroll):
            block = step * unroll + sub
            first, second = retain_ref[2 * block], retain_ref[2 * block + 1]
            base = pl.multiple_of(block * BT, BT)
            masks = tap_masks(first, second, 1.0, BT)
            seen, kept = block_flags(first, second)
            rows, cols, cross = pair_mask(second)
            strengths = sigmoid(
                packed_ref[pl.ds(HALO + base, BT), 3 * heads * DK : 3 * heads * DK + BT].astype(
                    jnp.float32
                )
            )
            for head in range(heads):
                parts = []
                for kind in range(3):
                    at = (kind * heads + head) * DK
                    window = packed_ref[pl.ds(base, HALO + BT), at : at + DK].astype(jnp.float32)
                    taps = [
                        taps_ref[kind * CONV + back : kind * CONV + back + 1, head * DK : head * DK + DK]
                        for back in range(CONV)
                    ]
                    conv = conv_of(window, taps, masks)
                    parts.append(conv * sigmoid(conv))
                query, key, value = parts
                query = query * lax.rsqrt(
                    jnp.sum(query * query, axis=1, keepdims=True) + EPS_NORM
                ) * DK ** (-0.5)
                key = key * lax.rsqrt(jnp.sum(key * key, axis=1, keepdims=True) + EPS_NORM)
                query_low, key_low = query.astype(jnp.bfloat16), key.astype(jnp.bfloat16)
                query, key = query_low.astype(jnp.float32), key_low.astype(jnp.float32)
                beta = strengths[:, head : head + 1]
                inner = bdot(jnp.concatenate([key_low, query_low], axis=0), key_low, NT)
                stricts.append(jnp.where(rows > cols, inner[:BT] * cross * beta, 0.0))
                scores = jnp.where(rows >= cols, inner[BT:] * cross, 0.0)
                sides = jnp.concatenate([key * (beta * seen), value * beta], axis=1)
                kept_values.append((scores, sides, key * kept, query * seen))
                places.append(head * blocks + block)
        inverses = unit_lower_inverses(stricts, mask_ref)
        solved = [
            bdot(inverse, values[1]) for inverse, values in zip(inverses, kept_values)
        ]
        through = [bdot(values[0], both) for values, both in zip(kept_values, solved)]
        onward = [bdot(values[2], both, TN) for values, both in zip(kept_values, solved)]
        for index, place in enumerate(places):
            inverse_ref[place] = inverses[index].astype(jnp.bfloat16)
            big_ref[place, 0:BT, :] = onward[index][:, :DK].astype(jnp.bfloat16)
            big_ref[place, BT : 2 * BT, :] = solved[index][:, :DK].astype(jnp.bfloat16)
            big_ref[place, 2 * BT : 3 * BT, :] = (
                kept_values[index][3] - through[index][:, :DK]
            ).astype(jnp.bfloat16)
            add_ref[place] = onward[index][:, DK:]
            fresh_ref[place] = solved[index][:, DK:]
            own_ref[place] = through[index][:, DK:]
        return carry

    lax.fori_loop(0, blocks // unroll, prepare, 0)

    def advance(block, states):
        through = retain_ref[2 * block] * retain_ref[2 * block + 1]
        base = pl.multiple_of(block * BT, BT)
        lows = [state.astype(jnp.bfloat16) for state in states]
        products = [bdot(big_ref[head * blocks + block], lows[head]) for head in range(heads)]
        following = []
        for head in range(heads):
            place = head * blocks + block
            product = products[head]
            state_ref[place] = lows[head]
            following.append(states[head] * through - product[:BT] + add_ref[place])
            update_ref[place] = (fresh_ref[place] - product[BT : 2 * BT]).astype(jnp.bfloat16)
            delta = own_ref[place] + product[2 * BT :]
            delta_ref[pl.ds(base, BT), head * DK : head * DK + DK] = delta
            inv = lax.rsqrt(jnp.mean(delta * delta, axis=1, keepdims=True) + EPS_NORM)
            normed_ref[pl.ds(base, BT), head * DK : head * DK + DK] = (
                delta * inv * gain_ref[...]
            ).astype(jnp.bfloat16)
        return tuple(following)

    zero = jnp.zeros((DK, DK), jnp.float32)
    lax.fori_loop(0, blocks, advance, (zero,) * heads)

    def unpermute(step, carry):
        base = pl.multiple_of(step * PB, PB)
        mixed_ref[pl.ds(base, PB), :] = unpermute_rows(
            row_ref[...], base, normed_ref[...], tokens
        ).astype(jnp.bfloat16)
        return carry

    lax.fori_loop(0, tokens // PB, unpermute, 0)


VMEM = pltpu.MemorySpace.VMEM
SMEM = pltpu.MemorySpace.SMEM


def spec(space=VMEM):
    return pl.BlockSpec(memory_space=space)


def mixer_forward(retain, column, row, proj, taps, gain):
    tokens, width = proj.shape
    heads = taps.shape[1] // DK
    blocks = tokens // BT
    count = heads * blocks
    low, full = jnp.bfloat16, jnp.float32
    return pl.pallas_call(
        functools.partial(mixer_forward_kernel, heads),
        out_shape=(
            jax.ShapeDtypeStruct((tokens, heads * DK), low),
            jax.ShapeDtypeStruct((HALO + tokens, width), low),
            jax.ShapeDtypeStruct((tokens, heads * DK), full),
            jax.ShapeDtypeStruct((count, BT, BT), low),
            jax.ShapeDtypeStruct((count, 3 * BT, BT), low),
            jax.ShapeDtypeStruct((count, BT, BT), low),
            jax.ShapeDtypeStruct((count, BT, BT), low),
        ),
        in_specs=[spec(SMEM)] + [spec()] * 5,
        out_specs=(spec(),) * 7,
        scratch_shapes=[
            pltpu.VMEM((7, BT, BT), full),
            pltpu.VMEM((count, BT, BT), full),
            pltpu.VMEM((count, BT, BT), full),
            pltpu.VMEM((count, BT, BT), full),
            pltpu.VMEM((tokens, heads * DK), low),
        ],
        compiler_params=pltpu.CompilerParams(vmem_limit_bytes=56 << 20),
        name="mixer_forward",
    )(retain, column, row, proj, taps, gain)


def mixer_backward_kernel(
    heads,
    retain_ref,
    column_ref,
    row_ref,
    grad_ref,
    packed_ref,
    taps_ref,
    gain_ref,
    delta_ref,
    inverse_ref,
    big_ref,
    update_ref,
    state_ref,
    out_ref,
    taps_out_ref,
    gain_out_ref,
    grad_delta_ref,
    add_ref,
    after_ref,
    conv_ref,
    grad_proj_ref,
):
    tokens = grad_ref.shape[0]
    blocks = tokens // BT
    width = 3 * heads * DK

    def head_norm(step, total):
        base = pl.multiple_of(step * PB, PB)
        picked = permute_rows(column_ref[pl.ds(base, PB), :], grad_ref[...], tokens)
        for head in range(heads):
            at = slice(head * DK, head * DK + DK)
            grad = picked[:, at]
            delta = delta_ref[pl.ds(base, PB), at]
            inv = lax.rsqrt(jnp.mean(delta * delta, axis=1, keepdims=True) + EPS_NORM)
            unit = delta * inv
            total = total + jnp.sum(grad * unit, axis=0, keepdims=True)
            grad_unit = grad * gain_ref[...]
            low = (
                inv * (grad_unit - unit * jnp.mean(grad_unit * unit, axis=1, keepdims=True))
            ).astype(jnp.bfloat16)
            grad_delta_ref[pl.ds(base, PB), at] = low
            for sub in range(PB // BT):
                place = head * blocks + step * (PB // BT) + sub
                add_ref[place] = bdot(
                    big_ref[place, 2 * BT : 3 * BT, :], low[sub * BT : sub * BT + BT], TN
                )
        return total

    gain_out_ref[...] = lax.fori_loop(
        0, tokens // PB, head_norm, jnp.zeros((1, DK), jnp.float32)
    )

    def retreat(step, grads):
        block = blocks - 1 - step
        through = retain_ref[2 * block] * retain_ref[2 * block + 1]
        lows = [grad.astype(jnp.bfloat16) for grad in grads]
        following = []
        for head in range(heads):
            place = head * blocks + block
            after_ref[place] = lows[head]
            following.append(
                grads[head] * through
                - bdot(big_ref[place, 0:BT, :], lows[head], TN)
                + add_ref[place]
            )
        return tuple(following)

    zero = jnp.zeros((DK, DK), jnp.float32)
    lax.fori_loop(0, blocks, retreat, (zero,) * heads)

    conv_ref[tokens : tokens + HALO, :] = jnp.zeros((HALO, width), jnp.float32)

    def gradients(block, carry):
        first, second = retain_ref[2 * block], retain_ref[2 * block + 1]
        base = pl.multiple_of(block * BT, BT)
        masks = tap_masks(first, second, 1.0, BT)
        seen, kept = block_flags(first, second)
        rows, cols, cross = pair_mask(second)
        _, _, _ = rows, cols, cross
        turned = jnp.where((rows < CH) & (cols >= CH), second, 1.0)
        lanes = iota((BT, BT), 1)
        strengths = sigmoid(
            packed_ref[pl.ds(HALO + base, BT), width : width + BT].astype(jnp.float32)
        )
        grad_strengths = jnp.zeros((BT, BT), jnp.float32)
        for head in range(heads):
            place = head * blocks + block
            convs, gates, acts = [], [], []
            for kind in range(3):
                at = (kind * heads + head) * DK
                window = packed_ref[pl.ds(base, HALO + BT), at : at + DK].astype(jnp.float32)
                taps = [
                    taps_ref[kind * CONV + back : kind * CONV + back + 1, head * DK : head * DK + DK]
                    for back in range(CONV)
                ]
                conv = conv_of(window, taps, masks)
                gate = sigmoid(conv)
                convs.append(conv)
                gates.append(gate)
                acts.append(conv * gate)
            inv_q = lax.rsqrt(jnp.sum(acts[0] * acts[0], axis=1, keepdims=True) + EPS_NORM)
            inv_k = lax.rsqrt(jnp.sum(acts[1] * acts[1], axis=1, keepdims=True) + EPS_NORM)
            query_low = (acts[0] * inv_q * DK ** (-0.5)).astype(jnp.bfloat16)
            key_low = (acts[1] * inv_k).astype(jnp.bfloat16)
            key = key_low.astype(jnp.float32)
            value = acts[2]
            beta = strengths[:, head : head + 1]
            grad_low = grad_delta_ref[pl.ds(base, BT), head * DK : head * DK + DK]
            after = after_ref[place]
            state = state_ref[place]
            update = update_ref[place]
            inner = bdot(key_low, jnp.concatenate([key_low, query_low], axis=0), NT)
            scores_t = jnp.where(rows <= cols, inner[:, BT:] * turned, 0.0)
            grad_update = bdot(scores_t, grad_low) + bdot(key * kept, after)
            solved = bdot(inverse_ref[place], grad_update, TN)
            solved_beta = solved * beta
            both = jnp.concatenate([grad_low, solved.astype(jnp.bfloat16)], axis=0)
            on_state = bdot(both, state, NT)
            on_update = bdot(both, update, NT)
            grad_scores = jnp.where(rows >= cols, on_update[:BT] * cross, 0.0)
            grad_strict = jnp.where(rows > cols, on_update[BT:] * cross, 0.0)
            grad_weighted = on_state[BT:] * seen
            turned_both = bdot(
                update,
                jnp.concatenate(
                    [grad_low, solved_beta.astype(jnp.bfloat16)], axis=0
                ),
                NT,
            )
            grad_scores_t = jnp.where(rows <= cols, turned_both[:, :BT] * turned, 0.0)
            strict_t = jnp.where(rows < cols, turned_both[:, BT:] * turned, 0.0)
            grad_query = on_state[:BT] * seen + bdot(grad_scores, key_low)
            grad_key = (
                bdot(grad_scores_t, query_low)
                + bdot(update, after, NT) * kept
                - beta * grad_weighted
                - bdot(grad_strict * beta + strict_t, key_low)
            )
            grad_value = solved_beta
            grad_beta = jnp.sum(
                solved * value - grad_strict * inner[:, :BT] - grad_weighted * key,
                axis=1,
                keepdims=True,
            )
            grad_strengths = jnp.where(lanes == head, grad_beta, grad_strengths)
            scaled = (
                inv_q
                * DK ** (-0.5)
                * (
                    grad_query
                    - acts[0]
                    * (inv_q * inv_q)
                    * jnp.sum(grad_query * acts[0], axis=1, keepdims=True)
                ),
                inv_k
                * (
                    grad_key
                    - acts[1] * (inv_k * inv_k) * jnp.sum(grad_key * acts[1], axis=1, keepdims=True)
                ),
                grad_value,
            )
            for kind in range(3):
                at = (kind * heads + head) * DK
                conv_ref[pl.ds(base, BT), at : at + DK] = (
                    scaled[kind] * gates[kind] * (1.0 + convs[kind] * (1.0 - gates[kind]))
                )
        grad_proj_ref[pl.ds(base, BT), width : width + BT] = (
            grad_strengths * strengths * (1.0 - strengths)
        ).astype(jnp.bfloat16)
        return carry

    lax.fori_loop(0, blocks, gradients, 0)

    taps_out_ref[...] = jnp.zeros(taps_out_ref.shape, jnp.float32)

    def conv_back(block, carry):
        first, second, third = (
            retain_ref[2 * block],
            retain_ref[2 * block + 1],
            retain_ref[2 * block + 2],
        )
        base = pl.multiple_of(block * BT, BT)
        masks = tap_masks(first, second, third, BT + HALO)
        for kind in range(3):
            for head in range(heads):
                at = (kind * heads + head) * DK
                grads = conv_ref[pl.ds(base, BT + HALO), at : at + DK]
                window = packed_ref[pl.ds(base, HALO + BT), at : at + DK].astype(jnp.float32)
                total = None
                for back in range(CONV):
                    row = kind * CONV + back
                    tap = taps_ref[row : row + 1, head * DK : head * DK + DK]
                    masked = grads if back == 0 else grads * masks[back]
                    shifted = (
                        masked if back == 0 else pltpu.roll(masked, BT + HALO - back, 0)
                    )[:BT]
                    total = shifted * tap if total is None else total + shifted * tap
                    past = (window if back == 0 else pltpu.roll(window, back, 0))[HALO:]
                    taps_out_ref[row : row + 1, head * DK : head * DK + DK] += jnp.sum(
                        masked[:BT] * past, axis=0, keepdims=True
                    )
                grad_proj_ref[pl.ds(base, BT), at : at + DK] = total.astype(jnp.bfloat16)
        return carry

    lax.fori_loop(0, blocks, conv_back, 0)

    def unpermute(step, carry):
        base = pl.multiple_of(step * PB, PB)
        out_ref[pl.ds(base, PB), :] = unpermute_rows(
            row_ref[...], base, grad_proj_ref[...], tokens
        ).astype(jnp.bfloat16)
        return carry

    lax.fori_loop(0, tokens // PB, unpermute, 0)


def mixer_backward(retain, column, row, grad_mixed, taps, gain, saved):
    packed, delta, inverse, big, update, state = saved
    tokens = grad_mixed.shape[0]
    width = packed.shape[1]
    heads = taps.shape[1] // DK
    count = heads * (tokens // BT)
    low, full = jnp.bfloat16, jnp.float32
    return pl.pallas_call(
        functools.partial(mixer_backward_kernel, heads),
        out_shape=(
            jax.ShapeDtypeStruct((tokens, width), low),
            jax.ShapeDtypeStruct(taps.shape, full),
            jax.ShapeDtypeStruct((1, DK), full),
        ),
        in_specs=[spec(SMEM)] + [spec()] * 11,
        out_specs=(spec(),) * 3,
        scratch_shapes=[
            pltpu.VMEM((tokens, heads * DK), low),
            pltpu.VMEM((count, BT, BT), full),
            pltpu.VMEM((count, BT, BT), low),
            pltpu.VMEM((tokens + HALO, 3 * heads * DK), full),
            pltpu.VMEM((tokens, width), low),
        ],
        compiler_params=pltpu.CompilerParams(vmem_limit_bytes=56 << 20),
        name="mixer_backward",
    )(retain, column, row, grad_mixed, packed, taps, gain, delta, inverse, big, update, state)


def matmul(first, second):
    return lax.dot_general(first, second, NN, preferred_element_type=jnp.float32)


def times_transposed(first, second):
    return lax.dot_general(first, second, NT, preferred_element_type=jnp.float32)


def contract_rows(first, second):
    return lax.dot_general(first, second, TN, preferred_element_type=jnp.float32)


def rms_forward(values, gain):
    inv_rms = lax.rsqrt(jnp.mean(values * values, axis=-1, keepdims=True) + EPS_NORM)
    unit_rows = values * inv_rms
    return (unit_rows * gain, unit_rows, inv_rms)


def rms_backward(grad_out, unit_rows, inv_rms, gain):
    grad_gain = jnp.sum(grad_out * unit_rows, axis=0)
    grad_unit = grad_out * gain
    grad_in = inv_rms * (
        grad_unit - unit_rows * jnp.mean(grad_unit * unit_rows, axis=-1, keepdims=True)
    )
    return (grad_in, grad_gain)


def retains(lengths, tokens):
    index = jnp.arange(lengths.shape[0])
    starts = jnp.sum(jnp.where(index[:, None] > index[None, :], lengths[None, :], 0), axis=1)
    spans = jnp.arange(tokens // CH, dtype=jnp.int32) * CH
    keep = 1.0 - jnp.any(starts[None, :] == spans[:, None], axis=1).astype(jnp.float32)
    return jnp.pad(keep, (0, 2))


def own_slice(array, place, size, axis):
    return lax.dynamic_slice_in_dim(array, place * size, size, axis)


def local(
    n_seq,
    n_fsdp,
    tokens,
    norm_gain,
    w_query,
    w_key,
    w_value,
    w_beta,
    conv_taps,
    head_gain,
    w_out,
    ffn_gain,
    w_gate,
    w_up,
    w_down,
    cotangent,
    token_order,
    seq_lengths,
):
    place = lax.axis_index("seq")
    model = tokens.shape[1]
    head_count = w_beta.shape[1]
    heads = head_count // n_seq
    width = heads * DK
    hidden_units = w_gate.shape[1]
    slab = hidden_units // (n_fsdp * n_seq)
    units = slab * n_fsdp
    own_rows = w_query.shape[0]

    def gather(array, axis_name, axis=0):
        return lax.all_gather(array, axis_name, axis=axis, tiled=True)

    def pick_units(array):
        split = array.reshape(array.shape[0], n_fsdp, n_seq, slab)
        return lax.dynamic_index_in_dim(split, place, 2, keepdims=False).reshape(-1, units)

    inputs = tokens.astype(jnp.float32)
    normed_f, unit_one, inv_one = rms_forward(inputs, norm_gain)
    normed = gather(normed_f.astype(jnp.bfloat16), "seq")
    cot_all = gather(cotangent, "seq")
    group_tokens = normed.shape[0]
    w_mixer = gather(
        jnp.concatenate(
            [own_slice(array, place, width, 1) for array in (w_query, w_key, w_value)]
            + [jnp.pad(own_slice(w_beta, place, heads, 1), ((0, 0), (0, DK - heads)))],
            axis=1,
        ),
        "fsdp",
    )
    full_o = gather(w_out, "fsdp")
    full_gate = gather(pick_units(w_gate), "fsdp")
    full_up = gather(pick_units(w_up), "fsdp")
    full_down = gather(own_slice(w_down, place, slab, 0), "fsdp")

    proj = matmul(normed, w_mixer).astype(jnp.bfloat16)
    retain = retains(seq_lengths[0], group_tokens)
    column, row = token_order.reshape(-1, 1), token_order.reshape(1, -1)
    taps = own_slice(conv_taps, place, width, 2).reshape(3 * CONV, width)
    gain = head_gain.reshape(1, DK)
    mixed, *saved = mixer_forward(retain, column, row, proj, taps, gain)
    mixed_tok = lax.all_to_all(mixed, "seq", split_axis=0, concat_axis=1, tiled=True)
    hidden = inputs + matmul(mixed_tok, full_o)
    second_f, unit_two, inv_two = rms_forward(hidden, ffn_gain)
    second = gather(second_f.astype(jnp.bfloat16), "seq")
    gate_lin = matmul(second, full_gate)
    upward = matmul(second, full_up)
    sigmoid_gate = jax.nn.sigmoid(gate_lin)
    active = (gate_lin * sigmoid_gate * upward).astype(jnp.bfloat16)
    grad_active = times_transposed(cot_all, full_down)
    grad_gate = (
        grad_active * upward * sigmoid_gate * (1.0 + gate_lin * (1.0 - sigmoid_gate))
    ).astype(jnp.bfloat16)
    grad_upward = (grad_active * gate_lin * sigmoid_gate).astype(jnp.bfloat16)

    def spread(partial):
        pieces = lax.all_to_all(
            partial.astype(jnp.bfloat16).reshape(n_seq, -1, model),
            "seq",
            split_axis=0,
            concat_axis=0,
            tiled=True,
        )
        return jnp.sum(pieces.astype(jnp.float32), axis=0)

    grad_second = spread(
        times_transposed(grad_gate, full_gate) + times_transposed(grad_upward, full_up)
    )
    grad_hidden, grad_ffn_gain = rms_backward(grad_second, unit_two, inv_two, ffn_gain)
    grad_hidden = grad_hidden + cotangent.astype(jnp.float32)
    grad_attn = grad_hidden.astype(jnp.bfloat16)
    grad_mixed = times_transposed(grad_attn, full_o).astype(jnp.bfloat16)
    grad_heads = lax.all_to_all(grad_mixed, "seq", split_axis=1, concat_axis=0, tiled=True)
    result = (hidden + spread(matmul(active, full_down))).astype(jnp.bfloat16)

    def scatter(array):
        return lax.psum_scatter(
            array.astype(jnp.bfloat16), "fsdp", scatter_dimension=0, tiled=True
        )

    part_gate = scatter(contract_rows(second, grad_gate))
    part_up = scatter(contract_rows(second, grad_upward))
    part_down = scatter(contract_rows(active, cot_all))
    part_out = scatter(contract_rows(mixed_tok, grad_attn))

    grad_proj, grad_taps, grad_gain = mixer_backward(
        retain, column, row, grad_heads, taps, gain, saved
    )
    grad_normed = spread(times_transposed(grad_proj, w_mixer))
    part_mixer = scatter(contract_rows(normed, grad_proj))
    grad_inputs, grad_norm_gain = rms_backward(grad_normed, unit_one, inv_one, norm_gain)
    grad_inputs = grad_inputs + grad_hidden

    all_mixer = gather(part_mixer[None], "seq").astype(jnp.float32)

    def mixer_columns(start, size):
        return (
            all_mixer[:, :, start : start + size].transpose(1, 0, 2).reshape(own_rows, n_seq * size)
        )

    sum_q, sum_k, sum_v = (mixer_columns(kind * width, width) for kind in range(3))
    sum_b = mixer_columns(3 * width, heads)

    def all_units(part):
        pieces = gather(part[None], "seq").astype(jnp.float32)
        return (
            pieces.reshape(n_seq, own_rows, n_fsdp, slab)
            .transpose(1, 2, 0, 3)
            .reshape(own_rows, hidden_units)
        )

    sum_gate, sum_up = all_units(part_gate), all_units(part_up)
    sum_down = gather(part_down, "seq").astype(jnp.float32)
    sum_out = lax.psum(part_out, "seq").astype(jnp.float32)
    conv_full = lax.dynamic_update_slice_in_dim(
        jnp.zeros_like(conv_taps), grad_taps.reshape(3, CONV, width), place * width, 2
    )
    norm_total, ffn_total, head_total, conv_total = lax.psum(
        (grad_norm_gain, grad_ffn_gain, grad_gain[0], conv_full), ("seq", "fsdp")
    )
    return (
        result,
        grad_inputs,
        norm_total,
        sum_q,
        sum_k,
        sum_v,
        sum_b,
        conv_total,
        head_total,
        sum_out,
        ffn_total,
        sum_gate,
        sum_up,
        sum_down,
    )


def solution(mesh):
    tokens = P(("seq", "fsdp"), None)
    rows = P("fsdp", None)
    in_specs = (
        (tokens, P()) + (rows,) * 4 + (P(), P(), rows, P()) + (rows,) * 3 + (tokens, rows, rows)
    )
    out_specs = (
        (tokens, tokens, P()) + (rows,) * 4 + (P(), P(), rows, P()) + (rows,) * 3
    )
    return jax.shard_map(
        functools.partial(local, mesh.shape["seq"], mesh.shape["fsdp"]),
        mesh=mesh,
        in_specs=in_specs,
        out_specs=out_specs,
        check_vma=False,
    )
```

```python
import functools

import jax
import jax.numpy as jnp
from jax import lax
from jax.experimental import pallas as pl
from jax.experimental.pallas import tpu as pltpu
from jax.sharding import PartitionSpec as P

DK = 128
CONV = 4
CH = 64
BT = 128
HALO = 16
PB = 256
EPS_NORM = 1e-06

NN = (((1,), (0,)), ((), ()))
NT = (((1,), (1,)), ((), ()))
TN = (((0,), (0,)), ((), ()))


def bdot(first, second, dims=NN):
    return lax.dot_general(
        first.astype(jnp.bfloat16),
        second.astype(jnp.bfloat16),
        dims,
        preferred_element_type=jnp.float32,
    )


def iota(shape, axis):
    return lax.broadcasted_iota(jnp.int32, shape, axis)


def sigmoid(values):
    return 1.0 / (1.0 + jnp.exp(-values))


def fill_masks(mask_ref):
    rows, cols = iota((BT, BT), 0), iota((BT, BT), 1)
    size, level = 1, 0
    while size < BT:
        inside = (rows // (2 * size) == cols // (2 * size)) & (rows // size > cols // size)
        mask_ref[level] = jnp.where(inside, 1.0, 0.0)
        size, level = 2 * size, level + 1


def unit_lower_inverses(stricts, mask_ref):
    rows, cols = iota((BT, BT), 0), iota((BT, BT), 1)
    eye = jnp.where(rows == cols, 1.0, 0.0)
    inverses = [eye - strict * mask_ref[0] for strict in stricts]
    for level in range(1, 7):
        lows = [inverse.astype(jnp.bfloat16) for inverse in inverses]
        inner = [bdot(strict * mask_ref[level], low) for strict, low in zip(stricts, lows)]
        inverses = [
            inverse - bdot(low, mid) for inverse, low, mid in zip(inverses, lows, inner)
        ]
    return inverses


def tap_masks(first, second, third, count):
    rows = iota((count, 1), 0)
    flag = jnp.where(rows < CH, first, jnp.where(rows < BT, second, third))
    return [None] + [jnp.where(rows % CH < back, flag, 1.0) for back in range(1, CONV)]


def conv_of(halo_rows, taps, masks):
    total = halo_rows[HALO:] * taps[0]
    for back in range(1, CONV):
        total = total + pltpu.roll(halo_rows, back, 0)[HALO:] * (taps[back] * masks[back])
    return total


def block_flags(first, second):
    upper = iota((BT, 1), 0) < CH
    seen = jnp.where(upper, first, first * second)
    kept = jnp.where(upper, second, 1.0)
    return seen, kept


def pair_mask(second):
    rows, cols = iota((BT, BT), 0), iota((BT, BT), 1)
    cross = (rows >= CH) & (cols < CH)
    return rows, cols, jnp.where(cross, second, 1.0)


def permute_rows(column, source, width):
    hot = jnp.where(column == iota((column.shape[0], width), 1), 1.0, 0.0).astype(jnp.bfloat16)
    return lax.dot_general(hot, source, NN, preferred_element_type=jnp.float32)


def unpermute_rows(row, base, source, width):
    hot = jnp.where(row == iota((PB, width), 0) + base, 1.0, 0.0).astype(jnp.bfloat16)
    return lax.dot_general(hot, source, NN, preferred_element_type=jnp.float32)


MESH = pl.DeviceIdType.MESH
ANY = pl.ANY


class Gather:
    outer = 4

    @classmethod
    def copies(cls, n_fsdp):
        inner = n_fsdp // cls.outer
        return (cls.outer - 1) + cls.outer * (inner - 1)

    def __init__(self, n_fsdp, source, slot, sems, base, local_sem):
        self.inner = n_fsdp // self.outer
        self.me = lax.axis_index("fsdp")
        self.seq = lax.axis_index("seq")
        self.high, self.low = self.me // self.inner, self.me % self.inner
        self.source, self.slot = source, slot
        self.send, self.recv = sems
        self.base, self.local_sem = base, local_sem

    def at(self, high, low):
        return (high % self.outer) * self.inner + (low % self.inner)

    def copy(self, source, owner, target, index):
        return pltpu.make_async_remote_copy(
            src_ref=source,
            dst_ref=self.slot(owner),
            send_sem=self.send.at[self.base + index],
            recv_sem=self.recv.at[self.base + index],
            device_id=(self.seq, target),
            device_id_type=MESH,
        )

    def along_outer(self, step):
        return self.copy(self.source, self.me, self.at(self.high + step, self.low), step - 1)

    def along_inner(self, hop):
        return self.copy(
            self.source, self.me, self.at(self.high, self.low + hop), self.outer - 2 + hop
        )

    def passed_on(self, step, hop):
        owner = self.at(self.high - step, self.low)
        index = self.outer - 1 + (self.inner - 1) * step + hop - 1
        return self.copy(self.slot(owner), owner, self.at(self.high, self.low + hop), index)

    def own(self):
        return pltpu.make_async_copy(self.source, self.slot(self.me), self.local_sem)

    def start(self):
        for step in range(1, self.outer):
            self.along_outer(step).start()
        for hop in range(1, self.inner):
            self.along_inner(hop).start()
        self.own().start()

    def relay(self):
        for step in range(1, self.outer):
            self.along_outer(step).wait_recv()
            for hop in range(1, self.inner):
                self.passed_on(step, hop).start()

    def finish(self):
        self.own().wait()
        for hop in range(1, self.inner):
            self.along_inner(hop).wait_recv()
            for step in range(1, self.outer):
                self.passed_on(step, hop).wait_recv()
        for step in range(1, self.outer):
            self.along_outer(step).wait_send()
        for hop in range(1, self.inner):
            self.along_inner(hop).wait_send()
            for step in range(1, self.outer):
                self.passed_on(step, hop).wait_send()


class Share:
    @staticmethod
    def copies(n_seq):
        return 1 + 2 * (n_seq // 2 - 1)

    def __init__(self, n_seq, source, slot, sems, base, local_sem):
        self.n_seq, self.chips = n_seq, n_seq // 2
        self.me = lax.axis_index("seq")
        self.fsdp = lax.axis_index("fsdp")
        self.mate = self.me + 1 - 2 * (self.me % 2)
        self.source, self.slot = source, slot
        self.send, self.recv = sems
        self.base, self.local_sem = base, local_sem

    def copy(self, source, owner, target, index):
        return pltpu.make_async_remote_copy(
            src_ref=source,
            dst_ref=self.slot(owner),
            send_sem=self.send.at[self.base + index],
            recv_sem=self.recv.at[self.base + index],
            device_id=(target, self.fsdp),
            device_id_type=MESH,
        )

    def to_mate(self):
        return self.copy(self.source, self.me, self.mate, 0)

    def across(self, step):
        return self.copy(self.source, self.me, (self.me + 2 * step) % self.n_seq, step)

    def passed_on(self, step):
        owner = (self.me + self.n_seq - 2 * step) % self.n_seq
        return self.copy(self.slot(owner), owner, self.mate, self.chips - 1 + step)

    def own(self):
        return pltpu.make_async_copy(self.source, self.slot(self.me), self.local_sem)

    def start(self):
        for step in range(1, self.chips):
            self.across(step).start()
        self.to_mate().start()
        self.own().start()

    def relay(self):
        for step in range(1, self.chips):
            self.across(step).wait_recv()
            self.passed_on(step).start()

    def finish(self):
        self.own().wait()
        self.to_mate().wait_recv()
        for step in range(1, self.chips):
            self.passed_on(step).wait_recv()
        self.to_mate().wait_send()
        for step in range(1, self.chips):
            self.across(step).wait_send()
            self.passed_on(step).wait_send()


def greet(n_seq, n_fsdp):
    seq, fsdp = lax.axis_index("seq"), lax.axis_index("fsdp")
    barrier = pltpu.get_barrier_semaphore()
    for step in range(1, n_seq):
        pl.semaphore_signal(
            barrier, inc=1, device_id=((seq + step) % n_seq, fsdp), device_id_type=MESH
        )
    for step in range(1, n_fsdp):
        pl.semaphore_signal(
            barrier, inc=1, device_id=(seq, (fsdp + step) % n_fsdp), device_id_type=MESH
        )
    pl.semaphore_wait(barrier, n_seq + n_fsdp - 2)


def aligned(value, unit):
    return pl.multiple_of(value, unit)


def mixer_forward_kernel(
    heads,
    n_seq,
    n_fsdp,
    retain_ref,
    column_ref,
    row_ref,
    taps_ref,
    gain_ref,
    normed_in,
    mixer_in,
    gate_in,
    up_in,
    down_in,
    out_in,
    cot_in,
    tokens_mixed,
    normed_all,
    mixer_all,
    gate_all,
    up_all,
    down_all,
    out_all,
    cot_all,
    packed_ref,
    delta_ref,
    inverse_ref,
    big_ref,
    update_ref,
    state_ref,
    mask_ref,
    fresh_ref,
    own_ref,
    add_ref,
    mixed_ref,
    ready_ref,
    proj_ref,
    normed_ref,
    weight_ref,
    gather_send,
    gather_recv,
    share_send,
    share_recv,
    local_sems,
):
    tokens, width = proj_ref.shape
    blocks = tokens // BT
    own_tokens = tokens // n_seq
    seq = lax.axis_index("seq")
    own_rows = mixer_in.shape[0]
    half_rows = own_rows // 2
    out_rows, out_width = out_in.shape
    half_width = out_width // 2
    core = seq % 2

    greet(n_seq, n_fsdp)

    gather_sems = (gather_send, gather_recv)
    share_sems = (share_send, share_recv)
    per_gather = Gather.copies(n_fsdp)
    per_share = Share.copies(n_seq)

    def rows_slot(ref, size, start=0, count=None):
        count = size if count is None else count
        return lambda owner: ref.at[pl.ds(aligned(owner * size + start, count), count)]

    def gather_piece(index, source, slot):
        return Gather(
            n_fsdp, source, slot, gather_sems, index * per_gather, local_sems.at[index]
        )

    mixers = [
        gather_piece(
            part,
            mixer_in.at[pl.ds(part * half_rows, half_rows)],
            rows_slot(weight_ref, own_rows, part * half_rows, half_rows),
        )
        for part in range(2)
    ]
    half_at = aligned(core * half_width, half_width)
    pieces = [
        gather_piece(
            2,
            out_in.at[:, pl.ds(half_at, half_width)],
            lambda owner: out_all.at[
                pl.ds(aligned(owner * out_rows, out_rows), out_rows), pl.ds(half_at, half_width)
            ],
        ),
        gather_piece(3, gate_in, rows_slot(gate_all, own_rows)),
        gather_piece(4, up_in, rows_slot(up_all, own_rows)),
        gather_piece(5, down_in, lambda owner: down_all.at[owner]),
    ]
    share_normed = Share(
        n_seq, normed_in, rows_slot(normed_ref, own_tokens), share_sems, 0, local_sems.at[6]
    )
    share_cot = Share(
        n_seq, cot_in, rows_slot(cot_all, own_tokens), share_sems, per_share, local_sems.at[7]
    )
    swap = pltpu.make_async_remote_copy(
        src_ref=out_all.at[:, pl.ds(half_at, half_width)],
        dst_ref=out_all.at[:, pl.ds(half_at, half_width)],
        send_sem=share_send.at[2 * per_share],
        recv_sem=share_recv.at[2 * per_share],
        device_id=(share_normed.mate, lax.axis_index("fsdp")),
        device_id_type=MESH,
    )

    mixers[0].start()
    share_normed.start()
    fill_masks(mask_ref)
    packed_ref[0:HALO, :] = jnp.zeros((HALO, packed_ref.shape[1]), jnp.bfloat16)
    mixers[0].relay()
    mixers[1].start()
    share_normed.relay()
    mixers[1].relay()
    pieces[0].start()
    share_cot.start()
    mixers[0].finish()
    mixers[1].finish()
    share_normed.finish()
    keep_normed = pltpu.make_async_copy(normed_ref, normed_all, local_sems.at[8])
    keep_mixer = pltpu.make_async_copy(weight_ref, mixer_all, local_sems.at[9])
    keep_normed.start()
    keep_mixer.start()

    def project(step, carry):
        base = aligned(step * PB, PB)
        proj_ref[pl.ds(base, PB), :] = lax.dot_general(
            normed_ref[pl.ds(base, PB), :],
            weight_ref[...],
            NN,
            preferred_element_type=jnp.float32,
        ).astype(jnp.bfloat16)
        return carry

    lax.fori_loop(0, tokens // PB, project, 0)
    pieces[0].relay()
    pieces[1].start()

    def permute(step, carry):
        base = pl.multiple_of(step * PB, PB)
        picked = permute_rows(column_ref[pl.ds(base, PB), :], proj_ref[...], tokens)
        packed_ref[pl.ds(HALO + base, PB), :] = picked.astype(jnp.bfloat16)
        return carry

    lax.fori_loop(0, tokens // PB, permute, 0)
    pieces[0].finish()
    swap.start()
    share_cot.relay()

    unroll = 2

    def prepare(step, carry):
        for number in (1, 2):

            @pl.when(step == (0, 1, 5)[number])
            def _():
                pieces[number].relay()
                pieces[number + 1].start()

        places, stricts, kept_values = [], [], []
        for sub in range(unroll):
            block = step * unroll + sub
            first, second = retain_ref[2 * block], retain_ref[2 * block + 1]
            base = pl.multiple_of(block * BT, BT)
            masks = tap_masks(first, second, 1.0, BT)
            seen, kept = block_flags(first, second)
            rows, cols, cross = pair_mask(second)
            strengths = sigmoid(
                packed_ref[pl.ds(HALO + base, BT), 3 * heads * DK : 3 * heads * DK + BT].astype(
                    jnp.float32
                )
            )
            for head in range(heads):
                parts = []
                for kind in range(3):
                    at = (kind * heads + head) * DK
                    window = packed_ref[pl.ds(base, HALO + BT), at : at + DK].astype(jnp.float32)
                    taps = [
                        taps_ref[kind * CONV + back : kind * CONV + back + 1, head * DK : head * DK + DK]
                        for back in range(CONV)
                    ]
                    conv = conv_of(window, taps, masks)
                    parts.append(conv * sigmoid(conv))
                query, key, value = parts
                query = query * lax.rsqrt(
                    jnp.sum(query * query, axis=1, keepdims=True) + EPS_NORM
                ) * DK ** (-0.5)
                key = key * lax.rsqrt(jnp.sum(key * key, axis=1, keepdims=True) + EPS_NORM)
                query_low, key_low = query.astype(jnp.bfloat16), key.astype(jnp.bfloat16)
                query, key = query_low.astype(jnp.float32), key_low.astype(jnp.float32)
                beta = strengths[:, head : head + 1]
                inner = bdot(jnp.concatenate([key_low, query_low], axis=0), key_low, NT)
                stricts.append(jnp.where(rows > cols, inner[:BT] * cross * beta, 0.0))
                scores = jnp.where(rows >= cols, inner[BT:] * cross, 0.0)
                sides = jnp.concatenate([key * (beta * seen), value * beta], axis=1)
                kept_values.append((scores, sides, key * kept, query * seen))
                places.append(head * blocks + block)
        inverses = unit_lower_inverses(stricts, mask_ref)
        solved = [
            bdot(inverse, values[1]) for inverse, values in zip(inverses, kept_values)
        ]
        through = [bdot(values[0], both) for values, both in zip(kept_values, solved)]
        onward = [bdot(values[2], both, TN) for values, both in zip(kept_values, solved)]
        for index, place in enumerate(places):
            inverse_ref[place] = inverses[index].astype(jnp.bfloat16)
            big_ref[place, 0:BT, :] = onward[index][:, :DK].astype(jnp.bfloat16)
            big_ref[place, BT : 2 * BT, :] = solved[index][:, :DK].astype(jnp.bfloat16)
            big_ref[place, 2 * BT : 3 * BT, :] = (
                kept_values[index][3] - through[index][:, :DK]
            ).astype(jnp.bfloat16)
            add_ref[place] = onward[index][:, DK:]
            fresh_ref[place] = solved[index][:, DK:]
            own_ref[place] = through[index][:, DK:]
        return carry

    lax.fori_loop(0, blocks // unroll, prepare, 0)

    def advance(block, states):
        through = retain_ref[2 * block] * retain_ref[2 * block + 1]
        base = pl.multiple_of(block * BT, BT)
        lows = [state.astype(jnp.bfloat16) for state in states]
        products = [bdot(big_ref[head * blocks + block], lows[head]) for head in range(heads)]
        following = []
        for head in range(heads):
            place = head * blocks + block
            product = products[head]
            state_ref[place] = lows[head]
            following.append(states[head] * through - product[:BT] + add_ref[place])
            update_ref[place] = (fresh_ref[place] - product[BT : 2 * BT]).astype(jnp.bfloat16)
            delta = own_ref[place] + product[2 * BT :]
            delta_ref[pl.ds(base, BT), head * DK : head * DK + DK] = delta
            inv = lax.rsqrt(jnp.mean(delta * delta, axis=1, keepdims=True) + EPS_NORM)
            ready_ref[pl.ds(base, BT), head * DK : head * DK + DK] = (
                delta * inv * gain_ref[...]
            ).astype(jnp.bfloat16)
        return tuple(following)

    zero = jnp.zeros((DK, DK), jnp.float32)
    lax.fori_loop(0, blocks, advance, (zero,) * heads)

    pieces[3].relay()

    def hand_over(shift):
        target = (seq + shift) % n_seq
        base = aligned(target * own_tokens, own_tokens)
        for part in range(max(own_tokens // PB, 1)):
            size = min(own_tokens, PB)
            first = aligned(base + part * size, size)
            hot = jnp.where(
                row_ref[...] == iota((size, tokens), 0) + first, 1.0, 0.0
            ).astype(jnp.bfloat16)
            mixed_ref[pl.ds(first, size), :] = lax.dot_general(
                hot, ready_ref[...], NN, preferred_element_type=jnp.float32
            ).astype(jnp.bfloat16)
        source = mixed_ref.at[pl.ds(base, own_tokens)]
        slot = tokens_mixed.at[:, pl.ds(aligned(seq * heads * DK, heads * DK), heads * DK)]
        if shift == 0:
            return pltpu.make_async_copy(source, slot, local_sems.at[10])
        return pltpu.make_async_remote_copy(
            src_ref=source,
            dst_ref=slot,
            send_sem=share_send.at[2 * per_share + shift],
            recv_sem=share_recv.at[2 * per_share + shift],
            device_id=(target, lax.axis_index("fsdp")),
            device_id_type=MESH,
        )

    handed = []
    for shift in list(range(1, n_seq)) + [0]:
        copy = hand_over(shift)
        copy.start()
        handed.append(copy)
    for copy in handed:
        copy.wait()
    swap.wait()
    keep_normed.wait()
    keep_mixer.wait()
    share_cot.finish()
    for piece in pieces[1:]:
        piece.finish()


VMEM = pltpu.MemorySpace.VMEM
SMEM = pltpu.MemorySpace.SMEM


def spec(space=VMEM):
    return pl.BlockSpec(memory_space=space)


def mixer_forward(n_seq, n_fsdp, retain, column, row, taps, gain, shards):
    normed, mixer, gate, up, down, out, cot = shards
    own_tokens, model = normed.shape
    tokens = own_tokens * n_seq
    width = mixer.shape[1]
    heads = taps.shape[1] // DK
    blocks = tokens // BT
    count = heads * blocks
    low, full = jnp.bfloat16, jnp.float32
    per_gather, per_share = Gather.copies(n_fsdp), Share.copies(n_seq)
    gathers = 6 * per_gather
    shares = 2 * per_share + n_seq

    def whole(array):
        return jax.ShapeDtypeStruct((array.shape[0] * n_fsdp, array.shape[1]), low)

    return pl.pallas_call(
        functools.partial(mixer_forward_kernel, heads, n_seq, n_fsdp),
        out_shape=(
            jax.ShapeDtypeStruct((own_tokens, n_seq * heads * DK), low),
            jax.ShapeDtypeStruct((tokens, model), low),
            whole(mixer),
            whole(gate),
            whole(up),
            jax.ShapeDtypeStruct((n_fsdp,) + down.shape, low),
            whole(out),
            jax.ShapeDtypeStruct((tokens, model), low),
            jax.ShapeDtypeStruct((HALO + tokens, width), low),
            jax.ShapeDtypeStruct((tokens, heads * DK), full),
            jax.ShapeDtypeStruct((count, BT, BT), low),
            jax.ShapeDtypeStruct((count, 3 * BT, BT), low),
            jax.ShapeDtypeStruct((count, BT, BT), low),
            jax.ShapeDtypeStruct((count, BT, BT), low),
        ),
        in_specs=[spec(SMEM)] + [spec()] * 4 + [spec(ANY)] * 7,
        out_specs=(spec(ANY),) * 8 + (spec(),) * 6,
        scratch_shapes=[
            pltpu.VMEM((7, BT, BT), full),
            pltpu.VMEM((count, BT, BT), full),
            pltpu.VMEM((count, BT, BT), full),
            pltpu.VMEM((count, BT, BT), full),
            pltpu.VMEM((tokens, heads * DK), low),
            pltpu.VMEM((tokens, heads * DK), low),
            pltpu.VMEM((tokens, width), low),
            pltpu.VMEM((tokens, model), low),
            pltpu.VMEM((mixer.shape[0] * n_fsdp, width), low),
            pltpu.SemaphoreType.DMA((gathers,)),
            pltpu.SemaphoreType.DMA((gathers,)),
            pltpu.SemaphoreType.DMA((shares,)),
            pltpu.SemaphoreType.DMA((shares,)),
            pltpu.SemaphoreType.DMA((11,)),
        ],
        compiler_params=pltpu.CompilerParams(
            vmem_limit_bytes=60 << 20, collective_id=1, has_side_effects=True
        ),
        name="mixer_forward",
    )(retain, column, row, taps, gain, normed, mixer, gate, up, down, out, cot)


def mixer_backward_kernel(
    heads,
    retain_ref,
    column_ref,
    row_ref,
    grad_ref,
    packed_ref,
    taps_ref,
    gain_ref,
    delta_ref,
    inverse_ref,
    big_ref,
    update_ref,
    state_ref,
    out_ref,
    taps_out_ref,
    gain_out_ref,
    grad_delta_ref,
    add_ref,
    after_ref,
    conv_ref,
    grad_proj_ref,
):
    tokens = grad_ref.shape[0]
    blocks = tokens // BT
    width = 3 * heads * DK

    def head_norm(step, total):
        base = pl.multiple_of(step * PB, PB)
        picked = permute_rows(column_ref[pl.ds(base, PB), :], grad_ref[...], tokens)
        for head in range(heads):
            at = slice(head * DK, head * DK + DK)
            grad = picked[:, at]
            delta = delta_ref[pl.ds(base, PB), at]
            inv = lax.rsqrt(jnp.mean(delta * delta, axis=1, keepdims=True) + EPS_NORM)
            unit = delta * inv
            total = total + jnp.sum(grad * unit, axis=0, keepdims=True)
            grad_unit = grad * gain_ref[...]
            low = (
                inv * (grad_unit - unit * jnp.mean(grad_unit * unit, axis=1, keepdims=True))
            ).astype(jnp.bfloat16)
            grad_delta_ref[pl.ds(base, PB), at] = low
            for sub in range(PB // BT):
                place = head * blocks + step * (PB // BT) + sub
                add_ref[place] = bdot(
                    big_ref[place, 2 * BT : 3 * BT, :], low[sub * BT : sub * BT + BT], TN
                )
        return total

    gain_out_ref[...] = lax.fori_loop(
        0, tokens // PB, head_norm, jnp.zeros((1, DK), jnp.float32)
    )

    def retreat(step, grads):
        block = blocks - 1 - step
        through = retain_ref[2 * block] * retain_ref[2 * block + 1]
        lows = [grad.astype(jnp.bfloat16) for grad in grads]
        following = []
        for head in range(heads):
            place = head * blocks + block
            after_ref[place] = lows[head]
            following.append(
                grads[head] * through
                - bdot(big_ref[place, 0:BT, :], lows[head], TN)
                + add_ref[place]
            )
        return tuple(following)

    zero = jnp.zeros((DK, DK), jnp.float32)
    lax.fori_loop(0, blocks, retreat, (zero,) * heads)

    conv_ref[tokens : tokens + HALO, :] = jnp.zeros((HALO, width), jnp.float32)

    def gradients(block, carry):
        first, second = retain_ref[2 * block], retain_ref[2 * block + 1]
        base = pl.multiple_of(block * BT, BT)
        masks = tap_masks(first, second, 1.0, BT)
        seen, kept = block_flags(first, second)
        rows, cols, cross = pair_mask(second)
        _, _, _ = rows, cols, cross
        turned = jnp.where((rows < CH) & (cols >= CH), second, 1.0)
        lanes = iota((BT, BT), 1)
        strengths = sigmoid(
            packed_ref[pl.ds(HALO + base, BT), width : width + BT].astype(jnp.float32)
        )
        grad_strengths = jnp.zeros((BT, BT), jnp.float32)
        for head in range(heads):
            place = head * blocks + block
            convs, gates, acts = [], [], []
            for kind in range(3):
                at = (kind * heads + head) * DK
                window = packed_ref[pl.ds(base, HALO + BT), at : at + DK].astype(jnp.float32)
                taps = [
                    taps_ref[kind * CONV + back : kind * CONV + back + 1, head * DK : head * DK + DK]
                    for back in range(CONV)
                ]
                conv = conv_of(window, taps, masks)
                gate = sigmoid(conv)
                convs.append(conv)
                gates.append(gate)
                acts.append(conv * gate)
            inv_q = lax.rsqrt(jnp.sum(acts[0] * acts[0], axis=1, keepdims=True) + EPS_NORM)
            inv_k = lax.rsqrt(jnp.sum(acts[1] * acts[1], axis=1, keepdims=True) + EPS_NORM)
            query_low = (acts[0] * inv_q * DK ** (-0.5)).astype(jnp.bfloat16)
            key_low = (acts[1] * inv_k).astype(jnp.bfloat16)
            key = key_low.astype(jnp.float32)
            value = acts[2]
            beta = strengths[:, head : head + 1]
            grad_low = grad_delta_ref[pl.ds(base, BT), head * DK : head * DK + DK]
            after = after_ref[place]
            state = state_ref[place]
            update = update_ref[place]
            inner = bdot(key_low, jnp.concatenate([key_low, query_low], axis=0), NT)
            scores_t = jnp.where(rows <= cols, inner[:, BT:] * turned, 0.0)
            grad_update = bdot(scores_t, grad_low) + bdot(key * kept, after)
            solved = bdot(inverse_ref[place], grad_update, TN)
            solved_beta = solved * beta
            both = jnp.concatenate([grad_low, solved.astype(jnp.bfloat16)], axis=0)
            on_state = bdot(both, state, NT)
            on_update = bdot(both, update, NT)
            grad_scores = jnp.where(rows >= cols, on_update[:BT] * cross, 0.0)
            grad_strict = jnp.where(rows > cols, on_update[BT:] * cross, 0.0)
            grad_weighted = on_state[BT:] * seen
            turned_both = bdot(
                update,
                jnp.concatenate(
                    [grad_low, solved_beta.astype(jnp.bfloat16)], axis=0
                ),
                NT,
            )
            grad_scores_t = jnp.where(rows <= cols, turned_both[:, :BT] * turned, 0.0)
            strict_t = jnp.where(rows < cols, turned_both[:, BT:] * turned, 0.0)
            grad_query = on_state[:BT] * seen + bdot(grad_scores, key_low)
            grad_key = (
                bdot(grad_scores_t, query_low)
                + bdot(update, after, NT) * kept
                - beta * grad_weighted
                - bdot(grad_strict * beta + strict_t, key_low)
            )
            grad_value = solved_beta
            grad_beta = jnp.sum(
                solved * value - grad_strict * inner[:, :BT] - grad_weighted * key,
                axis=1,
                keepdims=True,
            )
            grad_strengths = jnp.where(lanes == head, grad_beta, grad_strengths)
            scaled = (
                inv_q
                * DK ** (-0.5)
                * (
                    grad_query
                    - acts[0]
                    * (inv_q * inv_q)
                    * jnp.sum(grad_query * acts[0], axis=1, keepdims=True)
                ),
                inv_k
                * (
                    grad_key
                    - acts[1] * (inv_k * inv_k) * jnp.sum(grad_key * acts[1], axis=1, keepdims=True)
                ),
                grad_value,
            )
            for kind in range(3):
                at = (kind * heads + head) * DK
                conv_ref[pl.ds(base, BT), at : at + DK] = (
                    scaled[kind] * gates[kind] * (1.0 + convs[kind] * (1.0 - gates[kind]))
                )
        grad_proj_ref[pl.ds(base, BT), width : width + BT] = (
            grad_strengths * strengths * (1.0 - strengths)
        ).astype(jnp.bfloat16)
        return carry

    lax.fori_loop(0, blocks, gradients, 0)

    taps_out_ref[...] = jnp.zeros(taps_out_ref.shape, jnp.float32)

    def conv_back(block, carry):
        first, second, third = (
            retain_ref[2 * block],
            retain_ref[2 * block + 1],
            retain_ref[2 * block + 2],
        )
        base = pl.multiple_of(block * BT, BT)
        masks = tap_masks(first, second, third, BT + HALO)
        for kind in range(3):
            for head in range(heads):
                at = (kind * heads + head) * DK
                grads = conv_ref[pl.ds(base, BT + HALO), at : at + DK]
                window = packed_ref[pl.ds(base, HALO + BT), at : at + DK].astype(jnp.float32)
                total = None
                for back in range(CONV):
                    row = kind * CONV + back
                    tap = taps_ref[row : row + 1, head * DK : head * DK + DK]
                    masked = grads if back == 0 else grads * masks[back]
                    shifted = (
                        masked if back == 0 else pltpu.roll(masked, BT + HALO - back, 0)
                    )[:BT]
                    total = shifted * tap if total is None else total + shifted * tap
                    past = (window if back == 0 else pltpu.roll(window, back, 0))[HALO:]
                    taps_out_ref[row : row + 1, head * DK : head * DK + DK] += jnp.sum(
                        masked[:BT] * past, axis=0, keepdims=True
                    )
                grad_proj_ref[pl.ds(base, BT), at : at + DK] = total.astype(jnp.bfloat16)
        return carry

    lax.fori_loop(0, blocks, conv_back, 0)

    def unpermute(step, carry):
        base = pl.multiple_of(step * PB, PB)
        out_ref[pl.ds(base, PB), :] = unpermute_rows(
            row_ref[...], base, grad_proj_ref[...], tokens
        ).astype(jnp.bfloat16)
        return carry

    lax.fori_loop(0, tokens // PB, unpermute, 0)


def mixer_backward(retain, column, row, grad_mixed, taps, gain, saved):
    packed, delta, inverse, big, update, state = saved
    tokens = grad_mixed.shape[0]
    width = packed.shape[1]
    heads = taps.shape[1] // DK
    count = heads * (tokens // BT)
    low, full = jnp.bfloat16, jnp.float32
    return pl.pallas_call(
        functools.partial(mixer_backward_kernel, heads),
        out_shape=(
            jax.ShapeDtypeStruct((tokens, width), low),
            jax.ShapeDtypeStruct(taps.shape, full),
            jax.ShapeDtypeStruct((1, DK), full),
        ),
        in_specs=[spec(SMEM)] + [spec()] * 11,
        out_specs=(spec(),) * 3,
        scratch_shapes=[
            pltpu.VMEM((tokens, heads * DK), low),
            pltpu.VMEM((count, BT, BT), full),
            pltpu.VMEM((count, BT, BT), low),
            pltpu.VMEM((tokens + HALO, 3 * heads * DK), full),
            pltpu.VMEM((tokens, width), low),
        ],
        compiler_params=pltpu.CompilerParams(vmem_limit_bytes=56 << 20),
        name="mixer_backward",
    )(retain, column, row, grad_mixed, packed, taps, gain, delta, inverse, big, update, state)


def matmul(first, second):
    return lax.dot_general(first, second, NN, preferred_element_type=jnp.float32)


def times_transposed(first, second):
    return lax.dot_general(first, second, NT, preferred_element_type=jnp.float32)


def contract_rows(first, second):
    return lax.dot_general(first, second, TN, preferred_element_type=jnp.float32)


def rms_forward(values, gain):
    inv_rms = lax.rsqrt(jnp.mean(values * values, axis=-1, keepdims=True) + EPS_NORM)
    unit_rows = values * inv_rms
    return (unit_rows * gain, unit_rows, inv_rms)


def rms_backward(grad_out, unit_rows, inv_rms, gain):
    grad_gain = jnp.sum(grad_out * unit_rows, axis=0)
    grad_unit = grad_out * gain
    grad_in = inv_rms * (
        grad_unit - unit_rows * jnp.mean(grad_unit * unit_rows, axis=-1, keepdims=True)
    )
    return (grad_in, grad_gain)


def retains(lengths, tokens):
    index = jnp.arange(lengths.shape[0])
    starts = jnp.sum(jnp.where(index[:, None] > index[None, :], lengths[None, :], 0), axis=1)
    spans = jnp.arange(tokens // CH, dtype=jnp.int32) * CH
    keep = 1.0 - jnp.any(starts[None, :] == spans[:, None], axis=1).astype(jnp.float32)
    return jnp.pad(keep, (0, 2))


def own_slice(array, place, size, axis):
    return lax.dynamic_slice_in_dim(array, place * size, size, axis)


def local(
    n_seq,
    n_fsdp,
    tokens,
    norm_gain,
    w_query,
    w_key,
    w_value,
    w_beta,
    conv_taps,
    head_gain,
    w_out,
    ffn_gain,
    w_gate,
    w_up,
    w_down,
    cotangent,
    token_order,
    seq_lengths,
):
    place = lax.axis_index("seq")
    model = tokens.shape[1]
    head_count = w_beta.shape[1]
    heads = head_count // n_seq
    width = heads * DK
    hidden_units = w_gate.shape[1]
    slab = hidden_units // (n_fsdp * n_seq)
    units = slab * n_fsdp
    own_rows = w_query.shape[0]

    def gather(array, axis_name, axis=0):
        return lax.all_gather(array, axis_name, axis=axis, tiled=True)

    def pick_units(array):
        split = array.reshape(array.shape[0], n_fsdp, n_seq, slab)
        return lax.dynamic_index_in_dim(split, place, 2, keepdims=False).reshape(-1, units)

    inputs = tokens.astype(jnp.float32)
    normed_f, unit_one, inv_one = rms_forward(inputs, norm_gain)
    group_tokens = tokens.shape[0] * n_seq
    mixer_shard = jnp.concatenate(
        [own_slice(array, place, width, 1) for array in (w_query, w_key, w_value)]
        + [jnp.pad(own_slice(w_beta, place, heads, 1), ((0, 0), (0, DK - heads)))],
        axis=1,
    )
    retain = retains(seq_lengths[0], group_tokens)
    column, row = token_order.reshape(-1, 1), token_order.reshape(1, -1)
    taps = own_slice(conv_taps, place, width, 2).reshape(3 * CONV, width)
    gain = head_gain.reshape(1, DK)
    mixed_tok, normed, w_mixer, full_gate, full_up, full_down, full_o, cot_all, *saved = (
        mixer_forward(
            n_seq,
            n_fsdp,
            retain,
            column,
            row,
            taps,
            gain,
            (
                normed_f.astype(jnp.bfloat16),
                mixer_shard,
                pick_units(w_gate),
                pick_units(w_up),
                own_slice(w_down, place, slab, 0),
                w_out,
                cotangent,
            ),
        )
    )
    full_down = full_down.reshape(units, model)
    hidden = inputs + matmul(mixed_tok, full_o)
    second_f, unit_two, inv_two = rms_forward(hidden, ffn_gain)
    second = gather(second_f.astype(jnp.bfloat16), "seq")
    gate_lin = matmul(second, full_gate)
    upward = matmul(second, full_up)
    sigmoid_gate = jax.nn.sigmoid(gate_lin)
    active = (gate_lin * sigmoid_gate * upward).astype(jnp.bfloat16)
    grad_active = times_transposed(cot_all, full_down)
    grad_gate = (
        grad_active * upward * sigmoid_gate * (1.0 + gate_lin * (1.0 - sigmoid_gate))
    ).astype(jnp.bfloat16)
    grad_upward = (grad_active * gate_lin * sigmoid_gate).astype(jnp.bfloat16)

    def spread(partial):
        pieces = lax.all_to_all(
            partial.astype(jnp.bfloat16).reshape(n_seq, -1, model),
            "seq",
            split_axis=0,
            concat_axis=0,
            tiled=True,
        )
        return jnp.sum(pieces.astype(jnp.float32), axis=0)

    grad_second = spread(
        times_transposed(grad_gate, full_gate) + times_transposed(grad_upward, full_up)
    )
    grad_hidden, grad_ffn_gain = rms_backward(grad_second, unit_two, inv_two, ffn_gain)
    grad_hidden = grad_hidden + cotangent.astype(jnp.float32)
    grad_attn = grad_hidden.astype(jnp.bfloat16)
    grad_mixed = times_transposed(grad_attn, full_o).astype(jnp.bfloat16)
    grad_heads = lax.all_to_all(grad_mixed, "seq", split_axis=1, concat_axis=0, tiled=True)
    result = (hidden + spread(matmul(active, full_down))).astype(jnp.bfloat16)

    def scatter(array):
        return lax.psum_scatter(
            array.astype(jnp.bfloat16), "fsdp", scatter_dimension=0, tiled=True
        )

    part_gate = scatter(contract_rows(second, grad_gate))
    part_up = scatter(contract_rows(second, grad_upward))
    part_down = scatter(contract_rows(active, cot_all))
    part_out = scatter(contract_rows(mixed_tok, grad_attn))

    grad_proj, grad_taps, grad_gain = mixer_backward(
        retain, column, row, grad_heads, taps, gain, saved
    )
    grad_normed = spread(times_transposed(grad_proj, w_mixer))
    part_mixer = scatter(contract_rows(normed, grad_proj))
    grad_inputs, grad_norm_gain = rms_backward(grad_normed, unit_one, inv_one, norm_gain)
    grad_inputs = grad_inputs + grad_hidden

    all_mixer = gather(part_mixer[None], "seq").astype(jnp.float32)

    def mixer_columns(start, size):
        return (
            all_mixer[:, :, start : start + size].transpose(1, 0, 2).reshape(own_rows, n_seq * size)
        )

    sum_q, sum_k, sum_v = (mixer_columns(kind * width, width) for kind in range(3))
    sum_b = mixer_columns(3 * width, heads)

    def all_units(part):
        pieces = gather(part[None], "seq").astype(jnp.float32)
        return (
            pieces.reshape(n_seq, own_rows, n_fsdp, slab)
            .transpose(1, 2, 0, 3)
            .reshape(own_rows, hidden_units)
        )

    sum_gate, sum_up = all_units(part_gate), all_units(part_up)
    sum_down = gather(part_down, "seq").astype(jnp.float32)
    sum_out = lax.psum(part_out, "seq").astype(jnp.float32)
    conv_full = lax.dynamic_update_slice_in_dim(
        jnp.zeros_like(conv_taps), grad_taps.reshape(3, CONV, width), place * width, 2
    )
    norm_total, ffn_total, head_total, conv_total = lax.psum(
        (grad_norm_gain, grad_ffn_gain, grad_gain[0], conv_full), ("seq", "fsdp")
    )
    return (
        result,
        grad_inputs,
        norm_total,
        sum_q,
        sum_k,
        sum_v,
        sum_b,
        conv_total,
        head_total,
        sum_out,
        ffn_total,
        sum_gate,
        sum_up,
        sum_down,
    )


def solution(mesh):
    tokens = P(("seq", "fsdp"), None)
    rows = P("fsdp", None)
    in_specs = (
        (tokens, P()) + (rows,) * 4 + (P(), P(), rows, P()) + (rows,) * 3 + (tokens, rows, rows)
    )
    out_specs = (
        (tokens, tokens, P()) + (rows,) * 4 + (P(), P(), rows, P()) + (rows,) * 3
    )
    return jax.shard_map(
        functools.partial(local, mesh.shape["seq"], mesh.shape["fsdp"]),
        mesh=mesh,
        in_specs=in_specs,
        out_specs=out_specs,
        check_vma=False,
    )
```

```python
import functools

import jax
import jax.numpy as jnp
from jax import lax
from jax.experimental import pallas as pl
from jax.experimental.pallas import tpu as pltpu
from jax.sharding import PartitionSpec as P

DK = 128
CONV = 4
CH = 64
BT = 128
HALO = 16
PB = 256
EPS_NORM = 1e-06

NN = (((1,), (0,)), ((), ()))
NT = (((1,), (1,)), ((), ()))
TN = (((0,), (0,)), ((), ()))


def bdot(first, second, dims=NN):
    return lax.dot_general(
        first.astype(jnp.bfloat16),
        second.astype(jnp.bfloat16),
        dims,
        preferred_element_type=jnp.float32,
    )


def iota(shape, axis):
    return lax.broadcasted_iota(jnp.int32, shape, axis)


def sigmoid(values):
    return 1.0 / (1.0 + jnp.exp(-values))


def fill_masks(mask_ref):
    rows, cols = iota((BT, BT), 0), iota((BT, BT), 1)
    size, level = 1, 0
    while size < BT:
        inside = (rows // (2 * size) == cols // (2 * size)) & (rows // size > cols // size)
        mask_ref[level] = jnp.where(inside, 1.0, 0.0)
        size, level = 2 * size, level + 1


def unit_lower_inverses(stricts, mask_ref):
    rows, cols = iota((BT, BT), 0), iota((BT, BT), 1)
    eye = jnp.where(rows == cols, 1.0, 0.0)
    inverses = [eye - strict * mask_ref[0] for strict in stricts]
    for level in range(1, 7):
        lows = [inverse.astype(jnp.bfloat16) for inverse in inverses]
        inner = [bdot(strict * mask_ref[level], low) for strict, low in zip(stricts, lows)]
        inverses = [
            inverse - bdot(low, mid) for inverse, low, mid in zip(inverses, lows, inner)
        ]
    return inverses


def tap_masks(first, second, third, count):
    rows = iota((count, 1), 0)
    flag = jnp.where(rows < CH, first, jnp.where(rows < BT, second, third))
    return [None] + [jnp.where(rows % CH < back, flag, 1.0) for back in range(1, CONV)]


def conv_of(halo_rows, taps, masks):
    total = halo_rows[HALO:] * taps[0]
    for back in range(1, CONV):
        total = total + pltpu.roll(halo_rows, back, 0)[HALO:] * (taps[back] * masks[back])
    return total


def block_flags(first, second):
    upper = iota((BT, 1), 0) < CH
    seen = jnp.where(upper, first, first * second)
    kept = jnp.where(upper, second, 1.0)
    return seen, kept


def pair_mask(second):
    rows, cols = iota((BT, BT), 0), iota((BT, BT), 1)
    cross = (rows >= CH) & (cols < CH)
    return rows, cols, jnp.where(cross, second, 1.0)


def permute_rows(column, source, width):
    hot = jnp.where(column == iota((column.shape[0], width), 1), 1.0, 0.0).astype(jnp.bfloat16)
    return lax.dot_general(hot, source, NN, preferred_element_type=jnp.float32)


def unpermute_rows(row, base, source, width):
    hot = jnp.where(row == iota((PB, width), 0) + base, 1.0, 0.0).astype(jnp.bfloat16)
    return lax.dot_general(hot, source, NN, preferred_element_type=jnp.float32)


MESH = pl.DeviceIdType.MESH
ANY = pl.ANY


class Gather:
    outer = 4

    @classmethod
    def copies(cls, n_fsdp):
        inner = n_fsdp // cls.outer
        return (cls.outer - 1) + cls.outer * (inner - 1)

    def __init__(self, n_fsdp, source, slot, sems, base, local_sem):
        self.inner = n_fsdp // self.outer
        self.me = lax.axis_index("fsdp")
        self.seq = lax.axis_index("seq")
        self.high, self.low = self.me // self.inner, self.me % self.inner
        self.source, self.slot = source, slot
        self.send, self.recv = sems
        self.base, self.local_sem = base, local_sem

    def at(self, high, low):
        return (high % self.outer) * self.inner + (low % self.inner)

    def copy(self, source, owner, target, index):
        return pltpu.make_async_remote_copy(
            src_ref=source,
            dst_ref=self.slot(owner),
            send_sem=self.send.at[self.base + index],
            recv_sem=self.recv.at[self.base + index],
            device_id=(self.seq, target),
            device_id_type=MESH,
        )

    def along_outer(self, step):
        return self.copy(self.source, self.me, self.at(self.high + step, self.low), step - 1)

    def along_inner(self, hop):
        return self.copy(
            self.source, self.me, self.at(self.high, self.low + hop), self.outer - 2 + hop
        )

    def passed_on(self, step, hop):
        owner = self.at(self.high - step, self.low)
        index = self.outer - 1 + (self.inner - 1) * step + hop - 1
        return self.copy(self.slot(owner), owner, self.at(self.high, self.low + hop), index)

    def own(self):
        return pltpu.make_async_copy(self.source, self.slot(self.me), self.local_sem)

    def start(self):
        for step in range(1, self.outer):
            self.along_outer(step).start()
        for hop in range(1, self.inner):
            self.along_inner(hop).start()
        self.own().start()

    def relay(self):
        for step in range(1, self.outer):
            self.along_outer(step).wait_recv()
            for hop in range(1, self.inner):
                self.passed_on(step, hop).start()

    def finish(self):
        self.own().wait()
        for hop in range(1, self.inner):
            self.along_inner(hop).wait_recv()
            for step in range(1, self.outer):
                self.passed_on(step, hop).wait_recv()
        for step in range(1, self.outer):
            self.along_outer(step).wait_send()
        for hop in range(1, self.inner):
            self.along_inner(hop).wait_send()
            for step in range(1, self.outer):
                self.passed_on(step, hop).wait_send()


class Share:
    @staticmethod
    def copies(n_seq):
        return 1 + 2 * (n_seq // 2 - 1)

    def __init__(self, n_seq, source, slot, sems, base, local_sem):
        self.n_seq, self.chips = n_seq, n_seq // 2
        self.me = lax.axis_index("seq")
        self.fsdp = lax.axis_index("fsdp")
        self.mate = self.me + 1 - 2 * (self.me % 2)
        self.source, self.slot = source, slot
        self.send, self.recv = sems
        self.base, self.local_sem = base, local_sem

    def copy(self, source, owner, target, index):
        return pltpu.make_async_remote_copy(
            src_ref=source,
            dst_ref=self.slot(owner),
            send_sem=self.send.at[self.base + index],
            recv_sem=self.recv.at[self.base + index],
            device_id=(target, self.fsdp),
            device_id_type=MESH,
        )

    def to_mate(self):
        return self.copy(self.source, self.me, self.mate, 0)

    def across(self, step):
        return self.copy(self.source, self.me, (self.me + 2 * step) % self.n_seq, step)

    def passed_on(self, step):
        owner = (self.me + self.n_seq - 2 * step) % self.n_seq
        return self.copy(self.slot(owner), owner, self.mate, self.chips - 1 + step)

    def own(self):
        return pltpu.make_async_copy(self.source, self.slot(self.me), self.local_sem)

    def start(self):
        for step in range(1, self.chips):
            self.across(step).start()
        self.to_mate().start()
        self.own().start()

    def relay(self):
        for step in range(1, self.chips):
            self.across(step).wait_recv()
            self.passed_on(step).start()

    def finish(self):
        self.own().wait()
        self.to_mate().wait_recv()
        for step in range(1, self.chips):
            self.passed_on(step).wait_recv()
        self.to_mate().wait_send()
        for step in range(1, self.chips):
            self.across(step).wait_send()
            self.passed_on(step).wait_send()


def greet(n_seq, n_fsdp):
    seq, fsdp = lax.axis_index("seq"), lax.axis_index("fsdp")
    barrier = pltpu.get_barrier_semaphore()
    for step in range(1, n_seq):
        pl.semaphore_signal(
            barrier, inc=1, device_id=((seq + step) % n_seq, fsdp), device_id_type=MESH
        )
    for step in range(1, n_fsdp):
        pl.semaphore_signal(
            barrier, inc=1, device_id=(seq, (fsdp + step) % n_fsdp), device_id_type=MESH
        )
    pl.semaphore_wait(barrier, n_seq + n_fsdp - 2)


def aligned(value, unit):
    return pl.multiple_of(value, unit)


def mixer_forward_kernel(
    heads,
    n_seq,
    n_fsdp,
    retain_ref,
    column_ref,
    row_ref,
    taps_ref,
    gain_ref,
    normed_in,
    mixer_in,
    gate_in,
    up_in,
    down_in,
    out_in,
    cot_in,
    tokens_mixed,
    normed_all,
    mixer_all,
    gate_all,
    up_all,
    down_all,
    out_all,
    cot_all,
    packed_ref,
    delta_ref,
    inverse_ref,
    big_ref,
    update_ref,
    state_ref,
    mask_ref,
    fresh_ref,
    own_ref,
    add_ref,
    mixed_ref,
    ready_ref,
    proj_ref,
    normed_ref,
    weight_ref,
    gather_send,
    gather_recv,
    share_send,
    share_recv,
    local_sems,
):
    tokens, width = proj_ref.shape
    blocks = tokens // BT
    own_tokens = tokens // n_seq
    seq = lax.axis_index("seq")
    own_rows = mixer_in.shape[0]
    half_rows = own_rows // 2
    out_rows, out_width = out_in.shape
    half_width = out_width // 2
    core = seq % 2

    greet(n_seq, n_fsdp)

    gather_sems = (gather_send, gather_recv)
    share_sems = (share_send, share_recv)
    per_gather = Gather.copies(n_fsdp)
    per_share = Share.copies(n_seq)

    def rows_slot(ref, size, start=0, count=None):
        count = size if count is None else count
        return lambda owner: ref.at[pl.ds(aligned(owner * size + start, count), count)]

    def gather_piece(index, source, slot):
        return Gather(
            n_fsdp, source, slot, gather_sems, index * per_gather, local_sems.at[index]
        )

    mixers = [
        gather_piece(
            part,
            mixer_in.at[pl.ds(part * half_rows, half_rows)],
            rows_slot(weight_ref, own_rows, part * half_rows, half_rows),
        )
        for part in range(2)
    ]
    half_at = aligned(core * half_width, half_width)
    pieces = [
        gather_piece(
            2,
            out_in.at[:, pl.ds(half_at, half_width)],
            lambda owner: out_all.at[
                pl.ds(aligned(owner * out_rows, out_rows), out_rows), pl.ds(half_at, half_width)
            ],
        ),
        gather_piece(3, gate_in, rows_slot(gate_all, own_rows)),
        gather_piece(4, up_in, rows_slot(up_all, own_rows)),
        gather_piece(5, down_in, lambda owner: down_all.at[owner]),
    ]
    share_normed = Share(
        n_seq, normed_in, rows_slot(normed_ref, own_tokens), share_sems, 0, local_sems.at[6]
    )
    share_cot = Share(
        n_seq, cot_in, rows_slot(cot_all, own_tokens), share_sems, per_share, local_sems.at[7]
    )
    swap = pltpu.make_async_remote_copy(
        src_ref=out_all.at[:, pl.ds(half_at, half_width)],
        dst_ref=out_all.at[:, pl.ds(half_at, half_width)],
        send_sem=share_send.at[2 * per_share],
        recv_sem=share_recv.at[2 * per_share],
        device_id=(share_normed.mate, lax.axis_index("fsdp")),
        device_id_type=MESH,
    )

    mixers[0].start()
    share_normed.start()
    fill_masks(mask_ref)
    packed_ref[0:HALO, :] = jnp.zeros((HALO, packed_ref.shape[1]), jnp.bfloat16)
    mixers[0].relay()
    mixers[1].start()
    share_normed.relay()
    mixers[1].relay()
    pieces[0].start()
    share_cot.start()
    mixers[0].finish()
    mixers[1].finish()
    share_normed.finish()
    keep_normed = pltpu.make_async_copy(normed_ref, normed_all, local_sems.at[8])
    keep_mixer = pltpu.make_async_copy(weight_ref, mixer_all, local_sems.at[9])
    keep_normed.start()
    keep_mixer.start()

    def project(step, carry):
        base = aligned(step * PB, PB)
        proj_ref[pl.ds(base, PB), :] = lax.dot_general(
            normed_ref[pl.ds(base, PB), :],
            weight_ref[...],
            NN,
            preferred_element_type=jnp.float32,
        ).astype(jnp.bfloat16)
        return carry

    lax.fori_loop(0, tokens // PB, project, 0)
    pieces[0].relay()
    pieces[1].start()

    def permute(step, carry):
        base = pl.multiple_of(step * PB, PB)
        picked = permute_rows(column_ref[pl.ds(base, PB), :], proj_ref[...], tokens)
        packed_ref[pl.ds(HALO + base, PB), :] = picked.astype(jnp.bfloat16)
        return carry

    lax.fori_loop(0, tokens // PB, permute, 0)
    pieces[0].finish()
    swap.start()
    share_cot.relay()

    unroll = 2

    def prepare(step, carry):
        for number in (1, 2):

            @pl.when(step == (0, 1, 5)[number])
            def _():
                pieces[number].relay()
                pieces[number + 1].start()

        places, stricts, kept_values = [], [], []
        for sub in range(unroll):
            block = step * unroll + sub
            first, second = retain_ref[2 * block], retain_ref[2 * block + 1]
            base = pl.multiple_of(block * BT, BT)
            masks = tap_masks(first, second, 1.0, BT)
            seen, kept = block_flags(first, second)
            rows, cols, cross = pair_mask(second)
            strengths = sigmoid(
                packed_ref[pl.ds(HALO + base, BT), 3 * heads * DK : 3 * heads * DK + BT].astype(
                    jnp.float32
                )
            )
            for head in range(heads):
                parts = []
                for kind in range(3):
                    at = (kind * heads + head) * DK
                    window = packed_ref[pl.ds(base, HALO + BT), at : at + DK].astype(jnp.float32)
                    taps = [
                        taps_ref[kind * CONV + back : kind * CONV + back + 1, head * DK : head * DK + DK]
                        for back in range(CONV)
                    ]
                    conv = conv_of(window, taps, masks)
                    parts.append(conv * sigmoid(conv))
                query, key, value = parts
                query = query * lax.rsqrt(
                    jnp.sum(query * query, axis=1, keepdims=True) + EPS_NORM
                ) * DK ** (-0.5)
                key = key * lax.rsqrt(jnp.sum(key * key, axis=1, keepdims=True) + EPS_NORM)
                query_low, key_low = query.astype(jnp.bfloat16), key.astype(jnp.bfloat16)
                query, key = query_low.astype(jnp.float32), key_low.astype(jnp.float32)
                beta = strengths[:, head : head + 1]
                inner = bdot(jnp.concatenate([key_low, query_low], axis=0), key_low, NT)
                stricts.append(jnp.where(rows > cols, inner[:BT] * cross * beta, 0.0))
                scores = jnp.where(rows >= cols, inner[BT:] * cross, 0.0)
                sides = jnp.concatenate([key * (beta * seen), value * beta], axis=1)
                kept_values.append((scores, sides, key * kept, query * seen))
                places.append(head * blocks + block)
        inverses = unit_lower_inverses(stricts, mask_ref)
        solved = [
            bdot(inverse, values[1]) for inverse, values in zip(inverses, kept_values)
        ]
        through = [bdot(values[0], both) for values, both in zip(kept_values, solved)]
        onward = [bdot(values[2], both, TN) for values, both in zip(kept_values, solved)]
        for index, place in enumerate(places):
            inverse_ref[place] = inverses[index].astype(jnp.bfloat16)
            big_ref[place, 0:BT, :] = onward[index][:, :DK].astype(jnp.bfloat16)
            big_ref[place, BT : 2 * BT, :] = solved[index][:, :DK].astype(jnp.bfloat16)
            big_ref[place, 2 * BT : 3 * BT, :] = (
                kept_values[index][3] - through[index][:, :DK]
            ).astype(jnp.bfloat16)
            add_ref[place] = onward[index][:, DK:]
            fresh_ref[place] = solved[index][:, DK:]
            own_ref[place] = through[index][:, DK:]
        return carry

    lax.fori_loop(0, blocks // unroll, prepare, 0)

    def advance(block, states):
        through = retain_ref[2 * block] * retain_ref[2 * block + 1]
        base = pl.multiple_of(block * BT, BT)
        lows = [state.astype(jnp.bfloat16) for state in states]
        products = [bdot(big_ref[head * blocks + block], lows[head]) for head in range(heads)]
        following = []
        for head in range(heads):
            place = head * blocks + block
            product = products[head]
            state_ref[place] = lows[head]
            following.append(states[head] * through - product[:BT] + add_ref[place])
            update_ref[place] = (fresh_ref[place] - product[BT : 2 * BT]).astype(jnp.bfloat16)
            delta = own_ref[place] + product[2 * BT :]
            delta_ref[pl.ds(base, BT), head * DK : head * DK + DK] = delta
            inv = lax.rsqrt(jnp.mean(delta * delta, axis=1, keepdims=True) + EPS_NORM)
            ready_ref[pl.ds(base, BT), head * DK : head * DK + DK] = (
                delta * inv * gain_ref[...]
            ).astype(jnp.bfloat16)
        return tuple(following)

    zero = jnp.zeros((DK, DK), jnp.float32)
    lax.fori_loop(0, blocks, advance, (zero,) * heads)

    pieces[3].relay()

    def hand_over(shift):
        target = (seq + shift) % n_seq
        base = aligned(target * own_tokens, own_tokens)
        for part in range(max(own_tokens // PB, 1)):
            size = min(own_tokens, PB)
            first = aligned(base + part * size, size)
            hot = jnp.where(
                row_ref[...] == iota((size, tokens), 0) + first, 1.0, 0.0
            ).astype(jnp.bfloat16)
            mixed_ref[pl.ds(first, size), :] = lax.dot_general(
                hot, ready_ref[...], NN, preferred_element_type=jnp.float32
            ).astype(jnp.bfloat16)
        source = mixed_ref.at[pl.ds(base, own_tokens)]
        slot = tokens_mixed.at[:, pl.ds(aligned(seq * heads * DK, heads * DK), heads * DK)]
        if shift == 0:
            return pltpu.make_async_copy(source, slot, local_sems.at[10])
        return pltpu.make_async_remote_copy(
            src_ref=source,
            dst_ref=slot,
            send_sem=share_send.at[2 * per_share + shift],
            recv_sem=share_recv.at[2 * per_share + shift],
            device_id=(target, lax.axis_index("fsdp")),
            device_id_type=MESH,
        )

    handed = []
    for shift in list(range(1, n_seq)) + [0]:
        copy = hand_over(shift)
        copy.start()
        handed.append(copy)
    for copy in handed:
        copy.wait()
    swap.wait()
    keep_normed.wait()
    keep_mixer.wait()
    share_cot.finish()
    for piece in pieces[1:]:
        piece.finish()


VMEM = pltpu.MemorySpace.VMEM
SMEM = pltpu.MemorySpace.SMEM


def spec(space=VMEM):
    return pl.BlockSpec(memory_space=space)


def mixer_forward(n_seq, n_fsdp, retain, column, row, taps, gain, shards):
    normed, mixer, gate, up, down, out, cot = shards
    own_tokens, model = normed.shape
    tokens = own_tokens * n_seq
    width = mixer.shape[1]
    heads = taps.shape[1] // DK
    blocks = tokens // BT
    count = heads * blocks
    low, full = jnp.bfloat16, jnp.float32
    per_gather, per_share = Gather.copies(n_fsdp), Share.copies(n_seq)
    gathers = 6 * per_gather
    shares = 2 * per_share + n_seq

    def whole(array):
        return jax.ShapeDtypeStruct((array.shape[0] * n_fsdp, array.shape[1]), low)

    return pl.pallas_call(
        functools.partial(mixer_forward_kernel, heads, n_seq, n_fsdp),
        out_shape=(
            jax.ShapeDtypeStruct((own_tokens, n_seq * heads * DK), low),
            jax.ShapeDtypeStruct((tokens, model), low),
            whole(mixer),
            whole(gate),
            whole(up),
            jax.ShapeDtypeStruct((n_fsdp,) + down.shape, low),
            whole(out),
            jax.ShapeDtypeStruct((tokens, model), low),
            jax.ShapeDtypeStruct((HALO + tokens, width), low),
            jax.ShapeDtypeStruct((tokens, heads * DK), full),
            jax.ShapeDtypeStruct((count, BT, BT), low),
            jax.ShapeDtypeStruct((count, 3 * BT, BT), low),
            jax.ShapeDtypeStruct((count, BT, BT), low),
            jax.ShapeDtypeStruct((count, BT, BT), low),
        ),
        in_specs=[spec(SMEM)] + [spec()] * 4 + [spec(ANY)] * 7,
        out_specs=(spec(ANY),) * 8 + (spec(),) * 6,
        scratch_shapes=[
            pltpu.VMEM((7, BT, BT), full),
            pltpu.VMEM((count, BT, BT), full),
            pltpu.VMEM((count, BT, BT), full),
            pltpu.VMEM((count, BT, BT), full),
            pltpu.VMEM((tokens, heads * DK), low),
            pltpu.VMEM((tokens, heads * DK), low),
            pltpu.VMEM((tokens, width), low),
            pltpu.VMEM((tokens, model), low),
            pltpu.VMEM((mixer.shape[0] * n_fsdp, width), low),
            pltpu.SemaphoreType.DMA((gathers,)),
            pltpu.SemaphoreType.DMA((gathers,)),
            pltpu.SemaphoreType.DMA((shares,)),
            pltpu.SemaphoreType.DMA((shares,)),
            pltpu.SemaphoreType.DMA((11,)),
        ],
        compiler_params=pltpu.CompilerParams(
            vmem_limit_bytes=60 << 20, collective_id=1, has_side_effects=True
        ),
        name="mixer_forward",
    )(retain, column, row, taps, gain, normed, mixer, gate, up, down, out, cot)


def mixer_backward_kernel(
    heads,
    retain_ref,
    column_ref,
    row_ref,
    grad_ref,
    packed_ref,
    taps_ref,
    gain_ref,
    delta_ref,
    inverse_ref,
    big_ref,
    update_ref,
    state_ref,
    out_ref,
    taps_out_ref,
    gain_out_ref,
    grad_delta_ref,
    add_ref,
    after_ref,
    conv_ref,
    grad_proj_ref,
):
    tokens = grad_ref.shape[0]
    blocks = tokens // BT
    width = 3 * heads * DK

    def head_norm(step, total):
        base = pl.multiple_of(step * PB, PB)
        picked = permute_rows(column_ref[pl.ds(base, PB), :], grad_ref[...], tokens)
        for head in range(heads):
            at = slice(head * DK, head * DK + DK)
            grad = picked[:, at]
            delta = delta_ref[pl.ds(base, PB), at]
            inv = lax.rsqrt(jnp.mean(delta * delta, axis=1, keepdims=True) + EPS_NORM)
            unit = delta * inv
            total = total + jnp.sum(grad * unit, axis=0, keepdims=True)
            grad_unit = grad * gain_ref[...]
            low = (
                inv * (grad_unit - unit * jnp.mean(grad_unit * unit, axis=1, keepdims=True))
            ).astype(jnp.bfloat16)
            grad_delta_ref[pl.ds(base, PB), at] = low
            for sub in range(PB // BT):
                place = head * blocks + step * (PB // BT) + sub
                add_ref[place] = bdot(
                    big_ref[place, 2 * BT : 3 * BT, :], low[sub * BT : sub * BT + BT], TN
                )
        return total

    gain_out_ref[...] = lax.fori_loop(
        0, tokens // PB, head_norm, jnp.zeros((1, DK), jnp.float32)
    )

    def retreat(step, grads):
        block = blocks - 1 - step
        through = retain_ref[2 * block] * retain_ref[2 * block + 1]
        lows = [grad.astype(jnp.bfloat16) for grad in grads]
        following = []
        for head in range(heads):
            place = head * blocks + block
            after_ref[place] = lows[head]
            following.append(
                grads[head] * through
                - bdot(big_ref[place, 0:BT, :], lows[head], TN)
                + add_ref[place]
            )
        return tuple(following)

    zero = jnp.zeros((DK, DK), jnp.float32)
    lax.fori_loop(0, blocks, retreat, (zero,) * heads)

    conv_ref[tokens : tokens + HALO, :] = jnp.zeros((HALO, width), jnp.float32)

    def gradients(block, carry):
        first, second = retain_ref[2 * block], retain_ref[2 * block + 1]
        base = pl.multiple_of(block * BT, BT)
        masks = tap_masks(first, second, 1.0, BT)
        seen, kept = block_flags(first, second)
        rows, cols, cross = pair_mask(second)
        _, _, _ = rows, cols, cross
        turned = jnp.where((rows < CH) & (cols >= CH), second, 1.0)
        lanes = iota((BT, BT), 1)
        strengths = sigmoid(
            packed_ref[pl.ds(HALO + base, BT), width : width + BT].astype(jnp.float32)
        )
        grad_strengths = jnp.zeros((BT, BT), jnp.float32)
        for head in range(heads):
            place = head * blocks + block
            convs, gates, acts = [], [], []
            for kind in range(3):
                at = (kind * heads + head) * DK
                window = packed_ref[pl.ds(base, HALO + BT), at : at + DK].astype(jnp.float32)
                taps = [
                    taps_ref[kind * CONV + back : kind * CONV + back + 1, head * DK : head * DK + DK]
                    for back in range(CONV)
                ]
                conv = conv_of(window, taps, masks)
                gate = sigmoid(conv)
                convs.append(conv)
                gates.append(gate)
                acts.append(conv * gate)
            inv_q = lax.rsqrt(jnp.sum(acts[0] * acts[0], axis=1, keepdims=True) + EPS_NORM)
            inv_k = lax.rsqrt(jnp.sum(acts[1] * acts[1], axis=1, keepdims=True) + EPS_NORM)
            query_low = (acts[0] * inv_q * DK ** (-0.5)).astype(jnp.bfloat16)
            key_low = (acts[1] * inv_k).astype(jnp.bfloat16)
            key = key_low.astype(jnp.float32)
            value = acts[2]
            beta = strengths[:, head : head + 1]
            grad_low = grad_delta_ref[pl.ds(base, BT), head * DK : head * DK + DK]
            after = after_ref[place]
            state = state_ref[place]
            update = update_ref[place]
            inner = bdot(key_low, jnp.concatenate([key_low, query_low], axis=0), NT)
            scores_t = jnp.where(rows <= cols, inner[:, BT:] * turned, 0.0)
            grad_update = bdot(scores_t, grad_low) + bdot(key * kept, after)
            solved = bdot(inverse_ref[place], grad_update, TN)
            solved_beta = solved * beta
            both = jnp.concatenate([grad_low, solved.astype(jnp.bfloat16)], axis=0)
            on_state = bdot(both, state, NT)
            on_update = bdot(both, update, NT)
            grad_scores = jnp.where(rows >= cols, on_update[:BT] * cross, 0.0)
            grad_strict = jnp.where(rows > cols, on_update[BT:] * cross, 0.0)
            grad_weighted = on_state[BT:] * seen
            turned_both = bdot(
                update,
                jnp.concatenate(
                    [grad_low, solved_beta.astype(jnp.bfloat16)], axis=0
                ),
                NT,
            )
            grad_scores_t = jnp.where(rows <= cols, turned_both[:, :BT] * turned, 0.0)
            strict_t = jnp.where(rows < cols, turned_both[:, BT:] * turned, 0.0)
            grad_query = on_state[:BT] * seen + bdot(grad_scores, key_low)
            grad_key = (
                bdot(grad_scores_t, query_low)
                + bdot(update, after, NT) * kept
                - beta * grad_weighted
                - bdot(grad_strict * beta + strict_t, key_low)
            )
            grad_value = solved_beta
            grad_beta = jnp.sum(
                solved * value - grad_strict * inner[:, :BT] - grad_weighted * key,
                axis=1,
                keepdims=True,
            )
            grad_strengths = jnp.where(lanes == head, grad_beta, grad_strengths)
            scaled = (
                inv_q
                * DK ** (-0.5)
                * (
                    grad_query
                    - acts[0]
                    * (inv_q * inv_q)
                    * jnp.sum(grad_query * acts[0], axis=1, keepdims=True)
                ),
                inv_k
                * (
                    grad_key
                    - acts[1] * (inv_k * inv_k) * jnp.sum(grad_key * acts[1], axis=1, keepdims=True)
                ),
                grad_value,
            )
            for kind in range(3):
                at = (kind * heads + head) * DK
                conv_ref[pl.ds(base, BT), at : at + DK] = (
                    scaled[kind] * gates[kind] * (1.0 + convs[kind] * (1.0 - gates[kind]))
                )
        grad_proj_ref[pl.ds(base, BT), width : width + BT] = (
            grad_strengths * strengths * (1.0 - strengths)
        ).astype(jnp.bfloat16)
        return carry

    lax.fori_loop(0, blocks, gradients, 0)

    taps_out_ref[...] = jnp.zeros(taps_out_ref.shape, jnp.float32)

    def conv_back(block, carry):
        first, second, third = (
            retain_ref[2 * block],
            retain_ref[2 * block + 1],
            retain_ref[2 * block + 2],
        )
        base = pl.multiple_of(block * BT, BT)
        masks = tap_masks(first, second, third, BT + HALO)
        for kind in range(3):
            for head in range(heads):
                at = (kind * heads + head) * DK
                grads = conv_ref[pl.ds(base, BT + HALO), at : at + DK]
                window = packed_ref[pl.ds(base, HALO + BT), at : at + DK].astype(jnp.float32)
                total = None
                for back in range(CONV):
                    row = kind * CONV + back
                    tap = taps_ref[row : row + 1, head * DK : head * DK + DK]
                    masked = grads if back == 0 else grads * masks[back]
                    shifted = (
                        masked if back == 0 else pltpu.roll(masked, BT + HALO - back, 0)
                    )[:BT]
                    total = shifted * tap if total is None else total + shifted * tap
                    past = (window if back == 0 else pltpu.roll(window, back, 0))[HALO:]
                    taps_out_ref[row : row + 1, head * DK : head * DK + DK] += jnp.sum(
                        masked[:BT] * past, axis=0, keepdims=True
                    )
                grad_proj_ref[pl.ds(base, BT), at : at + DK] = total.astype(jnp.bfloat16)
        return carry

    lax.fori_loop(0, blocks, conv_back, 0)

    def unpermute(step, carry):
        base = pl.multiple_of(step * PB, PB)
        out_ref[pl.ds(base, PB), :] = unpermute_rows(
            row_ref[...], base, grad_proj_ref[...], tokens
        ).astype(jnp.bfloat16)
        return carry

    lax.fori_loop(0, tokens // PB, unpermute, 0)


def mixer_backward(retain, column, row, grad_mixed, taps, gain, saved):
    packed, delta, inverse, big, update, state = saved
    tokens = grad_mixed.shape[0]
    width = packed.shape[1]
    heads = taps.shape[1] // DK
    count = heads * (tokens // BT)
    low, full = jnp.bfloat16, jnp.float32
    return pl.pallas_call(
        functools.partial(mixer_backward_kernel, heads),
        out_shape=(
            jax.ShapeDtypeStruct((tokens, width), low),
            jax.ShapeDtypeStruct(taps.shape, full),
            jax.ShapeDtypeStruct((1, DK), full),
        ),
        in_specs=[spec(SMEM)] + [spec()] * 11,
        out_specs=(spec(),) * 3,
        scratch_shapes=[
            pltpu.VMEM((tokens, heads * DK), low),
            pltpu.VMEM((count, BT, BT), full),
            pltpu.VMEM((count, BT, BT), low),
            pltpu.VMEM((tokens + HALO, 3 * heads * DK), full),
            pltpu.VMEM((tokens, width), low),
        ],
        compiler_params=pltpu.CompilerParams(vmem_limit_bytes=56 << 20),
        name="mixer_backward",
    )(retain, column, row, grad_mixed, packed, taps, gain, delta, inverse, big, update, state)


class Wire:
    def __init__(self, send, recv):
        self.send, self.recv, self.used = send, recv, 0

    def copy(self, source, target, seq, fsdp):
        index = self.used
        self.used += 1
        return pltpu.make_async_remote_copy(
            src_ref=source,
            dst_ref=target,
            send_sem=self.send.at[index],
            recv_sem=self.recv.at[index],
            device_id=(seq, fsdp),
            device_id_type=MESH,
        )


def ffn_copies(n_seq, parts):
    chips = n_seq // 2
    return parts * (2 + 4 * (chips - 1)) + parts * (n_seq - 1)


def ffn_kernel(
    n_seq,
    n_fsdp,
    tokens_ref,
    mixed_ref,
    out_ref,
    gain_ref,
    gate_in,
    up_in,
    down_in,
    cot_in,
    hidden_ref,
    grad_hidden_ref,
    heads_ref,
    result_ref,
    grad_gate_ref,
    grad_up_ref,
    grad_down_ref,
    grad_out_ref,
    grad_gain_ref,
    gate_ref,
    up_ref,
    down_ref,
    cot_ref,
    second_ref,
    second_t_ref,
    active_t_ref,
    lin_gate_ref,
    lin_up_ref,
    keep_ref,
    give_ref,
    from_mate_ref,
    reduce_ref,
    from_far_ref,
    attn_ref,
    mixed_grad_ref,
    stage_ref,
    send_sems,
    recv_sems,
    local_sems,
):
    own, model = tokens_ref.shape
    group = own * n_seq
    part = min(PB, own)
    parts = own // part
    chips = n_seq // 2
    seq, fsdp = lax.axis_index("seq"), lax.axis_index("fsdp")
    mate = seq + 1 - 2 * (seq % 2)
    units = gate_ref.shape[1]
    low = jnp.bfloat16

    loads = [
        pltpu.make_async_copy(source, target, local_sems.at[index])
        for index, (source, target) in enumerate(
            ((gate_in, gate_ref), (up_in, up_ref), (down_in, down_ref), (cot_in, cot_ref))
        )
    ]
    for load in loads:
        load.start()

    wire = Wire(send_sems, recv_sems)

    def far(step):
        return (seq + n_seq - 2 * step) % n_seq

    def rows(ref, shard, index):
        return ref.at[pl.ds(aligned(shard * own + index * part, part), part)]

    def local_rows(ref, index):
        return ref.at[pl.ds(index * part, part)]

    to_mate, across, passed, give_mate, give_far, reduced = {}, {}, {}, {}, {}, {}
    for index in range(parts):
        mine = rows(second_ref, seq, index)
        to_mate[index] = wire.copy(mine, mine, mate, fsdp)
        give_mate[index] = wire.copy(
            local_rows(give_ref.at[0], index), local_rows(from_mate_ref.at[0], index), mate, fsdp
        )
        for step in range(1, chips):
            across[step, index] = wire.copy(mine, mine, (seq + 2 * step) % n_seq, fsdp)
            there = rows(second_ref, far(step), index)
            passed[step, index] = wire.copy(there, there, mate, fsdp)
            give_far[step, index] = wire.copy(
                local_rows(give_ref.at[step], index),
                local_rows(from_mate_ref.at[step], index),
                mate,
                fsdp,
            )
            reduced[step, index] = wire.copy(
                local_rows(reduce_ref.at[step - 1], index),
                local_rows(from_far_ref.at[step - 1], index),
                far(step),
                fsdp,
            )

    greet_near(n_seq)

    for index in range(parts):
        at = slice(index * part, index * part + part)
        hidden = tokens_ref[at, :].astype(jnp.float32) + bdot(mixed_ref[at, :], out_ref[...])
        hidden_ref[at, :] = hidden
        inv = lax.rsqrt(jnp.mean(hidden * hidden, axis=1, keepdims=True) + EPS_NORM)
        second_ref[pl.ds(aligned(seq * own + index * part, part), part), :] = (
            hidden * inv * gain_ref[...]
        ).astype(low)
        for step in range(1, chips):
            across[step, index].start()
        to_mate[index].start()
    for load in loads:
        load.wait()

    count = n_seq * parts

    def block(number, carry):
        near = number < 2 * parts
        late = number - 2 * parts
        step_at = late // (2 * parts) + 1
        rest = late % (2 * parts)
        far_at = (seq + 2 * n_seq - 2 * step_at) % n_seq
        far_mate = far_at + 1 - 2 * (far_at % 2)
        shard = jnp.where(
            near,
            jnp.where(number < parts, seq, mate),
            jnp.where(rest % 2 == 0, far_mate, far_at),
        )
        index_at = jnp.where(near, number % parts, rest // 2)
        base = aligned(shard * own + index_at * part, part)

        for index in range(parts):

            @pl.when(number == parts + index)
            def _():
                to_mate[index].wait_recv()

            for step in range(1, chips):

                @pl.when(number == 2 * parts * step + 2 * index)
                def _():
                    across[step, index].wait_recv()
                    passed[step, index].start()
                    passed[step, index].wait_recv()

        second = second_ref[pl.ds(base, part), :]
        second_t_ref[:, pl.ds(base, part)] = second.T
        gate_lin = bdot(second, gate_ref[...])
        up_lin = bdot(second, up_ref[...])
        cot = cot_ref[pl.ds(base, part), :]
        grad_active = bdot(cot, down_ref[...], NT)
        gate_sig = sigmoid(gate_lin)
        silu = gate_lin * gate_sig
        active = (silu * up_lin).astype(low)
        active_t_ref[:, pl.ds(base, part)] = active.T
        grad_gate = (grad_active * up_lin * (gate_sig + silu * (1.0 - gate_sig))).astype(low)
        grad_up = (grad_active * silu).astype(low)
        lin_gate_ref[pl.ds(base, part), :] = grad_gate
        lin_up_ref[pl.ds(base, part), :] = grad_up
        grad_second = bdot(grad_gate, gate_ref[...], NT) + bdot(grad_up, up_ref[...], NT)
        stage_ref[...] = grad_second
        result_ref[pl.ds(base, part), :] = bdot(active, down_ref[...]).astype(low)

        for index in range(parts):
            at = slice(index * part, index * part + part)

            @pl.when(number == index)
            def _():
                keep_ref[at, :] = stage_ref[...]

            @pl.when(number == parts + index)
            def _():
                give_ref[0, at, :] = stage_ref[...].astype(low)
                give_mate[index].start()

            for step in range(1, chips):

                @pl.when(number == 2 * parts * step + 2 * index)
                def _():
                    give_ref[step, at, :] = stage_ref[...].astype(low)
                    give_far[step, index].start()

                @pl.when(number == 2 * parts * step + 2 * index + 1)
                def _():
                    give_far[step, index].wait_recv()
                    reduce_ref[step - 1, at, :] = (
                        stage_ref[...] + from_mate_ref[step, at, :].astype(jnp.float32)
                    ).astype(low)
                    reduced[step, index].start()

        return carry

    lax.fori_loop(0, count, block, 0)

    tile = 256

    def down_tile(number, carry):
        base = aligned(number * tile, tile)
        grad_down_ref[:, pl.ds(base, tile)] = bdot(
            active_t_ref[...], cot_ref[:, pl.ds(base, tile)]
        ).astype(low)
        return carry

    lax.fori_loop(0, model // tile, down_tile, 0)

    grad_gain_ref[...] = jnp.zeros(grad_gain_ref.shape, jnp.float32)
    width = model // n_seq
    handed = []
    for index in range(parts):
        at = slice(index * part, index * part + part)
        give_mate[index].wait_recv()
        total = keep_ref[at, :] + from_mate_ref[0, at, :].astype(jnp.float32)
        for step in range(1, chips):
            reduced[step, index].wait_recv()
            total = total + from_far_ref[step - 1, at, :].astype(jnp.float32)
        hidden = hidden_ref[at, :]
        inv = lax.rsqrt(jnp.mean(hidden * hidden, axis=1, keepdims=True) + EPS_NORM)
        unit = hidden * inv
        grad_gain_ref[...] += jnp.sum(total * unit, axis=0, keepdims=True)
        grad_unit = total * gain_ref[...]
        grad_hidden = inv * (
            grad_unit - unit * jnp.mean(grad_unit * unit, axis=1, keepdims=True)
        ) + cot_ref[pl.ds(aligned(seq * own + index * part, part), part), :].astype(jnp.float32)
        grad_hidden_ref[at, :] = grad_hidden
        attn = grad_hidden.astype(low)
        attn_ref[at, :] = attn
        mixed_grad_ref[at, :] = bdot(attn, out_ref[...], NT).astype(low)
        for shift in range(1, n_seq):
            target = (seq + shift) % n_seq
            copy = wire.copy(
                mixed_grad_ref.at[at, pl.ds(aligned(target * width, width), width)],
                rows(heads_ref, seq, index),
                target,
                fsdp,
            )
            copy.start()
            handed.append(copy)
        heads_ref[pl.ds(aligned(seq * own + index * part, part), part), :] = mixed_grad_ref[
            at, pl.ds(aligned(seq * width, width), width)
        ]

    def wide_tile(number, carry):
        base = aligned(number * tile, tile)
        turned = second_t_ref[pl.ds(base, tile), :]
        grad_gate_ref[pl.ds(base, tile), :] = bdot(turned, lin_gate_ref[...]).astype(low)
        grad_up_ref[pl.ds(base, tile), :] = bdot(turned, lin_up_ref[...]).astype(low)
        return carry

    lax.fori_loop(0, model // tile, wide_tile, 0)
    for base in range(0, model, tile):
        grad_out_ref[base : base + tile, :] = bdot(
            mixed_ref[:, base : base + tile], attn_ref[...], TN
        ).astype(low)

    for index in range(parts):
        to_mate[index].wait_send()
        give_mate[index].wait_send()
        for step in range(1, chips):
            across[step, index].wait_send()
            passed[step, index].wait_send()
            give_far[step, index].wait_send()
            reduced[step, index].wait_send()
    for copy in handed:
        copy.wait()


def greet_near(n_seq):
    seq, fsdp = lax.axis_index("seq"), lax.axis_index("fsdp")
    barrier = pltpu.get_barrier_semaphore()
    for step in range(1, n_seq):
        pl.semaphore_signal(
            barrier, inc=1, device_id=((seq + step) % n_seq, fsdp), device_id_type=MESH
        )
    pl.semaphore_wait(barrier, n_seq - 1)


def ffn_block(n_seq, n_fsdp, tokens, mixed, out, gain, gate, up, down, cot):
    own, model = tokens.shape
    group = own * n_seq
    units = gate.shape[1]
    chips = n_seq // 2
    low, full = jnp.bfloat16, jnp.float32
    part = min(PB, own)
    copies = ffn_copies(n_seq, own // part)

    def shape(dims, kind=low):
        return jax.ShapeDtypeStruct(dims, kind)

    return pl.pallas_call(
        functools.partial(ffn_kernel, n_seq, n_fsdp),
        out_shape=(
            shape((own, model), full),
            shape((own, model), full),
            shape((group, model // n_seq)),
            shape((group, model)),
            shape((model, units)),
            shape((model, units)),
            shape((units, model)),
            shape((model, model)),
            shape((1, model), full),
        ),
        in_specs=[spec()] * 4 + [spec(ANY)] * 4,
        out_specs=(spec(),) * 9,
        scratch_shapes=[
            pltpu.VMEM((model, units), low),
            pltpu.VMEM((model, units), low),
            pltpu.VMEM((units, model), low),
            pltpu.VMEM((group, model), low),
            pltpu.VMEM((group, model), low),
            pltpu.VMEM((model, group), low),
            pltpu.VMEM((units, group), low),
            pltpu.VMEM((group, units), low),
            pltpu.VMEM((group, units), low),
            pltpu.VMEM((own, model), full),
            pltpu.VMEM((chips, own, model), low),
            pltpu.VMEM((chips, own, model), low),
            pltpu.VMEM((chips - 1, own, model), low),
            pltpu.VMEM((chips - 1, own, model), low),
            pltpu.VMEM((own, model), low),
            pltpu.VMEM((own, model), low),
            pltpu.VMEM((part, model), full),
            pltpu.SemaphoreType.DMA((copies,)),
            pltpu.SemaphoreType.DMA((copies,)),
            pltpu.SemaphoreType.DMA((4,)),
        ],
        compiler_params=pltpu.CompilerParams(
            vmem_limit_bytes=63 << 20, collective_id=2, has_side_effects=True
        ),
        name="ffn",
    )(tokens, mixed, out, gain, gate, up, down, cot)


def matmul(first, second):
    return lax.dot_general(first, second, NN, preferred_element_type=jnp.float32)


def times_transposed(first, second):
    return lax.dot_general(first, second, NT, preferred_element_type=jnp.float32)


def contract_rows(first, second):
    return lax.dot_general(first, second, TN, preferred_element_type=jnp.float32)


def rms_forward(values, gain):
    inv_rms = lax.rsqrt(jnp.mean(values * values, axis=-1, keepdims=True) + EPS_NORM)
    unit_rows = values * inv_rms
    return (unit_rows * gain, unit_rows, inv_rms)


def rms_backward(grad_out, unit_rows, inv_rms, gain):
    grad_gain = jnp.sum(grad_out * unit_rows, axis=0)
    grad_unit = grad_out * gain
    grad_in = inv_rms * (
        grad_unit - unit_rows * jnp.mean(grad_unit * unit_rows, axis=-1, keepdims=True)
    )
    return (grad_in, grad_gain)


def retains(lengths, tokens):
    index = jnp.arange(lengths.shape[0])
    starts = jnp.sum(jnp.where(index[:, None] > index[None, :], lengths[None, :], 0), axis=1)
    spans = jnp.arange(tokens // CH, dtype=jnp.int32) * CH
    keep = 1.0 - jnp.any(starts[None, :] == spans[:, None], axis=1).astype(jnp.float32)
    return jnp.pad(keep, (0, 2))


def own_slice(array, place, size, axis):
    return lax.dynamic_slice_in_dim(array, place * size, size, axis)


def local(
    n_seq,
    n_fsdp,
    tokens,
    norm_gain,
    w_query,
    w_key,
    w_value,
    w_beta,
    conv_taps,
    head_gain,
    w_out,
    ffn_gain,
    w_gate,
    w_up,
    w_down,
    cotangent,
    token_order,
    seq_lengths,
):
    place = lax.axis_index("seq")
    model = tokens.shape[1]
    head_count = w_beta.shape[1]
    heads = head_count // n_seq
    width = heads * DK
    hidden_units = w_gate.shape[1]
    slab = hidden_units // (n_fsdp * n_seq)
    units = slab * n_fsdp
    own_rows = w_query.shape[0]

    def gather(array, axis_name, axis=0):
        return lax.all_gather(array, axis_name, axis=axis, tiled=True)

    def pick_units(array):
        split = array.reshape(array.shape[0], n_fsdp, n_seq, slab)
        return lax.dynamic_index_in_dim(split, place, 2, keepdims=False).reshape(-1, units)

    inputs = tokens.astype(jnp.float32)
    normed_f, unit_one, inv_one = rms_forward(inputs, norm_gain)
    group_tokens = tokens.shape[0] * n_seq
    mixer_shard = jnp.concatenate(
        [own_slice(array, place, width, 1) for array in (w_query, w_key, w_value)]
        + [jnp.pad(own_slice(w_beta, place, heads, 1), ((0, 0), (0, DK - heads)))],
        axis=1,
    )
    retain = retains(seq_lengths[0], group_tokens)
    column, row = token_order.reshape(-1, 1), token_order.reshape(1, -1)
    taps = own_slice(conv_taps, place, width, 2).reshape(3 * CONV, width)
    gain = head_gain.reshape(1, DK)
    mixed_tok, normed, w_mixer, full_gate, full_up, full_down, full_o, cot_all, *saved = (
        mixer_forward(
            n_seq,
            n_fsdp,
            retain,
            column,
            row,
            taps,
            gain,
            (
                normed_f.astype(jnp.bfloat16),
                mixer_shard,
                pick_units(w_gate),
                pick_units(w_up),
                own_slice(w_down, place, slab, 0),
                w_out,
                cotangent,
            ),
        )
    )
    full_down = full_down.reshape(units, model)
    (
        hidden,
        grad_hidden,
        grad_heads,
        result_part,
        wide_gate,
        wide_up,
        wide_down,
        wide_out,
        grad_ffn_gain,
    ) = ffn_block(
        n_seq,
        n_fsdp,
        tokens,
        mixed_tok,
        full_o,
        ffn_gain.reshape(1, model),
        full_gate,
        full_up,
        full_down,
        cot_all,
    )
    grad_ffn_gain = grad_ffn_gain[0]

    def spread(partial):
        pieces = lax.all_to_all(
            partial.astype(jnp.bfloat16).reshape(n_seq, -1, model),
            "seq",
            split_axis=0,
            concat_axis=0,
            tiled=True,
        )
        return jnp.sum(pieces.astype(jnp.float32), axis=0)

    result = (hidden + spread(result_part)).astype(jnp.bfloat16)

    def scatter(array):
        return lax.psum_scatter(
            array.astype(jnp.bfloat16), "fsdp", scatter_dimension=0, tiled=True
        )

    part_gate, part_up, part_down, part_out = (
        scatter(array) for array in (wide_gate, wide_up, wide_down, wide_out)
    )
    grad_proj, grad_taps, grad_gain = mixer_backward(
        retain, column, row, grad_heads, taps, gain, saved
    )
    grad_normed = spread(times_transposed(grad_proj, w_mixer))
    part_mixer = scatter(contract_rows(normed, grad_proj))
    grad_inputs, grad_norm_gain = rms_backward(grad_normed, unit_one, inv_one, norm_gain)
    grad_inputs = grad_inputs + grad_hidden

    all_mixer = gather(part_mixer[None], "seq").astype(jnp.float32)

    def mixer_columns(start, size):
        return (
            all_mixer[:, :, start : start + size].transpose(1, 0, 2).reshape(own_rows, n_seq * size)
        )

    sum_q, sum_k, sum_v = (mixer_columns(kind * width, width) for kind in range(3))
    sum_b = mixer_columns(3 * width, heads)

    def all_units(part):
        pieces = gather(part[None], "seq").astype(jnp.float32)
        return (
            pieces.reshape(n_seq, own_rows, n_fsdp, slab)
            .transpose(1, 2, 0, 3)
            .reshape(own_rows, hidden_units)
        )

    sum_gate, sum_up = all_units(part_gate), all_units(part_up)
    sum_down = gather(part_down, "seq").astype(jnp.float32)
    sum_out = lax.psum(part_out, "seq").astype(jnp.float32)
    conv_full = lax.dynamic_update_slice_in_dim(
        jnp.zeros_like(conv_taps), grad_taps.reshape(3, CONV, width), place * width, 2
    )
    norm_total, ffn_total, head_total, conv_total = lax.psum(
        (grad_norm_gain, grad_ffn_gain, grad_gain[0], conv_full), ("seq", "fsdp")
    )
    return (
        result,
        grad_inputs,
        norm_total,
        sum_q,
        sum_k,
        sum_v,
        sum_b,
        conv_total,
        head_total,
        sum_out,
        ffn_total,
        sum_gate,
        sum_up,
        sum_down,
    )


def solution(mesh):
    tokens = P(("seq", "fsdp"), None)
    rows = P("fsdp", None)
    in_specs = (
        (tokens, P()) + (rows,) * 4 + (P(), P(), rows, P()) + (rows,) * 3 + (tokens, rows, rows)
    )
    out_specs = (
        (tokens, tokens, P()) + (rows,) * 4 + (P(), P(), rows, P()) + (rows,) * 3
    )
    return jax.shard_map(
        functools.partial(local, mesh.shape["seq"], mesh.shape["fsdp"]),
        mesh=mesh,
        in_specs=in_specs,
        out_specs=out_specs,
        check_vma=False,
    )
```

```python
import functools

import jax
import jax.numpy as jnp
from jax import lax
from jax.experimental import pallas as pl
from jax.experimental.pallas import tpu as pltpu
from jax.sharding import PartitionSpec as P

DK = 128
CONV = 4
CH = 64
BT = 128
HALO = 16
PB = 256
EPS_NORM = 1e-06

NN = (((1,), (0,)), ((), ()))
NT = (((1,), (1,)), ((), ()))
TN = (((0,), (0,)), ((), ()))


def bdot(first, second, dims=NN):
    return lax.dot_general(
        first.astype(jnp.bfloat16),
        second.astype(jnp.bfloat16),
        dims,
        preferred_element_type=jnp.float32,
    )


def iota(shape, axis):
    return lax.broadcasted_iota(jnp.int32, shape, axis)


def sigmoid(values):
    return 1.0 / (1.0 + jnp.exp(-values))


def fill_masks(mask_ref):
    rows, cols = iota((BT, BT), 0), iota((BT, BT), 1)
    size, level = 1, 0
    while size < BT:
        inside = (rows // (2 * size) == cols // (2 * size)) & (rows // size > cols // size)
        mask_ref[level] = jnp.where(inside, 1.0, 0.0)
        size, level = 2 * size, level + 1


def unit_lower_inverses(stricts, mask_ref):
    rows, cols = iota((BT, BT), 0), iota((BT, BT), 1)
    eye = jnp.where(rows == cols, 1.0, 0.0)
    inverses = [eye - strict * mask_ref[0] for strict in stricts]
    for level in range(1, 7):
        lows = [inverse.astype(jnp.bfloat16) for inverse in inverses]
        inner = [bdot(strict * mask_ref[level], low) for strict, low in zip(stricts, lows)]
        inverses = [
            inverse - bdot(low, mid) for inverse, low, mid in zip(inverses, lows, inner)
        ]
    return inverses


def tap_masks(first, second, third, count):
    rows = iota((count, 1), 0)
    flag = jnp.where(rows < CH, first, jnp.where(rows < BT, second, third))
    return [None] + [jnp.where(rows % CH < back, flag, 1.0) for back in range(1, CONV)]


def conv_of(halo_rows, taps, masks):
    total = halo_rows[HALO:] * taps[0]
    for back in range(1, CONV):
        total = total + pltpu.roll(halo_rows, back, 0)[HALO:] * (taps[back] * masks[back])
    return total


def block_flags(first, second):
    upper = iota((BT, 1), 0) < CH
    seen = jnp.where(upper, first, first * second)
    kept = jnp.where(upper, second, 1.0)
    return seen, kept


def pair_mask(second):
    rows, cols = iota((BT, BT), 0), iota((BT, BT), 1)
    cross = (rows >= CH) & (cols < CH)
    return rows, cols, jnp.where(cross, second, 1.0)


def permute_rows(column, source, width):
    hot = jnp.where(column == iota((column.shape[0], width), 1), 1.0, 0.0).astype(jnp.bfloat16)
    return lax.dot_general(hot, source, NN, preferred_element_type=jnp.float32)


def unpermute_rows(row, base, source, width):
    hot = jnp.where(row == iota((PB, width), 0) + base, 1.0, 0.0).astype(jnp.bfloat16)
    return lax.dot_general(hot, source, NN, preferred_element_type=jnp.float32)


MESH = pl.DeviceIdType.MESH
ANY = pl.ANY


class Gather:
    outer = 4

    @classmethod
    def copies(cls, n_fsdp):
        inner = n_fsdp // cls.outer
        return (cls.outer - 1) + cls.outer * (inner - 1)

    def __init__(self, n_fsdp, source, slot, sems, base, local_sem):
        self.inner = n_fsdp // self.outer
        self.me = lax.axis_index("fsdp")
        self.seq = lax.axis_index("seq")
        self.high, self.low = self.me // self.inner, self.me % self.inner
        self.source, self.slot = source, slot
        self.send, self.recv = sems
        self.base, self.local_sem = base, local_sem

    def at(self, high, low):
        return (high % self.outer) * self.inner + (low % self.inner)

    def copy(self, source, owner, target, index):
        return pltpu.make_async_remote_copy(
            src_ref=source,
            dst_ref=self.slot(owner),
            send_sem=self.send.at[self.base + index],
            recv_sem=self.recv.at[self.base + index],
            device_id=(self.seq, target),
            device_id_type=MESH,
        )

    def along_outer(self, step):
        return self.copy(self.source, self.me, self.at(self.high + step, self.low), step - 1)

    def along_inner(self, hop):
        return self.copy(
            self.source, self.me, self.at(self.high, self.low + hop), self.outer - 2 + hop
        )

    def passed_on(self, step, hop):
        owner = self.at(self.high - step, self.low)
        index = self.outer - 1 + (self.inner - 1) * step + hop - 1
        return self.copy(self.slot(owner), owner, self.at(self.high, self.low + hop), index)

    def own(self):
        return pltpu.make_async_copy(self.source, self.slot(self.me), self.local_sem)

    def start(self):
        for step in range(1, self.outer):
            self.along_outer(step).start()
        for hop in range(1, self.inner):
            self.along_inner(hop).start()
        self.own().start()

    def relay(self):
        for step in range(1, self.outer):
            self.along_outer(step).wait_recv()
            for hop in range(1, self.inner):
                self.passed_on(step, hop).start()

    def finish(self):
        self.own().wait()
        for hop in range(1, self.inner):
            self.along_inner(hop).wait_recv()
            for step in range(1, self.outer):
                self.passed_on(step, hop).wait_recv()
        for step in range(1, self.outer):
            self.along_outer(step).wait_send()
        for hop in range(1, self.inner):
            self.along_inner(hop).wait_send()
            for step in range(1, self.outer):
                self.passed_on(step, hop).wait_send()


class Share:
    @staticmethod
    def copies(n_seq):
        return 1 + 2 * (n_seq // 2 - 1)

    def __init__(self, n_seq, source, slot, sems, base, local_sem):
        self.n_seq, self.chips = n_seq, n_seq // 2
        self.me = lax.axis_index("seq")
        self.fsdp = lax.axis_index("fsdp")
        self.mate = self.me + 1 - 2 * (self.me % 2)
        self.source, self.slot = source, slot
        self.send, self.recv = sems
        self.base, self.local_sem = base, local_sem

    def copy(self, source, owner, target, index):
        return pltpu.make_async_remote_copy(
            src_ref=source,
            dst_ref=self.slot(owner),
            send_sem=self.send.at[self.base + index],
            recv_sem=self.recv.at[self.base + index],
            device_id=(target, self.fsdp),
            device_id_type=MESH,
        )

    def to_mate(self):
        return self.copy(self.source, self.me, self.mate, 0)

    def across(self, step):
        return self.copy(self.source, self.me, (self.me + 2 * step) % self.n_seq, step)

    def passed_on(self, step):
        owner = (self.me + self.n_seq - 2 * step) % self.n_seq
        return self.copy(self.slot(owner), owner, self.mate, self.chips - 1 + step)

    def own(self):
        return pltpu.make_async_copy(self.source, self.slot(self.me), self.local_sem)

    def start(self):
        for step in range(1, self.chips):
            self.across(step).start()
        self.to_mate().start()
        self.own().start()

    def relay(self):
        for step in range(1, self.chips):
            self.across(step).wait_recv()
            self.passed_on(step).start()

    def finish(self):
        self.own().wait()
        self.to_mate().wait_recv()
        for step in range(1, self.chips):
            self.passed_on(step).wait_recv()
        self.to_mate().wait_send()
        for step in range(1, self.chips):
            self.across(step).wait_send()
            self.passed_on(step).wait_send()


def greet(n_seq, n_fsdp):
    seq, fsdp = lax.axis_index("seq"), lax.axis_index("fsdp")
    barrier = pltpu.get_barrier_semaphore()
    for step in range(1, n_seq):
        pl.semaphore_signal(
            barrier, inc=1, device_id=((seq + step) % n_seq, fsdp), device_id_type=MESH
        )
    for step in range(1, n_fsdp):
        pl.semaphore_signal(
            barrier, inc=1, device_id=(seq, (fsdp + step) % n_fsdp), device_id_type=MESH
        )
    pl.semaphore_wait(barrier, n_seq + n_fsdp - 2)


def aligned(value, unit):
    return pl.multiple_of(value, unit)


def mixer_forward_kernel(
    heads,
    n_seq,
    n_fsdp,
    retain_ref,
    column_ref,
    row_ref,
    taps_ref,
    gain_ref,
    normed_in,
    mixer_in,
    gate_in,
    up_in,
    down_in,
    out_in,
    cot_in,
    tokens_mixed,
    normed_all,
    mixer_all,
    gate_all,
    up_all,
    down_all,
    out_all,
    cot_all,
    packed_ref,
    delta_ref,
    inverse_ref,
    keep_big,
    update_ref,
    state_ref,
    big_ref,
    mask_ref,
    fresh_ref,
    own_ref,
    add_ref,
    mixed_ref,
    ready_ref,
    proj_ref,
    normed_ref,
    weight_ref,
    gather_send,
    gather_recv,
    share_send,
    share_recv,
    local_sems,
):
    tokens, width = proj_ref.shape
    blocks = tokens // BT
    own_tokens = tokens // n_seq
    seq = lax.axis_index("seq")
    own_rows = mixer_in.shape[0]
    half_rows = own_rows // 2
    out_rows, out_width = out_in.shape
    half_width = out_width // 2
    core = seq % 2

    greet(n_seq, n_fsdp)

    gather_sems = (gather_send, gather_recv)
    share_sems = (share_send, share_recv)
    per_gather = Gather.copies(n_fsdp)
    per_share = Share.copies(n_seq)

    def rows_slot(ref, size, start=0, count=None):
        count = size if count is None else count
        return lambda owner: ref.at[pl.ds(aligned(owner * size + start, count), count)]

    def gather_piece(index, source, slot):
        return Gather(
            n_fsdp, source, slot, gather_sems, index * per_gather, local_sems.at[index]
        )

    mixers = [
        gather_piece(
            part,
            mixer_in.at[pl.ds(part * half_rows, half_rows)],
            rows_slot(weight_ref, own_rows, part * half_rows, half_rows),
        )
        for part in range(2)
    ]
    half_at = aligned(core * half_width, half_width)
    pieces = [
        gather_piece(
            2,
            out_in.at[:, pl.ds(half_at, half_width)],
            lambda owner: out_all.at[
                pl.ds(aligned(owner * out_rows, out_rows), out_rows), pl.ds(half_at, half_width)
            ],
        ),
        gather_piece(3, gate_in, rows_slot(gate_all, own_rows)),
        gather_piece(4, up_in, rows_slot(up_all, own_rows)),
        gather_piece(5, down_in, lambda owner: down_all.at[owner]),
    ]
    share_normed = Share(
        n_seq, normed_in, rows_slot(normed_ref, own_tokens), share_sems, 0, local_sems.at[6]
    )
    share_cot = Share(
        n_seq, cot_in, rows_slot(cot_all, own_tokens), share_sems, per_share, local_sems.at[7]
    )
    swap = pltpu.make_async_remote_copy(
        src_ref=out_all.at[:, pl.ds(half_at, half_width)],
        dst_ref=out_all.at[:, pl.ds(half_at, half_width)],
        send_sem=share_send.at[2 * per_share],
        recv_sem=share_recv.at[2 * per_share],
        device_id=(share_normed.mate, lax.axis_index("fsdp")),
        device_id_type=MESH,
    )

    mixers[0].start()
    share_normed.start()
    fill_masks(mask_ref)
    packed_ref[0:HALO, :] = jnp.zeros((HALO, packed_ref.shape[1]), jnp.bfloat16)
    mixers[0].relay()
    mixers[1].start()
    share_normed.relay()
    mixers[1].relay()
    pieces[0].start()
    share_cot.start()
    mixers[0].finish()
    mixers[1].finish()
    share_normed.finish()
    keep_normed = pltpu.make_async_copy(normed_ref, normed_all, local_sems.at[8])
    keep_mixer = pltpu.make_async_copy(weight_ref, mixer_all, local_sems.at[9])
    keep_normed.start()
    keep_mixer.start()

    def project(step, carry):
        base = aligned(step * PB, PB)
        proj_ref[pl.ds(base, PB), :] = lax.dot_general(
            normed_ref[pl.ds(base, PB), :],
            weight_ref[...],
            NN,
            preferred_element_type=jnp.float32,
        ).astype(jnp.bfloat16)
        return carry

    lax.fori_loop(0, tokens // PB, project, 0)
    pieces[0].relay()
    pieces[1].start()

    def permute(step, carry):
        base = pl.multiple_of(step * PB, PB)
        picked = permute_rows(column_ref[pl.ds(base, PB), :], proj_ref[...], tokens)
        packed_ref[pl.ds(HALO + base, PB), :] = picked.astype(jnp.bfloat16)
        return carry

    lax.fori_loop(0, tokens // PB, permute, 0)
    pieces[0].finish()
    swap.start()
    share_cot.relay()

    unroll = 2

    def prepare(step, carry):
        for number in (1, 2):

            @pl.when(step == (0, 1, 5)[number])
            def _():
                pieces[number].relay()
                pieces[number + 1].start()

        places, stricts, kept_values = [], [], []
        for sub in range(unroll):
            block = step * unroll + sub
            first, second = retain_ref[2 * block], retain_ref[2 * block + 1]
            base = pl.multiple_of(block * BT, BT)
            masks = tap_masks(first, second, 1.0, BT)
            seen, kept = block_flags(first, second)
            rows, cols, cross = pair_mask(second)
            strengths = sigmoid(
                packed_ref[pl.ds(HALO + base, BT), 3 * heads * DK : 3 * heads * DK + BT].astype(
                    jnp.float32
                )
            )
            for head in range(heads):
                parts = []
                for kind in range(3):
                    at = (kind * heads + head) * DK
                    window = packed_ref[pl.ds(base, HALO + BT), at : at + DK].astype(jnp.float32)
                    taps = [
                        taps_ref[kind * CONV + back : kind * CONV + back + 1, head * DK : head * DK + DK]
                        for back in range(CONV)
                    ]
                    conv = conv_of(window, taps, masks)
                    parts.append(conv * sigmoid(conv))
                query, key, value = parts
                query = query * lax.rsqrt(
                    jnp.sum(query * query, axis=1, keepdims=True) + EPS_NORM
                ) * DK ** (-0.5)
                key = key * lax.rsqrt(jnp.sum(key * key, axis=1, keepdims=True) + EPS_NORM)
                query_low, key_low = query.astype(jnp.bfloat16), key.astype(jnp.bfloat16)
                query, key = query_low.astype(jnp.float32), key_low.astype(jnp.float32)
                beta = strengths[:, head : head + 1]
                inner = bdot(jnp.concatenate([key_low, query_low], axis=0), key_low, NT)
                stricts.append(jnp.where(rows > cols, inner[:BT] * cross * beta, 0.0))
                scores = jnp.where(rows >= cols, inner[BT:] * cross, 0.0)
                sides = jnp.concatenate([key * (beta * seen), value * beta], axis=1)
                kept_values.append((scores, sides, key * kept, query * seen))
                places.append(head * blocks + block)
        inverses = unit_lower_inverses(stricts, mask_ref)
        solved = [
            bdot(inverse, values[1]) for inverse, values in zip(inverses, kept_values)
        ]
        through = [bdot(values[0], both) for values, both in zip(kept_values, solved)]
        onward = [bdot(values[2], both, TN) for values, both in zip(kept_values, solved)]
        for index, place in enumerate(places):
            inverse_ref[place] = inverses[index].astype(jnp.bfloat16)
            big_ref[place, 0:BT, :] = onward[index][:, :DK].astype(jnp.bfloat16)
            big_ref[place, BT : 2 * BT, :] = (
                kept_values[index][3] - through[index][:, :DK]
            ).astype(jnp.bfloat16)
            big_ref[place, 2 * BT : 3 * BT, :] = solved[index][:, :DK].astype(jnp.bfloat16)
            add_ref[place] = onward[index][:, DK:]
            fresh_ref[place] = solved[index][:, DK:]
            own_ref[place] = through[index][:, DK:]
        return carry

    lax.fori_loop(0, blocks // unroll, prepare, 0)

    def advance(block, states):
        through = retain_ref[2 * block] * retain_ref[2 * block + 1]
        base = pl.multiple_of(block * BT, BT)
        lows = [state.astype(jnp.bfloat16) for state in states]
        products = [bdot(big_ref[head * blocks + block], lows[head]) for head in range(heads)]
        following = []
        for head in range(heads):
            place = head * blocks + block
            product = products[head]
            state_ref[place] = lows[head]
            following.append(states[head] * through - product[:BT] + add_ref[place])
            update_ref[place] = (fresh_ref[place] - product[2 * BT :]).astype(jnp.bfloat16)
            delta = own_ref[place] + product[BT : 2 * BT]
            delta_ref[pl.ds(base, BT), head * DK : head * DK + DK] = delta
            inv = lax.rsqrt(jnp.mean(delta * delta, axis=1, keepdims=True) + EPS_NORM)
            ready_ref[pl.ds(base, BT), head * DK : head * DK + DK] = (
                delta * inv * gain_ref[...]
            ).astype(jnp.bfloat16)
        return tuple(following)

    zero = jnp.zeros((DK, DK), jnp.float32)
    lax.fori_loop(0, blocks, advance, (zero,) * heads)

    pieces[3].relay()
    keep_parts = pltpu.make_async_copy(
        big_ref.at[:, pl.ds(0, 2 * BT), :], keep_big, local_sems.at[11]
    )
    keep_parts.start()

    def hand_over(shift):
        target = (seq + shift) % n_seq
        base = aligned(target * own_tokens, own_tokens)
        for part in range(max(own_tokens // PB, 1)):
            size = min(own_tokens, PB)
            first = aligned(base + part * size, size)
            hot = jnp.where(
                row_ref[...] == iota((size, tokens), 0) + first, 1.0, 0.0
            ).astype(jnp.bfloat16)
            mixed_ref[pl.ds(first, size), :] = lax.dot_general(
                hot, ready_ref[...], NN, preferred_element_type=jnp.float32
            ).astype(jnp.bfloat16)
        source = mixed_ref.at[pl.ds(base, own_tokens)]
        slot = tokens_mixed.at[:, pl.ds(aligned(seq * heads * DK, heads * DK), heads * DK)]
        if shift == 0:
            return pltpu.make_async_copy(source, slot, local_sems.at[10])
        return pltpu.make_async_remote_copy(
            src_ref=source,
            dst_ref=slot,
            send_sem=share_send.at[2 * per_share + shift],
            recv_sem=share_recv.at[2 * per_share + shift],
            device_id=(target, lax.axis_index("fsdp")),
            device_id_type=MESH,
        )

    handed = []
    for shift in list(range(1, n_seq)) + [0]:
        copy = hand_over(shift)
        copy.start()
        handed.append(copy)
    for copy in handed:
        copy.wait()
    swap.wait()
    keep_normed.wait()
    keep_mixer.wait()
    keep_parts.wait()
    share_cot.finish()
    for piece in pieces[1:]:
        piece.finish()


VMEM = pltpu.MemorySpace.VMEM
SMEM = pltpu.MemorySpace.SMEM


def spec(space=VMEM):
    return pl.BlockSpec(memory_space=space)


def mixer_forward(n_seq, n_fsdp, retain, column, row, taps, gain, shards):
    normed, mixer, gate, up, down, out, cot = shards
    own_tokens, model = normed.shape
    tokens = own_tokens * n_seq
    width = mixer.shape[1]
    heads = taps.shape[1] // DK
    blocks = tokens // BT
    count = heads * blocks
    low, full = jnp.bfloat16, jnp.float32
    per_gather, per_share = Gather.copies(n_fsdp), Share.copies(n_seq)
    gathers = 6 * per_gather
    shares = 2 * per_share + n_seq

    def whole(array):
        return jax.ShapeDtypeStruct((array.shape[0] * n_fsdp, array.shape[1]), low)

    return pl.pallas_call(
        functools.partial(mixer_forward_kernel, heads, n_seq, n_fsdp),
        out_shape=(
            jax.ShapeDtypeStruct((own_tokens, n_seq * heads * DK), low),
            jax.ShapeDtypeStruct((tokens, model), low),
            whole(mixer),
            whole(gate),
            whole(up),
            jax.ShapeDtypeStruct((n_fsdp,) + down.shape, low),
            whole(out),
            jax.ShapeDtypeStruct((tokens, model), low),
            jax.ShapeDtypeStruct((HALO + tokens, width), low),
            jax.ShapeDtypeStruct((tokens, heads * DK), full),
            jax.ShapeDtypeStruct((count, BT, BT), low),
            jax.ShapeDtypeStruct((count, 2 * BT, BT), low),
            jax.ShapeDtypeStruct((count, BT, BT), low),
            jax.ShapeDtypeStruct((count, BT, BT), low),
        ),
        in_specs=[spec(SMEM)] + [spec()] * 4 + [spec(ANY)] * 7,
        out_specs=(spec(ANY),) * 8 + (spec(),) * 3 + (spec(ANY),) + (spec(),) * 2,
        scratch_shapes=[
            pltpu.VMEM((count, 3 * BT, BT), low),
            pltpu.VMEM((7, BT, BT), full),
            pltpu.VMEM((count, BT, BT), full),
            pltpu.VMEM((count, BT, BT), full),
            pltpu.VMEM((count, BT, BT), full),
            pltpu.VMEM((tokens, heads * DK), low),
            pltpu.VMEM((tokens, heads * DK), low),
            pltpu.VMEM((tokens, width), low),
            pltpu.VMEM((tokens, model), low),
            pltpu.VMEM((mixer.shape[0] * n_fsdp, width), low),
            pltpu.SemaphoreType.DMA((gathers,)),
            pltpu.SemaphoreType.DMA((gathers,)),
            pltpu.SemaphoreType.DMA((shares,)),
            pltpu.SemaphoreType.DMA((shares,)),
            pltpu.SemaphoreType.DMA((12,)),
        ],
        compiler_params=pltpu.CompilerParams(
            vmem_limit_bytes=60 << 20, collective_id=1, has_side_effects=True
        ),
        name="mixer_forward",
    )(retain, column, row, taps, gain, normed, mixer, gate, up, down, out, cot)


class Wire:
    def __init__(self, send, recv):
        self.send, self.recv, self.used = send, recv, 0

    def copy(self, source, target, seq, fsdp):
        index = self.used
        self.used += 1
        return pltpu.make_async_remote_copy(
            src_ref=source,
            dst_ref=target,
            send_sem=self.send.at[index],
            recv_sem=self.recv.at[index],
            device_id=(seq, fsdp),
            device_id_type=MESH,
        )


def ffn_copies(n_seq, parts):
    chips = n_seq // 2
    return parts * (2 + 4 * (chips - 1)) + parts * (n_seq - 1)


def ffn_kernel(
    n_seq,
    n_fsdp,
    tokens_ref,
    mixed_ref,
    out_ref,
    gain_ref,
    gate_in,
    up_in,
    down_in,
    cot_in,
    hidden_ref,
    grad_hidden_ref,
    heads_ref,
    result_ref,
    grad_gate_ref,
    grad_up_ref,
    grad_down_ref,
    grad_out_ref,
    grad_gain_ref,
    gate_ref,
    up_ref,
    down_ref,
    cot_ref,
    second_ref,
    second_t_ref,
    active_t_ref,
    lin_gate_ref,
    lin_up_ref,
    keep_ref,
    give_ref,
    from_mate_ref,
    reduce_ref,
    from_far_ref,
    attn_ref,
    mixed_grad_ref,
    stage_ref,
    send_sems,
    recv_sems,
    local_sems,
):
    own, model = tokens_ref.shape
    group = own * n_seq
    part = min(PB, own)
    parts = own // part
    chips = n_seq // 2
    seq, fsdp = lax.axis_index("seq"), lax.axis_index("fsdp")
    mate = seq + 1 - 2 * (seq % 2)
    units = gate_ref.shape[1]
    low = jnp.bfloat16

    loads = [
        pltpu.make_async_copy(source, target, local_sems.at[index])
        for index, (source, target) in enumerate(
            ((gate_in, gate_ref), (up_in, up_ref), (down_in, down_ref), (cot_in, cot_ref))
        )
    ]
    for load in loads:
        load.start()

    wire = Wire(send_sems, recv_sems)

    def far(step):
        return (seq + n_seq - 2 * step) % n_seq

    def rows(ref, shard, index):
        return ref.at[pl.ds(aligned(shard * own + index * part, part), part)]

    def local_rows(ref, index):
        return ref.at[pl.ds(index * part, part)]

    to_mate, across, passed, give_mate, give_far, reduced = {}, {}, {}, {}, {}, {}
    for index in range(parts):
        mine = rows(second_ref, seq, index)
        to_mate[index] = wire.copy(mine, mine, mate, fsdp)
        give_mate[index] = wire.copy(
            local_rows(give_ref.at[0], index), local_rows(from_mate_ref.at[0], index), mate, fsdp
        )
        for step in range(1, chips):
            across[step, index] = wire.copy(mine, mine, (seq + 2 * step) % n_seq, fsdp)
            there = rows(second_ref, far(step), index)
            passed[step, index] = wire.copy(there, there, mate, fsdp)
            give_far[step, index] = wire.copy(
                local_rows(give_ref.at[step], index),
                local_rows(from_mate_ref.at[step], index),
                mate,
                fsdp,
            )
            reduced[step, index] = wire.copy(
                local_rows(reduce_ref.at[step - 1], index),
                local_rows(from_far_ref.at[step - 1], index),
                far(step),
                fsdp,
            )

    greet_near(n_seq)

    for index in range(parts):
        at = slice(index * part, index * part + part)
        hidden = tokens_ref[at, :].astype(jnp.float32) + bdot(mixed_ref[at, :], out_ref[...])
        hidden_ref[at, :] = hidden
        inv = lax.rsqrt(jnp.mean(hidden * hidden, axis=1, keepdims=True) + EPS_NORM)
        second_ref[pl.ds(aligned(seq * own + index * part, part), part), :] = (
            hidden * inv * gain_ref[...]
        ).astype(low)
        for step in range(1, chips):
            across[step, index].start()
        to_mate[index].start()
    for load in loads:
        load.wait()

    count = n_seq * parts

    def block(number, carry):
        near = number < 2 * parts
        late = number - 2 * parts
        step_at = late // (2 * parts) + 1
        rest = late % (2 * parts)
        far_at = (seq + 2 * n_seq - 2 * step_at) % n_seq
        far_mate = far_at + 1 - 2 * (far_at % 2)
        shard = jnp.where(
            near,
            jnp.where(number < parts, seq, mate),
            jnp.where(rest % 2 == 0, far_mate, far_at),
        )
        index_at = jnp.where(near, number % parts, rest // 2)
        base = aligned(shard * own + index_at * part, part)

        for index in range(parts):

            @pl.when(number == parts + index)
            def _():
                to_mate[index].wait_recv()

            for step in range(1, chips):

                @pl.when(number == 2 * parts * step + 2 * index)
                def _():
                    across[step, index].wait_recv()
                    passed[step, index].start()
                    passed[step, index].wait_recv()

        second = second_ref[pl.ds(base, part), :]
        second_t_ref[:, pl.ds(base, part)] = second.T
        gate_lin = bdot(second, gate_ref[...])
        up_lin = bdot(second, up_ref[...])
        cot = cot_ref[pl.ds(base, part), :]
        grad_active = bdot(cot, down_ref[...], NT)
        gate_sig = sigmoid(gate_lin)
        silu = gate_lin * gate_sig
        active = (silu * up_lin).astype(low)
        active_t_ref[:, pl.ds(base, part)] = active.T
        grad_gate = (grad_active * up_lin * (gate_sig + silu * (1.0 - gate_sig))).astype(low)
        grad_up = (grad_active * silu).astype(low)
        lin_gate_ref[pl.ds(base, part), :] = grad_gate
        lin_up_ref[pl.ds(base, part), :] = grad_up
        grad_second = bdot(grad_gate, gate_ref[...], NT) + bdot(grad_up, up_ref[...], NT)
        stage_ref[...] = grad_second
        result_ref[pl.ds(base, part), :] = bdot(active, down_ref[...]).astype(low)

        for index in range(parts):
            at = slice(index * part, index * part + part)

            @pl.when(number == index)
            def _():
                keep_ref[at, :] = stage_ref[...]

            @pl.when(number == parts + index)
            def _():
                give_ref[0, at, :] = stage_ref[...].astype(low)
                give_mate[index].start()

            for step in range(1, chips):

                @pl.when(number == 2 * parts * step + 2 * index)
                def _():
                    give_ref[step, at, :] = stage_ref[...].astype(low)
                    give_far[step, index].start()

                @pl.when(number == 2 * parts * step + 2 * index + 1)
                def _():
                    give_far[step, index].wait_recv()
                    reduce_ref[step - 1, at, :] = (
                        stage_ref[...] + from_mate_ref[step, at, :].astype(jnp.float32)
                    ).astype(low)
                    reduced[step, index].start()

        return carry

    lax.fori_loop(0, count, block, 0)

    tile = 256

    def down_tile(number, carry):
        base = aligned(number * tile, tile)
        grad_down_ref[:, pl.ds(base, tile)] = bdot(
            active_t_ref[...], cot_ref[:, pl.ds(base, tile)]
        ).astype(low)
        return carry

    lax.fori_loop(0, model // tile, down_tile, 0)

    grad_gain_ref[...] = jnp.zeros(grad_gain_ref.shape, jnp.float32)
    width = model // n_seq
    handed = []
    for index in range(parts):
        at = slice(index * part, index * part + part)
        give_mate[index].wait_recv()
        total = keep_ref[at, :] + from_mate_ref[0, at, :].astype(jnp.float32)
        for step in range(1, chips):
            reduced[step, index].wait_recv()
            total = total + from_far_ref[step - 1, at, :].astype(jnp.float32)
        hidden = hidden_ref[at, :]
        inv = lax.rsqrt(jnp.mean(hidden * hidden, axis=1, keepdims=True) + EPS_NORM)
        unit = hidden * inv
        grad_gain_ref[...] += jnp.sum(total * unit, axis=0, keepdims=True)
        grad_unit = total * gain_ref[...]
        grad_hidden = inv * (
            grad_unit - unit * jnp.mean(grad_unit * unit, axis=1, keepdims=True)
        ) + cot_ref[pl.ds(aligned(seq * own + index * part, part), part), :].astype(jnp.float32)
        grad_hidden_ref[at, :] = grad_hidden
        attn = grad_hidden.astype(low)
        attn_ref[at, :] = attn
        mixed_grad_ref[at, :] = bdot(attn, out_ref[...], NT).astype(low)
        for shift in range(1, n_seq):
            target = (seq + shift) % n_seq
            copy = wire.copy(
                mixed_grad_ref.at[at, pl.ds(aligned(target * width, width), width)],
                rows(heads_ref, seq, index),
                target,
                fsdp,
            )
            copy.start()
            handed.append(copy)
        heads_ref[pl.ds(aligned(seq * own + index * part, part), part), :] = mixed_grad_ref[
            at, pl.ds(aligned(seq * width, width), width)
        ]

    def wide_tile(number, carry):
        base = aligned(number * tile, tile)
        turned = second_t_ref[pl.ds(base, tile), :]
        grad_gate_ref[pl.ds(base, tile), :] = bdot(turned, lin_gate_ref[...]).astype(low)
        grad_up_ref[pl.ds(base, tile), :] = bdot(turned, lin_up_ref[...]).astype(low)
        return carry

    lax.fori_loop(0, model // tile, wide_tile, 0)
    for base in range(0, model, tile):
        grad_out_ref[base : base + tile, :] = bdot(
            mixed_ref[:, base : base + tile], attn_ref[...], TN
        ).astype(low)

    for index in range(parts):
        to_mate[index].wait_send()
        give_mate[index].wait_send()
        for step in range(1, chips):
            across[step, index].wait_send()
            passed[step, index].wait_send()
            give_far[step, index].wait_send()
            reduced[step, index].wait_send()
    for copy in handed:
        copy.wait()


def greet_near(n_seq):
    seq, fsdp = lax.axis_index("seq"), lax.axis_index("fsdp")
    barrier = pltpu.get_barrier_semaphore()
    for step in range(1, n_seq):
        pl.semaphore_signal(
            barrier, inc=1, device_id=((seq + step) % n_seq, fsdp), device_id_type=MESH
        )
    pl.semaphore_wait(barrier, n_seq - 1)


def ffn_block(n_seq, n_fsdp, tokens, mixed, out, gain, gate, up, down, cot):
    own, model = tokens.shape
    group = own * n_seq
    units = gate.shape[1]
    chips = n_seq // 2
    low, full = jnp.bfloat16, jnp.float32
    part = min(PB, own)
    copies = ffn_copies(n_seq, own // part)

    def shape(dims, kind=low):
        return jax.ShapeDtypeStruct(dims, kind)

    return pl.pallas_call(
        functools.partial(ffn_kernel, n_seq, n_fsdp),
        out_shape=(
            shape((own, model), full),
            shape((own, model), full),
            shape((group, model // n_seq)),
            shape((group, model)),
            shape((model, units)),
            shape((model, units)),
            shape((units, model)),
            shape((model, model)),
            shape((1, model), full),
        ),
        in_specs=[spec()] * 4 + [spec(ANY)] * 4,
        out_specs=(spec(),) * 9,
        scratch_shapes=[
            pltpu.VMEM((model, units), low),
            pltpu.VMEM((model, units), low),
            pltpu.VMEM((units, model), low),
            pltpu.VMEM((group, model), low),
            pltpu.VMEM((group, model), low),
            pltpu.VMEM((model, group), low),
            pltpu.VMEM((units, group), low),
            pltpu.VMEM((group, units), low),
            pltpu.VMEM((group, units), low),
            pltpu.VMEM((own, model), full),
            pltpu.VMEM((chips, own, model), low),
            pltpu.VMEM((chips, own, model), low),
            pltpu.VMEM((chips - 1, own, model), low),
            pltpu.VMEM((chips - 1, own, model), low),
            pltpu.VMEM((own, model), low),
            pltpu.VMEM((own, model), low),
            pltpu.VMEM((part, model), full),
            pltpu.SemaphoreType.DMA((copies,)),
            pltpu.SemaphoreType.DMA((copies,)),
            pltpu.SemaphoreType.DMA((4,)),
        ],
        compiler_params=pltpu.CompilerParams(
            vmem_limit_bytes=63 << 20, collective_id=2, has_side_effects=True
        ),
        name="ffn",
    )(tokens, mixed, out, gain, gate, up, down, cot)


class Scatter:
    outer = 4

    @classmethod
    def copies(cls, n_fsdp):
        return cls.outer * (n_fsdp // cls.outer - 1) + cls.outer - 1

    def __init__(self, n_fsdp, wire, block, own, first, second):
        self.inner = n_fsdp // self.outer
        me = lax.axis_index("fsdp")
        seq = lax.axis_index("seq")
        self.high, self.low = me // self.inner, me % self.inner
        self.own, self.first, self.second = own, first, second
        self.near, self.away = [], []
        for hop in range(1, self.inner):
            lower = (self.low + hop) % self.inner
            for high in range(self.outer):
                self.near.append(
                    wire.copy(
                        block(high * self.inner + lower),
                        first.at[(hop - 1) * self.outer + high],
                        seq,
                        self.high * self.inner + lower,
                    )
                )
        for step in range(1, self.outer):
            higher = (self.high + step) % self.outer
            self.away.append(
                wire.copy(own(higher), second.at[step - 1], seq, higher * self.inner + self.low)
            )

    def start(self):
        for copy in self.near:
            copy.start()

    def combine(self):
        for copy in self.near:
            copy.wait_recv()
        for high in range(self.outer):
            block = self.own(high)
            total = block[...].astype(jnp.float32)
            for hop in range(1, self.inner):
                total = total + self.first[(hop - 1) * self.outer + high].astype(jnp.float32)
            block[...] = total.astype(jnp.bfloat16)
        for copy in self.away:
            copy.start()

    def total(self):
        for copy in self.away:
            copy.wait_recv()
        total = self.own(self.high)[...].astype(jnp.float32)
        for step in range(1, self.outer):
            total = total + self.second[step - 1].astype(jnp.float32)
        return total.astype(jnp.bfloat16)

    def drain(self):
        for copy in self.near + self.away:
            copy.wait_send()


CHUNK = 64


class SeqSum:
    def __init__(self, n_seq, wire, give, mine, from_mate, from_far):
        self.chips = n_seq // 2
        seq, fsdp = lax.axis_index("seq"), lax.axis_index("fsdp")
        mate = seq + 1 - 2 * (seq % 2)
        self.mine, self.from_mate, self.from_far = mine, from_mate, from_far
        self.gives = [
            wire.copy(give(step), from_mate.at[step], mate, fsdp) for step in range(self.chips)
        ]
        self.across = [
            wire.copy(
                mine(step),
                from_far.at[step - 1],
                (seq + n_seq - 2 * step) % n_seq,
                fsdp,
            )
            for step in range(1, self.chips)
        ]

    def reduce(self, step):
        self.gives[step].wait_recv()
        mine = self.mine(step)

        def add(number, carry):
            at = pl.ds(aligned(number * CHUNK, CHUNK), CHUNK)
            mine[at, :] = (
                mine[at, :].astype(jnp.float32) + self.from_mate[step, at, :].astype(jnp.float32)
            ).astype(jnp.bfloat16)
            return carry

        lax.fori_loop(0, mine.shape[0] // CHUNK, add, 0)
        self.across[step - 1].start()

    def arrive(self):
        self.gives[0].wait_recv()
        for copy in self.across:
            copy.wait_recv()

    def total(self, at):
        total = self.mine(0)[at, :].astype(jnp.float32) + self.from_mate[0, at, :].astype(
            jnp.float32
        )
        for step in range(1, self.chips):
            total = total + self.from_far[step - 1, at, :].astype(jnp.float32)
        return total

    def drain(self):
        for copy in self.gives + self.across:
            copy.wait_send()


def split_columns(width):
    first = (width // DK + 1) // 2 * DK
    return ((0, first), (first, width - first))


def mixer_backward_kernel(
    heads,
    n_seq,
    n_fsdp,
    retain_ref,
    column_ref,
    row_ref,
    grad_ref,
    taps_ref,
    gain_ref,
    delta_ref,
    inverse_ref,
    big_ref,
    update_ref,
    state_ref,
    norm_gain_ref,
    ffn_gain_ref,
    packed_in,
    normed_in,
    weight_in,
    tokens_in,
    hidden_in,
    grad_hidden_in,
    result_in,
    gate_in,
    up_in,
    down_in,
    out_in,
    result_out,
    tokens_out,
    gate_out,
    up_out,
    down_out,
    out_out,
    mixer_out,
    small_out,
    norm_out,
    packed_ref,
    grad_delta_ref,
    add_ref,
    after_ref,
    conv_ref,
    grad_proj_ref,
    arrived_ref,
    weight_ref,
    weight_grad_ref,
    wide_ref,
    tokens_ref,
    result_ref,
    result_mine,
    result_mate,
    result_far,
    normed_mine,
    normed_give,
    normed_mate,
    normed_far,
    gate_own,
    gate_first,
    gate_second,
    up_own,
    up_first,
    up_second,
    down_own,
    down_first,
    down_second,
    out_sum,
    out_mate,
    out_first,
    out_second,
    out_far,
    mixer_first_a,
    mixer_second_a,
    mixer_first_b,
    mixer_second_b,
    gate_total,
    up_total,
    down_total,
    out_total,
    mixer_total,
    small_ref,
    small_all,
    norm_ref,
    norm_all,
    send_sems,
    recv_sems,
    gather_send,
    gather_recv,
    share_send,
    share_recv,
    local_sems,
):
    tokens = grad_ref.shape[0]
    blocks = tokens // BT
    width = 3 * heads * DK
    own = tokens // n_seq
    model = tokens_ref.shape[1]
    own_rows = gate_own.shape[1]
    seq, fsdp = lax.axis_index("seq"), lax.axis_index("fsdp")
    mate = seq + 1 - 2 * (seq % 2)
    core = seq % 2
    chip = seq // 2
    chips = n_seq // 2
    inner = n_fsdp // Scatter.outer
    inner_low = fsdp % inner
    low, full = jnp.bfloat16, jnp.float32

    local = {}

    def bring(name, source, target):
        copy = pltpu.make_async_copy(source, target, local_sems.at[len(local)])
        local[name] = copy
        return copy

    def far(step):
        return (seq + n_seq - 2 * step) % n_seq

    def far_mate(step):
        there = far(step)
        return there + 1 - 2 * (there % 2)

    def shard(ref, index):
        return ref.at[pl.ds(aligned(index * own, own), own)]

    bring("packed", packed_in, packed_ref.at[:, pl.ds(0, packed_in.shape[1])]).start()
    wire = Wire(send_sems, recv_sems)
    result_sum = SeqSum(
        n_seq,
        wire,
        lambda step: shard(result_in, mate if step == 0 else far_mate(step)),
        lambda step: result_mine.at[step],
        result_mate,
        result_far,
    )
    normed_sum = SeqSum(
        n_seq,
        wire,
        lambda step: normed_give.at[step],
        lambda step: normed_mine.at[step],
        normed_mate,
        normed_far,
    )
    half = out_sum.shape[1]
    out_rows = out_sum.shape[0] // n_fsdp
    half_at = pl.ds(aligned(core * half, half), half)
    out_give = wire.copy(
        out_in.at[:, pl.ds(aligned((1 - core) * half, half), half)], out_mate, mate, fsdp
    )

    def rows_of(ref, size):
        return lambda owner: ref.at[pl.ds(aligned(owner * size, size), size)]

    def held(ref):
        return lambda high: ref.at[high]

    gate_sum = Scatter(
        n_fsdp, wire, rows_of(gate_in, own_rows), held(gate_own), gate_first, gate_second
    )
    up_sum = Scatter(n_fsdp, wire, rows_of(up_in, own_rows), held(up_own), up_first, up_second)
    down_sum = Scatter(
        n_fsdp, wire, lambda owner: down_in.at[owner], held(down_own), down_first, down_second
    )
    out_scatter = Scatter(
        n_fsdp,
        wire,
        rows_of(out_sum, out_rows),
        lambda high: rows_of(out_sum, out_rows)(high * inner + inner_low),
        out_first,
        out_second,
    )
    spans = split_columns(width + DK)

    def mixer_block(span):
        return lambda owner: weight_grad_ref.at[
            pl.ds(aligned(owner * own_rows, own_rows), own_rows), pl.ds(span[0], span[1])
        ]

    mixer_sums = [
        Scatter(
            n_fsdp,
            wire,
            mixer_block(span),
            (lambda at: lambda high: at(high * inner + inner_low))(mixer_block(span)),
            first,
            second,
        )
        for span, first, second in (
            (spans[0], mixer_first_a, mixer_second_a),
            (spans[1], mixer_first_b, mixer_second_b),
        )
    ]
    out_across = [
        wire.copy(out_far.at[chip], out_far.at[chip], (seq + 2 * step) % n_seq, fsdp)
        for step in range(1, chips)
    ]
    out_swap = wire.copy(out_total, out_out.at[:, half_at], mate, fsdp)

    share_sems = (share_send, share_recv)
    gather_sems = (gather_send, gather_recv)
    per_share, per_gather = Share.copies(n_seq), Gather.copies(n_fsdp)

    def share(index, source, ref):
        return Share(
            n_seq,
            source,
            lambda owner: ref.at[owner],
            share_sems,
            index * per_share,
            local_sems.at[50 + index],
        )

    gate_share = share(0, gate_total, gate_out)
    up_share = share(1, up_total, up_out)
    down_share = share(2, down_total, down_out)
    mixer_shares = [
        Share(
            n_seq,
            mixer_total.at[:, pl.ds(span[0], span[1])],
            (lambda place: lambda owner: mixer_out.at[owner, :, place])(pl.ds(span[0], span[1])),
            share_sems,
            (3 + index) * per_share,
            local_sems.at[53 + index],
        )
        for index, span in enumerate(spans)
    ]
    small_share = share(5, small_ref, small_out)
    norm_share = share(6, norm_ref, norm_out)
    small_gather = Gather(
        n_fsdp,
        small_ref,
        lambda owner: small_all.at[owner],
        gather_sems,
        0,
        local_sems.at[57],
    )
    norm_gather = Gather(
        n_fsdp,
        norm_ref,
        lambda owner: norm_all.at[owner],
        gather_sems,
        per_gather,
        local_sems.at[58],
    )

    for high in range(Scatter.outer):
        owner = high * inner + inner_low
        bring(("gate", high), rows_of(gate_in, own_rows)(owner), gate_own.at[high]).start()
        bring(("up", high), rows_of(up_in, own_rows)(owner), up_own.at[high]).start()
        bring(("down", high), down_in.at[owner], down_own.at[high]).start()
    bring("out", out_in.at[:, half_at], out_sum).start()
    bring("result", shard(result_in, seq), result_mine.at[0]).start()
    for step in range(1, chips):
        bring(("result", step), shard(result_in, far(step)), result_mine.at[step]).start()
    bring("hidden", hidden_in, wide_ref).start()

    greet(n_seq, n_fsdp)
    gate_sum.start()
    for copy in result_sum.gives:
        copy.start()
    out_give.start()

    def head_norm(step, total):
        base = pl.multiple_of(step * PB, PB)
        picked = permute_rows(column_ref[pl.ds(base, PB), :], grad_ref[...], tokens)
        for head in range(heads):
            at = slice(head * DK, head * DK + DK)
            grad = picked[:, at]
            delta = delta_ref[pl.ds(base, PB), at]
            inv = lax.rsqrt(jnp.mean(delta * delta, axis=1, keepdims=True) + EPS_NORM)
            unit = delta * inv
            total = total + jnp.sum(grad * unit, axis=0, keepdims=True)
            grad_unit = grad * gain_ref[...]
            shrunk = (
                inv * (grad_unit - unit * jnp.mean(grad_unit * unit, axis=1, keepdims=True))
            ).astype(low)
            grad_delta_ref[pl.ds(base, PB), at] = shrunk
            for sub in range(PB // BT):
                place = head * blocks + step * (PB // BT) + sub
                add_ref[place] = bdot(
                    big_ref[place, BT : 2 * BT, :], shrunk[sub * BT : sub * BT + BT], TN
                ).astype(low)
        return total

    small_ref[...] = jnp.zeros(small_ref.shape, full)
    small_ref[0:1, :] = ffn_gain_ref[...]
    small_ref[1:2, 0:DK] = lax.fori_loop(0, tokens // PB, head_norm, jnp.zeros((1, DK), full))

    for high in range(Scatter.outer):
        local["gate", high].wait()
    gate_sum.combine()
    up_sum.start()
    for step in range(1, chips):
        local["result", step].wait()
        result_sum.reduce(step)

    def retreat(step, grads):
        block = blocks - 1 - step
        through = retain_ref[2 * block] * retain_ref[2 * block + 1]
        lows = [grad.astype(low) for grad in grads]
        following = []
        for head in range(heads):
            place = head * blocks + block
            after_ref[place] = lows[head]
            following.append(
                grads[head] * through
                - bdot(big_ref[place, 0:BT, :], lows[head], TN)
                + add_ref[place].astype(full)
            )
        return tuple(following)

    zero = jnp.zeros((DK, DK), full)
    lax.fori_loop(0, blocks, retreat, (zero,) * heads)
    local["packed"].wait()

    conv_ref[BT : BT + HALO, :] = jnp.zeros((HALO, width), full)

    def up_stage():
        for high in range(Scatter.outer):
            local["up", high].wait()
        up_sum.combine()
        down_sum.start()
        gate_total[...] = gate_sum.total()
        gate_share.start()

    def add_out():
        local["out"].wait()
        out_give.wait_recv()

        def add(number, carry):
            at = pl.ds(aligned(number * CHUNK, CHUNK), CHUNK)
            out_sum[at, :] = (out_sum[at, :].astype(full) + out_mate[at, :].astype(full)).astype(
                low
            )
            return carry

        lax.fori_loop(0, out_sum.shape[0] // CHUNK, add, 0)

    def down_stage():
        for high in range(Scatter.outer):
            local["down", high].wait()
        down_sum.combine()
        out_scatter.start()
        gate_share.relay()
        up_total[...] = up_sum.total()
        up_share.start()

    def result_stage():
        local["hidden"].wait()
        local["result"].wait()
        result_sum.arrive()

        def add(number, carry):
            at = pl.ds(aligned(number * CHUNK, CHUNK), CHUNK)
            result_ref[at, :] = (wide_ref[at, :] + result_sum.total(at)).astype(low)
            return carry

        lax.fori_loop(0, own // CHUNK, add, 0)

    def gradients(step, carry):
        for moment, stage in ((3, up_stage), (6, add_out), (10, down_stage), (13, result_stage)):

            @pl.when(step == moment)
            def _():
                stage()

        block = blocks - 1 - step
        first, second, third = (
            retain_ref[2 * block],
            retain_ref[2 * block + 1],
            retain_ref[2 * block + 2],
        )
        base = pl.multiple_of(block * BT, BT)
        masks = tap_masks(first, second, third, BT + HALO)
        near_masks = [None] + [mask[:BT] for mask in masks[1:]]
        seen, kept = block_flags(first, second)
        rows, cols, cross = pair_mask(second)
        turned = jnp.where((rows < CH) & (cols >= CH), second, 1.0)
        lanes = iota((BT, BT), 1)
        strengths = sigmoid(
            packed_ref[pl.ds(HALO + base, BT), width : width + BT].astype(jnp.float32)
        )
        grad_strengths = jnp.zeros((BT, BT), jnp.float32)
        for head in range(heads):
            place = head * blocks + block
            convs, gates, acts = [], [], []
            for kind in range(3):
                at = (kind * heads + head) * DK
                window = packed_ref[pl.ds(base, HALO + BT), at : at + DK].astype(jnp.float32)
                taps = [
                    taps_ref[kind * CONV + back : kind * CONV + back + 1, head * DK : head * DK + DK]
                    for back in range(CONV)
                ]
                conv = conv_of(window, taps, near_masks)
                gate = sigmoid(conv)
                convs.append(conv)
                gates.append(gate)
                acts.append(conv * gate)
            inv_q = lax.rsqrt(jnp.sum(acts[0] * acts[0], axis=1, keepdims=True) + EPS_NORM)
            inv_k = lax.rsqrt(jnp.sum(acts[1] * acts[1], axis=1, keepdims=True) + EPS_NORM)
            query_low = (acts[0] * inv_q * DK ** (-0.5)).astype(jnp.bfloat16)
            key_low = (acts[1] * inv_k).astype(jnp.bfloat16)
            key = key_low.astype(jnp.float32)
            value = acts[2]
            beta = strengths[:, head : head + 1]
            grad_low = grad_delta_ref[pl.ds(base, BT), head * DK : head * DK + DK]
            after = after_ref[place]
            state = state_ref[place]
            update = update_ref[place]
            inner = bdot(key_low, jnp.concatenate([key_low, query_low], axis=0), NT)
            scores_t = jnp.where(rows <= cols, inner[:, BT:] * turned, 0.0)
            grad_update = bdot(scores_t, grad_low) + bdot(key * kept, after)
            solved = bdot(inverse_ref[place], grad_update, TN)
            solved_beta = solved * beta
            both = jnp.concatenate([grad_low, solved.astype(jnp.bfloat16)], axis=0)
            on_state = bdot(both, state, NT)
            on_update = bdot(both, update, NT)
            grad_scores = jnp.where(rows >= cols, on_update[:BT] * cross, 0.0)
            grad_strict = jnp.where(rows > cols, on_update[BT:] * cross, 0.0)
            grad_weighted = on_state[BT:] * seen
            turned_both = bdot(
                update,
                jnp.concatenate(
                    [grad_low, solved_beta.astype(jnp.bfloat16)], axis=0
                ),
                NT,
            )
            grad_scores_t = jnp.where(rows <= cols, turned_both[:, :BT] * turned, 0.0)
            strict_t = jnp.where(rows < cols, turned_both[:, BT:] * turned, 0.0)
            grad_query = on_state[:BT] * seen + bdot(grad_scores, key_low)
            grad_key = (
                bdot(grad_scores_t, query_low)
                + bdot(update, after, NT) * kept
                - beta * grad_weighted
                - bdot(grad_strict * beta + strict_t, key_low)
            )
            grad_value = solved_beta
            grad_beta = jnp.sum(
                solved * value - grad_strict * inner[:, :BT] - grad_weighted * key,
                axis=1,
                keepdims=True,
            )
            grad_strengths = jnp.where(lanes == head, grad_beta, grad_strengths)
            scaled = (
                inv_q
                * DK ** (-0.5)
                * (
                    grad_query
                    - acts[0]
                    * (inv_q * inv_q)
                    * jnp.sum(grad_query * acts[0], axis=1, keepdims=True)
                ),
                inv_k
                * (
                    grad_key
                    - acts[1] * (inv_k * inv_k) * jnp.sum(grad_key * acts[1], axis=1, keepdims=True)
                ),
                grad_value,
            )
            for kind in range(3):
                at = (kind * heads + head) * DK
                conv_ref[0:BT, at : at + DK] = (
                    scaled[kind] * gates[kind] * (1.0 + convs[kind] * (1.0 - gates[kind]))
                )
        grad_proj_ref[pl.ds(base, BT), width : width + BT] = (
            grad_strengths * strengths * (1.0 - strengths)
        ).astype(jnp.bfloat16)
        for kind in range(3):
            for head in range(heads):
                at = (kind * heads + head) * DK
                span = slice(head * DK, head * DK + DK)
                grads = conv_ref[:, at : at + DK]
                window = packed_ref[pl.ds(base, HALO + BT), at : at + DK].astype(jnp.float32)
                total = None
                for back in range(CONV):
                    row = kind * CONV + back
                    tap = taps_ref[row : row + 1, span]
                    masked = grads if back == 0 else grads * masks[back]
                    shifted = (
                        masked if back == 0 else pltpu.roll(masked, BT + HALO - back, 0)
                    )[:BT]
                    total = shifted * tap if total is None else total + shifted * tap
                    past = (window if back == 0 else pltpu.roll(window, back, 0))[HALO:]
                    small_ref[2 + row : 3 + row, span] += jnp.sum(
                        masked[:BT] * past, axis=0, keepdims=True
                    )
                grad_proj_ref[pl.ds(base, BT), at : at + DK] = total.astype(jnp.bfloat16)
        conv_ref[BT : BT + HALO, :] = conv_ref[0:HALO, :]
        return carry

    lax.fori_loop(0, blocks, gradients, 0)

    bring("keep_result", result_ref, result_out).start()
    bring("normed", normed_in, packed_ref.at[pl.ds(0, tokens)]).start()
    bring("weight", weight_in, weight_ref).start()
    bring("grad_hidden", grad_hidden_in, wide_ref).start()
    bring("tokens", tokens_in, tokens_ref).start()
    out_scatter.combine()
    small_gather.start()
    up_share.relay()
    down_total[...] = down_sum.total()
    down_share.start()

    def unpermute(index):
        part = min(PB, own)

        def step(number, carry):
            base = aligned(index * own + number * part, part)
            hot = jnp.where(row_ref[...] == iota((part, tokens), 0) + base, 1.0, 0.0).astype(low)
            arrived_ref[pl.ds(base, part), :] = lax.dot_general(
                hot, grad_proj_ref[...], NN, preferred_element_type=jnp.float32
            ).astype(low)
            return carry

        lax.fori_loop(0, own // part, step, 0)

    def push_back(index, target):
        part = min(PB, own)

        def step(number, carry):
            base = aligned(index * own + number * part, part)
            target[pl.ds(aligned(number * part, part), part), :] = bdot(
                arrived_ref[pl.ds(base, part), :], weight_ref[...], NT
            ).astype(low)
            return carry

        lax.fori_loop(0, own // part, step, 0)

    waited = False
    for step in range(1, chips):
        unpermute(far_mate(step))
        if not waited:
            local["weight"].wait()
            waited = True
        push_back(far_mate(step), normed_give.at[step])
        normed_sum.gives[step].start()
        unpermute(far(step))
        push_back(far(step), normed_mine.at[step])
        normed_sum.reduce(step)
    unpermute(mate)
    unpermute(seq)
    if not waited:
        local["weight"].wait()
    small_gather.relay()
    local["normed"].wait()

    def weight_grad(span):
        def step(number, carry):
            at = pl.ds(aligned(number * PB, PB), PB)
            weight_grad_ref[at, pl.ds(span[0], span[1])] = bdot(
                packed_ref[0:tokens, at], arrived_ref[:, pl.ds(span[0], span[1])], TN
            ).astype(low)
            return carry

        lax.fori_loop(0, model // PB, step, 0)

    weight_grad(spans[0])
    mixer_sums[0].start()
    weight_grad(spans[1])
    mixer_sums[1].start()
    push_back(mate, normed_give.at[0])
    normed_sum.gives[0].start()
    push_back(seq, normed_mine.at[0])

    out_far[chip] = out_scatter.total()
    for copy in out_across:
        copy.start()
    down_share.relay()
    small_gather.finish()
    total = small_all[0]
    for owner in range(1, n_fsdp):
        total = total + small_all[owner]
    small_ref[...] = total
    small_share.start()
    mixer_sums[0].combine()
    for copy in out_across:
        copy.wait_recv()
    total = out_far[0].astype(full)
    for index in range(1, chips):
        total = total + out_far[index].astype(full)
    out_total[...] = total.astype(low)
    out_swap.start()
    bring("keep_out", out_total, out_out.at[:, half_at]).start()

    local["grad_hidden"].wait()
    local["tokens"].wait()
    normed_sum.arrive()

    def norm_back(number, total):
        at = pl.ds(aligned(number * CHUNK, CHUNK), CHUNK)
        values = tokens_ref[at, :].astype(full)
        inv = lax.rsqrt(jnp.mean(values * values, axis=1, keepdims=True) + EPS_NORM)
        unit = values * inv
        grad = normed_sum.total(at)
        grad_unit = grad * norm_gain_ref[...]
        wide_ref[at, :] += inv * (
            grad_unit - unit * jnp.mean(grad_unit * unit, axis=1, keepdims=True)
        )
        return total + jnp.sum(grad * unit, axis=0, keepdims=True)

    norm_ref[...] = jnp.zeros(norm_ref.shape, full)
    norm_ref[0:1, :] = lax.fori_loop(0, own // CHUNK, norm_back, jnp.zeros((1, model), full))
    bring("keep_tokens", wide_ref, tokens_out).start()
    norm_gather.start()
    small_share.relay()
    mixer_sums[1].combine()
    norm_gather.relay()
    mixer_total[:, spans[0][0] : spans[0][0] + spans[0][1]] = mixer_sums[0].total()
    mixer_shares[0].start()
    norm_gather.finish()
    total = norm_all[0]
    for owner in range(1, n_fsdp):
        total = total + norm_all[owner]
    norm_ref[...] = total
    norm_share.start()
    mixer_shares[0].relay()
    norm_share.relay()
    mixer_total[:, spans[1][0] : spans[1][0] + spans[1][1]] = mixer_sums[1].total()
    mixer_shares[1].start()
    mixer_shares[1].relay()
    for each in [gate_share, up_share, down_share, small_share, norm_share] + mixer_shares:
        each.finish()
    for each in [gate_sum, up_sum, down_sum, out_scatter] + mixer_sums + [result_sum, normed_sum]:
        each.drain()
    for copy in out_across:
        copy.wait_send()
    out_give.wait_send()
    out_swap.wait()
    for name in ("keep_result", "keep_out", "keep_tokens"):
        local[name].wait()


def mixer_backward(n_seq, n_fsdp, small, saved, big):
    (retain, column, row, grad_heads, taps, gain, norm_gain, ffn_gain) = small
    packed, delta, inverse, parts, update, state = saved
    normed, weight, own_tokens, hidden, grad_hidden, result, gate, up, down, out = big
    tokens = grad_heads.shape[0]
    width = packed.shape[1]
    heads = taps.shape[1] // DK
    count = heads * (tokens // BT)
    own, model = own_tokens.shape
    units = gate.shape[1]
    own_rows = gate.shape[0] // n_fsdp
    slab = down.shape[1]
    out_rows = out.shape[0] // n_fsdp
    half = out.shape[1] // 2
    chips = n_seq // 2
    outer = Scatter.outer
    near = outer * (n_fsdp // outer - 1)
    low, full = jnp.bfloat16, jnp.float32
    spans = split_columns(width)
    copies = 6 * Scatter.copies(n_fsdp) + 2 * (2 * chips - 1) + 2 + chips - 1
    shares, gathers = 7 * Share.copies(n_seq), 2 * Gather.copies(n_fsdp)

    def shape(dims, kind=low):
        return jax.ShapeDtypeStruct(dims, kind)

    def sum_buffers(rows, cols):
        return [pltpu.VMEM((near, rows, cols), low), pltpu.VMEM((outer - 1, rows, cols), low)]

    def block_buffers(rows, cols):
        return [pltpu.VMEM((outer, rows, cols), low)] + sum_buffers(rows, cols)

    return pl.pallas_call(
        functools.partial(mixer_backward_kernel, heads, n_seq, n_fsdp),
        out_shape=(
            shape((own, model)),
            shape((own, model), full),
            shape((n_seq, own_rows, units)),
            shape((n_seq, own_rows, units)),
            shape((n_seq, slab, model)),
            shape((out_rows, 2 * half)),
            shape((n_seq, own_rows, width)),
            shape((n_seq, 16, model), full),
            shape((n_seq, 8, model), full),
        ),
        in_specs=[spec(SMEM)] + [spec()] * 12 + [spec(ANY)] * 11,
        out_specs=(spec(ANY),) * 9,
        scratch_shapes=[
            pltpu.VMEM((HALO + tokens, max(width, model)), low),
            pltpu.VMEM((tokens, heads * DK), low),
            pltpu.VMEM((count, BT, BT), low),
            pltpu.VMEM((count, BT, BT), low),
            pltpu.VMEM((BT + HALO, 3 * heads * DK), full),
            pltpu.VMEM((tokens, width), low),
            pltpu.VMEM((tokens, width), low),
            pltpu.VMEM((model, width), low),
            pltpu.VMEM((model, width), low),
            pltpu.VMEM((own, model), full),
            pltpu.VMEM((own, model), low),
            pltpu.VMEM((own, model), low),
            pltpu.VMEM((chips, own, model), low),
            pltpu.VMEM((chips, own, model), low),
            pltpu.VMEM((chips - 1, own, model), low),
            pltpu.VMEM((chips, own, model), low),
            pltpu.VMEM((chips, own, model), low),
            pltpu.VMEM((chips, own, model), low),
            pltpu.VMEM((chips - 1, own, model), low),
            *block_buffers(own_rows, units),
            *block_buffers(own_rows, units),
            *block_buffers(slab, model),
            pltpu.VMEM((out.shape[0], half), low),
            pltpu.VMEM((out.shape[0], half), low),
            *sum_buffers(out_rows, half),
            pltpu.VMEM((chips, out_rows, half), low),
            *sum_buffers(own_rows, spans[0][1]),
            *sum_buffers(own_rows, spans[1][1]),
            pltpu.VMEM((own_rows, units), low),
            pltpu.VMEM((own_rows, units), low),
            pltpu.VMEM((slab, model), low),
            pltpu.VMEM((out_rows, half), low),
            pltpu.VMEM((own_rows, width), low),
            pltpu.VMEM((16, model), full),
            pltpu.VMEM((n_fsdp, 16, model), full),
            pltpu.VMEM((8, model), full),
            pltpu.VMEM((n_fsdp, 8, model), full),
            pltpu.SemaphoreType.DMA((copies,)),
            pltpu.SemaphoreType.DMA((copies,)),
            pltpu.SemaphoreType.DMA((gathers,)),
            pltpu.SemaphoreType.DMA((gathers,)),
            pltpu.SemaphoreType.DMA((shares,)),
            pltpu.SemaphoreType.DMA((shares,)),
            pltpu.SemaphoreType.DMA((60,)),
        ],
        compiler_params=pltpu.CompilerParams(
            vmem_limit_bytes=63 << 20, collective_id=3, has_side_effects=True
        ),
        name="mixer_backward",
    )(
        retain, column, row, grad_heads, taps, gain, delta, inverse, parts, update, state,
        norm_gain, ffn_gain, packed, normed, weight, own_tokens, hidden, grad_hidden, result,
        gate, up, down, out,
    )


def rms_forward(values, gain):
    inv_rms = lax.rsqrt(jnp.mean(values * values, axis=-1, keepdims=True) + EPS_NORM)
    unit_rows = values * inv_rms
    return (unit_rows * gain, unit_rows, inv_rms)


def retains(lengths, tokens):
    index = jnp.arange(lengths.shape[0])
    starts = jnp.sum(jnp.where(index[:, None] > index[None, :], lengths[None, :], 0), axis=1)
    spans = jnp.arange(tokens // CH, dtype=jnp.int32) * CH
    keep = 1.0 - jnp.any(starts[None, :] == spans[:, None], axis=1).astype(jnp.float32)
    return jnp.pad(keep, (0, 2))


def own_slice(array, place, size, axis):
    return lax.dynamic_slice_in_dim(array, place * size, size, axis)


def local(
    n_seq,
    n_fsdp,
    tokens,
    norm_gain,
    w_query,
    w_key,
    w_value,
    w_beta,
    conv_taps,
    head_gain,
    w_out,
    ffn_gain,
    w_gate,
    w_up,
    w_down,
    cotangent,
    token_order,
    seq_lengths,
):
    place = lax.axis_index("seq")
    model = tokens.shape[1]
    head_count = w_beta.shape[1]
    heads = head_count // n_seq
    width = heads * DK
    hidden_units = w_gate.shape[1]
    slab = hidden_units // (n_fsdp * n_seq)
    units = slab * n_fsdp
    own_rows = w_query.shape[0]

    def pick_units(array):
        split = array.reshape(array.shape[0], n_fsdp, n_seq, slab)
        return lax.dynamic_index_in_dim(split, place, 2, keepdims=False).reshape(-1, units)

    inputs = tokens.astype(jnp.float32)
    normed_f, unit_one, inv_one = rms_forward(inputs, norm_gain)
    group_tokens = tokens.shape[0] * n_seq
    mixer_shard = jnp.concatenate(
        [own_slice(array, place, width, 1) for array in (w_query, w_key, w_value)]
        + [jnp.pad(own_slice(w_beta, place, heads, 1), ((0, 0), (0, DK - heads)))],
        axis=1,
    )
    retain = retains(seq_lengths[0], group_tokens)
    column, row = token_order.reshape(-1, 1), token_order.reshape(1, -1)
    taps = own_slice(conv_taps, place, width, 2).reshape(3 * CONV, width)
    gain = head_gain.reshape(1, DK)
    mixed_tok, normed, w_mixer, full_gate, full_up, full_down, full_o, cot_all, *saved = (
        mixer_forward(
            n_seq,
            n_fsdp,
            retain,
            column,
            row,
            taps,
            gain,
            (
                normed_f.astype(jnp.bfloat16),
                mixer_shard,
                pick_units(w_gate),
                pick_units(w_up),
                own_slice(w_down, place, slab, 0),
                w_out,
                cotangent,
            ),
        )
    )
    full_down = full_down.reshape(units, model)
    (
        hidden,
        grad_hidden,
        grad_heads,
        result_part,
        wide_gate,
        wide_up,
        wide_down,
        wide_out,
        grad_ffn_gain,
    ) = ffn_block(
        n_seq,
        n_fsdp,
        tokens,
        mixed_tok,
        full_o,
        ffn_gain.reshape(1, model),
        full_gate,
        full_up,
        full_down,
        cot_all,
    )
    result, grad_inputs, part_gate, part_up, part_down, sum_out, part_mixer, small, norm_sum = (
        mixer_backward(
            n_seq,
            n_fsdp,
            (
                retain,
                column,
                row,
                grad_heads,
                taps,
                gain,
                norm_gain.reshape(1, model),
                grad_ffn_gain,
            ),
            saved,
            (
                normed,
                w_mixer,
                tokens,
                hidden,
                grad_hidden,
                result_part,
                wide_gate,
                wide_up,
                wide_down.reshape(n_fsdp, slab, model),
                wide_out,
            ),
        )
    )
    all_mixer = part_mixer.astype(jnp.float32)

    def mixer_columns(start, size):
        return (
            all_mixer[:, :, start : start + size].transpose(1, 0, 2).reshape(own_rows, n_seq * size)
        )

    sum_q, sum_k, sum_v = (mixer_columns(kind * width, width) for kind in range(3))
    sum_b = mixer_columns(3 * width, heads)

    def all_units(pieces):
        return (
            pieces.astype(jnp.float32)
            .reshape(n_seq, own_rows, n_fsdp, slab)
            .transpose(1, 2, 0, 3)
            .reshape(own_rows, hidden_units)
        )

    sum_gate, sum_up = all_units(part_gate), all_units(part_up)
    sum_down = part_down.astype(jnp.float32).reshape(n_seq * slab, model)
    sum_out = sum_out.astype(jnp.float32)
    norm_total = jnp.sum(norm_sum[:, 0], axis=0)
    ffn_total = jnp.sum(small[:, 0], axis=0)
    head_total = jnp.sum(small[:, 1, :DK], axis=0)
    conv_total = (
        small[:, 2 : 2 + 3 * CONV, :width]
        .transpose(1, 0, 2)
        .reshape(3, CONV, n_seq * width)
    )
    return (
        result,
        grad_inputs,
        norm_total,
        sum_q,
        sum_k,
        sum_v,
        sum_b,
        conv_total,
        head_total,
        sum_out,
        ffn_total,
        sum_gate,
        sum_up,
        sum_down,
    )


def solution(mesh):
    tokens = P(("seq", "fsdp"), None)
    rows = P("fsdp", None)
    in_specs = (
        (tokens, P()) + (rows,) * 4 + (P(), P(), rows, P()) + (rows,) * 3 + (tokens, rows, rows)
    )
    out_specs = (
        (tokens, tokens, P()) + (rows,) * 4 + (P(), P(), rows, P()) + (rows,) * 3
    )
    return jax.shard_map(
        functools.partial(local, mesh.shape["seq"], mesh.shape["fsdp"]),
        mesh=mesh,
        in_specs=in_specs,
        out_specs=out_specs,
        check_vma=False,
    )
```

```python
import functools

import jax
import jax.numpy as jnp
from jax import lax
from jax.experimental import pallas as pl
from jax.experimental.pallas import tpu as pltpu
from jax.sharding import PartitionSpec as P

DK = 128
CONV = 4
CH = 64
BT = 128
HALO = 16
PB = 256
EPS_NORM = 1e-06

NN = (((1,), (0,)), ((), ()))
NT = (((1,), (1,)), ((), ()))
TN = (((0,), (0,)), ((), ()))


def bdot(first, second, dims=NN):
    return lax.dot_general(
        first.astype(jnp.bfloat16),
        second.astype(jnp.bfloat16),
        dims,
        preferred_element_type=jnp.float32,
    )


def iota(shape, axis):
    return lax.broadcasted_iota(jnp.int32, shape, axis)


def sigmoid(values):
    return 1.0 / (1.0 + jnp.exp(-values))


def fill_masks(mask_ref):
    rows, cols = iota((BT, BT), 0), iota((BT, BT), 1)
    size, level = 1, 0
    while size < BT:
        inside = (rows // (2 * size) == cols // (2 * size)) & (rows // size > cols // size)
        mask_ref[level] = jnp.where(inside, 1.0, 0.0)
        size, level = 2 * size, level + 1


def unit_lower_inverses(stricts, mask_ref):
    rows, cols = iota((BT, BT), 0), iota((BT, BT), 1)
    eye = jnp.where(rows == cols, 1.0, 0.0)
    inverses = [eye - strict * mask_ref[0] for strict in stricts]
    for level in range(1, 7):
        lows = [inverse.astype(jnp.bfloat16) for inverse in inverses]
        inner = [bdot(strict * mask_ref[level], low) for strict, low in zip(stricts, lows)]
        inverses = [
            inverse - bdot(low, mid) for inverse, low, mid in zip(inverses, lows, inner)
        ]
    return inverses


def tap_masks(first, second, third, count):
    rows = iota((count, 1), 0)
    flag = jnp.where(rows < CH, first, jnp.where(rows < BT, second, third))
    return [None] + [jnp.where(rows % CH < back, flag, 1.0) for back in range(1, CONV)]


def conv_of(halo_rows, taps, masks):
    total = halo_rows[HALO:] * taps[0]
    for back in range(1, CONV):
        total = total + pltpu.roll(halo_rows, back, 0)[HALO:] * (taps[back] * masks[back])
    return total


def block_flags(first, second):
    upper = iota((BT, 1), 0) < CH
    seen = jnp.where(upper, first, first * second)
    kept = jnp.where(upper, second, 1.0)
    return seen, kept


def pair_mask(second):
    rows, cols = iota((BT, BT), 0), iota((BT, BT), 1)
    cross = (rows >= CH) & (cols < CH)
    return rows, cols, jnp.where(cross, second, 1.0)


def permute_rows(column, source, width):
    hot = jnp.where(column == iota((column.shape[0], width), 1), 1.0, 0.0).astype(jnp.bfloat16)
    return lax.dot_general(hot, source, NN, preferred_element_type=jnp.float32)


def unpermute_rows(row, base, source, width):
    hot = jnp.where(row == iota((PB, width), 0) + base, 1.0, 0.0).astype(jnp.bfloat16)
    return lax.dot_general(hot, source, NN, preferred_element_type=jnp.float32)


MESH = pl.DeviceIdType.MESH
ANY = pl.ANY


class Gather:
    outer = 4

    @classmethod
    def copies(cls, n_fsdp):
        inner = n_fsdp // cls.outer
        return (cls.outer - 1) + cls.outer * (inner - 1)

    def __init__(self, n_fsdp, source, slot, sems, base, local_sem):
        self.inner = n_fsdp // self.outer
        self.me = lax.axis_index("fsdp")
        self.seq = lax.axis_index("seq")
        self.high, self.low = self.me // self.inner, self.me % self.inner
        self.source, self.slot = source, slot
        self.send, self.recv = sems
        self.base, self.local_sem = base, local_sem

    def at(self, high, low):
        return (high % self.outer) * self.inner + (low % self.inner)

    def copy(self, source, owner, target, index):
        return pltpu.make_async_remote_copy(
            src_ref=source,
            dst_ref=self.slot(owner),
            send_sem=self.send.at[self.base + index],
            recv_sem=self.recv.at[self.base + index],
            device_id=(self.seq, target),
            device_id_type=MESH,
        )

    def along_outer(self, step):
        return self.copy(self.source, self.me, self.at(self.high + step, self.low), step - 1)

    def along_inner(self, hop):
        return self.copy(
            self.source, self.me, self.at(self.high, self.low + hop), self.outer - 2 + hop
        )

    def passed_on(self, step, hop):
        owner = self.at(self.high - step, self.low)
        index = self.outer - 1 + (self.inner - 1) * step + hop - 1
        return self.copy(self.slot(owner), owner, self.at(self.high, self.low + hop), index)

    def own(self):
        return pltpu.make_async_copy(self.source, self.slot(self.me), self.local_sem)

    def start(self):
        for step in range(1, self.outer):
            self.along_outer(step).start()
        for hop in range(1, self.inner):
            self.along_inner(hop).start()
        self.own().start()

    def relay(self):
        for step in range(1, self.outer):
            self.along_outer(step).wait_recv()
            for hop in range(1, self.inner):
                self.passed_on(step, hop).start()

    def finish(self):
        self.own().wait()
        for hop in range(1, self.inner):
            self.along_inner(hop).wait_recv()
            for step in range(1, self.outer):
                self.passed_on(step, hop).wait_recv()
        for step in range(1, self.outer):
            self.along_outer(step).wait_send()
        for hop in range(1, self.inner):
            self.along_inner(hop).wait_send()
            for step in range(1, self.outer):
                self.passed_on(step, hop).wait_send()


class Share:
    @staticmethod
    def copies(n_seq):
        return 1 + 2 * (n_seq // 2 - 1)

    def __init__(self, n_seq, source, slot, sems, base, local_sem):
        self.n_seq, self.chips = n_seq, n_seq // 2
        self.me = lax.axis_index("seq")
        self.fsdp = lax.axis_index("fsdp")
        self.mate = self.me + 1 - 2 * (self.me % 2)
        self.source, self.slot = source, slot
        self.send, self.recv = sems
        self.base, self.local_sem = base, local_sem

    def copy(self, source, owner, target, index):
        return pltpu.make_async_remote_copy(
            src_ref=source,
            dst_ref=self.slot(owner),
            send_sem=self.send.at[self.base + index],
            recv_sem=self.recv.at[self.base + index],
            device_id=(target, self.fsdp),
            device_id_type=MESH,
        )

    def to_mate(self):
        return self.copy(self.source, self.me, self.mate, 0)

    def across(self, step):
        return self.copy(self.source, self.me, (self.me + 2 * step) % self.n_seq, step)

    def passed_on(self, step):
        owner = (self.me + self.n_seq - 2 * step) % self.n_seq
        return self.copy(self.slot(owner), owner, self.mate, self.chips - 1 + step)

    def own(self):
        return pltpu.make_async_copy(self.source, self.slot(self.me), self.local_sem)

    def start(self):
        for step in range(1, self.chips):
            self.across(step).start()
        self.to_mate().start()
        if self.local_sem is not None:
            self.own().start()

    def relay(self):
        for step in range(1, self.chips):
            self.across(step).wait_recv()
            self.passed_on(step).start()

    def waits(self):
        steps = range(1, self.chips)
        return [self.to_mate()] + [each(step) for step in steps for each in (self.across, self.passed_on)]

    def finish(self):
        if self.local_sem is not None:
            self.own().wait()
        self.to_mate().wait_recv()
        for step in range(1, self.chips):
            self.passed_on(step).wait_recv()
        self.to_mate().wait_send()
        for step in range(1, self.chips):
            self.across(step).wait_send()
            self.passed_on(step).wait_send()


def greet_signal(n_seq, n_fsdp):
    seq, fsdp = lax.axis_index("seq"), lax.axis_index("fsdp")
    barrier = pltpu.get_barrier_semaphore()
    for step in range(1, n_seq):
        pl.semaphore_signal(
            barrier, inc=1, device_id=((seq + step) % n_seq, fsdp), device_id_type=MESH
        )
    for step in range(1, n_fsdp):
        pl.semaphore_signal(
            barrier, inc=1, device_id=(seq, (fsdp + step) % n_fsdp), device_id_type=MESH
        )


def greet_wait(n_seq, n_fsdp):
    pl.semaphore_wait(pltpu.get_barrier_semaphore(), n_seq + n_fsdp - 2)


def greet(n_seq, n_fsdp):
    greet_signal(n_seq, n_fsdp)
    greet_wait(n_seq, n_fsdp)


def aligned(value, unit):
    return pl.multiple_of(value, unit)


def fill_flags(flags_ref, lengths_ref):
    def fill(span, carry):
        start, hit = 0, span == 0
        for index in range(lengths_ref.shape[1] - 1):
            start = start + lengths_ref[0, index]
            hit = hit | (span * CH == start)
        flags_ref[span] = jnp.where(hit, 0.0, 1.0)
        return carry

    lax.fori_loop(0, flags_ref.shape[0], fill, 0)


def fill_taps(taps_ref, taps_in, seq, width):
    for kind in range(3):
        for back in range(CONV):
            row = kind * CONV + back
            taps_ref[row : row + 1, :] = taps_in[
                kind, back : back + 1, pl.ds(aligned(seq * width, width), width)
            ]


def fill_column(column_ref, row_ref):
    for base in range(0, row_ref.shape[1], BT):
        rows = jnp.broadcast_to(row_ref[:, base : base + BT], (8, BT))
        column_ref[base : base + BT, :] = rows.T[:, 0:1]


def pick_units(target, source, seq, n_seq, slab):
    units, hidden = target.shape[1], source.shape[1]
    jump = slab * (n_seq - 1)
    for base in range(0, units, BT):
        size = min(BT, units - base)
        first, last = base // slab, (base + size - 1) // slab
        low = (base + jump * first) // BT * BT
        high = min(-(-(base + size + jump * (last + 1)) // BT) * BT, hidden)
        col = iota((high - low, size), 1) + base
        origin = col + jump * first + slab * seq - low
        for owner in range(first + 1, last + 1):
            origin = origin + jnp.where(col >= owner * slab, jump, 0)
        hot = jnp.where(iota((high - low, size), 0) == origin, 1.0, 0.0)
        target[:, base : base + size] = bdot(source[:, low:high], hot).astype(jnp.bfloat16)


def mixer_forward_kernel(
    heads,
    n_seq,
    n_fsdp,
    lengths_ref,
    row_ref,
    taps_in,
    gain_ref,
    norm_gain_ref,
    tokens_ref,
    beta_ref,
    cot_in,
    query_in,
    key_in,
    value_in,
    gate_in,
    up_in,
    down_in,
    out_in,
    tokens_mixed,
    normed_out,
    mixer_out,
    gate_all,
    up_all,
    down_all,
    out_all,
    cot_all,
    packed_out,
    delta_out,
    inverse_out,
    big_out,
    update_out,
    state_out,
    retain_ref,
    taps_ref,
    column_ref,
    packed_ref,
    delta_ref,
    inverse_ref,
    update_ref,
    state_ref,
    big_ref,
    mask_ref,
    fresh_ref,
    own_ref,
    add_ref,
    mixed_ref,
    ready_ref,
    chosen_ref,
    normed_ref,
    weight_ref,
    betas_ref,
    raw_ref,
    gate_mine,
    up_mine,
    down_mine,
    out_mine,
    gather_send,
    gather_recv,
    share_send,
    share_recv,
    local_sems,
):
    own_tokens = tokens_ref.shape[0]
    tokens = own_tokens * n_seq
    width = packed_ref.shape[1]
    head_width = heads * DK
    blocks = tokens // BT
    seq = lax.axis_index("seq")
    own_rows, _ = query_in.shape
    slab = down_mine.shape[0]
    out_rows, out_width = out_in.shape
    out_part = out_width // n_seq
    low = jnp.bfloat16

    local = {}

    def bring(name, source, target):
        copy = pltpu.make_async_copy(source, target, local_sems.at[len(local)])
        local[name] = copy
        copy.start()

    out_at = aligned(seq * out_part, out_part)
    bring("gate", gate_in, raw_ref.at[0])
    bring("up", up_in, raw_ref.at[1])
    bring("out", out_in.at[:, pl.ds(out_at, out_part)], out_mine)
    whole_shard = down_in.shape[0] > slab
    bring(
        "down",
        down_in.at[pl.ds(aligned(seq * slab, slab), slab)] if whole_shard else down_in,
        down_mine,
    )
    greet_signal(n_seq, n_fsdp)

    part = min(PB, own_tokens)
    for base in range(0, own_tokens, part):
        values = tokens_ref[base : base + part, :].astype(jnp.float32)
        inv = lax.rsqrt(jnp.mean(values * values, axis=1, keepdims=True) + EPS_NORM)
        normed_ref[pl.ds(aligned(seq * own_tokens + base, part), part), :] = (
            values * inv * norm_gain_ref[...]
        ).astype(low)
    greet_wait(n_seq, n_fsdp)

    gather_sems = (gather_send, gather_recv)
    share_sems = (share_send, share_recv)
    per_gather = Gather.copies(n_fsdp)
    per_share = Share.copies(n_seq)

    def rows_slot(ref, size):
        return lambda owner: ref.at[pl.ds(aligned(owner * size, size), size)]

    def gather_piece(index, source, slot):
        return Gather(
            n_fsdp, source, slot, gather_sems, index * per_gather, local_sems.at[30 + index]
        )

    def head_columns(kind):
        return lambda owner: weight_ref.at[
            pl.ds(aligned(owner * own_rows, own_rows), own_rows),
            pl.ds(kind * head_width, head_width),
        ]

    pieces = [
        gather_piece(
            kind,
            source.at[:, pl.ds(aligned(seq * head_width, head_width), head_width)],
            head_columns(kind),
        )
        for kind, source in enumerate((query_in, key_in, value_in))
    ] + [
        gather_piece(
            3,
            out_mine,
            lambda owner: out_all.at[
                pl.ds(aligned(owner * out_rows, out_rows), out_rows), pl.ds(out_at, out_part)
            ],
        ),
        gather_piece(4, gate_mine, rows_slot(gate_all, own_rows)),
        gather_piece(5, up_mine, rows_slot(up_all, own_rows)),
        gather_piece(6, down_mine, lambda owner: down_all.at[owner]),
    ]
    betas = gather_piece(7, beta_ref, lambda owner: betas_ref.at[owner])
    share_normed = Share(
        n_seq,
        normed_ref.at[pl.ds(aligned(seq * own_tokens, own_tokens), own_tokens)],
        rows_slot(normed_ref, own_tokens),
        share_sems,
        0,
        None,
    )
    share_cot = Share(
        n_seq, cot_in, rows_slot(cot_all, own_tokens), share_sems, per_share, local_sems.at[38]
    )
    share_out = Share(
        n_seq,
        out_all.at[:, pl.ds(out_at, out_part)],
        lambda owner: out_all.at[:, pl.ds(aligned(owner * out_part, out_part), out_part)],
        share_sems,
        2 * per_share,
        None,
    )

    share_normed.start()
    pieces[0].start()
    betas.start()
    pieces[1].start()
    fill_flags(retain_ref, lengths_ref)
    fill_taps(taps_ref, taps_in, seq, head_width)
    fill_column(column_ref, row_ref)
    fill_masks(mask_ref)
    packed_ref[0:HALO, :] = jnp.zeros((HALO, width), low)
    local["gate"].wait()
    pick_units(gate_mine, raw_ref.at[0], seq, n_seq, slab)
    pieces[0].relay()
    pieces[2].start()
    betas.relay()
    pieces[1].relay()
    local["out"].wait()
    pieces[3].start()
    local["up"].wait()
    pick_units(up_mine, raw_ref.at[1], seq, n_seq, slab)
    share_normed.to_mate().wait_recv()

    def permute(step, carry, source, first):
        base = aligned(step * PB, PB)
        picked = permute_rows(
            column_ref[pl.ds(base, PB), :] - source * own_tokens,
            normed_ref[pl.ds(aligned(source * own_tokens, own_tokens), 2 * own_tokens), :],
            2 * own_tokens,
        )
        if not first:
            picked = picked + chosen_ref[pl.ds(base, PB), :].astype(jnp.float32)
        chosen_ref[pl.ds(base, PB), :] = picked.astype(low)
        return carry

    lax.fori_loop(
        0, tokens // PB, functools.partial(permute, source=seq // 2 * 2, first=True), 0
    )
    pieces[2].relay()
    pieces[4].start()
    betas.finish()
    mine = jnp.where(
        iota((beta_ref.shape[0], DK), 0) == iota((beta_ref.shape[0], DK), 1) + seq * heads, 1.0, 0.0
    )
    mine = jnp.where(iota(mine.shape, 1) < heads, mine, 0.0)
    for owner in range(n_fsdp):
        weight_ref[owner * own_rows : (owner + 1) * own_rows, 3 * head_width :] = bdot(
            betas_ref[owner], mine, TN
        ).astype(low)
    share_normed.relay()
    share_cot.start()
    for step in range(1, n_seq // 2):
        share_normed.passed_on(step).wait_recv()
        lax.fori_loop(
            0,
            tokens // PB,
            functools.partial(permute, source=(seq // 2 * 2 + n_seq - 2 * step) % n_seq, first=False),
            0,
        )
    pieces[3].relay()
    pieces[5].start()
    for piece in pieces[:3]:
        piece.finish()
    bring("keep_normed", chosen_ref, normed_out)
    bring("keep_mixer", weight_ref, mixer_out)

    def project(step, carry):
        base = aligned(step * PB, PB)
        packed_ref[pl.ds(HALO + base, PB), :] = bdot(
            chosen_ref[pl.ds(base, PB), :], weight_ref[...]
        ).astype(low)
        return carry

    lax.fori_loop(0, tokens // PB, project, 0)
    bring("keep_packed", packed_ref, packed_out)

    def middle(number):
        if number == 0:
            pieces[3].finish()
            share_out.start()
            pieces[4].relay()
        if number == 1:
            local["down"].wait()
            pieces[6].start()
            share_cot.relay()
        if number == 2:
            pieces[5].relay()
            share_out.relay()


    unroll = 2

    def prepare(step, carry):
        for number, moment in enumerate((1, 3, 6)):

            @pl.when(step == moment)
            def _():
                middle(number)

        places, stricts, kept_values = [], [], []
        for sub in range(unroll):
            block = step * unroll + sub
            first, second = retain_ref[2 * block], retain_ref[2 * block + 1]
            base = pl.multiple_of(block * BT, BT)
            masks = tap_masks(first, second, 1.0, BT)
            seen, kept = block_flags(first, second)
            rows, cols, cross = pair_mask(second)
            strengths = sigmoid(
                packed_ref[pl.ds(HALO + base, BT), 3 * heads * DK : 3 * heads * DK + BT].astype(
                    jnp.float32
                )
            )
            for head in range(heads):
                parts = []
                for kind in range(3):
                    at = (kind * heads + head) * DK
                    window = packed_ref[pl.ds(base, HALO + BT), at : at + DK].astype(jnp.float32)
                    taps = [
                        taps_ref[kind * CONV + back : kind * CONV + back + 1, head * DK : head * DK + DK]
                        for back in range(CONV)
                    ]
                    conv = conv_of(window, taps, masks)
                    parts.append(conv * sigmoid(conv))
                query, key, value = parts
                query = query * lax.rsqrt(
                    jnp.sum(query * query, axis=1, keepdims=True) + EPS_NORM
                ) * DK ** (-0.5)
                key = key * lax.rsqrt(jnp.sum(key * key, axis=1, keepdims=True) + EPS_NORM)
                query_low, key_low = query.astype(jnp.bfloat16), key.astype(jnp.bfloat16)
                query, key = query_low.astype(jnp.float32), key_low.astype(jnp.float32)
                beta = strengths[:, head : head + 1]
                inner = bdot(jnp.concatenate([key_low, query_low], axis=0), key_low, NT)
                stricts.append(jnp.where(rows > cols, inner[:BT] * cross * beta, 0.0))
                scores = jnp.where(rows >= cols, inner[BT:] * cross, 0.0)
                sides = jnp.concatenate([key * (beta * seen), value * beta], axis=1)
                kept_values.append((scores, sides, key * kept, query * seen))
                places.append(head * blocks + block)
        inverses = unit_lower_inverses(stricts, mask_ref)
        solved = [
            bdot(inverse, values[1]) for inverse, values in zip(inverses, kept_values)
        ]
        through = [bdot(values[0], both) for values, both in zip(kept_values, solved)]
        onward = [bdot(values[2], both, TN) for values, both in zip(kept_values, solved)]
        for index, place in enumerate(places):
            inverse_ref[place] = inverses[index].astype(jnp.bfloat16)
            big_ref[place, 0:BT, :] = onward[index][:, :DK].astype(jnp.bfloat16)
            big_ref[place, BT : 2 * BT, :] = (
                kept_values[index][3] - through[index][:, :DK]
            ).astype(jnp.bfloat16)
            big_ref[place, 2 * BT : 3 * BT, :] = solved[index][:, :DK].astype(jnp.bfloat16)
            add_ref[place] = onward[index][:, DK:]
            fresh_ref[place] = solved[index][:, DK:]
            own_ref[place] = through[index][:, DK:]
        return carry

    lax.fori_loop(0, blocks // unroll, prepare, 0)
    bring("keep_inverse", inverse_ref, inverse_out)
    bring("keep_big", big_ref.at[:, pl.ds(0, 2 * BT), :], big_out)

    def advance(block, states):
        through = retain_ref[2 * block] * retain_ref[2 * block + 1]
        base = pl.multiple_of(block * BT, BT)
        lows = [state.astype(jnp.bfloat16) for state in states]
        products = [bdot(big_ref[head * blocks + block], lows[head]) for head in range(heads)]
        following = []
        for head in range(heads):
            place = head * blocks + block
            product = products[head]
            state_ref[place] = lows[head]
            following.append(states[head] * through - product[:BT] + add_ref[place])
            update_ref[place] = (fresh_ref[place] - product[2 * BT :]).astype(jnp.bfloat16)
            delta = own_ref[place] + product[BT : 2 * BT]
            delta_ref[pl.ds(base, BT), head * DK : head * DK + DK] = delta
            inv = lax.rsqrt(jnp.mean(delta * delta, axis=1, keepdims=True) + EPS_NORM)
            ready_ref[pl.ds(base, BT), head * DK : head * DK + DK] = (
                delta * inv * gain_ref[...]
            ).astype(jnp.bfloat16)
        return tuple(following)

    zero = jnp.zeros((DK, DK), jnp.float32)
    lax.fori_loop(0, blocks, advance, (zero,) * heads)
    bring("keep_delta", delta_ref, delta_out)
    bring("keep_update", update_ref, update_out)
    bring("keep_state", state_ref, state_out)

    def hand_over(shift):
        target = (seq + shift) % n_seq
        base = aligned(target * own_tokens, own_tokens)
        for at in range(0, own_tokens, part):
            first = aligned(base + at, part)
            hot = jnp.where(
                row_ref[...] == iota((part, tokens), 0) + first, 1.0, 0.0
            ).astype(low)
            mixed_ref[pl.ds(first, part), :] = lax.dot_general(
                hot, ready_ref[...], NN, preferred_element_type=jnp.float32
            ).astype(low)
        source = mixed_ref.at[pl.ds(base, own_tokens)]
        slot = tokens_mixed.at[:, pl.ds(aligned(seq * head_width, head_width), head_width)]
        if shift == 0:
            return pltpu.make_async_copy(source, slot, local_sems.at[39])
        return pltpu.make_async_remote_copy(
            src_ref=source,
            dst_ref=slot,
            send_sem=share_send.at[3 * per_share + shift],
            recv_sem=share_recv.at[3 * per_share + shift],
            device_id=(target, lax.axis_index("fsdp")),
            device_id_type=MESH,
        )

    handed = []
    for shift in sorted(range(n_seq), key=lambda shift: (shift in (0, 1), -shift)):
        copy = hand_over(shift)
        copy.start()
        handed.append(copy)
    pieces[6].relay()
    for copy in share_normed.waits():
        copy.wait_send()
    share_cot.finish()
    share_out.finish()
    for piece in pieces[4:]:
        piece.finish()
    for name, copy in local.items():
        if name.startswith("keep_"):
            copy.wait()
    for copy in handed:
        copy.wait()


VMEM = pltpu.MemorySpace.VMEM
SMEM = pltpu.MemorySpace.SMEM


def spec(space=VMEM):
    return pl.BlockSpec(memory_space=space)


def mixer_forward(n_seq, n_fsdp, lengths, row, taps, gain, norm_gain, shards):
    tokens_in, beta, cot, query, key, value, gate, up, down, out = shards
    own_tokens, model = tokens_in.shape
    tokens = own_tokens * n_seq
    heads = beta.shape[0] // n_seq
    width = (3 * heads + 1) * DK
    blocks = tokens // BT
    count = heads * blocks
    own_rows, hidden = gate.shape
    slab = hidden // (n_seq * n_fsdp)
    units = slab * n_fsdp
    low, full = jnp.bfloat16, jnp.float32
    gathers = 8 * Gather.copies(n_fsdp)
    shares = 3 * Share.copies(n_seq) + n_seq

    def shape(dims, kind=low):
        return jax.ShapeDtypeStruct(dims, kind)

    return pl.pallas_call(
        functools.partial(mixer_forward_kernel, heads, n_seq, n_fsdp),
        out_shape=(
            shape((own_tokens, n_seq * heads * DK)),
            shape((tokens, model)),
            shape((own_rows * n_fsdp, width)),
            shape((own_rows * n_fsdp, units)),
            shape((own_rows * n_fsdp, units)),
            shape((n_fsdp, slab, model)),
            shape((out.shape[0] * n_fsdp, out.shape[1])),
            shape((tokens, model)),
            shape((HALO + tokens, width)),
            shape((tokens, heads * DK), full),
            shape((count, BT, BT)),
            shape((count, 2 * BT, BT)),
            shape((count, BT, BT)),
            shape((count, BT, BT)),
        ),
        in_specs=[spec(SMEM)] + [spec()] * 7 + [spec(ANY)] * 7,
        out_specs=(spec(ANY),) * 14,
        scratch_shapes=[
            pltpu.SMEM((tokens // CH + 2,), full),
            pltpu.VMEM((3 * CONV, heads * DK), full),
            pltpu.VMEM((tokens, 1), jnp.int32),
            pltpu.VMEM((HALO + tokens, width), low),
            pltpu.VMEM((tokens, heads * DK), full),
            pltpu.VMEM((count, BT, BT), low),
            pltpu.VMEM((count, BT, BT), low),
            pltpu.VMEM((count, BT, BT), low),
            pltpu.VMEM((count, 3 * BT, BT), low),
            pltpu.VMEM((7, BT, BT), full),
            pltpu.VMEM((count, BT, BT), full),
            pltpu.VMEM((count, BT, BT), full),
            pltpu.VMEM((count, BT, BT), full),
            pltpu.VMEM((tokens, heads * DK), low),
            pltpu.VMEM((tokens, heads * DK), low),
            pltpu.VMEM((tokens, model), low),
            pltpu.VMEM((tokens, model), low),
            pltpu.VMEM((own_rows * n_fsdp, width), low),
            pltpu.VMEM((n_fsdp,) + beta.shape, low),
            pltpu.VMEM((2, own_rows, hidden), low),
            pltpu.VMEM((own_rows, units), low),
            pltpu.VMEM((own_rows, units), low),
            pltpu.VMEM((slab, model), low),
            pltpu.VMEM((out.shape[0], out.shape[1] // n_seq), low),
            pltpu.SemaphoreType.DMA((gathers,)),
            pltpu.SemaphoreType.DMA((gathers,)),
            pltpu.SemaphoreType.DMA((shares,)),
            pltpu.SemaphoreType.DMA((shares,)),
            pltpu.SemaphoreType.DMA((40,)),
        ],
        compiler_params=pltpu.CompilerParams(
            vmem_limit_bytes=60 << 20, collective_id=1, has_side_effects=True
        ),
        name="mixer_forward",
    )(
        lengths, row, taps, gain, norm_gain, tokens_in, beta, cot,
        query, key, value, gate, up, down, out,
    )


class Wire:
    def __init__(self, send, recv):
        self.send, self.recv, self.used = send, recv, 0

    def copy(self, source, target, seq, fsdp):
        index = self.used
        self.used += 1
        return pltpu.make_async_remote_copy(
            src_ref=source,
            dst_ref=target,
            send_sem=self.send.at[index],
            recv_sem=self.recv.at[index],
            device_id=(seq, fsdp),
            device_id_type=MESH,
        )


def ffn_copies(n_seq, parts):
    chips = n_seq // 2
    return parts * (2 + 4 * (chips - 1)) + parts * (n_seq - 1)


def ffn_kernel(
    n_seq,
    n_fsdp,
    tokens_ref,
    mixed_ref,
    out_ref,
    gain_ref,
    gate_in,
    up_in,
    down_in,
    cot_in,
    hidden_ref,
    grad_hidden_ref,
    heads_ref,
    result_ref,
    gate_parts,
    grad_up_ref,
    grad_down_ref,
    grad_out_ref,
    grad_gain_ref,
    grad_gate_ref,
    gate_first,
    gate_ref,
    up_ref,
    down_ref,
    cot_ref,
    second_ref,
    second_t_ref,
    active_t_ref,
    lin_gate_ref,
    lin_up_ref,
    keep_ref,
    give_ref,
    from_mate_ref,
    reduce_ref,
    from_far_ref,
    attn_ref,
    mixed_grad_ref,
    stage_ref,
    outgo_ref,
    send_sems,
    recv_sems,
    local_sems,
):
    own, model = tokens_ref.shape
    group = own * n_seq
    part = min(PB, own)
    parts = own // part
    chips = n_seq // 2
    seq, fsdp = lax.axis_index("seq"), lax.axis_index("fsdp")
    mate = seq + 1 - 2 * (seq % 2)
    units = gate_ref.shape[1]
    low = jnp.bfloat16

    loads = [
        pltpu.make_async_copy(source, target, local_sems.at[index])
        for index, (source, target) in enumerate(
            ((gate_in, gate_ref), (up_in, up_ref), (down_in, down_ref), (cot_in, cot_ref))
        )
    ]
    for load in loads:
        load.start()

    wire = Wire(send_sems, recv_sems)

    def far(step):
        return (seq + n_seq - 2 * step) % n_seq

    def rows(ref, shard, index):
        return ref.at[pl.ds(aligned(shard * own + index * part, part), part)]

    def local_rows(ref, index):
        return ref.at[pl.ds(index * part, part)]

    to_mate, across, passed, give_mate, give_far, reduced = {}, {}, {}, {}, {}, {}
    for index in range(parts):
        mine = rows(second_ref, seq, index)
        to_mate[index] = wire.copy(mine, mine, mate, fsdp)
        give_mate[index] = wire.copy(
            local_rows(give_ref.at[0], index), local_rows(from_mate_ref.at[0], index), mate, fsdp
        )
        for step in range(1, chips):
            across[step, index] = wire.copy(mine, mine, (seq + 2 * step) % n_seq, fsdp)
            there = rows(second_ref, far(step), index)
            passed[step, index] = wire.copy(there, there, mate, fsdp)
            give_far[step, index] = wire.copy(
                local_rows(give_ref.at[step], index),
                local_rows(from_mate_ref.at[step], index),
                mate,
                fsdp,
            )
            reduced[step, index] = wire.copy(
                local_rows(reduce_ref.at[step - 1], index),
                local_rows(from_far_ref.at[step - 1], index),
                far(step),
                fsdp,
            )

    own_rows = model // n_fsdp
    inner = n_fsdp // 4
    high_at, low_at = fsdp // inner, fsdp % inner

    def wide_copies(source, target):
        copies = []
        for hop in range(1, inner):
            lower = (low_at + hop) % inner
            for high in range(4):
                block = aligned((high * inner + lower) * own_rows, own_rows)
                copies.append(
                    wire.copy(
                        source.at[pl.ds(block, own_rows)],
                        target.at[(hop - 1) * 4 + high],
                        seq,
                        high_at * inner + lower,
                    )
                )
        return copies

    gate_copies = wide_copies(grad_gate_ref, gate_first)

    greet(n_seq, n_fsdp)

    for index in range(parts):
        at = slice(index * part, index * part + part)
        hidden = tokens_ref[at, :].astype(jnp.float32) + bdot(mixed_ref[at, :], out_ref[...])
        hidden_ref[at, :] = hidden
        inv = lax.rsqrt(jnp.mean(hidden * hidden, axis=1, keepdims=True) + EPS_NORM)
        second_ref[pl.ds(aligned(seq * own + index * part, part), part), :] = (
            hidden * inv * gain_ref[...]
        ).astype(low)
        for step in range(1, chips):
            across[step, index].start()
        to_mate[index].start()
    for load in loads:
        load.wait()

    count = n_seq * parts

    def block(number, carry):
        near = number < 2 * parts
        late = number - 2 * parts
        step_at = late // (2 * parts) + 1
        rest = late % (2 * parts)
        far_at = (seq + 2 * n_seq - 2 * step_at) % n_seq
        far_mate = far_at + 1 - 2 * (far_at % 2)
        shard = jnp.where(
            near,
            jnp.where(number < parts, seq, mate),
            jnp.where(rest % 2 == 0, far_mate, far_at),
        )
        index_at = jnp.where(near, number % parts, rest // 2)
        base = aligned(shard * own + index_at * part, part)

        for index in range(parts):

            @pl.when(number == parts + index)
            def _():
                to_mate[index].wait_recv()

            for step in range(1, chips):

                @pl.when(number == 2 * parts * step + 2 * index)
                def _():
                    across[step, index].wait_recv()
                    passed[step, index].start()
                    passed[step, index].wait_recv()

        second = second_ref[pl.ds(base, part), :]
        second_t_ref[:, pl.ds(base, part)] = second.T
        gate_lin = bdot(second, gate_ref[...])
        up_lin = bdot(second, up_ref[...])
        cot = cot_ref[pl.ds(base, part), :]
        grad_active = bdot(cot, down_ref[...], NT)
        gate_sig = sigmoid(gate_lin)
        silu = gate_lin * gate_sig
        active = (silu * up_lin).astype(low)
        active_t_ref[:, pl.ds(base, part)] = active.T
        grad_gate = (grad_active * up_lin * (gate_sig + silu * (1.0 - gate_sig))).astype(low)
        grad_up = (grad_active * silu).astype(low)
        lin_gate_ref[pl.ds(base, part), :] = grad_gate
        lin_up_ref[pl.ds(base, part), :] = grad_up
        grad_second = bdot(grad_gate, gate_ref[...], NT) + bdot(grad_up, up_ref[...], NT)
        stage_ref[...] = grad_second
        slot = number % 2

        def leaving(where):
            return pltpu.make_async_copy(
                outgo_ref.at[slot],
                result_ref.at[pl.ds(where, part)],
                local_sems.at[4 + slot],
            )

        @pl.when(number >= 2)
        def _():
            leaving(base).wait()

        outgo_ref[slot] = bdot(active, down_ref[...]).astype(low)
        leaving(base).start()

        for index in range(parts):
            at = slice(index * part, index * part + part)

            @pl.when(number == index)
            def _():
                keep_ref[at, :] = stage_ref[...]

            @pl.when(number == parts + index)
            def _():
                give_ref[0, at, :] = stage_ref[...].astype(low)
                give_mate[index].start()

            for step in range(1, chips):

                @pl.when(number == 2 * parts * step + 2 * index)
                def _():
                    give_ref[step, at, :] = stage_ref[...].astype(low)
                    give_far[step, index].start()

                @pl.when(number == 2 * parts * step + 2 * index + 1)
                def _():
                    give_far[step, index].wait_recv()
                    reduce_ref[step - 1, at, :] = (
                        stage_ref[...] + from_mate_ref[step, at, :].astype(jnp.float32)
                    ).astype(low)
                    reduced[step, index].start()

        return carry

    lax.fori_loop(0, count, block, 0)

    for slot in range(2):
        pltpu.make_async_copy(
            outgo_ref.at[slot], result_ref.at[pl.ds(0, part)], local_sems.at[4 + slot]
        ).wait()

    tile = 256

    def wide_tile(target, lines):
        def step(number, carry):
            base = aligned(number * tile, tile)
            target[pl.ds(base, tile), :] = bdot(
                second_t_ref[pl.ds(base, tile), :], lines[...]
            ).astype(low)
            return carry

        lax.fori_loop(0, model // tile, step, 0)

    wide_tile(grad_gate_ref, lin_gate_ref)
    for copy in gate_copies:
        copy.start()
    wide_tile(grad_up_ref, lin_up_ref)

    grad_gain_ref[...] = jnp.zeros(grad_gain_ref.shape, jnp.float32)
    width = model // n_seq
    handed = []
    for index in range(parts):
        at = slice(index * part, index * part + part)
        give_mate[index].wait_recv()
        total = keep_ref[at, :] + from_mate_ref[0, at, :].astype(jnp.float32)
        for step in range(1, chips):
            reduced[step, index].wait_recv()
            total = total + from_far_ref[step - 1, at, :].astype(jnp.float32)
        hidden = hidden_ref[at, :]
        inv = lax.rsqrt(jnp.mean(hidden * hidden, axis=1, keepdims=True) + EPS_NORM)
        unit = hidden * inv
        grad_gain_ref[...] += jnp.sum(total * unit, axis=0, keepdims=True)
        grad_unit = total * gain_ref[...]
        grad_hidden = inv * (
            grad_unit - unit * jnp.mean(grad_unit * unit, axis=1, keepdims=True)
        ) + cot_ref[pl.ds(aligned(seq * own + index * part, part), part), :].astype(jnp.float32)
        grad_hidden_ref[at, :] = grad_hidden
        attn = grad_hidden.astype(low)
        attn_ref[at, :] = attn
        mixed_grad_ref[at, :] = bdot(attn, out_ref[...], NT).astype(low)
        for shift in range(1, n_seq):
            target = (seq + shift) % n_seq
            copy = wire.copy(
                mixed_grad_ref.at[at, pl.ds(aligned(target * width, width), width)],
                rows(heads_ref, seq, index),
                target,
                fsdp,
            )
            copy.start()
            handed.append(copy)
        heads_ref[pl.ds(aligned(seq * own + index * part, part), part), :] = mixed_grad_ref[
            at, pl.ds(aligned(seq * width, width), width)
        ]

    def down_tile(number, carry):
        base = aligned(number * tile, tile)
        grad_down_ref[:, pl.ds(base, tile)] = bdot(
            active_t_ref[...], cot_ref[:, pl.ds(base, tile)]
        ).astype(low)
        return carry

    lax.fori_loop(0, model // tile, down_tile, 0)

    for base in range(0, model, tile):
        grad_out_ref[base : base + tile, :] = bdot(
            mixed_ref[:, base : base + tile], attn_ref[...], TN
        ).astype(low)

    for index in range(parts):
        to_mate[index].wait_send()
        give_mate[index].wait_send()
        for step in range(1, chips):
            across[step, index].wait_send()
            passed[step, index].wait_send()
            give_far[step, index].wait_send()
            reduced[step, index].wait_send()
    for copy in handed:
        copy.wait()
    for copy in gate_copies:
        copy.wait_recv()
    for high in range(4):
        block = aligned((high * inner + low_at) * own_rows, own_rows)
        total = grad_gate_ref[pl.ds(block, own_rows), :].astype(jnp.float32)
        for hop in range(1, inner):
            total = total + gate_first[(hop - 1) * 4 + high].astype(jnp.float32)
        gate_parts[high] = total.astype(low)
    for copy in gate_copies:
        copy.wait_send()


def ffn_block(n_seq, n_fsdp, tokens, mixed, out, gain, gate, up, down, cot):
    own, model = tokens.shape
    group = own * n_seq
    units = gate.shape[1]
    chips = n_seq // 2
    low, full = jnp.bfloat16, jnp.float32
    part = min(PB, own)
    near = 4 * (n_fsdp // 4 - 1)
    own_rows = model // n_fsdp
    copies = ffn_copies(n_seq, own // part) + near

    def shape(dims, kind=low):
        return jax.ShapeDtypeStruct(dims, kind)

    return pl.pallas_call(
        functools.partial(ffn_kernel, n_seq, n_fsdp),
        out_shape=(
            shape((own, model), full),
            shape((own, model), full),
            shape((group, model // n_seq)),
            shape((group, model)),
            shape((4, own_rows, units)),
            shape((model, units)),
            shape((units, model)),
            shape((model, model)),
            shape((1, model), full),
        ),
        in_specs=[spec()] * 4 + [spec(ANY)] * 4,
        out_specs=(spec(),) * 3 + (spec(ANY),) + (spec(),) * 5,
        scratch_shapes=[
            pltpu.VMEM((model, units), low),
            pltpu.VMEM((near, own_rows, units), low),
            pltpu.VMEM((model, units), low),
            pltpu.VMEM((model, units), low),
            pltpu.VMEM((units, model), low),
            pltpu.VMEM((group, model), low),
            pltpu.VMEM((group, model), low),
            pltpu.VMEM((model, group), low),
            pltpu.VMEM((units, group), low),
            pltpu.VMEM((group, units), low),
            pltpu.VMEM((group, units), low),
            pltpu.VMEM((own, model), full),
            pltpu.VMEM((chips, own, model), low),
            pltpu.VMEM((chips, own, model), low),
            pltpu.VMEM((chips - 1, own, model), low),
            pltpu.VMEM((chips - 1, own, model), low),
            pltpu.VMEM((own, model), low),
            pltpu.VMEM((own, model), low),
            pltpu.VMEM((part, model), full),
            pltpu.VMEM((2, part, model), low),
            pltpu.SemaphoreType.DMA((copies,)),
            pltpu.SemaphoreType.DMA((copies,)),
            pltpu.SemaphoreType.DMA((6,)),
        ],
        compiler_params=pltpu.CompilerParams(
            vmem_limit_bytes=63 << 20, collective_id=2, has_side_effects=True
        ),
        name="ffn",
    )(tokens, mixed, out, gain, gate, up, down, cot)


class Scatter:
    outer = 4

    @classmethod
    def copies(cls, n_fsdp):
        return cls.outer * (n_fsdp // cls.outer - 1) + cls.outer - 1

    def __init__(self, n_fsdp, wire, block, parts, mine, first, second):
        self.inner = n_fsdp // self.outer
        me = lax.axis_index("fsdp")
        seq = lax.axis_index("seq")
        self.high, self.low = me // self.inner, me % self.inner
        self.parts, self.mine, self.first, self.second = parts, mine, first, second
        self.near, self.away = [], []
        for hop in range(1, self.inner if first is not None else 1):
            lower = (self.low + hop) % self.inner
            for high in range(self.outer):
                self.near.append(
                    wire.copy(
                        block(high * self.inner + lower),
                        first.at[(hop - 1) * self.outer + high],
                        seq,
                        self.high * self.inner + lower,
                    )
                )
        for step in range(1, self.outer):
            higher = (self.high + step) % self.outer
            self.away.append(
                wire.copy(parts(higher), second.at[step - 1], seq, higher * self.inner + self.low)
            )

    def start(self):
        for copy in self.near:
            copy.start()

    def combine(self):
        for copy in self.near:
            copy.wait_recv()
        for high in range(self.outer):
            block = self.parts(high)
            total = block[...].astype(jnp.float32)
            for hop in range(1, self.inner):
                total = total + self.first[(hop - 1) * self.outer + high].astype(jnp.float32)
            block[...] = total.astype(jnp.bfloat16)

    def leave(self):
        for copy in self.away:
            copy.start()

    def total(self):
        for copy in self.away:
            copy.wait_recv()
        total = self.mine()[...].astype(jnp.float32)
        for step in range(1, self.outer):
            total = total + self.second[step - 1].astype(jnp.float32)
        return total.astype(jnp.bfloat16)

    def drain(self):
        for copy in self.near + self.away:
            copy.wait_send()


CHUNK = 64


class SeqSum:
    def __init__(self, n_seq, wire, give, mine, from_mate, from_far):
        self.chips = n_seq // 2
        seq, fsdp = lax.axis_index("seq"), lax.axis_index("fsdp")
        mate = seq + 1 - 2 * (seq % 2)
        self.mine, self.from_mate, self.from_far = mine, from_mate, from_far
        self.gives = [
            wire.copy(give(step), from_mate.at[step], mate, fsdp) for step in range(self.chips)
        ]
        self.across = [
            wire.copy(
                mine(step),
                from_far.at[step - 1],
                (seq + n_seq - 2 * step) % n_seq,
                fsdp,
            )
            for step in range(1, self.chips)
        ]

    def reduce(self, step):
        self.gives[step].wait_recv()
        mine = self.mine(step)

        def add(number, carry):
            at = pl.ds(aligned(number * CHUNK, CHUNK), CHUNK)
            mine[at, :] = (
                mine[at, :].astype(jnp.float32) + self.from_mate[step, at, :].astype(jnp.float32)
            ).astype(jnp.bfloat16)
            return carry

        lax.fori_loop(0, mine.shape[0] // CHUNK, add, 0)
        self.across[step - 1].start()

    def arrive(self):
        self.gives[0].wait_recv()
        for copy in self.across:
            copy.wait_recv()

    def total(self, at):
        total = self.mine(0)[at, :].astype(jnp.float32) + self.from_mate[0, at, :].astype(
            jnp.float32
        )
        for step in range(1, self.chips):
            total = total + self.from_far[step - 1, at, :].astype(jnp.float32)
        return total

    def drain(self):
        for copy in self.gives + self.across:
            copy.wait_send()


def spread_units(target, pieces, n_seq, slab):
    units, hidden = pieces.shape[2], target.shape[1]
    whole = slab * n_seq
    for base in range(0, hidden, BT):
        total = None
        for owner in range(n_seq):
            first, last = base // whole, (base + BT - 1) // whole
            low = first * slab // BT * BT
            high = min(-(-((last + 1) * slab) // BT) * BT, units)
            col = iota((high - low, BT), 1) + base
            origin = col - first * whole - owner * slab
            inside = (origin >= 0) & (origin < slab)
            origin = origin + first * slab
            for shard in range(first + 1, last + 1):
                there = col - shard * whole - owner * slab
                ours = (there >= 0) & (there < slab)
                origin = jnp.where(ours, there + shard * slab, origin)
                inside = inside | ours
            hot = jnp.where((iota((high - low, BT), 0) + low == origin) & inside, 1.0, 0.0)
            part = bdot(pieces[owner, :, low:high], hot)
            total = part if total is None else total + part
        target[:, base : base + BT] = total.astype(jnp.bfloat16)


SMALL_ROWS = 24


def mixer_backward_kernel(
    heads,
    n_seq,
    n_fsdp,
    lengths_ref,
    row_ref,
    grad_ref,
    taps_in,
    gain_ref,
    norm_gain_ref,
    ffn_gain_ref,
    delta_in,
    inverse_in,
    big_in,
    update_in,
    state_in,
    packed_in,
    normed_in,
    weight_in,
    tokens_in,
    hidden_in,
    grad_hidden_in,
    result_in,
    gate_in,
    up_in,
    down_in,
    out_in,
    result_out,
    tokens_out,
    gate_out,
    up_out,
    down_out,
    out_out,
    query_out,
    key_out,
    value_out,
    beta_out,
    small_out,
    norm_out,
    retain_ref,
    taps_ref,
    column_ref,
    delta_ref,
    inverse_ref,
    big_ref,
    update_ref,
    state_ref,
    packed_ref,
    grad_delta_ref,
    add_ref,
    after_ref,
    conv_ref,
    grad_proj_ref,
    arrived_ref,
    weight_ref,
    weight_grad_ref,
    wide_ref,
    tokens_ref,
    result_ref,
    result_mine,
    result_mate,
    result_far,
    normed_mine,
    normed_give,
    normed_mate,
    normed_far,
    gate_own,
    gate_second,
    up_own,
    up_first,
    up_second,
    down_own,
    down_first,
    down_second,
    out_sum,
    out_mate,
    out_first,
    out_second,
    out_far,
    query_first,
    query_second,
    key_first,
    key_second,
    value_first,
    value_second,
    beta_first,
    beta_second,
    gate_total,
    up_total,
    down_total,
    out_total,
    mixer_total,
    gate_all,
    up_all,
    spread_ref,
    taps_grad_ref,
    small_ref,
    small_all,
    small_seq,
    small_sum,
    norm_ref,
    norm_all,
    norm_seq,
    send_sems,
    recv_sems,
    gather_send,
    gather_recv,
    share_send,
    share_recv,
    local_sems,
):
    tokens = grad_ref.shape[0]
    blocks = tokens // BT
    head_width = heads * DK
    width = 3 * head_width
    own = tokens // n_seq
    model = tokens_ref.shape[1]
    own_rows, units = gate_own.shape
    slab = down_own.shape[1]
    seq, fsdp = lax.axis_index("seq"), lax.axis_index("fsdp")
    mate = seq + 1 - 2 * (seq % 2)
    core = seq % 2
    chip = seq // 2
    chips = n_seq // 2
    inner = n_fsdp // Scatter.outer
    inner_high, inner_low = fsdp // inner, fsdp % inner
    low, full = jnp.bfloat16, jnp.float32

    local = {}

    def bring(name, source, target):
        copy = pltpu.make_async_copy(source, target, local_sems.at[len(local)])
        local[name] = copy
        copy.start()

    def far(step):
        return (seq + n_seq - 2 * step) % n_seq

    def far_mate(step):
        there = far(step)
        return there + 1 - 2 * (there % 2)

    def shard(ref, index):
        return ref.at[pl.ds(aligned(index * own, own), own)]

    for name, source, target in (
        ("delta", delta_in, delta_ref),
        ("big", big_in, big_ref),
        ("packed", packed_in, packed_ref.at[:, pl.ds(0, packed_in.shape[1])]),
        ("inverse", inverse_in, inverse_ref),
        ("update", update_in, update_ref),
        ("state", state_in, state_ref),
    ):
        bring(name, source, target)
    greet_signal(n_seq, n_fsdp)
    wire = Wire(send_sems, recv_sems)
    result_sum = SeqSum(
        n_seq,
        wire,
        lambda step: shard(result_in, mate if step == 0 else far_mate(step)),
        lambda step: result_mine.at[step],
        result_mate,
        result_far,
    )
    normed_sum = SeqSum(
        n_seq,
        wire,
        lambda step: normed_give.at[step],
        lambda step: normed_mine.at[step],
        normed_mate,
        normed_far,
    )
    half = out_sum.shape[1]
    out_rows = out_sum.shape[0] // n_fsdp
    half_at = pl.ds(aligned(core * half, half), half)
    out_give = wire.copy(
        out_in.at[:, pl.ds(aligned((1 - core) * half, half), half)], out_mate, mate, fsdp
    )

    def rows_of(ref, size):
        return lambda owner: ref.at[pl.ds(aligned(owner * size, size), size)]

    def scatter(block, first, second):
        def parts(high):
            return block(high * inner + inner_low)

        return Scatter(n_fsdp, wire, block, parts, lambda: parts(inner_high), first, second)

    gate_sum = Scatter(
        n_fsdp, wire, None, lambda high: gate_in.at[high], lambda: gate_own, None, gate_second
    )
    up_sum = Scatter(
        n_fsdp,
        wire,
        rows_of(up_in, own_rows),
        lambda high: up_own.at[high],
        lambda: up_own.at[inner_high],
        up_first,
        up_second,
    )
    down_sum = Scatter(
        n_fsdp,
        wire,
        lambda owner: down_in.at[owner],
        lambda high: down_own.at[high],
        lambda: down_own.at[inner_high],
        down_first,
        down_second,
    )
    out_scatter = scatter(rows_of(out_sum, out_rows), out_first, out_second)
    spans = [(kind * head_width, head_width) for kind in range(3)] + [(width, DK)]

    def mixer_block(span):
        return lambda owner: weight_grad_ref.at[
            pl.ds(aligned(owner * own_rows, own_rows), own_rows), pl.ds(span[0], span[1])
        ]

    mixer_sums = [
        scatter(mixer_block(span), first, second)
        for span, first, second in zip(
            spans,
            (query_first, key_first, value_first, beta_first),
            (query_second, key_second, value_second, beta_second),
        )
    ]
    out_across = [
        wire.copy(out_far.at[chip], out_far.at[chip], (seq + 2 * step) % n_seq, fsdp)
        for step in range(1, chips)
    ]
    out_swap = wire.copy(out_total, out_out.at[:, half_at], mate, fsdp)

    share_sems = (share_send, share_recv)
    gather_sems = (gather_send, gather_recv)
    per_share, per_gather = Share.copies(n_seq), Gather.copies(n_fsdp)

    def share(index, source, slot):
        return Share(
            n_seq, source, slot, share_sems, index * per_share, local_sems.at[50 + index]
        )

    def stacked(ref):
        return lambda owner: ref.at[owner]

    def head_columns(ref):
        return lambda owner: ref.at[:, pl.ds(aligned(owner * head_width, head_width), head_width)]

    gate_share = share(0, gate_total, stacked(gate_all))
    up_share = share(1, up_total, stacked(up_all))
    down_share = share(2, down_total, stacked(down_out))
    mixer_shares = [
        share(3 + index, mixer_total.at[:, pl.ds(span[0], span[1])], slot)
        for index, (span, slot) in enumerate(
            zip(
                spans,
                (
                    head_columns(query_out),
                    head_columns(key_out),
                    head_columns(value_out),
                    stacked(beta_out),
                ),
            )
        )
    ]
    small_share = share(7, small_ref, stacked(small_seq))
    norm_share = share(8, norm_ref, stacked(norm_seq))
    small_gather = Gather(
        n_fsdp, small_ref, stacked(small_all), gather_sems, 0, local_sems.at[59]
    )
    norm_gather = Gather(
        n_fsdp, norm_ref, stacked(norm_all), gather_sems, per_gather, local_sems.at[60]
    )

    for high in range(Scatter.outer):
        owner = high * inner + inner_low
        bring(("up", high), rows_of(up_in, own_rows)(owner), up_own.at[high])
        bring(("down", high), down_in.at[owner], down_own.at[high])
    bring("out", out_in.at[:, half_at], out_sum)
    bring("gate", gate_in.at[inner_high], gate_own)
    for step in range(1, chips):
        bring(("result", step), shard(result_in, far(step)), result_mine.at[step])
    bring("result", shard(result_in, seq), result_mine.at[0])
    bring("hidden", hidden_in, wide_ref)
    bring("weight", weight_in, weight_ref)
    bring("tokens", tokens_in, tokens_ref)
    fill_flags(retain_ref, lengths_ref)
    fill_taps(taps_ref, taps_in, seq, head_width)
    fill_column(column_ref, row_ref)
    small_ref[...] = jnp.zeros(small_ref.shape, full)
    taps_grad_ref[...] = jnp.zeros(taps_grad_ref.shape, full)
    greet_wait(n_seq, n_fsdp)
    gate_sum.leave()
    up_sum.start()
    for copy in result_sum.gives:
        copy.start()
    out_give.start()
    local["delta"].wait()
    local["big"].wait()

    def head_norm(step, total):
        base = pl.multiple_of(step * PB, PB)
        picked = permute_rows(column_ref[pl.ds(base, PB), :], grad_ref[...], tokens)
        for head in range(heads):
            at = slice(head * DK, head * DK + DK)
            grad = picked[:, at]
            delta = delta_ref[pl.ds(base, PB), at]
            inv = lax.rsqrt(jnp.mean(delta * delta, axis=1, keepdims=True) + EPS_NORM)
            unit = delta * inv
            total = total + jnp.sum(grad * unit, axis=0, keepdims=True)
            grad_unit = grad * gain_ref[...]
            shrunk = (
                inv * (grad_unit - unit * jnp.mean(grad_unit * unit, axis=1, keepdims=True))
            ).astype(low)
            grad_delta_ref[pl.ds(base, PB), at] = shrunk
            for sub in range(PB // BT):
                place = head * blocks + step * (PB // BT) + sub
                add_ref[place] = bdot(
                    big_ref[place, BT : 2 * BT, :], shrunk[sub * BT : sub * BT + BT], TN
                ).astype(low)
        return total

    gain_row = 3 * CONV
    small_ref[gain_row : gain_row + 1, 0:DK] = lax.fori_loop(
        0, tokens // PB, head_norm, jnp.zeros((1, DK), full)
    )
    for index in range(model // head_width):
        small_ref[gain_row + 1 + index : gain_row + 2 + index, :] = ffn_gain_ref[
            :, index * head_width : (index + 1) * head_width
        ]
    for step in range(1, chips):
        local["result", step].wait()
        result_sum.reduce(step)

    def retreat(step, grads):
        block = blocks - 1 - step
        through = retain_ref[2 * block] * retain_ref[2 * block + 1]
        lows = [grad.astype(low) for grad in grads]
        following = []
        for head in range(heads):
            place = head * blocks + block
            after_ref[place] = lows[head]
            following.append(
                grads[head] * through
                - bdot(big_ref[place, 0:BT, :], lows[head], TN)
                + add_ref[place].astype(full)
            )
        return tuple(following)

    zero = jnp.zeros((DK, DK), full)
    lax.fori_loop(0, blocks, retreat, (zero,) * heads)
    for name in ("packed", "inverse", "update", "state"):
        local[name].wait()

    conv_ref[BT : BT + HALO, :] = jnp.zeros((HALO, width), full)

    def first_stage():
        for high in range(Scatter.outer):
            local["up", high].wait()
        up_sum.combine()
        up_sum.leave()
        down_sum.start()
        local["gate"].wait()
        gate_total[...] = gate_sum.total()
        gate_share.start()

    def add_out():
        local["out"].wait()
        out_give.wait_recv()

        def add(number, carry):
            at = pl.ds(aligned(number * CHUNK, CHUNK), CHUNK)
            out_sum[at, :] = (out_sum[at, :].astype(full) + out_mate[at, :].astype(full)).astype(
                low
            )
            return carry

        lax.fori_loop(0, out_sum.shape[0] // CHUNK, add, 0)

    def second_stage():
        for high in range(Scatter.outer):
            local["down", high].wait()
        down_sum.combine()
        down_sum.leave()
        out_scatter.start()
        up_total[...] = up_sum.total()
        up_share.start()
        gate_share.relay()

    def result_stage():
        local["hidden"].wait()
        local["result"].wait()
        result_sum.arrive()

        def add(number, carry):
            at = pl.ds(aligned(number * CHUNK, CHUNK), CHUNK)
            result_ref[at, :] = (wide_ref[at, :] + result_sum.total(at)).astype(low)
            return carry

        lax.fori_loop(0, own // CHUNK, add, 0)

    first_stage()

    def gradients(step, carry):
        for moment, stage in ((4, add_out), (8, second_stage), (12, result_stage)):

            @pl.when(step == moment)
            def _():
                stage()

        block = blocks - 1 - step
        first, second, third = (
            retain_ref[2 * block],
            retain_ref[2 * block + 1],
            retain_ref[2 * block + 2],
        )
        base = pl.multiple_of(block * BT, BT)
        masks = tap_masks(first, second, third, BT + HALO)
        near_masks = [None] + [mask[:BT] for mask in masks[1:]]
        seen, kept = block_flags(first, second)
        rows, cols, cross = pair_mask(second)
        turned = jnp.where((rows < CH) & (cols >= CH), second, 1.0)
        lanes = iota((BT, BT), 1)
        strengths = sigmoid(
            packed_ref[pl.ds(HALO + base, BT), width : width + BT].astype(jnp.float32)
        )
        grad_strengths = jnp.zeros((BT, BT), jnp.float32)
        for head in range(heads):
            place = head * blocks + block
            convs, gates, acts = [], [], []
            for kind in range(3):
                at = (kind * heads + head) * DK
                window = packed_ref[pl.ds(base, HALO + BT), at : at + DK].astype(jnp.float32)
                taps = [
                    taps_ref[kind * CONV + back : kind * CONV + back + 1, head * DK : head * DK + DK]
                    for back in range(CONV)
                ]
                conv = conv_of(window, taps, near_masks)
                gate = sigmoid(conv)
                convs.append(conv)
                gates.append(gate)
                acts.append(conv * gate)
            inv_q = lax.rsqrt(jnp.sum(acts[0] * acts[0], axis=1, keepdims=True) + EPS_NORM)
            inv_k = lax.rsqrt(jnp.sum(acts[1] * acts[1], axis=1, keepdims=True) + EPS_NORM)
            query_low = (acts[0] * inv_q * DK ** (-0.5)).astype(jnp.bfloat16)
            key_low = (acts[1] * inv_k).astype(jnp.bfloat16)
            key = key_low.astype(jnp.float32)
            value = acts[2]
            beta = strengths[:, head : head + 1]
            grad_low = grad_delta_ref[pl.ds(base, BT), head * DK : head * DK + DK]
            after = after_ref[place]
            state = state_ref[place]
            update = update_ref[place]
            inner = bdot(key_low, jnp.concatenate([key_low, query_low], axis=0), NT)
            scores_t = jnp.where(rows <= cols, inner[:, BT:] * turned, 0.0)
            grad_update = bdot(scores_t, grad_low) + bdot(key * kept, after)
            solved = bdot(inverse_ref[place], grad_update, TN)
            solved_beta = solved * beta
            both = jnp.concatenate([grad_low, solved.astype(jnp.bfloat16)], axis=0)
            on_state = bdot(both, state, NT)
            on_update = bdot(both, update, NT)
            grad_scores = jnp.where(rows >= cols, on_update[:BT] * cross, 0.0)
            grad_strict = jnp.where(rows > cols, on_update[BT:] * cross, 0.0)
            grad_weighted = on_state[BT:] * seen
            turned_both = bdot(
                update,
                jnp.concatenate(
                    [grad_low, solved_beta.astype(jnp.bfloat16)], axis=0
                ),
                NT,
            )
            grad_scores_t = jnp.where(rows <= cols, turned_both[:, :BT] * turned, 0.0)
            strict_t = jnp.where(rows < cols, turned_both[:, BT:] * turned, 0.0)
            grad_query = on_state[:BT] * seen + bdot(grad_scores, key_low)
            grad_key = (
                bdot(grad_scores_t, query_low)
                + bdot(update, after, NT) * kept
                - beta * grad_weighted
                - bdot(grad_strict * beta + strict_t, key_low)
            )
            grad_value = solved_beta
            grad_beta = jnp.sum(
                solved * value - grad_strict * inner[:, :BT] - grad_weighted * key,
                axis=1,
                keepdims=True,
            )
            grad_strengths = jnp.where(lanes == head, grad_beta, grad_strengths)
            scaled = (
                inv_q
                * DK ** (-0.5)
                * (
                    grad_query
                    - acts[0]
                    * (inv_q * inv_q)
                    * jnp.sum(grad_query * acts[0], axis=1, keepdims=True)
                ),
                inv_k
                * (
                    grad_key
                    - acts[1] * (inv_k * inv_k) * jnp.sum(grad_key * acts[1], axis=1, keepdims=True)
                ),
                grad_value,
            )
            for kind in range(3):
                at = (kind * heads + head) * DK
                conv_ref[0:BT, at : at + DK] = (
                    scaled[kind] * gates[kind] * (1.0 + convs[kind] * (1.0 - gates[kind]))
                )
        grad_proj_ref[pl.ds(base, BT), width : width + BT] = (
            grad_strengths * strengths * (1.0 - strengths)
        ).astype(jnp.bfloat16)
        for kind in range(3):
            for head in range(heads):
                at = (kind * heads + head) * DK
                span = slice(head * DK, head * DK + DK)
                grads = conv_ref[:, at : at + DK]
                window = packed_ref[pl.ds(base, HALO + BT), at : at + DK].astype(jnp.float32)
                total = None
                for back in range(CONV):
                    row = kind * CONV + back
                    tap = taps_ref[row : row + 1, span]
                    masked = grads if back == 0 else grads * masks[back]
                    shifted = (
                        masked if back == 0 else pltpu.roll(masked, BT + HALO - back, 0)
                    )[:BT]
                    total = shifted * tap if total is None else total + shifted * tap
                    past = (window if back == 0 else pltpu.roll(window, back, 0))[HALO:]
                    taps_grad_ref[row : row + 1, span] += jnp.sum(
                        masked[:BT] * past, axis=0, keepdims=True
                    )
                grad_proj_ref[pl.ds(base, BT), at : at + DK] = total.astype(jnp.bfloat16)
        conv_ref[BT : BT + HALO, :] = conv_ref[0:HALO, :]
        return carry

    lax.fori_loop(0, blocks, gradients, 0)

    bring("keep_result", result_ref, result_out)
    bring("normed", normed_in, packed_ref.at[pl.ds(0, tokens)])
    bring("grad_hidden", grad_hidden_in, wide_ref)
    small_ref[0:gain_row, :] = taps_grad_ref[0:gain_row, :]
    small_gather.start()
    out_scatter.combine()
    out_scatter.leave()
    part = min(PB, own)

    def push_back(index, target):
        def step(number, carry):
            base = aligned(index * own + number * part, part)
            hot = jnp.where(row_ref[...] == iota((part, tokens), 0) + base, 1.0, 0.0).astype(low)
            arrived_ref[...] = lax.dot_general(
                hot, grad_proj_ref[...], NN, preferred_element_type=jnp.float32
            ).astype(low)
            target[pl.ds(aligned(number * part, part), part), :] = bdot(
                arrived_ref[...], weight_ref[...], NT
            ).astype(low)
            return carry

        lax.fori_loop(0, own // part, step, 0)

    local["weight"].wait()
    for step in range(1, chips):
        push_back(far_mate(step), normed_give.at[step])
        normed_sum.gives[step].start()
        push_back(far(step), normed_mine.at[step])
        normed_sum.reduce(step)
    local["normed"].wait()

    def weight_grad(span):
        def step(number, carry):
            at = pl.ds(aligned(number * PB, PB), PB)
            weight_grad_ref[at, pl.ds(span[0], span[1])] = bdot(
                packed_ref[0:tokens, at], grad_proj_ref[:, pl.ds(span[0], span[1])], TN
            ).astype(low)
            return carry

        lax.fori_loop(0, model // PB, step, 0)

    weight_grad(spans[0])
    mixer_sums[0].start()
    weight_grad(spans[1])
    mixer_sums[1].start()
    down_total[...] = down_sum.total()
    down_share.start()
    up_share.relay()
    small_gather.relay()
    push_back(mate, normed_give.at[0])
    normed_sum.gives[0].start()
    weight_grad(spans[2])
    weight_grad(spans[3])
    mixer_sums[0].combine()
    mixer_sums[0].leave()
    mixer_sums[2].start()
    push_back(seq, normed_mine.at[0])
    out_far[chip] = out_scatter.total()
    for copy in out_across:
        copy.start()
    mixer_sums[1].combine()
    mixer_sums[1].leave()
    mixer_sums[3].start()
    gate_share.finish()
    spread_units(spread_ref.at[0], gate_all, n_seq, slab)
    bring("keep_gate", spread_ref.at[0], gate_out)
    small_gather.finish()
    total = small_all[0]
    for owner in range(1, n_fsdp):
        total = total + small_all[owner]
    small_ref[...] = total
    small_share.start()
    down_share.relay()
    mixer_sums[2].combine()
    mixer_sums[2].leave()
    mixer_total[:, spans[0][0] : spans[0][0] + spans[0][1]] = mixer_sums[0].total()
    mixer_shares[0].start()
    up_share.finish()
    spread_units(spread_ref.at[1], up_all, n_seq, slab)
    bring("keep_up", spread_ref.at[1], up_out)
    mixer_sums[3].combine()
    mixer_sums[3].leave()
    local["grad_hidden"].wait()
    local["tokens"].wait()
    normed_sum.arrive()

    def norm_back(number, total):
        at = pl.ds(aligned(number * CHUNK, CHUNK), CHUNK)
        values = tokens_ref[at, :].astype(full)
        inv = lax.rsqrt(jnp.mean(values * values, axis=1, keepdims=True) + EPS_NORM)
        unit = values * inv
        grad = normed_sum.total(at)
        grad_unit = grad * norm_gain_ref[...]
        wide_ref[at, :] += inv * (
            grad_unit - unit * jnp.mean(grad_unit * unit, axis=1, keepdims=True)
        )
        return total + jnp.sum(grad * unit, axis=0, keepdims=True)

    total = lax.fori_loop(0, own // CHUNK, norm_back, jnp.zeros((1, model), full))
    for index in range(model // DK):
        norm_ref[index : index + 1, :] = total[:, index * DK : (index + 1) * DK]
    norm_gather.start()
    bring("keep_tokens", wide_ref, tokens_out)
    mixer_shares[0].relay()
    mixer_total[:, spans[1][0] : spans[1][0] + spans[1][1]] = mixer_sums[1].total()
    mixer_shares[1].start()
    norm_gather.relay()
    for copy in out_across:
        copy.wait_recv()
    total = out_far[0].astype(full)
    for index in range(1, chips):
        total = total + out_far[index].astype(full)
    out_total[...] = total.astype(low)
    out_swap.start()
    bring("keep_out", out_total, out_out.at[:, half_at])
    mixer_shares[1].relay()
    mixer_total[:, spans[2][0] : spans[2][0] + spans[2][1]] = mixer_sums[2].total()
    mixer_shares[2].start()
    small_share.relay()
    norm_gather.finish()
    total = norm_all[0]
    for owner in range(1, n_fsdp):
        total = total + norm_all[owner]
    norm_ref[...] = total
    norm_share.start()
    mixer_total[:, spans[3][0] : spans[3][0] + spans[3][1]] = mixer_sums[3].total()
    mixer_shares[3].start()
    mixer_shares[2].relay()
    small_share.finish()
    total = small_seq[0]
    for owner in range(1, n_seq):
        total = total + small_seq[owner]
    for owner in range(n_seq):
        small_sum[0:gain_row, owner * head_width : (owner + 1) * head_width] = small_seq[
            owner, 0:gain_row, :
        ]
    small_sum[gain_row : gain_row + 2, :] = jnp.zeros((2, model), full)
    small_sum[gain_row : gain_row + 1, 0:DK] = total[gain_row : gain_row + 1, 0:DK]
    for index in range(model // head_width):
        small_sum[
            gain_row + 1 : gain_row + 2, index * head_width : (index + 1) * head_width
        ] = total[gain_row + 1 + index : gain_row + 2 + index, :]
    bring("keep_small", small_sum, small_out)
    norm_share.relay()
    mixer_shares[3].relay()
    norm_share.finish()
    total = norm_seq[0]
    for owner in range(1, n_seq):
        total = total + norm_seq[owner]
    norm_ref[...] = total
    bring("keep_norm", norm_ref, norm_out)
    for each in [down_share] + mixer_shares:
        each.finish()
    for each in [gate_sum, up_sum, down_sum, out_scatter] + mixer_sums + [result_sum, normed_sum]:
        each.drain()
    for copy in out_across:
        copy.wait_send()
    out_give.wait_send()
    out_swap.wait()
    for name, copy in local.items():
        if str(name).startswith("keep_"):
            copy.wait()


def mixer_backward(n_seq, n_fsdp, small, saved, big):
    (lengths, row, grad_heads, taps, gain, norm_gain, ffn_gain) = small
    packed, delta, inverse, parts, update, state = saved
    normed, weight, own_tokens, hidden, grad_hidden, result, gate, up, down, out = big
    tokens = grad_heads.shape[0]
    width = packed.shape[1]
    head_width = grad_heads.shape[1]
    heads = head_width // DK
    count = heads * (tokens // BT)
    own, model = own_tokens.shape
    _, own_rows, units = gate.shape
    slab = down.shape[1]
    hidden_units = slab * n_fsdp * n_seq
    out_rows = out.shape[0] // n_fsdp
    half = out.shape[1] // 2
    chips = n_seq // 2
    outer = Scatter.outer
    near = outer * (n_fsdp // outer - 1)
    low, full = jnp.bfloat16, jnp.float32
    copies = 8 * Scatter.copies(n_fsdp) + 2 * (2 * chips - 1) + 2 + chips - 1
    shares, gathers = 9 * Share.copies(n_seq), 2 * Gather.copies(n_fsdp)

    def shape(dims, kind=low):
        return jax.ShapeDtypeStruct(dims, kind)

    def held(*dims, kind=low):
        return pltpu.VMEM(dims, kind)

    def sum_buffers(rows, cols):
        return [held(near, rows, cols), held(outer - 1, rows, cols)]

    return pl.pallas_call(
        functools.partial(mixer_backward_kernel, heads, n_seq, n_fsdp),
        out_shape=(
            shape((own, model)),
            shape((own, model), full),
            shape((own_rows, hidden_units)),
            shape((own_rows, hidden_units)),
            shape((n_seq, slab, model)),
            shape((out_rows, 2 * half)),
            shape((own_rows, n_seq * head_width)),
            shape((own_rows, n_seq * head_width)),
            shape((own_rows, n_seq * head_width)),
            shape((n_seq, own_rows, DK)),
            shape((16, model), full),
            shape((model // DK, DK), full),
        ),
        in_specs=[spec(SMEM)] + [spec()] * 6 + [spec(ANY)] * 16,
        out_specs=(spec(ANY),) * 12,
        scratch_shapes=[
            pltpu.SMEM((tokens // CH + 2,), full),
            held(3 * CONV, head_width, kind=full),
            held(tokens, 1, kind=jnp.int32),
            held(tokens, head_width, kind=full),
            held(count, BT, BT),
            held(count, 2 * BT, BT),
            held(count, BT, BT),
            held(count, BT, BT),
            held(HALO + tokens, max(width, model)),
            held(tokens, head_width),
            held(count, BT, BT),
            held(count, BT, BT),
            held(BT + HALO, 3 * head_width, kind=full),
            held(tokens, width),
            held(min(PB, own), width),
            held(model, width),
            held(model, width),
            held(own, model, kind=full),
            held(own, model),
            held(own, model),
            held(chips, own, model),
            held(chips, own, model),
            held(chips - 1, own, model),
            held(chips, own, model),
            held(chips, own, model),
            held(chips, own, model),
            held(chips - 1, own, model),
            held(own_rows, units),
            held(outer - 1, own_rows, units),
            held(outer, own_rows, units),
            *sum_buffers(own_rows, units),
            held(outer, slab, model),
            *sum_buffers(slab, model),
            held(out.shape[0], half),
            held(out.shape[0], half),
            *sum_buffers(out_rows, half),
            held(chips, out_rows, half),
            *sum_buffers(own_rows, head_width),
            *sum_buffers(own_rows, head_width),
            *sum_buffers(own_rows, head_width),
            *sum_buffers(own_rows, DK),
            held(own_rows, units),
            held(own_rows, units),
            held(slab, model),
            held(out_rows, half),
            held(own_rows, width),
            held(n_seq, own_rows, units),
            held(n_seq, own_rows, units),
            held(2, own_rows, hidden_units),
            held(16, head_width, kind=full),
            held(SMALL_ROWS, head_width, kind=full),
            held(n_fsdp, SMALL_ROWS, head_width, kind=full),
            held(n_seq, SMALL_ROWS, head_width, kind=full),
            held(16, model, kind=full),
            held(model // DK, DK, kind=full),
            held(n_fsdp, model // DK, DK, kind=full),
            held(n_seq, model // DK, DK, kind=full),
            pltpu.SemaphoreType.DMA((copies,)),
            pltpu.SemaphoreType.DMA((copies,)),
            pltpu.SemaphoreType.DMA((gathers,)),
            pltpu.SemaphoreType.DMA((gathers,)),
            pltpu.SemaphoreType.DMA((shares,)),
            pltpu.SemaphoreType.DMA((shares,)),
            pltpu.SemaphoreType.DMA((61,)),
        ],
        compiler_params=pltpu.CompilerParams(
            vmem_limit_bytes=63 << 20, collective_id=3, has_side_effects=True
        ),
        name="mixer_backward",
    )(
        lengths, row, grad_heads, taps, gain, norm_gain, ffn_gain, delta, inverse, parts,
        update, state, packed, normed, weight, own_tokens, hidden, grad_hidden, result,
        gate, up, down, out,
    )


def finish_kernel(
    heads,
    result_in,
    tokens_in,
    gate_in,
    up_in,
    down_in,
    out_in,
    query_in,
    key_in,
    value_in,
    beta_in,
    small_in,
    norm_in,
    result_ref,
    tokens_ref,
    norm_ref,
    query_ref,
    key_ref,
    value_ref,
    beta_ref,
    taps_ref,
    gain_ref,
    out_ref,
    ffn_ref,
    gate_ref,
    up_ref,
    down_ref,
):
    full = jnp.float32
    result_ref[...] = result_in[...]
    tokens_ref[...] = tokens_in[...]
    for source, target in (
        (gate_in, gate_ref),
        (up_in, up_ref),
        (out_in, out_ref),
        (query_in, query_ref),
        (key_in, key_ref),
        (value_in, value_ref),
        (down_in, down_ref),
    ):
        target[...] = source[...].astype(full)
    total = None
    row, col = iota((DK, beta_ref.shape[1]), 0), iota((DK, beta_ref.shape[1]), 1)
    for owner in range(beta_in.shape[0]):
        hot = jnp.where((row + owner * heads == col) & (row < heads), 1.0, 0.0)
        part = bdot(beta_in[owner], hot)
        total = part if total is None else total + part
    beta_ref[...] = total
    for kind in range(3):
        for back in range(CONV):
            at = kind * CONV + back
            taps_ref[kind, back : back + 1, :] = small_in[at : at + 1, :]
    gain_ref[...] = small_in[3 * CONV : 3 * CONV + 1, 0:DK]
    ffn_ref[...] = small_in[3 * CONV + 1 : 3 * CONV + 2, :]
    for index in range(norm_in.shape[0]):
        norm_ref[:, index * DK : (index + 1) * DK] = norm_in[index : index + 1, :]


def finish(heads, arrays):
    result, tokens, gate, up, down, out, query, key, value, beta, small, norm = arrays
    full = jnp.float32
    model = small.shape[1]
    head_count = heads * beta.shape[0]

    def wide(array):
        return jax.ShapeDtypeStruct(array.shape, full)

    return pl.pallas_call(
        functools.partial(finish_kernel, heads),
        out_shape=(
            jax.ShapeDtypeStruct(result.shape, result.dtype),
            wide(tokens),
            jax.ShapeDtypeStruct((1, model), full),
            wide(query),
            wide(key),
            wide(value),
            jax.ShapeDtypeStruct((query.shape[0], head_count), full),
            jax.ShapeDtypeStruct((3, CONV, model), full),
            jax.ShapeDtypeStruct((1, DK), full),
            wide(out),
            jax.ShapeDtypeStruct((1, model), full),
            wide(gate),
            wide(up),
            wide(down),
        ),
        in_specs=[spec()] * 12,
        out_specs=(spec(),) * 14,
        compiler_params=pltpu.CompilerParams(vmem_limit_bytes=63 << 20),
        name="finish",
    )(*arrays)


def own_slice(array, place, size, axis):
    return lax.dynamic_slice_in_dim(array, place * size, size, axis)


def local(
    n_seq,
    n_fsdp,
    tokens,
    norm_gain,
    w_query,
    w_key,
    w_value,
    w_beta,
    conv_taps,
    head_gain,
    w_out,
    ffn_gain,
    w_gate,
    w_up,
    w_down,
    cotangent,
    token_order,
    seq_lengths,
):
    place = lax.axis_index("seq")
    model = tokens.shape[1]
    head_count = w_beta.shape[1]
    heads = head_count // n_seq
    hidden_units = w_gate.shape[1]
    slab = hidden_units // (n_fsdp * n_seq)
    units = slab * n_fsdp

    row = token_order.reshape(1, -1)
    gain = head_gain.reshape(1, DK)
    mixed_tok, normed, w_mixer, full_gate, full_up, full_down, full_o, cot_all, *saved = (
        mixer_forward(
            n_seq,
            n_fsdp,
            seq_lengths,
            row,
            conv_taps,
            gain,
            norm_gain.reshape(1, model),
            (
                tokens,
                w_beta.T,
                cotangent,
                w_query,
                w_key,
                w_value,
                w_gate,
                w_up,
                w_down if slab % 8 == 0 else own_slice(w_down, place, slab, 0),
                w_out,
            ),
        )
    )
    full_down = full_down.reshape(units, model)
    (
        hidden,
        grad_hidden,
        grad_heads,
        result_part,
        wide_gate,
        wide_up,
        wide_down,
        wide_out,
        grad_ffn_gain,
    ) = ffn_block(
        n_seq,
        n_fsdp,
        tokens,
        mixed_tok,
        full_o,
        ffn_gain.reshape(1, model),
        full_gate,
        full_up,
        full_down,
        cot_all,
    )
    (
        result,
        grad_inputs,
        all_gate,
        all_up,
        part_down,
        all_out,
        all_query,
        all_key,
        all_value,
        part_beta,
        small,
        norm_sum,
    ) = mixer_backward(
        n_seq,
        n_fsdp,
        (
            seq_lengths,
            row,
            grad_heads,
            conv_taps,
            gain,
            norm_gain.reshape(1, model),
            grad_ffn_gain,
        ),
        saved,
        (
            normed,
            w_mixer,
            tokens,
            hidden,
            grad_hidden,
            result_part,
            wide_gate,
            wide_up,
            wide_down.reshape(n_fsdp, slab, model),
            wide_out,
        ),
    )
    outputs = finish(
        heads,
        (
            result,
            grad_inputs,
            all_gate,
            all_up,
            part_down.reshape(n_seq * slab, model),
            all_out,
            all_query,
            all_key,
            all_value,
            part_beta,
            small,
            norm_sum,
        ),
    )
    flat = (2, 8, 10)
    return tuple(
        output.reshape(-1) if index in flat else output for index, output in enumerate(outputs)
    )


def solution(mesh):
    tokens = P(("seq", "fsdp"), None)
    rows = P("fsdp", None)
    in_specs = (
        (tokens, P()) + (rows,) * 4 + (P(), P(), rows, P()) + (rows,) * 3 + (tokens, rows, rows)
    )
    out_specs = (
        (tokens, tokens, P()) + (rows,) * 4 + (P(), P(), rows, P()) + (rows,) * 3
    )
    return jax.shard_map(
        functools.partial(local, mesh.shape["seq"], mesh.shape["fsdp"]),
        mesh=mesh,
        in_specs=in_specs,
        out_specs=out_specs,
        check_vma=False,
    )
```

```python
import functools

import jax
import jax.numpy as jnp
from jax import lax
from jax.experimental import pallas as pl
from jax.experimental.pallas import tpu as pltpu
from jax.sharding import PartitionSpec as P

DK = 128
CONV = 4
CH = 64
BT = 128
HALO = 16
PB = 256
EPS_NORM = 1e-06

NN = (((1,), (0,)), ((), ()))
NT = (((1,), (1,)), ((), ()))
TN = (((0,), (0,)), ((), ()))


def bdot(first, second, dims=NN):
    return lax.dot_general(
        first.astype(jnp.bfloat16),
        second.astype(jnp.bfloat16),
        dims,
        preferred_element_type=jnp.float32,
    )


def iota(shape, axis):
    return lax.broadcasted_iota(jnp.int32, shape, axis)


def sigmoid(values):
    return 1.0 / (1.0 + jnp.exp(-values))


def fill_masks(mask_ref):
    rows, cols = iota((BT, BT), 0), iota((BT, BT), 1)
    size, level = 1, 0
    while size < BT:
        inside = (rows // (2 * size) == cols // (2 * size)) & (rows // size > cols // size)
        mask_ref[level] = jnp.where(inside, 1.0, 0.0)
        size, level = 2 * size, level + 1


def unit_lower_inverses(stricts, mask_ref):
    rows, cols = iota((BT, BT), 0), iota((BT, BT), 1)
    eye = jnp.where(rows == cols, 1.0, 0.0)
    inverses = [eye - strict * mask_ref[0] for strict in stricts]
    for level in range(1, 7):
        lows = [inverse.astype(jnp.bfloat16) for inverse in inverses]
        inner = [bdot(strict * mask_ref[level], low) for strict, low in zip(stricts, lows)]
        inverses = [
            inverse - bdot(low, mid) for inverse, low, mid in zip(inverses, lows, inner)
        ]
    return inverses


def tap_masks(first, second, third, count):
    rows = iota((count, 1), 0)
    flag = jnp.where(rows < CH, first, jnp.where(rows < BT, second, third))
    return [None] + [jnp.where(rows % CH < back, flag, 1.0) for back in range(1, CONV)]


def conv_of(halo_rows, taps, masks):
    total = halo_rows[HALO:] * taps[0]
    for back in range(1, CONV):
        total = total + pltpu.roll(halo_rows, back, 0)[HALO:] * (taps[back] * masks[back])
    return total


def block_flags(first, second):
    upper = iota((BT, 1), 0) < CH
    seen = jnp.where(upper, first, first * second)
    kept = jnp.where(upper, second, 1.0)
    return seen, kept


def pair_mask(second):
    rows, cols = iota((BT, BT), 0), iota((BT, BT), 1)
    cross = (rows >= CH) & (cols < CH)
    return rows, cols, jnp.where(cross, second, 1.0)


def permute_rows(column, source, width):
    hot = jnp.where(column == iota((column.shape[0], width), 1), 1.0, 0.0).astype(jnp.bfloat16)
    return lax.dot_general(hot, source, NN, preferred_element_type=jnp.float32)


def unpermute_rows(row, base, source, width):
    hot = jnp.where(row == iota((PB, width), 0) + base, 1.0, 0.0).astype(jnp.bfloat16)
    return lax.dot_general(hot, source, NN, preferred_element_type=jnp.float32)


MESH = pl.DeviceIdType.MESH
ANY = pl.ANY


class Gather:
    outer = 4

    @classmethod
    def copies(cls, n_fsdp):
        inner = n_fsdp // cls.outer
        return (cls.outer - 1) + cls.outer * (inner - 1)

    def __init__(self, n_fsdp, source, slot, sems, base, local_sem):
        self.inner = n_fsdp // self.outer
        self.me = lax.axis_index("fsdp")
        self.seq = lax.axis_index("seq")
        self.high, self.low = self.me // self.inner, self.me % self.inner
        self.source, self.slot = source, slot
        self.send, self.recv = sems
        self.base, self.local_sem = base, local_sem

    def at(self, high, low):
        return (high % self.outer) * self.inner + (low % self.inner)

    def copy(self, source, owner, target, index):
        return pltpu.make_async_remote_copy(
            src_ref=source,
            dst_ref=self.slot(owner),
            send_sem=self.send.at[self.base + index],
            recv_sem=self.recv.at[self.base + index],
            device_id=(self.seq, target),
            device_id_type=MESH,
        )

    def along_outer(self, step):
        return self.copy(self.source, self.me, self.at(self.high + step, self.low), step - 1)

    def along_inner(self, hop):
        return self.copy(
            self.source, self.me, self.at(self.high, self.low + hop), self.outer - 2 + hop
        )

    def passed_on(self, step, hop):
        owner = self.at(self.high - step, self.low)
        index = self.outer - 1 + (self.inner - 1) * step + hop - 1
        return self.copy(self.slot(owner), owner, self.at(self.high, self.low + hop), index)

    def own(self):
        return pltpu.make_async_copy(self.source, self.slot(self.me), self.local_sem)

    def start(self):
        for step in range(1, self.outer):
            self.along_outer(step).start()
        for hop in range(1, self.inner):
            self.along_inner(hop).start()
        self.own().start()

    def relay(self):
        for step in range(1, self.outer):
            self.along_outer(step).wait_recv()
            for hop in range(1, self.inner):
                self.passed_on(step, hop).start()

    def finish(self):
        self.own().wait()
        for hop in range(1, self.inner):
            self.along_inner(hop).wait_recv()
            for step in range(1, self.outer):
                self.passed_on(step, hop).wait_recv()
        for step in range(1, self.outer):
            self.along_outer(step).wait_send()
        for hop in range(1, self.inner):
            self.along_inner(hop).wait_send()
            for step in range(1, self.outer):
                self.passed_on(step, hop).wait_send()


class Share:
    @staticmethod
    def copies(n_seq):
        return 1 + 2 * (n_seq // 2 - 1)

    def __init__(self, n_seq, source, slot, sems, base, local_sem):
        self.n_seq, self.chips = n_seq, n_seq // 2
        self.me = lax.axis_index("seq")
        self.fsdp = lax.axis_index("fsdp")
        self.mate = self.me + 1 - 2 * (self.me % 2)
        self.source, self.slot = source, slot
        self.send, self.recv = sems
        self.base, self.local_sem = base, local_sem

    def copy(self, source, owner, target, index):
        return pltpu.make_async_remote_copy(
            src_ref=source,
            dst_ref=self.slot(owner),
            send_sem=self.send.at[self.base + index],
            recv_sem=self.recv.at[self.base + index],
            device_id=(target, self.fsdp),
            device_id_type=MESH,
        )

    def to_mate(self):
        return self.copy(self.source, self.me, self.mate, 0)

    def across(self, step):
        return self.copy(self.source, self.me, (self.me + 2 * step) % self.n_seq, step)

    def passed_on(self, step):
        owner = (self.me + self.n_seq - 2 * step) % self.n_seq
        return self.copy(self.slot(owner), owner, self.mate, self.chips - 1 + step)

    def own(self):
        return pltpu.make_async_copy(self.source, self.slot(self.me), self.local_sem)

    def start(self):
        for step in range(1, self.chips):
            self.across(step).start()
        self.to_mate().start()
        if self.local_sem is not None:
            self.own().start()

    def relay(self):
        for step in range(1, self.chips):
            self.across(step).wait_recv()
            self.passed_on(step).start()

    def waits(self):
        steps = range(1, self.chips)
        return [self.to_mate()] + [each(step) for step in steps for each in (self.across, self.passed_on)]

    def finish(self):
        if self.local_sem is not None:
            self.own().wait()
        self.to_mate().wait_recv()
        for step in range(1, self.chips):
            self.passed_on(step).wait_recv()
        self.to_mate().wait_send()
        for step in range(1, self.chips):
            self.across(step).wait_send()
            self.passed_on(step).wait_send()


def greet_signal(n_seq, n_fsdp):
    seq, fsdp = lax.axis_index("seq"), lax.axis_index("fsdp")
    barrier = pltpu.get_barrier_semaphore()
    for step in range(1, n_seq):
        pl.semaphore_signal(
            barrier, inc=1, device_id=((seq + step) % n_seq, fsdp), device_id_type=MESH
        )
    for step in range(1, n_fsdp):
        pl.semaphore_signal(
            barrier, inc=1, device_id=(seq, (fsdp + step) % n_fsdp), device_id_type=MESH
        )


def greet_wait(n_seq, n_fsdp):
    pl.semaphore_wait(pltpu.get_barrier_semaphore(), n_seq + n_fsdp - 2)


def greet(n_seq, n_fsdp):
    greet_signal(n_seq, n_fsdp)
    greet_wait(n_seq, n_fsdp)


def aligned(value, unit):
    return pl.multiple_of(value, unit)


def fill_flags(flags_ref, lengths_ref):
    def fill(span, carry):
        start, hit = 0, span == 0
        for index in range(lengths_ref.shape[1] - 1):
            start = start + lengths_ref[0, index]
            hit = hit | (span * CH == start)
        flags_ref[span] = jnp.where(hit, 0.0, 1.0)
        return carry

    lax.fori_loop(0, flags_ref.shape[0], fill, 0)


def fill_taps(taps_ref, taps_in, seq, width):
    for kind in range(3):
        for back in range(CONV):
            row = kind * CONV + back
            taps_ref[row : row + 1, :] = taps_in[
                kind, back : back + 1, pl.ds(aligned(seq * width, width), width)
            ]


def fill_column(column_ref, row_ref):
    for base in range(0, row_ref.shape[1], BT):
        rows = jnp.broadcast_to(row_ref[:, base : base + BT], (8, BT))
        column_ref[base : base + BT, :] = rows.T[:, 0:1]


def pick_units(target, source, seq, n_seq, slab):
    units, hidden = target.shape[1], source.shape[1]
    jump = slab * (n_seq - 1)
    for base in range(0, units, BT):
        size = min(BT, units - base)
        first, last = base // slab, (base + size - 1) // slab
        low = (base + jump * first) // BT * BT
        high = min(-(-(base + size + jump * (last + 1)) // BT) * BT, hidden)
        col = iota((high - low, size), 1) + base
        origin = col + jump * first + slab * seq - low
        for owner in range(first + 1, last + 1):
            origin = origin + jnp.where(col >= owner * slab, jump, 0)
        hot = jnp.where(iota((high - low, size), 0) == origin, 1.0, 0.0)
        target[:, base : base + size] = bdot(source[:, low:high], hot).astype(jnp.bfloat16)


def mixer_forward_kernel(
    heads,
    n_seq,
    n_fsdp,
    lengths_ref,
    row_ref,
    taps_in,
    gain_ref,
    norm_gain_ref,
    tokens_ref,
    beta_ref,
    cot_in,
    query_in,
    key_in,
    value_in,
    gate_in,
    up_in,
    down_in,
    out_in,
    tokens_mixed,
    normed_out,
    mixer_out,
    gate_all,
    up_all,
    down_all,
    out_all,
    cot_all,
    packed_out,
    delta_out,
    inverse_out,
    big_out,
    update_out,
    state_out,
    retain_ref,
    taps_ref,
    column_ref,
    packed_ref,
    delta_ref,
    inverse_ref,
    update_ref,
    state_ref,
    big_ref,
    mask_ref,
    fresh_ref,
    own_ref,
    add_ref,
    mixed_ref,
    ready_ref,
    chosen_ref,
    normed_ref,
    weight_ref,
    betas_ref,
    raw_ref,
    gate_mine,
    up_mine,
    down_mine,
    out_mine,
    gather_send,
    gather_recv,
    share_send,
    share_recv,
    local_sems,
):
    own_tokens = tokens_ref.shape[0]
    tokens = own_tokens * n_seq
    width = packed_ref.shape[1]
    head_width = heads * DK
    blocks = tokens // BT
    seq = lax.axis_index("seq")
    own_rows, _ = query_in.shape
    slab = down_mine.shape[0]
    out_rows, out_width = out_in.shape
    out_part = out_width // n_seq
    low = jnp.bfloat16

    local = {}

    def bring(name, source, target):
        copy = pltpu.make_async_copy(source, target, local_sems.at[len(local)])
        local[name] = copy
        copy.start()

    out_at = aligned(seq * out_part, out_part)
    bring("gate", gate_in, raw_ref.at[0])
    bring("up", up_in, raw_ref.at[1])
    bring("out", out_in.at[:, pl.ds(out_at, out_part)], out_mine)
    whole_shard = down_in.shape[0] > slab
    bring(
        "down",
        down_in.at[pl.ds(aligned(seq * slab, slab), slab)] if whole_shard else down_in,
        down_mine,
    )
    greet_signal(n_seq, n_fsdp)

    half_model = down_mine.shape[1] // 2
    part = min(PB, own_tokens)
    for base in range(0, own_tokens, part):
        values = tokens_ref[base : base + part, :].astype(jnp.float32)
        inv = lax.rsqrt(jnp.mean(values * values, axis=1, keepdims=True) + EPS_NORM)
        normed_ref[pl.ds(aligned(seq * own_tokens + base, part), part), :] = (
            values * inv * norm_gain_ref[...]
        ).astype(low)
    greet_wait(n_seq, n_fsdp)

    gather_sems = (gather_send, gather_recv)
    share_sems = (share_send, share_recv)
    per_gather = Gather.copies(n_fsdp)
    per_share = Share.copies(n_seq)

    def rows_slot(ref, size):
        return lambda owner: ref.at[pl.ds(aligned(owner * size, size), size)]

    def gather_piece(index, source, slot):
        return Gather(
            n_fsdp, source, slot, gather_sems, index * per_gather, local_sems.at[30 + index]
        )

    def head_columns(kind):
        return lambda owner: weight_ref.at[
            pl.ds(aligned(owner * own_rows, own_rows), own_rows),
            pl.ds(kind * head_width, head_width),
        ]

    pieces = [
        gather_piece(
            kind,
            source.at[:, pl.ds(aligned(seq * head_width, head_width), head_width)],
            head_columns(kind),
        )
        for kind, source in enumerate((query_in, key_in, value_in))
    ] + [
        gather_piece(
            3,
            out_mine,
            lambda owner: out_all.at[
                pl.ds(aligned(owner * out_rows, out_rows), out_rows), pl.ds(out_at, out_part)
            ],
        ),
        gather_piece(4, gate_mine, rows_slot(gate_all, own_rows)),
        gather_piece(5, up_mine, rows_slot(up_all, own_rows)),
    ] + [
        gather_piece(
            6 + index,
            down_mine.at[:, pl.ds(index * half_model, half_model)],
            (lambda place: lambda owner: down_all.at[owner, :, place])(
                pl.ds(index * half_model, half_model)
            ),
        )
        for index in range(2)
    ]
    betas = gather_piece(8, beta_ref, lambda owner: betas_ref.at[owner])
    share_normed = Share(
        n_seq,
        normed_ref.at[pl.ds(aligned(seq * own_tokens, own_tokens), own_tokens)],
        rows_slot(normed_ref, own_tokens),
        share_sems,
        0,
        None,
    )
    share_cot = Share(
        n_seq, cot_in, rows_slot(cot_all, own_tokens), share_sems, per_share, local_sems.at[39]
    )
    share_out = Share(
        n_seq,
        out_all.at[:, pl.ds(out_at, out_part)],
        lambda owner: out_all.at[:, pl.ds(aligned(owner * out_part, out_part), out_part)],
        share_sems,
        2 * per_share,
        None,
    )

    share_normed.start()
    pieces[0].start()
    betas.start()
    pieces[1].start()
    fill_flags(retain_ref, lengths_ref)
    fill_taps(taps_ref, taps_in, seq, head_width)
    fill_column(column_ref, row_ref)
    fill_masks(mask_ref)
    packed_ref[0:HALO, :] = jnp.zeros((HALO, width), low)
    local["gate"].wait()
    pick_units(gate_mine, raw_ref.at[0], seq, n_seq, slab)
    pieces[0].relay()
    pieces[2].start()
    betas.relay()
    pieces[1].relay()
    local["out"].wait()
    pieces[3].start()
    local["up"].wait()
    pick_units(up_mine, raw_ref.at[1], seq, n_seq, slab)
    share_normed.to_mate().wait_recv()

    def permute(step, carry, source, first):
        base = aligned(step * PB, PB)
        picked = permute_rows(
            column_ref[pl.ds(base, PB), :] - source * own_tokens,
            normed_ref[pl.ds(aligned(source * own_tokens, own_tokens), 2 * own_tokens), :],
            2 * own_tokens,
        )
        if not first:
            picked = picked + chosen_ref[pl.ds(base, PB), :].astype(jnp.float32)
        chosen_ref[pl.ds(base, PB), :] = picked.astype(low)
        return carry

    lax.fori_loop(
        0, tokens // PB, functools.partial(permute, source=seq // 2 * 2, first=True), 0
    )
    pieces[2].relay()
    pieces[4].start()
    betas.finish()
    mine = jnp.where(
        iota((beta_ref.shape[0], DK), 0) == iota((beta_ref.shape[0], DK), 1) + seq * heads, 1.0, 0.0
    )
    mine = jnp.where(iota(mine.shape, 1) < heads, mine, 0.0)
    for owner in range(n_fsdp):
        weight_ref[owner * own_rows : (owner + 1) * own_rows, 3 * head_width :] = bdot(
            betas_ref[owner], mine, TN
        ).astype(low)
    share_normed.relay()
    share_cot.start()
    for step in range(1, n_seq // 2):
        share_normed.passed_on(step).wait_recv()
        lax.fori_loop(
            0,
            tokens // PB,
            functools.partial(permute, source=(seq // 2 * 2 + n_seq - 2 * step) % n_seq, first=False),
            0,
        )
    pieces[3].relay()
    for piece in pieces[:3]:
        piece.finish()
    bring("keep_normed", chosen_ref, normed_out)
    bring("keep_mixer", weight_ref, mixer_out)

    def project(step, carry):
        base = aligned(step * PB, PB)
        packed_ref[pl.ds(HALO + base, PB), :] = bdot(
            chosen_ref[pl.ds(base, PB), :], weight_ref[...]
        ).astype(low)
        return carry

    lax.fori_loop(0, tokens // PB, project, 0)
    bring("keep_packed", packed_ref, packed_out)

    def middle(number):
        if number == 0:
            pieces[3].finish()
            share_out.start()
            pieces[4].relay()
            pieces[5].start()
        if number == 1:
            share_cot.relay()
        if number == 2:
            pieces[5].relay()
            local["down"].wait()
            pieces[6].start()
            share_out.relay()

    unroll = 2

    def prepare(step, carry):
        for number, moment in enumerate((1, 4, 7)):

            @pl.when(step == moment)
            def _():
                middle(number)

        places, stricts, kept_values = [], [], []
        for sub in range(unroll):
            block = step * unroll + sub
            first, second = retain_ref[2 * block], retain_ref[2 * block + 1]
            base = pl.multiple_of(block * BT, BT)
            masks = tap_masks(first, second, 1.0, BT)
            seen, kept = block_flags(first, second)
            rows, cols, cross = pair_mask(second)
            strengths = sigmoid(
                packed_ref[pl.ds(HALO + base, BT), 3 * heads * DK : 3 * heads * DK + BT].astype(
                    jnp.float32
                )
            )
            for head in range(heads):
                parts = []
                for kind in range(3):
                    at = (kind * heads + head) * DK
                    window = packed_ref[pl.ds(base, HALO + BT), at : at + DK].astype(jnp.float32)
                    taps = [
                        taps_ref[kind * CONV + back : kind * CONV + back + 1, head * DK : head * DK + DK]
                        for back in range(CONV)
                    ]
                    conv = conv_of(window, taps, masks)
                    parts.append(conv * sigmoid(conv))
                query, key, value = parts
                query = query * lax.rsqrt(
                    jnp.sum(query * query, axis=1, keepdims=True) + EPS_NORM
                ) * DK ** (-0.5)
                key = key * lax.rsqrt(jnp.sum(key * key, axis=1, keepdims=True) + EPS_NORM)
                query_low, key_low = query.astype(jnp.bfloat16), key.astype(jnp.bfloat16)
                query, key = query_low.astype(jnp.float32), key_low.astype(jnp.float32)
                beta = strengths[:, head : head + 1]
                inner = bdot(jnp.concatenate([key_low, query_low], axis=0), key_low, NT)
                stricts.append(jnp.where(rows > cols, inner[:BT] * cross * beta, 0.0))
                scores = jnp.where(rows >= cols, inner[BT:] * cross, 0.0)
                sides = jnp.concatenate([key * (beta * seen), value * beta], axis=1)
                kept_values.append((scores, sides, key * kept, query * seen))
                places.append(head * blocks + block)
        inverses = unit_lower_inverses(stricts, mask_ref)
        solved = [
            bdot(inverse, values[1]) for inverse, values in zip(inverses, kept_values)
        ]
        through = [bdot(values[0], both) for values, both in zip(kept_values, solved)]
        onward = [bdot(values[2], both, TN) for values, both in zip(kept_values, solved)]
        for index, place in enumerate(places):
            inverse_ref[place] = inverses[index].astype(jnp.bfloat16)
            big_ref[place, 0:BT, :] = onward[index][:, :DK].astype(jnp.bfloat16)
            big_ref[place, BT : 2 * BT, :] = (
                kept_values[index][3] - through[index][:, :DK]
            ).astype(jnp.bfloat16)
            big_ref[place, 2 * BT : 3 * BT, :] = solved[index][:, :DK].astype(jnp.bfloat16)
            add_ref[place] = onward[index][:, DK:]
            fresh_ref[place] = solved[index][:, DK:]
            own_ref[place] = through[index][:, DK:]
        return carry

    lax.fori_loop(0, blocks // unroll, prepare, 0)
    bring("keep_inverse", inverse_ref, inverse_out)
    bring("keep_big", big_ref.at[:, pl.ds(0, 2 * BT), :], big_out)

    def advance(block, states):
        through = retain_ref[2 * block] * retain_ref[2 * block + 1]
        base = pl.multiple_of(block * BT, BT)
        lows = [state.astype(jnp.bfloat16) for state in states]
        products = [bdot(big_ref[head * blocks + block], lows[head]) for head in range(heads)]
        following = []
        for head in range(heads):
            place = head * blocks + block
            product = products[head]
            state_ref[place] = lows[head]
            following.append(states[head] * through - product[:BT] + add_ref[place])
            update_ref[place] = (fresh_ref[place] - product[2 * BT :]).astype(jnp.bfloat16)
            delta = own_ref[place] + product[BT : 2 * BT]
            delta_ref[pl.ds(base, BT), head * DK : head * DK + DK] = delta
            inv = lax.rsqrt(jnp.mean(delta * delta, axis=1, keepdims=True) + EPS_NORM)
            ready_ref[pl.ds(base, BT), head * DK : head * DK + DK] = (
                delta * inv * gain_ref[...]
            ).astype(jnp.bfloat16)
        return tuple(following)

    zero = jnp.zeros((DK, DK), jnp.float32)
    lax.fori_loop(0, blocks, advance, (zero,) * heads)
    bring("keep_delta", delta_ref, delta_out)
    bring("keep_update", update_ref, update_out)
    bring("keep_state", state_ref, state_out)
    pieces[6].relay()
    pieces[7].start()

    def hand_over(shift):
        target = (seq + shift) % n_seq
        base = aligned(target * own_tokens, own_tokens)
        for at in range(0, own_tokens, part):
            first = aligned(base + at, part)
            hot = jnp.where(
                row_ref[...] == iota((part, tokens), 0) + first, 1.0, 0.0
            ).astype(low)
            mixed_ref[pl.ds(first, part), :] = lax.dot_general(
                hot, ready_ref[...], NN, preferred_element_type=jnp.float32
            ).astype(low)
        source = mixed_ref.at[pl.ds(base, own_tokens)]
        slot = tokens_mixed.at[:, pl.ds(aligned(seq * head_width, head_width), head_width)]
        if shift == 0:
            return pltpu.make_async_copy(source, slot, local_sems.at[40])
        return pltpu.make_async_remote_copy(
            src_ref=source,
            dst_ref=slot,
            send_sem=share_send.at[3 * per_share + shift],
            recv_sem=share_recv.at[3 * per_share + shift],
            device_id=(target, lax.axis_index("fsdp")),
            device_id_type=MESH,
        )

    handed = []
    for shift in sorted(range(n_seq), key=lambda shift: (shift in (0, 1), -shift)):
        copy = hand_over(shift)
        copy.start()
        handed.append(copy)
    pieces[7].relay()
    for copy in share_normed.waits():
        copy.wait_send()
    share_cot.finish()
    share_out.finish()
    for piece in pieces[4:]:
        piece.finish()
    for name, copy in local.items():
        if name.startswith("keep_"):
            copy.wait()
    for copy in handed:
        copy.wait()


VMEM = pltpu.MemorySpace.VMEM
SMEM = pltpu.MemorySpace.SMEM


def spec(space=VMEM):
    return pl.BlockSpec(memory_space=space)


def mixer_forward(n_seq, n_fsdp, lengths, row, taps, gain, norm_gain, shards):
    tokens_in, beta, cot, query, key, value, gate, up, down, out = shards
    own_tokens, model = tokens_in.shape
    tokens = own_tokens * n_seq
    heads = beta.shape[0] // n_seq
    width = (3 * heads + 1) * DK
    blocks = tokens // BT
    count = heads * blocks
    own_rows, hidden = gate.shape
    slab = hidden // (n_seq * n_fsdp)
    units = slab * n_fsdp
    low, full = jnp.bfloat16, jnp.float32
    gathers = 9 * Gather.copies(n_fsdp)
    shares = 3 * Share.copies(n_seq) + n_seq

    def shape(dims, kind=low):
        return jax.ShapeDtypeStruct(dims, kind)

    return pl.pallas_call(
        functools.partial(mixer_forward_kernel, heads, n_seq, n_fsdp),
        out_shape=(
            shape((own_tokens, n_seq * heads * DK)),
            shape((tokens, model)),
            shape((own_rows * n_fsdp, width)),
            shape((own_rows * n_fsdp, units)),
            shape((own_rows * n_fsdp, units)),
            shape((n_fsdp, slab, model)),
            shape((out.shape[0] * n_fsdp, out.shape[1])),
            shape((tokens, model)),
            shape((HALO + tokens, width)),
            shape((tokens, heads * DK), full),
            shape((count, BT, BT)),
            shape((count, 2 * BT, BT)),
            shape((count, BT, BT)),
            shape((count, BT, BT)),
        ),
        in_specs=[spec(SMEM)] + [spec()] * 7 + [spec(ANY)] * 7,
        out_specs=(spec(ANY),) * 14,
        scratch_shapes=[
            pltpu.SMEM((tokens // CH + 2,), full),
            pltpu.VMEM((3 * CONV, heads * DK), full),
            pltpu.VMEM((tokens, 1), jnp.int32),
            pltpu.VMEM((HALO + tokens, width), low),
            pltpu.VMEM((tokens, heads * DK), full),
            pltpu.VMEM((count, BT, BT), low),
            pltpu.VMEM((count, BT, BT), low),
            pltpu.VMEM((count, BT, BT), low),
            pltpu.VMEM((count, 3 * BT, BT), low),
            pltpu.VMEM((7, BT, BT), full),
            pltpu.VMEM((count, BT, BT), full),
            pltpu.VMEM((count, BT, BT), full),
            pltpu.VMEM((count, BT, BT), full),
            pltpu.VMEM((tokens, heads * DK), low),
            pltpu.VMEM((tokens, heads * DK), low),
            pltpu.VMEM((tokens, model), low),
            pltpu.VMEM((tokens, model), low),
            pltpu.VMEM((own_rows * n_fsdp, width), low),
            pltpu.VMEM((n_fsdp,) + beta.shape, low),
            pltpu.VMEM((2, own_rows, hidden), low),
            pltpu.VMEM((own_rows, units), low),
            pltpu.VMEM((own_rows, units), low),
            pltpu.VMEM((slab, model), low),
            pltpu.VMEM((out.shape[0], out.shape[1] // n_seq), low),
            pltpu.SemaphoreType.DMA((gathers,)),
            pltpu.SemaphoreType.DMA((gathers,)),
            pltpu.SemaphoreType.DMA((shares,)),
            pltpu.SemaphoreType.DMA((shares,)),
            pltpu.SemaphoreType.DMA((41,)),
        ],
        compiler_params=pltpu.CompilerParams(
            vmem_limit_bytes=60 << 20, collective_id=1, has_side_effects=True
        ),
        name="mixer_forward",
    )(
        lengths, row, taps, gain, norm_gain, tokens_in, beta, cot,
        query, key, value, gate, up, down, out,
    )


class Wire:
    def __init__(self, send, recv):
        self.send, self.recv, self.used = send, recv, 0

    def copy(self, source, target, seq, fsdp):
        index = self.used
        self.used += 1
        return pltpu.make_async_remote_copy(
            src_ref=source,
            dst_ref=target,
            send_sem=self.send.at[index],
            recv_sem=self.recv.at[index],
            device_id=(seq, fsdp),
            device_id_type=MESH,
        )


def ffn_copies(n_seq, parts):
    chips = n_seq // 2
    return parts * (2 + 4 * (chips - 1)) + parts * (n_seq - 1)


def ffn_kernel(
    n_seq,
    n_fsdp,
    tokens_ref,
    mixed_ref,
    out_ref,
    gain_ref,
    gate_in,
    up_in,
    down_in,
    cot_in,
    hidden_ref,
    grad_hidden_ref,
    heads_ref,
    result_ref,
    gate_parts,
    grad_up_ref,
    grad_down_ref,
    grad_out_ref,
    grad_gain_ref,
    grad_gate_ref,
    gate_first,
    gate_ref,
    up_ref,
    down_ref,
    cot_ref,
    second_ref,
    second_t_ref,
    active_t_ref,
    lin_gate_ref,
    lin_up_ref,
    keep_ref,
    give_ref,
    from_mate_ref,
    reduce_ref,
    from_far_ref,
    attn_ref,
    mixed_grad_ref,
    stage_ref,
    outgo_ref,
    send_sems,
    recv_sems,
    local_sems,
):
    own, model = tokens_ref.shape
    group = own * n_seq
    part = min(PB, own)
    parts = own // part
    chips = n_seq // 2
    seq, fsdp = lax.axis_index("seq"), lax.axis_index("fsdp")
    mate = seq + 1 - 2 * (seq % 2)
    units = gate_ref.shape[1]
    low = jnp.bfloat16

    loads = [
        pltpu.make_async_copy(source, target, local_sems.at[index])
        for index, (source, target) in enumerate(
            ((gate_in, gate_ref), (up_in, up_ref), (down_in, down_ref), (cot_in, cot_ref))
        )
    ]
    for load in loads:
        load.start()

    wire = Wire(send_sems, recv_sems)

    def far(step):
        return (seq + n_seq - 2 * step) % n_seq

    def rows(ref, shard, index):
        return ref.at[pl.ds(aligned(shard * own + index * part, part), part)]

    def local_rows(ref, index):
        return ref.at[pl.ds(index * part, part)]

    to_mate, across, passed, give_mate, give_far, reduced = {}, {}, {}, {}, {}, {}
    for index in range(parts):
        mine = rows(second_ref, seq, index)
        to_mate[index] = wire.copy(mine, mine, mate, fsdp)
        give_mate[index] = wire.copy(
            local_rows(give_ref.at[0], index), local_rows(from_mate_ref.at[0], index), mate, fsdp
        )
        for step in range(1, chips):
            across[step, index] = wire.copy(mine, mine, (seq + 2 * step) % n_seq, fsdp)
            there = rows(second_ref, far(step), index)
            passed[step, index] = wire.copy(there, there, mate, fsdp)
            give_far[step, index] = wire.copy(
                local_rows(give_ref.at[step], index),
                local_rows(from_mate_ref.at[step], index),
                mate,
                fsdp,
            )
            reduced[step, index] = wire.copy(
                local_rows(reduce_ref.at[step - 1], index),
                local_rows(from_far_ref.at[step - 1], index),
                far(step),
                fsdp,
            )

    own_rows = model // n_fsdp
    inner = n_fsdp // 4
    high_at, low_at = fsdp // inner, fsdp % inner

    def wide_copies(source, target):
        copies = []
        for hop in range(1, inner):
            lower = (low_at + hop) % inner
            for high in range(4):
                block = aligned((high * inner + lower) * own_rows, own_rows)
                copies.append(
                    wire.copy(
                        source.at[pl.ds(block, own_rows)],
                        target.at[(hop - 1) * 4 + high],
                        seq,
                        high_at * inner + lower,
                    )
                )
        return copies

    gate_copies = wide_copies(grad_gate_ref, gate_first)

    greet(n_seq, n_fsdp)

    for index in range(parts):
        at = slice(index * part, index * part + part)
        hidden = tokens_ref[at, :].astype(jnp.float32) + bdot(mixed_ref[at, :], out_ref[...])
        hidden_ref[at, :] = hidden
        inv = lax.rsqrt(jnp.mean(hidden * hidden, axis=1, keepdims=True) + EPS_NORM)
        second_ref[pl.ds(aligned(seq * own + index * part, part), part), :] = (
            hidden * inv * gain_ref[...]
        ).astype(low)
        for step in range(1, chips if index == 0 else 1):
            across[step, index].start()
        to_mate[index].start()
    for load in loads:
        load.wait()

    count = n_seq * parts

    def block(number, carry):
        near = number < 2 * parts
        late = number - 2 * parts
        step_at = late // (2 * parts) + 1
        rest = late % (2 * parts)
        far_at = (seq + 2 * n_seq - 2 * step_at) % n_seq
        far_mate = far_at + 1 - 2 * (far_at % 2)
        shard = jnp.where(
            near,
            jnp.where(number < parts, seq, mate),
            jnp.where(rest % 2 == 0, far_mate, far_at),
        )
        index_at = jnp.where(near, number % parts, rest // 2)
        base = aligned(shard * own + index_at * part, part)

        for index in range(1, parts):

            @pl.when(number == 2 * parts - parts + index)
            def _():
                for step in range(1, chips):
                    across[step, index - 1].wait_send()
                    across[step, index].start()

        for index in range(parts):

            @pl.when(number == parts + index)
            def _():
                to_mate[index].wait_recv()

            for step in range(1, chips):

                @pl.when(number == 2 * parts * step + 2 * index)
                def _():
                    across[step, index].wait_recv()
                    passed[step, index].start()
                    passed[step, index].wait_recv()

        second = second_ref[pl.ds(base, part), :]
        second_t_ref[:, pl.ds(base, part)] = second.T
        gate_lin = bdot(second, gate_ref[...])
        up_lin = bdot(second, up_ref[...])
        cot = cot_ref[pl.ds(base, part), :]
        grad_active = bdot(cot, down_ref[...], NT)
        gate_sig = sigmoid(gate_lin)
        silu = gate_lin * gate_sig
        active = (silu * up_lin).astype(low)
        active_t_ref[:, pl.ds(base, part)] = active.T
        grad_gate = (grad_active * up_lin * (gate_sig + silu * (1.0 - gate_sig))).astype(low)
        grad_up = (grad_active * silu).astype(low)
        lin_gate_ref[pl.ds(base, part), :] = grad_gate
        lin_up_ref[pl.ds(base, part), :] = grad_up
        grad_second = bdot(grad_gate, gate_ref[...], NT) + bdot(grad_up, up_ref[...], NT)
        stage_ref[...] = grad_second
        slot = number % 2

        def leaving(where):
            return pltpu.make_async_copy(
                outgo_ref.at[slot],
                result_ref.at[pl.ds(where, part)],
                local_sems.at[4 + slot],
            )

        @pl.when(number >= 2)
        def _():
            leaving(base).wait()

        outgo_ref[slot] = bdot(active, down_ref[...]).astype(low)
        leaving(base).start()

        for index in range(parts):
            at = slice(index * part, index * part + part)

            @pl.when(number == index)
            def _():
                keep_ref[at, :] = stage_ref[...]

            @pl.when(number == parts + index)
            def _():
                give_ref[0, at, :] = stage_ref[...].astype(low)
                give_mate[index].start()

            for step in range(1, chips):

                @pl.when(number == 2 * parts * step + 2 * index)
                def _():
                    give_ref[step, at, :] = stage_ref[...].astype(low)
                    give_far[step, index].start()

                @pl.when(number == 2 * parts * step + 2 * index + 1)
                def _():
                    give_far[step, index].wait_recv()
                    reduce_ref[step - 1, at, :] = (
                        stage_ref[...] + from_mate_ref[step, at, :].astype(jnp.float32)
                    ).astype(low)
                    reduced[step, index].start()

        return carry

    lax.fori_loop(0, count, block, 0)

    for slot in range(2):
        pltpu.make_async_copy(
            outgo_ref.at[slot], result_ref.at[pl.ds(0, part)], local_sems.at[4 + slot]
        ).wait()

    tile = 256

    def wide_tile(target, lines):
        def step(number, carry):
            base = aligned(number * tile, tile)
            target[pl.ds(base, tile), :] = bdot(
                second_t_ref[pl.ds(base, tile), :], lines[...]
            ).astype(low)
            return carry

        lax.fori_loop(0, model // tile, step, 0)

    wide_tile(grad_gate_ref, lin_gate_ref)
    for copy in gate_copies:
        copy.start()
    wide_tile(grad_up_ref, lin_up_ref)

    grad_gain_ref[...] = jnp.zeros(grad_gain_ref.shape, jnp.float32)
    width = model // n_seq
    handed = []
    for index in range(parts):
        at = slice(index * part, index * part + part)
        give_mate[index].wait_recv()
        total = keep_ref[at, :] + from_mate_ref[0, at, :].astype(jnp.float32)
        for step in range(1, chips):
            reduced[step, index].wait_recv()
            total = total + from_far_ref[step - 1, at, :].astype(jnp.float32)
        hidden = hidden_ref[at, :]
        inv = lax.rsqrt(jnp.mean(hidden * hidden, axis=1, keepdims=True) + EPS_NORM)
        unit = hidden * inv
        grad_gain_ref[...] += jnp.sum(total * unit, axis=0, keepdims=True)
        grad_unit = total * gain_ref[...]
        grad_hidden = inv * (
            grad_unit - unit * jnp.mean(grad_unit * unit, axis=1, keepdims=True)
        ) + cot_ref[pl.ds(aligned(seq * own + index * part, part), part), :].astype(jnp.float32)
        grad_hidden_ref[at, :] = grad_hidden
        attn = grad_hidden.astype(low)
        attn_ref[at, :] = attn
        mixed_grad_ref[at, :] = bdot(attn, out_ref[...], NT).astype(low)
        for shift in range(1, n_seq):
            target = (seq + shift) % n_seq
            copy = wire.copy(
                mixed_grad_ref.at[at, pl.ds(aligned(target * width, width), width)],
                rows(heads_ref, seq, index),
                target,
                fsdp,
            )
            copy.start()
            handed.append(copy)
        heads_ref[pl.ds(aligned(seq * own + index * part, part), part), :] = mixed_grad_ref[
            at, pl.ds(aligned(seq * width, width), width)
        ]

    def down_tile(number, carry):
        base = aligned(number * tile, tile)
        grad_down_ref[:, pl.ds(base, tile)] = bdot(
            active_t_ref[...], cot_ref[:, pl.ds(base, tile)]
        ).astype(low)
        return carry

    lax.fori_loop(0, model // tile, down_tile, 0)

    for base in range(0, model, tile):
        grad_out_ref[base : base + tile, :] = bdot(
            mixed_ref[:, base : base + tile], attn_ref[...], TN
        ).astype(low)

    for index in range(parts):
        to_mate[index].wait_send()
        give_mate[index].wait_send()
        for step in range(1, chips):
            if index == parts - 1:
                across[step, index].wait_send()
            passed[step, index].wait_send()
            give_far[step, index].wait_send()
            reduced[step, index].wait_send()
    for copy in handed:
        copy.wait()
    for copy in gate_copies:
        copy.wait_recv()
    for high in range(4):
        block = aligned((high * inner + low_at) * own_rows, own_rows)
        total = grad_gate_ref[pl.ds(block, own_rows), :].astype(jnp.float32)
        for hop in range(1, inner):
            total = total + gate_first[(hop - 1) * 4 + high].astype(jnp.float32)
        gate_parts[high] = total.astype(low)
    for copy in gate_copies:
        copy.wait_send()


def ffn_block(n_seq, n_fsdp, tokens, mixed, out, gain, gate, up, down, cot):
    own, model = tokens.shape
    group = own * n_seq
    units = gate.shape[1]
    chips = n_seq // 2
    low, full = jnp.bfloat16, jnp.float32
    part = min(PB, own)
    near = 4 * (n_fsdp // 4 - 1)
    own_rows = model // n_fsdp
    copies = ffn_copies(n_seq, own // part) + near

    def shape(dims, kind=low):
        return jax.ShapeDtypeStruct(dims, kind)

    return pl.pallas_call(
        functools.partial(ffn_kernel, n_seq, n_fsdp),
        out_shape=(
            shape((own, model), full),
            shape((own, model), full),
            shape((group, model // n_seq)),
            shape((group, model)),
            shape((4, own_rows, units)),
            shape((model, units)),
            shape((units, model)),
            shape((model, model)),
            shape((1, model), full),
        ),
        in_specs=[spec()] * 4 + [spec(ANY)] * 4,
        out_specs=(spec(),) * 3 + (spec(ANY),) + (spec(),) * 5,
        scratch_shapes=[
            pltpu.VMEM((model, units), low),
            pltpu.VMEM((near, own_rows, units), low),
            pltpu.VMEM((model, units), low),
            pltpu.VMEM((model, units), low),
            pltpu.VMEM((units, model), low),
            pltpu.VMEM((group, model), low),
            pltpu.VMEM((group, model), low),
            pltpu.VMEM((model, group), low),
            pltpu.VMEM((units, group), low),
            pltpu.VMEM((group, units), low),
            pltpu.VMEM((group, units), low),
            pltpu.VMEM((own, model), full),
            pltpu.VMEM((chips, own, model), low),
            pltpu.VMEM((chips, own, model), low),
            pltpu.VMEM((chips - 1, own, model), low),
            pltpu.VMEM((chips - 1, own, model), low),
            pltpu.VMEM((own, model), low),
            pltpu.VMEM((own, model), low),
            pltpu.VMEM((part, model), full),
            pltpu.VMEM((2, part, model), low),
            pltpu.SemaphoreType.DMA((copies,)),
            pltpu.SemaphoreType.DMA((copies,)),
            pltpu.SemaphoreType.DMA((6,)),
        ],
        compiler_params=pltpu.CompilerParams(
            vmem_limit_bytes=63 << 20, collective_id=2, has_side_effects=True
        ),
        name="ffn",
    )(tokens, mixed, out, gain, gate, up, down, cot)


class Scatter:
    outer = 4

    @classmethod
    def copies(cls, n_fsdp):
        return cls.outer * (n_fsdp // cls.outer - 1) + cls.outer - 1

    def __init__(self, n_fsdp, wire, block, parts, mine, first, second):
        self.inner = n_fsdp // self.outer
        me = lax.axis_index("fsdp")
        seq = lax.axis_index("seq")
        self.high, self.low = me // self.inner, me % self.inner
        self.parts, self.mine, self.first, self.second = parts, mine, first, second
        self.near, self.away = [], []
        for hop in range(1, self.inner if first is not None else 1):
            lower = (self.low + hop) % self.inner
            for high in range(self.outer):
                self.near.append(
                    wire.copy(
                        block(high * self.inner + lower),
                        first.at[(hop - 1) * self.outer + high],
                        seq,
                        self.high * self.inner + lower,
                    )
                )
        for step in range(1, self.outer):
            higher = (self.high + step) % self.outer
            self.away.append(
                wire.copy(parts(higher), second.at[step - 1], seq, higher * self.inner + self.low)
            )

    def start(self):
        for copy in self.near:
            copy.start()

    def combine(self):
        for copy in self.near:
            copy.wait_recv()
        for high in range(self.outer):
            block = self.parts(high)
            total = block[...].astype(jnp.float32)
            for hop in range(1, self.inner):
                total = total + self.first[(hop - 1) * self.outer + high].astype(jnp.float32)
            block[...] = total.astype(jnp.bfloat16)

    def leave(self):
        for copy in self.away:
            copy.start()

    def total(self):
        for copy in self.away:
            copy.wait_recv()
        total = self.mine()[...].astype(jnp.float32)
        for step in range(1, self.outer):
            total = total + self.second[step - 1].astype(jnp.float32)
        return total.astype(jnp.bfloat16)

    def drain(self):
        for copy in self.near + self.away:
            copy.wait_send()


CHUNK = 64


class SeqSum:
    @staticmethod
    def copies(n_seq, parts):
        return (n_seq - 1) * parts

    def __init__(self, n_seq, wire, give, mine, from_mate, from_far, parts=1):
        self.chips = n_seq // 2
        self.size = from_mate.shape[1] // parts
        seq, fsdp = lax.axis_index("seq"), lax.axis_index("fsdp")
        mate = seq + 1 - 2 * (seq % 2)
        self.mine, self.from_mate, self.from_far = mine, from_mate, from_far
        self.gives, self.across = {}, {}
        for part in range(parts):
            rows = pl.ds(part * self.size, self.size)
            for step in range(self.chips):
                self.gives[step, part] = wire.copy(
                    give(step).at[rows], from_mate.at[step, rows], mate, fsdp
                )
            for step in range(1, self.chips):
                self.across[step, part] = wire.copy(
                    mine(step).at[rows],
                    from_far.at[step - 1, rows],
                    (seq + n_seq - 2 * step) % n_seq,
                    fsdp,
                )

    def reduce(self, step, part=0):
        self.gives[step, part].wait_recv()
        mine = self.mine(step)

        def add(number, carry):
            at = pl.ds(aligned(part * self.size + number * CHUNK, CHUNK), CHUNK)
            mine[at, :] = (
                mine[at, :].astype(jnp.float32) + self.from_mate[step, at, :].astype(jnp.float32)
            ).astype(jnp.bfloat16)
            return carry

        lax.fori_loop(0, self.size // CHUNK, add, 0)
        self.across[step, part].start()

    def arrive(self, part=0):
        self.gives[0, part].wait_recv()
        for step in range(1, self.chips):
            self.across[step, part].wait_recv()

    def total(self, at):
        total = self.mine(0)[at, :].astype(jnp.float32) + self.from_mate[0, at, :].astype(
            jnp.float32
        )
        for step in range(1, self.chips):
            total = total + self.from_far[step - 1, at, :].astype(jnp.float32)
        return total

    def drain(self):
        for copy in [*self.gives.values(), *self.across.values()]:
            copy.wait_send()


class Direct:
    def __init__(self, size, axis, wire, source, slots):
        seq, fsdp = lax.axis_index("seq"), lax.axis_index("fsdp")
        self.me, self.source, self.slots = lax.axis_index(axis), source, slots
        self.sent = [
            wire.copy(
                source,
                slots.at[self.me],
                (seq + step) % size if axis == "seq" else seq,
                (fsdp + step) % size if axis == "fsdp" else fsdp,
            )
            for step in range(1, size)
        ]

    def start(self):
        for copy in self.sent:
            copy.start()
        self.slots[self.me] = self.source[...]

    def total(self):
        for copy in self.sent:
            copy.wait()
        total = self.slots[0]
        for index in range(1, self.slots.shape[0]):
            total = total + self.slots[index]
        return total


def spread_units(target, pieces, n_seq, slab):
    units, hidden = pieces.shape[2], target.shape[1]
    whole = slab * n_seq
    for base in range(0, hidden, BT):
        total = None
        for owner in range(n_seq):
            first, last = base // whole, (base + BT - 1) // whole
            low = first * slab // BT * BT
            high = min(-(-((last + 1) * slab) // BT) * BT, units)
            col = iota((high - low, BT), 1) + base
            origin = col - first * whole - owner * slab
            inside = (origin >= 0) & (origin < slab)
            origin = origin + first * slab
            for shard in range(first + 1, last + 1):
                there = col - shard * whole - owner * slab
                ours = (there >= 0) & (there < slab)
                origin = jnp.where(ours, there + shard * slab, origin)
                inside = inside | ours
            hot = jnp.where((iota((high - low, BT), 0) + low == origin) & inside, 1.0, 0.0)
            part = bdot(pieces[owner, :, low:high], hot)
            total = part if total is None else total + part
        target[:, base : base + BT] = total.astype(jnp.bfloat16)


SMALL_ROWS = 24


def mixer_backward_kernel(
    heads,
    n_seq,
    n_fsdp,
    lengths_ref,
    row_ref,
    grad_ref,
    taps_in,
    gain_ref,
    norm_gain_ref,
    ffn_gain_ref,
    delta_in,
    inverse_in,
    big_in,
    update_in,
    state_in,
    packed_in,
    normed_in,
    weight_in,
    tokens_in,
    hidden_in,
    grad_hidden_in,
    result_in,
    gate_in,
    up_in,
    down_in,
    out_in,
    result_out,
    tokens_out,
    gate_out,
    up_out,
    down_out,
    out_out,
    query_out,
    key_out,
    value_out,
    beta_out,
    small_out,
    norm_out,
    retain_ref,
    taps_ref,
    column_ref,
    delta_ref,
    inverse_ref,
    big_ref,
    update_ref,
    state_ref,
    packed_ref,
    grad_delta_ref,
    add_ref,
    after_ref,
    conv_ref,
    grad_proj_ref,
    arrived_ref,
    weight_ref,
    weight_grad_ref,
    wide_ref,
    tokens_ref,
    result_ref,
    result_mine,
    result_mate,
    result_far,
    normed_mine,
    normed_give,
    normed_mate,
    normed_far,
    gate_own,
    gate_second,
    up_own,
    up_first,
    up_second,
    down_own,
    down_first,
    down_second,
    out_sum,
    out_mate,
    out_first,
    out_second,
    out_far,
    query_first,
    query_second,
    key_first,
    key_second,
    value_first,
    value_second,
    beta_first,
    beta_second,
    gate_total,
    up_total,
    down_total,
    out_total,
    mixer_total,
    gate_all,
    up_all,
    spread_ref,
    taps_grad_ref,
    small_ref,
    small_all,
    small_seq,
    small_sum,
    norm_ref,
    norm_half,
    norm_all,
    norm_seq,
    send_sems,
    recv_sems,
    gather_send,
    gather_recv,
    share_send,
    share_recv,
    local_sems,
):
    tokens = grad_ref.shape[0]
    blocks = tokens // BT
    head_width = heads * DK
    width = 3 * head_width
    own = tokens // n_seq
    model = tokens_ref.shape[1]
    own_rows, units = gate_own.shape
    slab = down_own.shape[1]
    seq, fsdp = lax.axis_index("seq"), lax.axis_index("fsdp")
    mate = seq + 1 - 2 * (seq % 2)
    core = seq % 2
    chip = seq // 2
    chips = n_seq // 2
    inner = n_fsdp // Scatter.outer
    inner_high, inner_low = fsdp // inner, fsdp % inner
    low, full = jnp.bfloat16, jnp.float32

    local = {}

    def bring(name, source, target):
        copy = pltpu.make_async_copy(source, target, local_sems.at[len(local)])
        local[name] = copy
        copy.start()

    def far(step):
        return (seq + n_seq - 2 * step) % n_seq

    def far_mate(step):
        there = far(step)
        return there + 1 - 2 * (there % 2)

    def shard(ref, index):
        return ref.at[pl.ds(aligned(index * own, own), own)]

    for name, source, target in (
        ("delta", delta_in, delta_ref),
        ("big", big_in, big_ref),
        ("packed", packed_in, packed_ref.at[:, pl.ds(0, packed_in.shape[1])]),
        ("inverse", inverse_in, inverse_ref),
        ("update", update_in, update_ref),
        ("state", state_in, state_ref),
    ):
        bring(name, source, target)
    greet_signal(n_seq, n_fsdp)
    wire = Wire(send_sems, recv_sems)
    result_sum = SeqSum(
        n_seq,
        wire,
        lambda step: shard(result_in, mate if step == 0 else far_mate(step)),
        lambda step: result_mine.at[step],
        result_mate,
        result_far,
    )
    normed_sum = SeqSum(
        n_seq,
        wire,
        lambda step: normed_give.at[step],
        lambda step: normed_mine.at[step],
        normed_mate,
        normed_far,
        own // min(PB, own),
    )
    half = out_sum.shape[1]
    out_rows = out_sum.shape[0] // n_fsdp
    half_at = pl.ds(aligned(core * half, half), half)
    out_give = wire.copy(
        out_in.at[:, pl.ds(aligned((1 - core) * half, half), half)], out_mate, mate, fsdp
    )

    def rows_of(ref, size):
        return lambda owner: ref.at[pl.ds(aligned(owner * size, size), size)]

    def scatter(block, first, second):
        def parts(high):
            return block(high * inner + inner_low)

        return Scatter(n_fsdp, wire, block, parts, lambda: parts(inner_high), first, second)

    gate_sum = Scatter(
        n_fsdp, wire, None, lambda high: gate_in.at[high], lambda: gate_own, None, gate_second
    )
    up_sum = Scatter(
        n_fsdp,
        wire,
        rows_of(up_in, own_rows),
        lambda high: up_own.at[high],
        lambda: up_own.at[inner_high],
        up_first,
        up_second,
    )
    down_sum = Scatter(
        n_fsdp,
        wire,
        lambda owner: down_in.at[owner],
        lambda high: down_own.at[high],
        lambda: down_own.at[inner_high],
        down_first,
        down_second,
    )
    out_scatter = scatter(rows_of(out_sum, out_rows), out_first, out_second)
    spans = [(kind * head_width, head_width) for kind in range(3)] + [(width, DK)]

    def mixer_block(span):
        return lambda owner: weight_grad_ref.at[
            pl.ds(aligned(owner * own_rows, own_rows), own_rows), pl.ds(span[0], span[1])
        ]

    mixer_sums = [
        scatter(mixer_block(span), first, second)
        for span, first, second in zip(
            spans,
            (query_first, key_first, value_first, beta_first),
            (query_second, key_second, value_second, beta_second),
        )
    ]
    out_across = [
        wire.copy(out_far.at[chip], out_far.at[chip], (seq + 2 * step) % n_seq, fsdp)
        for step in range(1, chips)
    ]
    out_swap = wire.copy(out_total, out_out.at[:, half_at], mate, fsdp)

    share_sems = (share_send, share_recv)
    gather_sems = (gather_send, gather_recv)
    per_share, per_gather = Share.copies(n_seq), Gather.copies(n_fsdp)

    def share(index, source, slot):
        return Share(
            n_seq, source, slot, share_sems, index * per_share, local_sems.at[50 + index]
        )

    def stacked(ref):
        return lambda owner: ref.at[owner]

    def head_columns(ref):
        return lambda owner: ref.at[:, pl.ds(aligned(owner * head_width, head_width), head_width)]

    gate_share = share(0, gate_total, stacked(gate_all))
    up_share = share(1, up_total, stacked(up_all))
    down_share = share(2, down_total, stacked(down_out))
    mixer_shares = [
        share(3 + index, mixer_total.at[:, pl.ds(span[0], span[1])], slot)
        for index, (span, slot) in enumerate(
            zip(
                spans,
                (
                    head_columns(query_out),
                    head_columns(key_out),
                    head_columns(value_out),
                    stacked(beta_out),
                ),
            )
        )
    ]
    small_spread = Direct(n_seq, "seq", wire, small_ref, small_seq)
    norm_first = Direct(n_fsdp, "fsdp", wire, norm_ref, norm_all)
    norm_spread = Direct(n_seq, "seq", wire, norm_half, norm_seq)
    small_gather = Gather(
        n_fsdp, small_ref, stacked(small_all), gather_sems, 0, local_sems.at[59]
    )
    for high in range(Scatter.outer):
        owner = high * inner + inner_low
        bring(("up", high), rows_of(up_in, own_rows)(owner), up_own.at[high])
        bring(("down", high), down_in.at[owner], down_own.at[high])
    bring("out", out_in.at[:, half_at], out_sum)
    bring("gate", gate_in.at[inner_high], gate_own)
    for step in range(1, chips):
        bring(("result", step), shard(result_in, far(step)), result_mine.at[step])
    bring("result", shard(result_in, seq), result_mine.at[0])
    bring("hidden", hidden_in, wide_ref)
    bring("weight", weight_in, weight_ref)
    bring("tokens", tokens_in, tokens_ref)
    fill_flags(retain_ref, lengths_ref)
    fill_taps(taps_ref, taps_in, seq, head_width)
    fill_column(column_ref, row_ref)
    small_ref[...] = jnp.zeros(small_ref.shape, full)
    taps_grad_ref[...] = jnp.zeros(taps_grad_ref.shape, full)
    greet_wait(n_seq, n_fsdp)
    gate_sum.leave()
    up_sum.start()
    for copy in result_sum.gives.values():
        copy.start()
    out_give.start()
    local["delta"].wait()
    local["big"].wait()

    def head_norm(step, total):
        base = pl.multiple_of(step * PB, PB)
        picked = permute_rows(column_ref[pl.ds(base, PB), :], grad_ref[...], tokens)
        for head in range(heads):
            at = slice(head * DK, head * DK + DK)
            grad = picked[:, at]
            delta = delta_ref[pl.ds(base, PB), at]
            inv = lax.rsqrt(jnp.mean(delta * delta, axis=1, keepdims=True) + EPS_NORM)
            unit = delta * inv
            total = total + jnp.sum(grad * unit, axis=0, keepdims=True)
            grad_unit = grad * gain_ref[...]
            shrunk = (
                inv * (grad_unit - unit * jnp.mean(grad_unit * unit, axis=1, keepdims=True))
            ).astype(low)
            grad_delta_ref[pl.ds(base, PB), at] = shrunk
            for sub in range(PB // BT):
                place = head * blocks + step * (PB // BT) + sub
                add_ref[place] = bdot(
                    big_ref[place, BT : 2 * BT, :], shrunk[sub * BT : sub * BT + BT], TN
                ).astype(low)
        return total

    gain_row = 3 * CONV
    small_ref[gain_row : gain_row + 1, 0:DK] = lax.fori_loop(
        0, tokens // PB, head_norm, jnp.zeros((1, DK), full)
    )
    for index in range(model // head_width):
        small_ref[gain_row + 1 + index : gain_row + 2 + index, :] = ffn_gain_ref[
            :, index * head_width : (index + 1) * head_width
        ]
    for step in range(1, chips):
        local["result", step].wait()
        result_sum.reduce(step)

    def retreat(step, grads):
        block = blocks - 1 - step
        through = retain_ref[2 * block] * retain_ref[2 * block + 1]
        lows = [grad.astype(low) for grad in grads]
        following = []
        for head in range(heads):
            place = head * blocks + block
            after_ref[place] = lows[head]
            following.append(
                grads[head] * through
                - bdot(big_ref[place, 0:BT, :], lows[head], TN)
                + add_ref[place].astype(full)
            )
        return tuple(following)

    zero = jnp.zeros((DK, DK), full)
    lax.fori_loop(0, blocks, retreat, (zero,) * heads)
    for name in ("packed", "inverse", "update", "state"):
        local[name].wait()

    conv_ref[BT : BT + HALO, :] = jnp.zeros((HALO, width), full)

    def first_stage():
        for high in range(Scatter.outer):
            local["up", high].wait()
        up_sum.combine()
        up_sum.leave()
        down_sum.start()
        local["gate"].wait()
        gate_total[...] = gate_sum.total()
        gate_share.start()

    def add_out():
        local["out"].wait()
        out_give.wait_recv()

        def add(number, carry):
            at = pl.ds(aligned(number * CHUNK, CHUNK), CHUNK)
            out_sum[at, :] = (out_sum[at, :].astype(full) + out_mate[at, :].astype(full)).astype(
                low
            )
            return carry

        lax.fori_loop(0, out_sum.shape[0] // CHUNK, add, 0)

    def second_stage():
        for high in range(Scatter.outer):
            local["down", high].wait()
        down_sum.combine()
        down_sum.leave()
        out_scatter.start()
        up_total[...] = up_sum.total()
        up_share.start()
        gate_share.relay()

    def result_stage():
        local["hidden"].wait()
        local["result"].wait()
        result_sum.arrive()

        def add(number, carry):
            at = pl.ds(aligned(number * CHUNK, CHUNK), CHUNK)
            result_ref[at, :] = (wide_ref[at, :] + result_sum.total(at)).astype(low)
            return carry

        lax.fori_loop(0, own // CHUNK, add, 0)

    def gradients(step, carry):
        for moment, stage in (
            (3, first_stage),
            (6, add_out),
            (10, second_stage),
            (13, result_stage),
        ):

            @pl.when(step == moment)
            def _():
                stage()

        block = blocks - 1 - step
        first, second, third = (
            retain_ref[2 * block],
            retain_ref[2 * block + 1],
            retain_ref[2 * block + 2],
        )
        base = pl.multiple_of(block * BT, BT)
        masks = tap_masks(first, second, third, BT + HALO)
        near_masks = [None] + [mask[:BT] for mask in masks[1:]]
        seen, kept = block_flags(first, second)
        rows, cols, cross = pair_mask(second)
        turned = jnp.where((rows < CH) & (cols >= CH), second, 1.0)
        lanes = iota((BT, BT), 1)
        strengths = sigmoid(
            packed_ref[pl.ds(HALO + base, BT), width : width + BT].astype(jnp.float32)
        )
        grad_strengths = jnp.zeros((BT, BT), jnp.float32)
        for head in range(heads):
            place = head * blocks + block
            convs, gates, acts = [], [], []
            for kind in range(3):
                at = (kind * heads + head) * DK
                window = packed_ref[pl.ds(base, HALO + BT), at : at + DK].astype(jnp.float32)
                taps = [
                    taps_ref[kind * CONV + back : kind * CONV + back + 1, head * DK : head * DK + DK]
                    for back in range(CONV)
                ]
                conv = conv_of(window, taps, near_masks)
                gate = sigmoid(conv)
                convs.append(conv)
                gates.append(gate)
                acts.append(conv * gate)
            inv_q = lax.rsqrt(jnp.sum(acts[0] * acts[0], axis=1, keepdims=True) + EPS_NORM)
            inv_k = lax.rsqrt(jnp.sum(acts[1] * acts[1], axis=1, keepdims=True) + EPS_NORM)
            query_low = (acts[0] * inv_q * DK ** (-0.5)).astype(jnp.bfloat16)
            key_low = (acts[1] * inv_k).astype(jnp.bfloat16)
            key = key_low.astype(jnp.float32)
            value = acts[2]
            beta = strengths[:, head : head + 1]
            grad_low = grad_delta_ref[pl.ds(base, BT), head * DK : head * DK + DK]
            after = after_ref[place]
            state = state_ref[place]
            update = update_ref[place]
            inner = bdot(key_low, jnp.concatenate([key_low, query_low], axis=0), NT)
            scores_t = jnp.where(rows <= cols, inner[:, BT:] * turned, 0.0)
            grad_update = bdot(scores_t, grad_low) + bdot(key * kept, after)
            solved = bdot(inverse_ref[place], grad_update, TN)
            solved_beta = solved * beta
            both = jnp.concatenate([grad_low, solved.astype(jnp.bfloat16)], axis=0)
            on_state = bdot(both, state, NT)
            on_update = bdot(both, update, NT)
            grad_scores = jnp.where(rows >= cols, on_update[:BT] * cross, 0.0)
            grad_strict = jnp.where(rows > cols, on_update[BT:] * cross, 0.0)
            grad_weighted = on_state[BT:] * seen
            turned_both = bdot(
                update,
                jnp.concatenate(
                    [grad_low, solved_beta.astype(jnp.bfloat16)], axis=0
                ),
                NT,
            )
            grad_scores_t = jnp.where(rows <= cols, turned_both[:, :BT] * turned, 0.0)
            strict_t = jnp.where(rows < cols, turned_both[:, BT:] * turned, 0.0)
            grad_query = on_state[:BT] * seen + bdot(grad_scores, key_low)
            grad_key = (
                bdot(grad_scores_t, query_low)
                + bdot(update, after, NT) * kept
                - beta * grad_weighted
                - bdot(grad_strict * beta + strict_t, key_low)
            )
            grad_value = solved_beta
            grad_beta = jnp.sum(
                solved * value - grad_strict * inner[:, :BT] - grad_weighted * key,
                axis=1,
                keepdims=True,
            )
            grad_strengths = jnp.where(lanes == head, grad_beta, grad_strengths)
            scaled = (
                inv_q
                * DK ** (-0.5)
                * (
                    grad_query
                    - acts[0]
                    * (inv_q * inv_q)
                    * jnp.sum(grad_query * acts[0], axis=1, keepdims=True)
                ),
                inv_k
                * (
                    grad_key
                    - acts[1] * (inv_k * inv_k) * jnp.sum(grad_key * acts[1], axis=1, keepdims=True)
                ),
                grad_value,
            )
            for kind in range(3):
                at = (kind * heads + head) * DK
                conv_ref[0:BT, at : at + DK] = (
                    scaled[kind] * gates[kind] * (1.0 + convs[kind] * (1.0 - gates[kind]))
                )
        grad_proj_ref[pl.ds(base, BT), width : width + BT] = (
            grad_strengths * strengths * (1.0 - strengths)
        ).astype(jnp.bfloat16)
        for kind in range(3):
            for head in range(heads):
                at = (kind * heads + head) * DK
                span = slice(head * DK, head * DK + DK)
                grads = conv_ref[:, at : at + DK]
                window = packed_ref[pl.ds(base, HALO + BT), at : at + DK].astype(jnp.float32)
                total = None
                for back in range(CONV):
                    row = kind * CONV + back
                    tap = taps_ref[row : row + 1, span]
                    masked = grads if back == 0 else grads * masks[back]
                    shifted = (
                        masked if back == 0 else pltpu.roll(masked, BT + HALO - back, 0)
                    )[:BT]
                    total = shifted * tap if total is None else total + shifted * tap
                    past = (window if back == 0 else pltpu.roll(window, back, 0))[HALO:]
                    taps_grad_ref[row : row + 1, span] += jnp.sum(
                        masked[:BT] * past, axis=0, keepdims=True
                    )
                grad_proj_ref[pl.ds(base, BT), at : at + DK] = total.astype(jnp.bfloat16)
        conv_ref[BT : BT + HALO, :] = conv_ref[0:HALO, :]
        return carry

    lax.fori_loop(0, blocks, gradients, 0)

    bring("keep_result", result_ref, result_out)
    bring("normed", normed_in, packed_ref.at[pl.ds(0, tokens)])
    bring("grad_hidden", grad_hidden_in, wide_ref)
    small_ref[0:gain_row, :] = taps_grad_ref[0:gain_row, :]
    small_gather.start()
    out_scatter.combine()
    out_scatter.leave()
    part = min(PB, own)

    def push_back(index, target, number):
        base = aligned(index * own + number * part, part)
        hot = jnp.where(row_ref[...] == iota((part, tokens), 0) + base, 1.0, 0.0).astype(low)
        arrived_ref[...] = lax.dot_general(
            hot, grad_proj_ref[...], NN, preferred_element_type=jnp.float32
        ).astype(low)
        target[number * part : (number + 1) * part, :] = bdot(
            arrived_ref[...], weight_ref[...], NT
        ).astype(low)

    local["weight"].wait()
    parts = own // part
    for step in range(1, chips):
        for number in range(parts):
            push_back(far_mate(step), normed_give.at[step], number)
            normed_sum.gives[step, number].start()
            push_back(far(step), normed_mine.at[step], number)
            normed_sum.reduce(step, number)
    local["normed"].wait()

    def weight_grad(span):
        def step(number, carry):
            at = pl.ds(aligned(number * PB, PB), PB)
            weight_grad_ref[at, pl.ds(span[0], span[1])] = bdot(
                packed_ref[0:tokens, at], grad_proj_ref[:, pl.ds(span[0], span[1])], TN
            ).astype(low)
            return carry

        lax.fori_loop(0, model // PB, step, 0)

    weight_grad(spans[0])
    mixer_sums[0].start()
    weight_grad(spans[1])
    mixer_sums[1].start()
    up_share.relay()
    small_gather.relay()
    for number in range(parts):
        push_back(mate, normed_give.at[0], number)
        normed_sum.gives[0, number].start()
    weight_grad(spans[2])
    weight_grad(spans[3])
    mixer_sums[0].combine()
    mixer_sums[0].leave()
    mixer_sums[2].start()
    for number in range(parts):
        push_back(seq, normed_mine.at[0], number)
    small_gather.finish()
    total = small_all[0]
    for owner in range(1, n_fsdp):
        total = total + small_all[owner]
    small_ref[...] = total
    small_spread.start()
    mixer_sums[1].combine()
    mixer_sums[1].leave()
    mixer_sums[3].start()
    gate_share.finish()
    spread_units(spread_ref.at[0], gate_all, n_seq, slab)
    bring("keep_gate", spread_ref.at[0], gate_out)
    down_total[...] = down_sum.total()
    out_far[chip] = out_scatter.total()
    mixer_sums[2].combine()
    mixer_sums[2].leave()
    up_share.finish()
    spread_units(spread_ref.at[1], up_all, n_seq, slab)
    bring("keep_up", spread_ref.at[1], up_out)
    mixer_total[:, spans[0][0] : spans[0][0] + spans[0][1]] = mixer_sums[0].total()
    mixer_sums[3].combine()
    mixer_sums[3].leave()
    local["grad_hidden"].wait()
    local["tokens"].wait()

    def norm_back(number, total):
        at = pl.ds(aligned(number * CHUNK, CHUNK), CHUNK)
        values = tokens_ref[at, :].astype(full)
        inv = lax.rsqrt(jnp.mean(values * values, axis=1, keepdims=True) + EPS_NORM)
        unit = values * inv
        grad = normed_sum.total(at)
        grad_unit = grad * norm_gain_ref[...]
        wide_ref[at, :] += inv * (
            grad_unit - unit * jnp.mean(grad_unit * unit, axis=1, keepdims=True)
        )
        return total + jnp.sum(grad * unit, axis=0, keepdims=True)

    total = jnp.zeros((1, model), full)
    for number in range(parts):
        normed_sum.arrive(number)
        if number == parts - 1:
            down_share.start()
            for copy in out_across:
                copy.start()
            mixer_shares[0].start()
        total = lax.fori_loop(
            number * part // CHUNK, (number + 1) * part // CHUNK, norm_back, total
        )
    for index in range(model // DK):
        norm_ref[index : index + 1, :] = total[:, index * DK : (index + 1) * DK]
    norm_first.start()
    bring("keep_tokens", wide_ref, tokens_out)
    mixer_total[:, spans[1][0] : spans[1][0] + spans[1][1]] = mixer_sums[1].total()
    mixer_shares[1].start()
    norm_half[...] = norm_first.total()
    norm_spread.start()
    total = small_spread.total()
    for owner in range(n_seq):
        small_sum[0:gain_row, owner * head_width : (owner + 1) * head_width] = small_seq[
            owner, 0:gain_row, :
        ]
    small_sum[gain_row : gain_row + 2, :] = jnp.zeros((2, model), full)
    small_sum[gain_row : gain_row + 1, 0:DK] = total[gain_row : gain_row + 1, 0:DK]
    for index in range(model // head_width):
        small_sum[
            gain_row + 1 : gain_row + 2, index * head_width : (index + 1) * head_width
        ] = total[gain_row + 1 + index : gain_row + 2 + index, :]
    bring("keep_small", small_sum, small_out)
    mixer_total[:, spans[2][0] : spans[2][0] + spans[2][1]] = mixer_sums[2].total()
    mixer_shares[2].start()
    down_share.relay()
    for copy in out_across:
        copy.wait_recv()
    total = out_far[0].astype(full)
    for index in range(1, chips):
        total = total + out_far[index].astype(full)
    out_total[...] = total.astype(low)
    out_swap.start()
    bring("keep_out", out_total, out_out.at[:, half_at])
    mixer_total[:, spans[3][0] : spans[3][0] + spans[3][1]] = mixer_sums[3].total()
    mixer_shares[3].start()
    norm_ref[...] = norm_spread.total()
    bring("keep_norm", norm_ref, norm_out)
    for each in mixer_shares:
        each.relay()
    for each in [down_share] + mixer_shares:
        each.finish()
    for each in [gate_sum, up_sum, down_sum, out_scatter] + mixer_sums + [result_sum, normed_sum]:
        each.drain()
    for copy in out_across:
        copy.wait_send()
    out_give.wait_send()
    out_swap.wait()
    for name, copy in local.items():
        if str(name).startswith("keep_"):
            copy.wait()


def mixer_backward(n_seq, n_fsdp, small, saved, big):
    (lengths, row, grad_heads, taps, gain, norm_gain, ffn_gain) = small
    packed, delta, inverse, parts, update, state = saved
    normed, weight, own_tokens, hidden, grad_hidden, result, gate, up, down, out = big
    tokens = grad_heads.shape[0]
    width = packed.shape[1]
    head_width = grad_heads.shape[1]
    heads = head_width // DK
    count = heads * (tokens // BT)
    own, model = own_tokens.shape
    _, own_rows, units = gate.shape
    slab = down.shape[1]
    hidden_units = slab * n_fsdp * n_seq
    out_rows = out.shape[0] // n_fsdp
    half = out.shape[1] // 2
    chips = n_seq // 2
    outer = Scatter.outer
    near = outer * (n_fsdp // outer - 1)
    low, full = jnp.bfloat16, jnp.float32
    copies = (
        8 * Scatter.copies(n_fsdp)
        + SeqSum.copies(n_seq, 1 + own // min(PB, own))
        + 1
        + chips
        + 2 * (n_seq - 1)
        + n_fsdp
    )
    shares, gathers = 7 * Share.copies(n_seq), Gather.copies(n_fsdp)

    def shape(dims, kind=low):
        return jax.ShapeDtypeStruct(dims, kind)

    def held(*dims, kind=low):
        return pltpu.VMEM(dims, kind)

    def sum_buffers(rows, cols):
        return [held(near, rows, cols), held(outer - 1, rows, cols)]

    return pl.pallas_call(
        functools.partial(mixer_backward_kernel, heads, n_seq, n_fsdp),
        out_shape=(
            shape((own, model)),
            shape((own, model), full),
            shape((own_rows, hidden_units)),
            shape((own_rows, hidden_units)),
            shape((n_seq, slab, model)),
            shape((out_rows, 2 * half)),
            shape((own_rows, n_seq * head_width)),
            shape((own_rows, n_seq * head_width)),
            shape((own_rows, n_seq * head_width)),
            shape((n_seq, own_rows, DK)),
            shape((16, model), full),
            shape((model // DK, DK), full),
        ),
        in_specs=[spec(SMEM)] + [spec()] * 6 + [spec(ANY)] * 16,
        out_specs=(spec(ANY),) * 12,
        scratch_shapes=[
            pltpu.SMEM((tokens // CH + 2,), full),
            held(3 * CONV, head_width, kind=full),
            held(tokens, 1, kind=jnp.int32),
            held(tokens, head_width, kind=full),
            held(count, BT, BT),
            held(count, 2 * BT, BT),
            held(count, BT, BT),
            held(count, BT, BT),
            held(HALO + tokens, max(width, model)),
            held(tokens, head_width),
            held(count, BT, BT),
            held(count, BT, BT),
            held(BT + HALO, 3 * head_width, kind=full),
            held(tokens, width),
            held(min(PB, own), width),
            held(model, width),
            held(model, width),
            held(own, model, kind=full),
            held(own, model),
            held(own, model),
            held(chips, own, model),
            held(chips, own, model),
            held(chips - 1, own, model),
            held(chips, own, model),
            held(chips, own, model),
            held(chips, own, model),
            held(chips - 1, own, model),
            held(own_rows, units),
            held(outer - 1, own_rows, units),
            held(outer, own_rows, units),
            *sum_buffers(own_rows, units),
            held(outer, slab, model),
            *sum_buffers(slab, model),
            held(out.shape[0], half),
            held(out.shape[0], half),
            *sum_buffers(out_rows, half),
            held(chips, out_rows, half),
            *sum_buffers(own_rows, head_width),
            *sum_buffers(own_rows, head_width),
            *sum_buffers(own_rows, head_width),
            *sum_buffers(own_rows, DK),
            held(own_rows, units),
            held(own_rows, units),
            held(slab, model),
            held(out_rows, half),
            held(own_rows, width),
            held(n_seq, own_rows, units),
            held(n_seq, own_rows, units),
            held(2, own_rows, hidden_units),
            held(16, head_width, kind=full),
            held(SMALL_ROWS, head_width, kind=full),
            held(n_fsdp, SMALL_ROWS, head_width, kind=full),
            held(n_seq, SMALL_ROWS, head_width, kind=full),
            held(16, model, kind=full),
            held(model // DK, DK, kind=full),
            held(model // DK, DK, kind=full),
            held(n_fsdp, model // DK, DK, kind=full),
            held(n_seq, model // DK, DK, kind=full),
            pltpu.SemaphoreType.DMA((copies,)),
            pltpu.SemaphoreType.DMA((copies,)),
            pltpu.SemaphoreType.DMA((gathers,)),
            pltpu.SemaphoreType.DMA((gathers,)),
            pltpu.SemaphoreType.DMA((shares,)),
            pltpu.SemaphoreType.DMA((shares,)),
            pltpu.SemaphoreType.DMA((61,)),
        ],
        compiler_params=pltpu.CompilerParams(
            vmem_limit_bytes=63 << 20, collective_id=3, has_side_effects=True
        ),
        name="mixer_backward",
    )(
        lengths, row, grad_heads, taps, gain, norm_gain, ffn_gain, delta, inverse, parts,
        update, state, packed, normed, weight, own_tokens, hidden, grad_hidden, result,
        gate, up, down, out,
    )


def finish_kernel(
    heads,
    result_in,
    tokens_in,
    gate_in,
    up_in,
    down_in,
    out_in,
    query_in,
    key_in,
    value_in,
    beta_in,
    small_in,
    norm_in,
    result_ref,
    tokens_ref,
    norm_ref,
    query_ref,
    key_ref,
    value_ref,
    beta_ref,
    taps_ref,
    gain_ref,
    out_ref,
    ffn_ref,
    gate_ref,
    up_ref,
    down_ref,
):
    full = jnp.float32
    result_ref[...] = result_in[...]
    tokens_ref[...] = tokens_in[...]
    for source, target in (
        (gate_in, gate_ref),
        (up_in, up_ref),
        (out_in, out_ref),
        (query_in, query_ref),
        (key_in, key_ref),
        (value_in, value_ref),
        (down_in, down_ref),
    ):
        target[...] = source[...].astype(full)
    total = None
    row, col = iota((beta_ref.shape[0], DK), 0), iota((beta_ref.shape[0], DK), 1)
    for owner in range(beta_in.shape[0]):
        hot = jnp.where((col + owner * heads == row) & (col < heads), 1.0, 0.0)
        part = bdot(hot, beta_in[owner], NT)
        total = part if total is None else total + part
    beta_ref[...] = total
    for kind in range(3):
        for back in range(CONV):
            at = kind * CONV + back
            taps_ref[kind, back : back + 1, :] = small_in[at : at + 1, :]
    gain_ref[...] = small_in[3 * CONV : 3 * CONV + 1, 0:DK]
    ffn_ref[...] = small_in[3 * CONV + 1 : 3 * CONV + 2, :]
    for index in range(norm_in.shape[0]):
        norm_ref[:, index * DK : (index + 1) * DK] = norm_in[index : index + 1, :]


def finish(heads, arrays):
    result, tokens, gate, up, down, out, query, key, value, beta, small, norm = arrays
    full = jnp.float32
    model = small.shape[1]
    head_count = heads * beta.shape[0]

    def wide(array):
        return jax.ShapeDtypeStruct(array.shape, full)

    return pl.pallas_call(
        functools.partial(finish_kernel, heads),
        out_shape=(
            jax.ShapeDtypeStruct(result.shape, result.dtype),
            wide(tokens),
            jax.ShapeDtypeStruct((1, model), full),
            wide(query),
            wide(key),
            wide(value),
            jax.ShapeDtypeStruct((head_count, query.shape[0]), full),
            jax.ShapeDtypeStruct((3, CONV, model), full),
            jax.ShapeDtypeStruct((1, DK), full),
            wide(out),
            jax.ShapeDtypeStruct((1, model), full),
            wide(gate),
            wide(up),
            wide(down),
        ),
        in_specs=[spec()] * 12,
        out_specs=(spec(),) * 14,
        compiler_params=pltpu.CompilerParams(vmem_limit_bytes=63 << 20),
        name="finish",
    )(*arrays)


def own_slice(array, place, size, axis):
    return lax.dynamic_slice_in_dim(array, place * size, size, axis)


def local(
    n_seq,
    n_fsdp,
    tokens,
    norm_gain,
    w_query,
    w_key,
    w_value,
    w_beta,
    conv_taps,
    head_gain,
    w_out,
    ffn_gain,
    w_gate,
    w_up,
    w_down,
    cotangent,
    token_order,
    seq_lengths,
):
    place = lax.axis_index("seq")
    model = tokens.shape[1]
    head_count = w_beta.shape[1]
    heads = head_count // n_seq
    hidden_units = w_gate.shape[1]
    slab = hidden_units // (n_fsdp * n_seq)
    units = slab * n_fsdp

    row = token_order.reshape(1, -1)
    gain = head_gain.reshape(1, DK)
    mixed_tok, normed, w_mixer, full_gate, full_up, full_down, full_o, cot_all, *saved = (
        mixer_forward(
            n_seq,
            n_fsdp,
            seq_lengths,
            row,
            conv_taps,
            gain,
            norm_gain.reshape(1, model),
            (
                tokens,
                w_beta.T,
                cotangent,
                w_query,
                w_key,
                w_value,
                w_gate,
                w_up,
                w_down if slab % 8 == 0 else own_slice(w_down, place, slab, 0),
                w_out,
            ),
        )
    )
    full_down = full_down.reshape(units, model)
    (
        hidden,
        grad_hidden,
        grad_heads,
        result_part,
        wide_gate,
        wide_up,
        wide_down,
        wide_out,
        grad_ffn_gain,
    ) = ffn_block(
        n_seq,
        n_fsdp,
        tokens,
        mixed_tok,
        full_o,
        ffn_gain.reshape(1, model),
        full_gate,
        full_up,
        full_down,
        cot_all,
    )
    (
        result,
        grad_inputs,
        all_gate,
        all_up,
        part_down,
        all_out,
        all_query,
        all_key,
        all_value,
        part_beta,
        small,
        norm_sum,
    ) = mixer_backward(
        n_seq,
        n_fsdp,
        (
            seq_lengths,
            row,
            grad_heads,
            conv_taps,
            gain,
            norm_gain.reshape(1, model),
            grad_ffn_gain,
        ),
        saved,
        (
            normed,
            w_mixer,
            tokens,
            hidden,
            grad_hidden,
            result_part,
            wide_gate,
            wide_up,
            wide_down.reshape(n_fsdp, slab, model),
            wide_out,
        ),
    )
    outputs = finish(
        heads,
        (
            result,
            grad_inputs,
            all_gate,
            all_up,
            part_down.reshape(n_seq * slab, model),
            all_out,
            all_query,
            all_key,
            all_value,
            part_beta,
            small,
            norm_sum,
        ),
    )
    flat, turned = (2, 8, 10), (6,)
    return tuple(
        output.reshape(-1) if index in flat else output.T if index in turned else output
        for index, output in enumerate(outputs)
    )


def solution(mesh):
    tokens = P(("seq", "fsdp"), None)
    rows = P("fsdp", None)
    in_specs = (
        (tokens, P()) + (rows,) * 4 + (P(), P(), rows, P()) + (rows,) * 3 + (tokens, rows, rows)
    )
    out_specs = (
        (tokens, tokens, P()) + (rows,) * 4 + (P(), P(), rows, P()) + (rows,) * 3
    )
    return jax.shard_map(
        functools.partial(local, mesh.shape["seq"], mesh.shape["fsdp"]),
        mesh=mesh,
        in_specs=in_specs,
        out_specs=out_specs,
        check_vma=False,
    )
```

```python
import functools

import jax
import jax.numpy as jnp
from jax import lax
from jax.experimental import pallas as pl
from jax.experimental.pallas import tpu as pltpu
from jax.sharding import PartitionSpec as P

DK = 128
CONV = 4
CH = 64
BT = 128
HALO = 16
PB = 256
WIDE = 512
EPS_NORM = 1e-06

NN = (((1,), (0,)), ((), ()))
NT = (((1,), (1,)), ((), ()))
TN = (((0,), (0,)), ((), ()))


def bdot(first, second, dims=NN):
    return lax.dot_general(
        first.astype(jnp.bfloat16),
        second.astype(jnp.bfloat16),
        dims,
        preferred_element_type=jnp.float32,
    )


def iota(shape, axis):
    return lax.broadcasted_iota(jnp.int32, shape, axis)


def sigmoid(values):
    return 1.0 / (1.0 + jnp.exp(-values))


def fill_masks(mask_ref):
    rows, cols = iota((BT, BT), 0), iota((BT, BT), 1)
    size, level = 1, 0
    while size < BT:
        inside = (rows // (2 * size) == cols // (2 * size)) & (rows // size > cols // size)
        mask_ref[level] = jnp.where(inside, 1.0, 0.0)
        size, level = 2 * size, level + 1


def unit_lower_inverses(stricts, mask_ref):
    rows, cols = iota((BT, BT), 0), iota((BT, BT), 1)
    eye = jnp.where(rows == cols, 1.0, 0.0)
    inverses = [eye - strict * mask_ref[0] for strict in stricts]
    for level in range(1, 7):
        lows = [inverse.astype(jnp.bfloat16) for inverse in inverses]
        inner = [bdot(strict * mask_ref[level], low) for strict, low in zip(stricts, lows)]
        inverses = [
            inverse - bdot(low, mid) for inverse, low, mid in zip(inverses, lows, inner)
        ]
    return inverses


def tap_masks(first, second, third, count):
    rows = iota((count, 1), 0)
    flag = jnp.where(rows < CH, first, jnp.where(rows < BT, second, third))
    return [None] + [jnp.where(rows % CH < back, flag, 1.0) for back in range(1, CONV)]


def conv_of(halo_rows, taps, masks):
    total = halo_rows[HALO:] * taps[0]
    for back in range(1, CONV):
        total = total + pltpu.roll(halo_rows, back, 0)[HALO:] * (taps[back] * masks[back])
    return total


def block_flags(first, second):
    upper = iota((BT, 1), 0) < CH
    seen = jnp.where(upper, first, first * second)
    kept = jnp.where(upper, second, 1.0)
    return seen, kept


def pair_mask(second):
    rows, cols = iota((BT, BT), 0), iota((BT, BT), 1)
    cross = (rows >= CH) & (cols < CH)
    return rows, cols, jnp.where(cross, second, 1.0)


def permute_rows(column, source, width):
    hot = jnp.where(column == iota((column.shape[0], width), 1), 1.0, 0.0).astype(jnp.bfloat16)
    return lax.dot_general(hot, source, NN, preferred_element_type=jnp.float32)


def unpermute_rows(row, base, source, width):
    hot = jnp.where(row == iota((PB, width), 0) + base, 1.0, 0.0).astype(jnp.bfloat16)
    return lax.dot_general(hot, source, NN, preferred_element_type=jnp.float32)


MESH = pl.DeviceIdType.MESH
ANY = pl.ANY


class Gather:
    outer = 4

    @classmethod
    def copies(cls, n_fsdp):
        inner = n_fsdp // cls.outer
        return (cls.outer - 1) + cls.outer * (inner - 1)

    def __init__(self, n_fsdp, source, slot, sems, base, local_sem):
        self.inner = n_fsdp // self.outer
        self.me = lax.axis_index("fsdp")
        self.seq = lax.axis_index("seq")
        self.high, self.low = self.me // self.inner, self.me % self.inner
        self.source, self.slot = source, slot
        self.send, self.recv = sems
        self.base, self.local_sem = base, local_sem

    def at(self, high, low):
        return (high % self.outer) * self.inner + (low % self.inner)

    def copy(self, source, owner, target, index):
        return pltpu.make_async_remote_copy(
            src_ref=source,
            dst_ref=self.slot(owner),
            send_sem=self.send.at[self.base + index],
            recv_sem=self.recv.at[self.base + index],
            device_id=(self.seq, target),
            device_id_type=MESH,
        )

    def along_outer(self, step):
        return self.copy(self.source, self.me, self.at(self.high + step, self.low), step - 1)

    def along_inner(self, hop):
        return self.copy(
            self.source, self.me, self.at(self.high, self.low + hop), self.outer - 2 + hop
        )

    def passed_on(self, step, hop):
        owner = self.at(self.high - step, self.low)
        index = self.outer - 1 + (self.inner - 1) * step + hop - 1
        return self.copy(self.slot(owner), owner, self.at(self.high, self.low + hop), index)

    def own(self):
        return pltpu.make_async_copy(self.source, self.slot(self.me), self.local_sem)

    def start(self):
        for step in range(1, self.outer):
            self.along_outer(step).start()
        for hop in range(1, self.inner):
            self.along_inner(hop).start()
        self.own().start()

    def relay(self):
        for step in range(1, self.outer):
            self.along_outer(step).wait_recv()
            for hop in range(1, self.inner):
                self.passed_on(step, hop).start()

    def finish(self):
        self.own().wait()
        for hop in range(1, self.inner):
            self.along_inner(hop).wait_recv()
            for step in range(1, self.outer):
                self.passed_on(step, hop).wait_recv()
        for step in range(1, self.outer):
            self.along_outer(step).wait_send()
        for hop in range(1, self.inner):
            self.along_inner(hop).wait_send()
            for step in range(1, self.outer):
                self.passed_on(step, hop).wait_send()


class Share:
    @staticmethod
    def copies(n_seq):
        return 1 + 2 * (n_seq // 2 - 1)

    def __init__(self, n_seq, source, slot, sems, base, local_sem):
        self.n_seq, self.chips = n_seq, n_seq // 2
        self.me = lax.axis_index("seq")
        self.fsdp = lax.axis_index("fsdp")
        self.mate = self.me + 1 - 2 * (self.me % 2)
        self.source, self.slot = source, slot
        self.send, self.recv = sems
        self.base, self.local_sem = base, local_sem

    def copy(self, source, owner, target, index):
        return pltpu.make_async_remote_copy(
            src_ref=source,
            dst_ref=self.slot(owner),
            send_sem=self.send.at[self.base + index],
            recv_sem=self.recv.at[self.base + index],
            device_id=(target, self.fsdp),
            device_id_type=MESH,
        )

    def to_mate(self):
        return self.copy(self.source, self.me, self.mate, 0)

    def across(self, step):
        return self.copy(self.source, self.me, (self.me + 2 * step) % self.n_seq, step)

    def passed_on(self, step):
        owner = (self.me + self.n_seq - 2 * step) % self.n_seq
        return self.copy(self.slot(owner), owner, self.mate, self.chips - 1 + step)

    def own(self):
        return pltpu.make_async_copy(self.source, self.slot(self.me), self.local_sem)

    def start(self):
        for step in range(1, self.chips):
            self.across(step).start()
        self.to_mate().start()
        if self.local_sem is not None:
            self.own().start()

    def relay(self):
        for step in range(1, self.chips):
            self.across(step).wait_recv()
            self.passed_on(step).start()

    def waits(self):
        steps = range(1, self.chips)
        return [self.to_mate()] + [each(step) for step in steps for each in (self.across, self.passed_on)]

    def finish(self):
        if self.local_sem is not None:
            self.own().wait()
        self.to_mate().wait_recv()
        for step in range(1, self.chips):
            self.passed_on(step).wait_recv()
        self.to_mate().wait_send()
        for step in range(1, self.chips):
            self.across(step).wait_send()
            self.passed_on(step).wait_send()


def greet_signal(n_seq, n_fsdp):
    seq, fsdp = lax.axis_index("seq"), lax.axis_index("fsdp")
    barrier = pltpu.get_barrier_semaphore()
    for step in range(1, n_seq):
        pl.semaphore_signal(
            barrier, inc=1, device_id=((seq + step) % n_seq, fsdp), device_id_type=MESH
        )
    for step in range(1, n_fsdp):
        pl.semaphore_signal(
            barrier, inc=1, device_id=(seq, (fsdp + step) % n_fsdp), device_id_type=MESH
        )


def greet_wait(n_seq, n_fsdp):
    pl.semaphore_wait(pltpu.get_barrier_semaphore(), n_seq + n_fsdp - 2)


def greet(n_seq, n_fsdp):
    greet_signal(n_seq, n_fsdp)
    greet_wait(n_seq, n_fsdp)


def aligned(value, unit):
    return pl.multiple_of(value, unit)


def fill_flags(flags_ref, lengths_ref):
    def fill(span, carry):
        start, hit = 0, span == 0
        for index in range(lengths_ref.shape[1] - 1):
            start = start + lengths_ref[0, index]
            hit = hit | (span * CH == start)
        flags_ref[span] = jnp.where(hit, 0.0, 1.0)
        return carry

    lax.fori_loop(0, flags_ref.shape[0], fill, 0)


def fill_taps(taps_ref, taps_in, seq, width):
    for kind in range(3):
        for back in range(CONV):
            row = kind * CONV + back
            taps_ref[row : row + 1, :] = taps_in[
                kind, back : back + 1, pl.ds(aligned(seq * width, width), width)
            ]


def fill_column(column_ref, row_ref):
    for base in range(0, row_ref.shape[1], BT):
        rows = jnp.broadcast_to(row_ref[:, base : base + BT], (8, BT))
        column_ref[base : base + BT, :] = rows.T[:, 0:1]


def pick_units(target, source, seq, n_seq, slab):
    units, hidden = target.shape[1], source.shape[1]
    jump = slab * (n_seq - 1)
    for base in range(0, units, BT):
        size = min(BT, units - base)
        first, last = base // slab, (base + size - 1) // slab
        low = (base + jump * first) // BT * BT
        high = min(-(-(base + size + jump * (last + 1)) // BT) * BT, hidden)
        col = iota((high - low, size), 1) + base
        origin = col + jump * first + slab * seq - low
        for owner in range(first + 1, last + 1):
            origin = origin + jnp.where(col >= owner * slab, jump, 0)
        hot = jnp.where(iota((high - low, size), 0) == origin, 1.0, 0.0)
        target[:, base : base + size] = bdot(source[:, low:high], hot).astype(jnp.bfloat16)


def mixer_forward_kernel(
    heads,
    n_seq,
    n_fsdp,
    lengths_ref,
    row_ref,
    taps_in,
    gain_ref,
    norm_gain_ref,
    tokens_ref,
    beta_ref,
    cot_in,
    query_in,
    key_in,
    value_in,
    gate_in,
    up_in,
    down_in,
    out_in,
    tokens_mixed,
    normed_out,
    mixer_out,
    gate_all,
    up_all,
    down_all,
    out_all,
    cot_all,
    packed_out,
    delta_out,
    inverse_out,
    big_out,
    update_out,
    state_out,
    retain_ref,
    taps_ref,
    column_ref,
    packed_ref,
    delta_ref,
    inverse_ref,
    update_ref,
    state_ref,
    big_ref,
    mask_ref,
    fresh_ref,
    own_ref,
    add_ref,
    mixed_ref,
    ready_ref,
    chosen_ref,
    normed_ref,
    weight_ref,
    betas_ref,
    raw_ref,
    gate_mine,
    up_mine,
    down_mine,
    out_mine,
    gather_send,
    gather_recv,
    share_send,
    share_recv,
    local_sems,
):
    own_tokens = tokens_ref.shape[0]
    tokens = own_tokens * n_seq
    width = packed_ref.shape[1]
    head_width = heads * DK
    blocks = tokens // BT
    seq = lax.axis_index("seq")
    own_rows, _ = query_in.shape
    slab = down_mine.shape[0]
    out_rows, out_width = out_in.shape
    out_part = out_width // n_seq
    low = jnp.bfloat16

    local = {}

    def bring(name, source, target):
        copy = pltpu.make_async_copy(source, target, local_sems.at[len(local)])
        local[name] = copy
        copy.start()

    out_at = aligned(seq * out_part, out_part)
    bring("gate", gate_in, raw_ref.at[0])
    bring("up", up_in, raw_ref.at[1])
    bring("out", out_in.at[:, pl.ds(out_at, out_part)], out_mine)
    whole_shard = down_in.shape[0] > slab
    bring(
        "down",
        down_in.at[pl.ds(aligned(seq * slab, slab), slab)] if whole_shard else down_in,
        down_mine,
    )
    greet_signal(n_seq, n_fsdp)

    half_model = down_mine.shape[1] // 2
    part = min(PB, own_tokens)
    for base in range(0, own_tokens, part):
        values = tokens_ref[base : base + part, :].astype(jnp.float32)
        inv = lax.rsqrt(jnp.mean(values * values, axis=1, keepdims=True) + EPS_NORM)
        normed_ref[pl.ds(aligned(seq * own_tokens + base, part), part), :] = (
            values * inv * norm_gain_ref[...]
        ).astype(low)
    greet_wait(n_seq, n_fsdp)

    gather_sems = (gather_send, gather_recv)
    share_sems = (share_send, share_recv)
    per_gather = Gather.copies(n_fsdp)
    per_share = Share.copies(n_seq)

    def rows_slot(ref, size):
        return lambda owner: ref.at[pl.ds(aligned(owner * size, size), size)]

    def gather_piece(index, source, slot):
        return Gather(
            n_fsdp, source, slot, gather_sems, index * per_gather, local_sems.at[30 + index]
        )

    def head_columns(kind):
        return lambda owner: weight_ref.at[
            pl.ds(aligned(owner * own_rows, own_rows), own_rows),
            pl.ds(kind * head_width, head_width),
        ]

    pieces = [
        gather_piece(
            kind,
            source.at[:, pl.ds(aligned(seq * head_width, head_width), head_width)],
            head_columns(kind),
        )
        for kind, source in enumerate((query_in, key_in, value_in))
    ] + [
        gather_piece(
            3,
            out_mine,
            lambda owner: out_all.at[
                pl.ds(aligned(owner * out_rows, out_rows), out_rows), pl.ds(out_at, out_part)
            ],
        ),
        gather_piece(4, gate_mine, rows_slot(gate_all, own_rows)),
        gather_piece(5, up_mine, rows_slot(up_all, own_rows)),
    ] + [
        gather_piece(
            6 + index,
            down_mine.at[:, pl.ds(index * half_model, half_model)],
            (lambda place: lambda owner: down_all.at[owner, :, place])(
                pl.ds(index * half_model, half_model)
            ),
        )
        for index in range(2)
    ]
    betas = gather_piece(8, beta_ref, lambda owner: betas_ref.at[owner])
    share_normed = Share(
        n_seq,
        normed_ref.at[pl.ds(aligned(seq * own_tokens, own_tokens), own_tokens)],
        rows_slot(normed_ref, own_tokens),
        share_sems,
        0,
        None,
    )
    share_cot = Share(
        n_seq, cot_in, rows_slot(cot_all, own_tokens), share_sems, per_share, local_sems.at[39]
    )
    share_out = Share(
        n_seq,
        out_all.at[:, pl.ds(out_at, out_part)],
        lambda owner: out_all.at[:, pl.ds(aligned(owner * out_part, out_part), out_part)],
        share_sems,
        2 * per_share,
        None,
    )

    share_normed.start()
    pieces[0].start()
    betas.start()
    pieces[1].start()
    fill_flags(retain_ref, lengths_ref)
    fill_taps(taps_ref, taps_in, seq, head_width)
    fill_column(column_ref, row_ref)
    fill_masks(mask_ref)
    packed_ref[0:HALO, :] = jnp.zeros((HALO, width), low)
    local["gate"].wait()
    pick_units(gate_mine, raw_ref.at[0], seq, n_seq, slab)
    pieces[0].relay()
    pieces[2].start()
    betas.relay()
    pieces[1].relay()
    local["out"].wait()
    pieces[3].start()
    local["up"].wait()
    pick_units(up_mine, raw_ref.at[1], seq, n_seq, slab)
    share_normed.to_mate().wait_recv()

    def permute(step, carry, source, first):
        base = aligned(step * WIDE, WIDE)
        picked = permute_rows(
            column_ref[pl.ds(base, WIDE), :] - source * own_tokens,
            normed_ref[pl.ds(aligned(source * own_tokens, own_tokens), 2 * own_tokens), :],
            2 * own_tokens,
        )
        if not first:
            picked = picked + chosen_ref[pl.ds(base, WIDE), :].astype(jnp.float32)
        chosen_ref[pl.ds(base, WIDE), :] = picked.astype(low)
        return carry

    lax.fori_loop(
        0, tokens // WIDE, functools.partial(permute, source=seq // 2 * 2, first=True), 0
    )
    pieces[2].relay()
    pieces[4].start()
    betas.finish()
    mine = jnp.where(
        iota((beta_ref.shape[0], DK), 0) == iota((beta_ref.shape[0], DK), 1) + seq * heads, 1.0, 0.0
    )
    mine = jnp.where(iota(mine.shape, 1) < heads, mine, 0.0)
    for owner in range(n_fsdp):
        weight_ref[owner * own_rows : (owner + 1) * own_rows, 3 * head_width :] = bdot(
            betas_ref[owner], mine, TN
        ).astype(low)
    share_normed.relay()
    share_cot.start()
    for step in range(1, n_seq // 2):
        share_normed.passed_on(step).wait_recv()
        lax.fori_loop(
            0,
            tokens // WIDE,
            functools.partial(permute, source=(seq // 2 * 2 + n_seq - 2 * step) % n_seq, first=False),
            0,
        )
    pieces[3].relay()
    for piece in pieces[:3]:
        piece.finish()
    bring("keep_normed", chosen_ref, normed_out)
    bring("keep_mixer", weight_ref, mixer_out)

    def project(step, carry):
        base = aligned(step * WIDE, WIDE)
        packed_ref[pl.ds(HALO + base, WIDE), :] = bdot(
            chosen_ref[pl.ds(base, WIDE), :], weight_ref[...]
        ).astype(low)
        return carry

    lax.fori_loop(0, tokens // WIDE, project, 0)
    bring("keep_packed", packed_ref, packed_out)

    def middle(number):
        if number == 0:
            pieces[3].finish()
            share_out.start()
            pieces[4].relay()
            pieces[5].start()
        if number == 1:
            share_cot.relay()
        if number == 2:
            pieces[5].relay()
            local["down"].wait()
            pieces[6].start()
            share_out.relay()

    unroll = 2

    def prepare(step, carry):
        for number, moment in enumerate((1, 4, 7)):

            @pl.when(step == moment)
            def _():
                middle(number)

        places, stricts, kept_values = [], [], []
        for sub in range(unroll):
            block = step * unroll + sub
            first, second = retain_ref[2 * block], retain_ref[2 * block + 1]
            base = pl.multiple_of(block * BT, BT)
            masks = tap_masks(first, second, 1.0, BT)
            seen, kept = block_flags(first, second)
            rows, cols, cross = pair_mask(second)
            strengths = sigmoid(
                packed_ref[pl.ds(HALO + base, BT), 3 * heads * DK : 3 * heads * DK + BT].astype(
                    jnp.float32
                )
            )
            for head in range(heads):
                parts = []
                for kind in range(3):
                    at = (kind * heads + head) * DK
                    window = packed_ref[pl.ds(base, HALO + BT), at : at + DK].astype(jnp.float32)
                    taps = [
                        taps_ref[kind * CONV + back : kind * CONV + back + 1, head * DK : head * DK + DK]
                        for back in range(CONV)
                    ]
                    conv = conv_of(window, taps, masks)
                    parts.append(conv * sigmoid(conv))
                query, key, value = parts
                query = query * lax.rsqrt(
                    jnp.sum(query * query, axis=1, keepdims=True) + EPS_NORM
                ) * DK ** (-0.5)
                key = key * lax.rsqrt(jnp.sum(key * key, axis=1, keepdims=True) + EPS_NORM)
                query_low, key_low = query.astype(jnp.bfloat16), key.astype(jnp.bfloat16)
                query, key = query_low.astype(jnp.float32), key_low.astype(jnp.float32)
                beta = strengths[:, head : head + 1]
                inner = bdot(jnp.concatenate([key_low, query_low], axis=0), key_low, NT)
                stricts.append(jnp.where(rows > cols, inner[:BT] * cross * beta, 0.0))
                scores = jnp.where(rows >= cols, inner[BT:] * cross, 0.0)
                sides = jnp.concatenate([key * (beta * seen), value * beta], axis=1)
                kept_values.append((scores, sides, key * kept, query * seen))
                places.append(head * blocks + block)
        inverses = unit_lower_inverses(stricts, mask_ref)
        solved = [
            bdot(inverse, values[1]) for inverse, values in zip(inverses, kept_values)
        ]
        through = [bdot(values[0], both) for values, both in zip(kept_values, solved)]
        onward = [bdot(values[2], both, TN) for values, both in zip(kept_values, solved)]
        for index, place in enumerate(places):
            inverse_ref[place] = inverses[index].astype(jnp.bfloat16)
            big_ref[place, 0:BT, :] = onward[index][:, :DK].astype(jnp.bfloat16)
            big_ref[place, BT : 2 * BT, :] = (
                kept_values[index][3] - through[index][:, :DK]
            ).astype(jnp.bfloat16)
            big_ref[place, 2 * BT : 3 * BT, :] = solved[index][:, :DK].astype(jnp.bfloat16)
            add_ref[place] = onward[index][:, DK:]
            fresh_ref[place] = solved[index][:, DK:]
            own_ref[place] = through[index][:, DK:]
        return carry

    lax.fori_loop(0, blocks // unroll, prepare, 0)
    bring("keep_inverse", inverse_ref, inverse_out)
    bring("keep_big", big_ref.at[:, pl.ds(0, 2 * BT), :], big_out)

    def advance(block, states):
        through = retain_ref[2 * block] * retain_ref[2 * block + 1]
        base = pl.multiple_of(block * BT, BT)
        lows = [state.astype(jnp.bfloat16) for state in states]
        products = [bdot(big_ref[head * blocks + block], lows[head]) for head in range(heads)]
        following = []
        for head in range(heads):
            place = head * blocks + block
            product = products[head]
            state_ref[place] = lows[head]
            following.append(states[head] * through - product[:BT] + add_ref[place])
            update_ref[place] = (fresh_ref[place] - product[2 * BT :]).astype(jnp.bfloat16)
            delta = own_ref[place] + product[BT : 2 * BT]
            delta_ref[pl.ds(base, BT), head * DK : head * DK + DK] = delta
            inv = lax.rsqrt(jnp.mean(delta * delta, axis=1, keepdims=True) + EPS_NORM)
            ready_ref[pl.ds(base, BT), head * DK : head * DK + DK] = (
                delta * inv * gain_ref[...]
            ).astype(jnp.bfloat16)
        return tuple(following)

    zero = jnp.zeros((DK, DK), jnp.float32)
    lax.fori_loop(0, blocks, advance, (zero,) * heads)
    bring("keep_delta", delta_ref, delta_out)
    bring("keep_update", update_ref, update_out)
    bring("keep_state", state_ref, state_out)
    pieces[6].relay()
    pieces[7].start()

    def hand_over(shift):
        target = (seq + shift) % n_seq
        base = aligned(target * own_tokens, own_tokens)
        for at in range(0, own_tokens, part):
            first = aligned(base + at, part)
            hot = jnp.where(
                row_ref[...] == iota((part, tokens), 0) + first, 1.0, 0.0
            ).astype(low)
            mixed_ref[pl.ds(first, part), :] = lax.dot_general(
                hot, ready_ref[...], NN, preferred_element_type=jnp.float32
            ).astype(low)
        source = mixed_ref.at[pl.ds(base, own_tokens)]
        slot = tokens_mixed.at[:, pl.ds(aligned(seq * head_width, head_width), head_width)]
        if shift == 0:
            return pltpu.make_async_copy(source, slot, local_sems.at[40])
        return pltpu.make_async_remote_copy(
            src_ref=source,
            dst_ref=slot,
            send_sem=share_send.at[3 * per_share + shift],
            recv_sem=share_recv.at[3 * per_share + shift],
            device_id=(target, lax.axis_index("fsdp")),
            device_id_type=MESH,
        )

    handed = []
    for shift in sorted(range(n_seq), key=lambda shift: (shift in (0, 1), -shift)):
        copy = hand_over(shift)
        copy.start()
        handed.append(copy)
    pieces[7].relay()
    for copy in share_normed.waits():
        copy.wait_send()
    share_cot.finish()
    share_out.finish()
    for piece in pieces[4:]:
        piece.finish()
    for name, copy in local.items():
        if name.startswith("keep_"):
            copy.wait()
    for copy in handed:
        copy.wait()


VMEM = pltpu.MemorySpace.VMEM
SMEM = pltpu.MemorySpace.SMEM


def spec(space=VMEM):
    return pl.BlockSpec(memory_space=space)


def mixer_forward(n_seq, n_fsdp, lengths, row, taps, gain, norm_gain, shards):
    tokens_in, beta, cot, query, key, value, gate, up, down, out = shards
    own_tokens, model = tokens_in.shape
    tokens = own_tokens * n_seq
    heads = beta.shape[0] // n_seq
    width = (3 * heads + 1) * DK
    blocks = tokens // BT
    count = heads * blocks
    own_rows, hidden = gate.shape
    slab = hidden // (n_seq * n_fsdp)
    units = slab * n_fsdp
    low, full = jnp.bfloat16, jnp.float32
    gathers = 9 * Gather.copies(n_fsdp)
    shares = 3 * Share.copies(n_seq) + n_seq

    def shape(dims, kind=low):
        return jax.ShapeDtypeStruct(dims, kind)

    return pl.pallas_call(
        functools.partial(mixer_forward_kernel, heads, n_seq, n_fsdp),
        out_shape=(
            shape((own_tokens, n_seq * heads * DK)),
            shape((tokens, model)),
            shape((own_rows * n_fsdp, width)),
            shape((own_rows * n_fsdp, units)),
            shape((own_rows * n_fsdp, units)),
            shape((n_fsdp, slab, model)),
            shape((out.shape[0] * n_fsdp, out.shape[1])),
            shape((tokens, model)),
            shape((HALO + tokens, width)),
            shape((tokens, heads * DK), full),
            shape((count, BT, BT)),
            shape((count, 2 * BT, BT)),
            shape((count, BT, BT)),
            shape((count, BT, BT)),
        ),
        in_specs=[spec(SMEM)] + [spec()] * 7 + [spec(ANY)] * 7,
        out_specs=(spec(ANY),) * 14,
        scratch_shapes=[
            pltpu.SMEM((tokens // CH + 2,), full),
            pltpu.VMEM((3 * CONV, heads * DK), full),
            pltpu.VMEM((tokens, 1), jnp.int32),
            pltpu.VMEM((HALO + tokens, width), low),
            pltpu.VMEM((tokens, heads * DK), full),
            pltpu.VMEM((count, BT, BT), low),
            pltpu.VMEM((count, BT, BT), low),
            pltpu.VMEM((count, BT, BT), low),
            pltpu.VMEM((count, 3 * BT, BT), low),
            pltpu.VMEM((7, BT, BT), full),
            pltpu.VMEM((count, BT, BT), full),
            pltpu.VMEM((count, BT, BT), full),
            pltpu.VMEM((count, BT, BT), full),
            pltpu.VMEM((tokens, heads * DK), low),
            pltpu.VMEM((tokens, heads * DK), low),
            pltpu.VMEM((tokens, model), low),
            pltpu.VMEM((tokens, model), low),
            pltpu.VMEM((own_rows * n_fsdp, width), low),
            pltpu.VMEM((n_fsdp,) + beta.shape, low),
            pltpu.VMEM((2, own_rows, hidden), low),
            pltpu.VMEM((own_rows, units), low),
            pltpu.VMEM((own_rows, units), low),
            pltpu.VMEM((slab, model), low),
            pltpu.VMEM((out.shape[0], out.shape[1] // n_seq), low),
            pltpu.SemaphoreType.DMA((gathers,)),
            pltpu.SemaphoreType.DMA((gathers,)),
            pltpu.SemaphoreType.DMA((shares,)),
            pltpu.SemaphoreType.DMA((shares,)),
            pltpu.SemaphoreType.DMA((41,)),
        ],
        compiler_params=pltpu.CompilerParams(
            vmem_limit_bytes=60 << 20, collective_id=1, has_side_effects=True
        ),
        name="mixer_forward",
    )(
        lengths, row, taps, gain, norm_gain, tokens_in, beta, cot,
        query, key, value, gate, up, down, out,
    )


class Wire:
    def __init__(self, send, recv):
        self.send, self.recv, self.used = send, recv, 0

    def copy(self, source, target, seq, fsdp):
        index = self.used
        self.used += 1
        return pltpu.make_async_remote_copy(
            src_ref=source,
            dst_ref=target,
            send_sem=self.send.at[index],
            recv_sem=self.recv.at[index],
            device_id=(seq, fsdp),
            device_id_type=MESH,
        )


def ffn_copies(n_seq, parts):
    chips = n_seq // 2
    return parts * (2 + 4 * (chips - 1)) + parts * (n_seq - 1)


def ffn_kernel(
    n_seq,
    n_fsdp,
    tokens_ref,
    mixed_ref,
    out_ref,
    gain_ref,
    gate_in,
    up_in,
    down_in,
    cot_in,
    hidden_ref,
    grad_hidden_ref,
    heads_ref,
    result_ref,
    gate_parts,
    grad_up_ref,
    grad_down_ref,
    grad_out_ref,
    grad_gain_ref,
    grad_gate_ref,
    gate_first,
    gate_ref,
    up_ref,
    down_ref,
    cot_ref,
    second_ref,
    second_t_ref,
    active_t_ref,
    lin_gate_ref,
    lin_up_ref,
    keep_ref,
    give_ref,
    from_mate_ref,
    reduce_ref,
    from_far_ref,
    attn_ref,
    mixed_grad_ref,
    stage_ref,
    outgo_ref,
    send_sems,
    recv_sems,
    local_sems,
):
    own, model = tokens_ref.shape
    group = own * n_seq
    part = min(PB, own)
    parts = own // part
    chips = n_seq // 2
    seq, fsdp = lax.axis_index("seq"), lax.axis_index("fsdp")
    mate = seq + 1 - 2 * (seq % 2)
    units = gate_ref.shape[1]
    low = jnp.bfloat16

    loads = [
        pltpu.make_async_copy(source, target, local_sems.at[index])
        for index, (source, target) in enumerate(
            ((gate_in, gate_ref), (up_in, up_ref), (down_in, down_ref), (cot_in, cot_ref))
        )
    ]
    for load in loads:
        load.start()

    wire = Wire(send_sems, recv_sems)

    def far(step):
        return (seq + n_seq - 2 * step) % n_seq

    def rows(ref, shard, index):
        return ref.at[pl.ds(aligned(shard * own + index * part, part), part)]

    def local_rows(ref, index):
        return ref.at[pl.ds(index * part, part)]

    to_mate, across, passed, give_mate, give_far, reduced = {}, {}, {}, {}, {}, {}
    for index in range(parts):
        mine = rows(second_ref, seq, index)
        to_mate[index] = wire.copy(mine, mine, mate, fsdp)
        give_mate[index] = wire.copy(
            local_rows(give_ref.at[0], index), local_rows(from_mate_ref.at[0], index), mate, fsdp
        )
        for step in range(1, chips):
            across[step, index] = wire.copy(mine, mine, (seq + 2 * step) % n_seq, fsdp)
            there = rows(second_ref, far(step), index)
            passed[step, index] = wire.copy(there, there, mate, fsdp)
            give_far[step, index] = wire.copy(
                local_rows(give_ref.at[step], index),
                local_rows(from_mate_ref.at[step], index),
                mate,
                fsdp,
            )
            reduced[step, index] = wire.copy(
                local_rows(reduce_ref.at[step - 1], index),
                local_rows(from_far_ref.at[step - 1], index),
                far(step),
                fsdp,
            )

    own_rows = model // n_fsdp
    inner = n_fsdp // 4
    high_at, low_at = fsdp // inner, fsdp % inner

    def wide_copies(source, target):
        copies = []
        for hop in range(1, inner):
            lower = (low_at + hop) % inner
            for high in range(4):
                block = aligned((high * inner + lower) * own_rows, own_rows)
                copies.append(
                    wire.copy(
                        source.at[pl.ds(block, own_rows)],
                        target.at[(hop - 1) * 4 + high],
                        seq,
                        high_at * inner + lower,
                    )
                )
        return copies

    gate_copies = wide_copies(grad_gate_ref, gate_first)

    greet(n_seq, n_fsdp)

    for index in range(parts):
        at = slice(index * part, index * part + part)
        hidden = tokens_ref[at, :].astype(jnp.float32) + bdot(mixed_ref[at, :], out_ref[...])
        hidden_ref[at, :] = hidden
        inv = lax.rsqrt(jnp.mean(hidden * hidden, axis=1, keepdims=True) + EPS_NORM)
        second_ref[pl.ds(aligned(seq * own + index * part, part), part), :] = (
            hidden * inv * gain_ref[...]
        ).astype(low)
        for step in range(1, chips if index == 0 else 1):
            across[step, index].start()
        to_mate[index].start()
    for load in loads:
        load.wait()

    count = n_seq * parts

    def block(number, carry):
        near = number < 2 * parts
        late = number - 2 * parts
        step_at = late // (2 * parts) + 1
        rest = late % (2 * parts)
        far_at = (seq + 2 * n_seq - 2 * step_at) % n_seq
        far_mate = far_at + 1 - 2 * (far_at % 2)
        shard = jnp.where(
            near,
            jnp.where(number < parts, seq, mate),
            jnp.where(rest % 2 == 0, far_mate, far_at),
        )
        index_at = jnp.where(near, number % parts, rest // 2)
        base = aligned(shard * own + index_at * part, part)

        for index in range(1, parts):

            @pl.when(number == 2 * parts - parts + index)
            def _():
                for step in range(1, chips):
                    across[step, index - 1].wait_send()
                    across[step, index].start()

        for index in range(parts):

            @pl.when(number == parts + index)
            def _():
                to_mate[index].wait_recv()

            for step in range(1, chips):

                @pl.when(number == 2 * parts * step + 2 * index)
                def _():
                    across[step, index].wait_recv()
                    passed[step, index].start()
                    passed[step, index].wait_recv()

        second = second_ref[pl.ds(base, part), :]
        second_t_ref[:, pl.ds(base, part)] = second.T
        gate_lin = bdot(second, gate_ref[...])
        up_lin = bdot(second, up_ref[...])
        cot = cot_ref[pl.ds(base, part), :]
        grad_active = bdot(cot, down_ref[...], NT)
        gate_sig = sigmoid(gate_lin)
        silu = gate_lin * gate_sig
        active = (silu * up_lin).astype(low)
        active_t_ref[:, pl.ds(base, part)] = active.T
        grad_gate = (grad_active * up_lin * (gate_sig + silu * (1.0 - gate_sig))).astype(low)
        grad_up = (grad_active * silu).astype(low)
        lin_gate_ref[pl.ds(base, part), :] = grad_gate
        lin_up_ref[pl.ds(base, part), :] = grad_up
        grad_second = bdot(grad_gate, gate_ref[...], NT) + bdot(grad_up, up_ref[...], NT)
        stage_ref[...] = grad_second
        slot = number % 2

        def leaving(where):
            return pltpu.make_async_copy(
                outgo_ref.at[slot],
                result_ref.at[pl.ds(where, part)],
                local_sems.at[4 + slot],
            )

        @pl.when(number >= 2)
        def _():
            leaving(base).wait()

        outgo_ref[slot] = bdot(active, down_ref[...]).astype(low)
        leaving(base).start()

        for index in range(parts):
            at = slice(index * part, index * part + part)

            @pl.when(number == index)
            def _():
                keep_ref[at, :] = stage_ref[...]

            @pl.when(number == parts + index)
            def _():
                give_ref[0, at, :] = stage_ref[...].astype(low)
                give_mate[index].start()

            for step in range(1, chips):

                @pl.when(number == 2 * parts * step + 2 * index)
                def _():
                    give_ref[step, at, :] = stage_ref[...].astype(low)
                    give_far[step, index].start()

                @pl.when(number == 2 * parts * step + 2 * index + 1)
                def _():
                    give_far[step, index].wait_recv()
                    reduce_ref[step - 1, at, :] = (
                        stage_ref[...] + from_mate_ref[step, at, :].astype(jnp.float32)
                    ).astype(low)
                    reduced[step, index].start()

        return carry

    lax.fori_loop(0, count, block, 0)

    for slot in range(2):
        pltpu.make_async_copy(
            outgo_ref.at[slot], result_ref.at[pl.ds(0, part)], local_sems.at[4 + slot]
        ).wait()

    tile = 256

    def wide_tile(target, lines):
        def step(number, carry):
            base = aligned(number * tile, tile)
            target[pl.ds(base, tile), :] = bdot(
                second_t_ref[pl.ds(base, tile), :], lines[...]
            ).astype(low)
            return carry

        lax.fori_loop(0, model // tile, step, 0)

    wide_tile(grad_gate_ref, lin_gate_ref)
    for copy in gate_copies:
        copy.start()
    wide_tile(grad_up_ref, lin_up_ref)

    grad_gain_ref[...] = jnp.zeros(grad_gain_ref.shape, jnp.float32)
    width = model // n_seq
    handed = []
    for index in range(parts):
        at = slice(index * part, index * part + part)
        give_mate[index].wait_recv()
        total = keep_ref[at, :] + from_mate_ref[0, at, :].astype(jnp.float32)
        for step in range(1, chips):
            reduced[step, index].wait_recv()
            total = total + from_far_ref[step - 1, at, :].astype(jnp.float32)
        hidden = hidden_ref[at, :]
        inv = lax.rsqrt(jnp.mean(hidden * hidden, axis=1, keepdims=True) + EPS_NORM)
        unit = hidden * inv
        grad_gain_ref[...] += jnp.sum(total * unit, axis=0, keepdims=True)
        grad_unit = total * gain_ref[...]
        grad_hidden = inv * (
            grad_unit - unit * jnp.mean(grad_unit * unit, axis=1, keepdims=True)
        ) + cot_ref[pl.ds(aligned(seq * own + index * part, part), part), :].astype(jnp.float32)
        grad_hidden_ref[at, :] = grad_hidden
        attn = grad_hidden.astype(low)
        attn_ref[at, :] = attn
        mixed_grad_ref[at, :] = bdot(attn, out_ref[...], NT).astype(low)
        for shift in range(1, n_seq):
            target = (seq + shift) % n_seq
            copy = wire.copy(
                mixed_grad_ref.at[at, pl.ds(aligned(target * width, width), width)],
                rows(heads_ref, seq, index),
                target,
                fsdp,
            )
            copy.start()
            handed.append(copy)
        heads_ref[pl.ds(aligned(seq * own + index * part, part), part), :] = mixed_grad_ref[
            at, pl.ds(aligned(seq * width, width), width)
        ]

    def down_tile(number, carry):
        base = aligned(number * tile, tile)
        grad_down_ref[:, pl.ds(base, tile)] = bdot(
            active_t_ref[...], cot_ref[:, pl.ds(base, tile)]
        ).astype(low)
        return carry

    lax.fori_loop(0, model // tile, down_tile, 0)

    for base in range(0, model, tile):
        grad_out_ref[base : base + tile, :] = bdot(
            mixed_ref[:, base : base + tile], attn_ref[...], TN
        ).astype(low)

    for index in range(parts):
        to_mate[index].wait_send()
        give_mate[index].wait_send()
        for step in range(1, chips):
            if index == parts - 1:
                across[step, index].wait_send()
            passed[step, index].wait_send()
            give_far[step, index].wait_send()
            reduced[step, index].wait_send()
    for copy in handed:
        copy.wait()
    for copy in gate_copies:
        copy.wait_recv()
    for high in range(4):
        block = aligned((high * inner + low_at) * own_rows, own_rows)
        total = grad_gate_ref[pl.ds(block, own_rows), :].astype(jnp.float32)
        for hop in range(1, inner):
            total = total + gate_first[(hop - 1) * 4 + high].astype(jnp.float32)
        gate_parts[high] = total.astype(low)
    for copy in gate_copies:
        copy.wait_send()


def ffn_block(n_seq, n_fsdp, tokens, mixed, out, gain, gate, up, down, cot):
    own, model = tokens.shape
    group = own * n_seq
    units = gate.shape[1]
    chips = n_seq // 2
    low, full = jnp.bfloat16, jnp.float32
    part = min(PB, own)
    near = 4 * (n_fsdp // 4 - 1)
    own_rows = model // n_fsdp
    copies = ffn_copies(n_seq, own // part) + near

    def shape(dims, kind=low):
        return jax.ShapeDtypeStruct(dims, kind)

    return pl.pallas_call(
        functools.partial(ffn_kernel, n_seq, n_fsdp),
        out_shape=(
            shape((own, model), full),
            shape((own, model), full),
            shape((group, model // n_seq)),
            shape((group, model)),
            shape((4, own_rows, units)),
            shape((model, units)),
            shape((units, model)),
            shape((model, model)),
            shape((1, model), full),
        ),
        in_specs=[spec()] * 4 + [spec(ANY)] * 4,
        out_specs=(spec(),) * 3 + (spec(ANY),) + (spec(),) * 5,
        scratch_shapes=[
            pltpu.VMEM((model, units), low),
            pltpu.VMEM((near, own_rows, units), low),
            pltpu.VMEM((model, units), low),
            pltpu.VMEM((model, units), low),
            pltpu.VMEM((units, model), low),
            pltpu.VMEM((group, model), low),
            pltpu.VMEM((group, model), low),
            pltpu.VMEM((model, group), low),
            pltpu.VMEM((units, group), low),
            pltpu.VMEM((group, units), low),
            pltpu.VMEM((group, units), low),
            pltpu.VMEM((own, model), full),
            pltpu.VMEM((chips, own, model), low),
            pltpu.VMEM((chips, own, model), low),
            pltpu.VMEM((chips - 1, own, model), low),
            pltpu.VMEM((chips - 1, own, model), low),
            pltpu.VMEM((own, model), low),
            pltpu.VMEM((own, model), low),
            pltpu.VMEM((part, model), full),
            pltpu.VMEM((2, part, model), low),
            pltpu.SemaphoreType.DMA((copies,)),
            pltpu.SemaphoreType.DMA((copies,)),
            pltpu.SemaphoreType.DMA((6,)),
        ],
        compiler_params=pltpu.CompilerParams(
            vmem_limit_bytes=63 << 20, collective_id=2, has_side_effects=True
        ),
        name="ffn",
    )(tokens, mixed, out, gain, gate, up, down, cot)


class Scatter:
    outer = 4

    @classmethod
    def copies(cls, n_fsdp):
        return cls.outer * (n_fsdp // cls.outer - 1) + cls.outer - 1

    def __init__(self, n_fsdp, wire, block, parts, mine, first, second):
        self.inner = n_fsdp // self.outer
        me = lax.axis_index("fsdp")
        seq = lax.axis_index("seq")
        self.high, self.low = me // self.inner, me % self.inner
        self.parts, self.mine, self.first, self.second = parts, mine, first, second
        self.near, self.away = [], []
        for hop in range(1, self.inner if first is not None else 1):
            lower = (self.low + hop) % self.inner
            for high in range(self.outer):
                self.near.append(
                    wire.copy(
                        block(high * self.inner + lower),
                        first.at[(hop - 1) * self.outer + high],
                        seq,
                        self.high * self.inner + lower,
                    )
                )
        for step in range(1, self.outer):
            higher = (self.high + step) % self.outer
            self.away.append(
                wire.copy(parts(higher), second.at[step - 1], seq, higher * self.inner + self.low)
            )

    def start(self):
        for copy in self.near:
            copy.start()

    def combine(self):
        for copy in self.near:
            copy.wait_recv()
        for high in range(self.outer):
            block = self.parts(high)
            total = block[...].astype(jnp.float32)
            for hop in range(1, self.inner):
                total = total + self.first[(hop - 1) * self.outer + high].astype(jnp.float32)
            block[...] = total.astype(jnp.bfloat16)

    def leave(self):
        for copy in self.away:
            copy.start()

    def total(self):
        for copy in self.away:
            copy.wait_recv()
        total = self.mine()[...].astype(jnp.float32)
        for step in range(1, self.outer):
            total = total + self.second[step - 1].astype(jnp.float32)
        return total.astype(jnp.bfloat16)

    def drain(self):
        for copy in self.near + self.away:
            copy.wait_send()


CHUNK = 64


class SeqSum:
    @staticmethod
    def copies(n_seq, parts):
        return (n_seq - 1) * parts

    def __init__(self, n_seq, wire, give, mine, from_mate, from_far, parts=1):
        self.chips = n_seq // 2
        self.size = from_mate.shape[1] // parts
        seq, fsdp = lax.axis_index("seq"), lax.axis_index("fsdp")
        mate = seq + 1 - 2 * (seq % 2)
        self.mine, self.from_mate, self.from_far = mine, from_mate, from_far
        self.gives, self.across = {}, {}
        for part in range(parts):
            rows = pl.ds(part * self.size, self.size)
            for step in range(self.chips):
                self.gives[step, part] = wire.copy(
                    give(step).at[rows], from_mate.at[step, rows], mate, fsdp
                )
            for step in range(1, self.chips):
                self.across[step, part] = wire.copy(
                    mine(step).at[rows],
                    from_far.at[step - 1, rows],
                    (seq + n_seq - 2 * step) % n_seq,
                    fsdp,
                )

    def reduce(self, step, part=0):
        self.gives[step, part].wait_recv()
        mine = self.mine(step)

        def add(number, carry):
            at = pl.ds(aligned(part * self.size + number * CHUNK, CHUNK), CHUNK)
            mine[at, :] = (
                mine[at, :].astype(jnp.float32) + self.from_mate[step, at, :].astype(jnp.float32)
            ).astype(jnp.bfloat16)
            return carry

        lax.fori_loop(0, self.size // CHUNK, add, 0)
        self.across[step, part].start()

    def arrive(self, part=0):
        self.gives[0, part].wait_recv()
        for step in range(1, self.chips):
            self.across[step, part].wait_recv()

    def total(self, at):
        total = self.mine(0)[at, :].astype(jnp.float32) + self.from_mate[0, at, :].astype(
            jnp.float32
        )
        for step in range(1, self.chips):
            total = total + self.from_far[step - 1, at, :].astype(jnp.float32)
        return total

    def drain(self):
        for copy in [*self.gives.values(), *self.across.values()]:
            copy.wait_send()


class Direct:
    def __init__(self, size, axis, wire, source, slots):
        seq, fsdp = lax.axis_index("seq"), lax.axis_index("fsdp")
        self.me, self.source, self.slots = lax.axis_index(axis), source, slots
        self.sent = [
            wire.copy(
                source,
                slots.at[self.me],
                (seq + step) % size if axis == "seq" else seq,
                (fsdp + step) % size if axis == "fsdp" else fsdp,
            )
            for step in range(1, size)
        ]

    def start(self):
        for copy in self.sent:
            copy.start()
        self.slots[self.me] = self.source[...]

    def total(self):
        for copy in self.sent:
            copy.wait()
        total = self.slots[0]
        for index in range(1, self.slots.shape[0]):
            total = total + self.slots[index]
        return total


def spread_units(target, pieces, n_seq, slab):
    units, hidden = pieces.shape[2], target.shape[1]
    whole = slab * n_seq
    for base in range(0, hidden, BT):
        total = None
        for owner in range(n_seq):
            first, last = base // whole, (base + BT - 1) // whole
            low = first * slab // BT * BT
            high = min(-(-((last + 1) * slab) // BT) * BT, units)
            col = iota((high - low, BT), 1) + base
            origin = col - first * whole - owner * slab
            inside = (origin >= 0) & (origin < slab)
            origin = origin + first * slab
            for shard in range(first + 1, last + 1):
                there = col - shard * whole - owner * slab
                ours = (there >= 0) & (there < slab)
                origin = jnp.where(ours, there + shard * slab, origin)
                inside = inside | ours
            hot = jnp.where((iota((high - low, BT), 0) + low == origin) & inside, 1.0, 0.0)
            part = bdot(pieces[owner, :, low:high], hot)
            total = part if total is None else total + part
        target[:, base : base + BT] = total.astype(jnp.bfloat16)


SMALL_ROWS = 24


def mixer_backward_kernel(
    heads,
    n_seq,
    n_fsdp,
    lengths_ref,
    row_ref,
    grad_ref,
    taps_in,
    gain_ref,
    norm_gain_ref,
    ffn_gain_ref,
    delta_in,
    inverse_in,
    big_in,
    update_in,
    state_in,
    packed_in,
    normed_in,
    weight_in,
    tokens_in,
    hidden_in,
    grad_hidden_in,
    result_in,
    gate_in,
    up_in,
    down_in,
    out_in,
    result_out,
    tokens_out,
    gate_out,
    up_out,
    down_out,
    out_out,
    query_out,
    key_out,
    value_out,
    beta_out,
    small_out,
    norm_out,
    retain_ref,
    taps_ref,
    column_ref,
    delta_ref,
    inverse_ref,
    big_ref,
    update_ref,
    state_ref,
    packed_ref,
    grad_delta_ref,
    add_ref,
    after_ref,
    conv_ref,
    grad_proj_ref,
    arrived_ref,
    weight_ref,
    weight_grad_ref,
    wide_ref,
    tokens_ref,
    result_ref,
    result_mine,
    result_mate,
    result_far,
    normed_mine,
    normed_give,
    normed_mate,
    normed_far,
    gate_own,
    gate_second,
    up_own,
    up_first,
    up_second,
    down_own,
    down_first,
    down_second,
    out_sum,
    out_mate,
    out_first,
    out_second,
    out_far,
    query_first,
    query_second,
    key_first,
    key_second,
    value_first,
    value_second,
    beta_first,
    beta_second,
    gate_total,
    up_total,
    down_total,
    out_total,
    mixer_total,
    gate_all,
    up_all,
    spread_ref,
    taps_grad_ref,
    small_ref,
    small_all,
    small_seq,
    small_sum,
    norm_ref,
    norm_half,
    norm_all,
    norm_seq,
    send_sems,
    recv_sems,
    gather_send,
    gather_recv,
    share_send,
    share_recv,
    local_sems,
):
    tokens = grad_ref.shape[0]
    blocks = tokens // BT
    head_width = heads * DK
    width = 3 * head_width
    own = tokens // n_seq
    model = tokens_ref.shape[1]
    own_rows, units = gate_own.shape
    slab = down_own.shape[1]
    seq, fsdp = lax.axis_index("seq"), lax.axis_index("fsdp")
    mate = seq + 1 - 2 * (seq % 2)
    core = seq % 2
    chip = seq // 2
    chips = n_seq // 2
    inner = n_fsdp // Scatter.outer
    inner_high, inner_low = fsdp // inner, fsdp % inner
    low, full = jnp.bfloat16, jnp.float32

    local = {}

    def bring(name, source, target):
        copy = pltpu.make_async_copy(source, target, local_sems.at[len(local)])
        local[name] = copy
        copy.start()

    def far(step):
        return (seq + n_seq - 2 * step) % n_seq

    def far_mate(step):
        there = far(step)
        return there + 1 - 2 * (there % 2)

    def shard(ref, index):
        return ref.at[pl.ds(aligned(index * own, own), own)]

    for name, source, target in (
        ("delta", delta_in, delta_ref),
        ("big", big_in, big_ref),
        ("packed", packed_in, packed_ref.at[:, pl.ds(0, packed_in.shape[1])]),
        ("inverse", inverse_in, inverse_ref),
        ("update", update_in, update_ref),
        ("state", state_in, state_ref),
    ):
        bring(name, source, target)
    greet_signal(n_seq, n_fsdp)
    wire = Wire(send_sems, recv_sems)
    result_sum = SeqSum(
        n_seq,
        wire,
        lambda step: shard(result_in, mate if step == 0 else far_mate(step)),
        lambda step: result_mine.at[step],
        result_mate,
        result_far,
    )
    normed_sum = SeqSum(
        n_seq,
        wire,
        lambda step: normed_give.at[step],
        lambda step: normed_mine.at[step],
        normed_mate,
        normed_far,
        own // min(PB, own),
    )
    half = out_sum.shape[1]
    out_rows = out_sum.shape[0] // n_fsdp
    half_at = pl.ds(aligned(core * half, half), half)
    out_give = wire.copy(
        out_in.at[:, pl.ds(aligned((1 - core) * half, half), half)], out_mate, mate, fsdp
    )

    def rows_of(ref, size):
        return lambda owner: ref.at[pl.ds(aligned(owner * size, size), size)]

    def scatter(block, first, second):
        def parts(high):
            return block(high * inner + inner_low)

        return Scatter(n_fsdp, wire, block, parts, lambda: parts(inner_high), first, second)

    gate_sum = Scatter(
        n_fsdp, wire, None, lambda high: gate_in.at[high], lambda: gate_own, None, gate_second
    )
    up_sum = Scatter(
        n_fsdp,
        wire,
        rows_of(up_in, own_rows),
        lambda high: up_own.at[high],
        lambda: up_own.at[inner_high],
        up_first,
        up_second,
    )
    down_sum = Scatter(
        n_fsdp,
        wire,
        lambda owner: down_in.at[owner],
        lambda high: down_own.at[high],
        lambda: down_own.at[inner_high],
        down_first,
        down_second,
    )
    out_scatter = scatter(rows_of(out_sum, out_rows), out_first, out_second)
    spans = [(kind * head_width, head_width) for kind in range(3)] + [(width, DK)]

    def mixer_block(span):
        return lambda owner: weight_grad_ref.at[
            pl.ds(aligned(owner * own_rows, own_rows), own_rows), pl.ds(span[0], span[1])
        ]

    mixer_sums = [
        scatter(mixer_block(span), first, second)
        for span, first, second in zip(
            spans,
            (query_first, key_first, value_first, beta_first),
            (query_second, key_second, value_second, beta_second),
        )
    ]
    out_across = [
        wire.copy(out_far.at[chip], out_far.at[chip], (seq + 2 * step) % n_seq, fsdp)
        for step in range(1, chips)
    ]
    out_swap = wire.copy(out_total, out_out.at[:, half_at], mate, fsdp)

    share_sems = (share_send, share_recv)
    gather_sems = (gather_send, gather_recv)
    per_share, per_gather = Share.copies(n_seq), Gather.copies(n_fsdp)

    def share(index, source, slot):
        return Share(
            n_seq, source, slot, share_sems, index * per_share, local_sems.at[50 + index]
        )

    def stacked(ref):
        return lambda owner: ref.at[owner]

    def head_columns(ref):
        return lambda owner: ref.at[:, pl.ds(aligned(owner * head_width, head_width), head_width)]

    gate_share = share(0, gate_total, stacked(gate_all))
    up_share = share(1, up_total, stacked(up_all))
    down_share = share(2, down_total, stacked(down_out))
    mixer_shares = [
        share(3 + index, mixer_total.at[:, pl.ds(span[0], span[1])], slot)
        for index, (span, slot) in enumerate(
            zip(
                spans,
                (
                    head_columns(query_out),
                    head_columns(key_out),
                    head_columns(value_out),
                    stacked(beta_out),
                ),
            )
        )
    ]
    small_spread = Direct(n_seq, "seq", wire, small_ref, small_seq)
    norm_first = Direct(n_fsdp, "fsdp", wire, norm_ref, norm_all)
    norm_spread = Direct(n_seq, "seq", wire, norm_half, norm_seq)
    small_gather = Gather(
        n_fsdp, small_ref, stacked(small_all), gather_sems, 0, local_sems.at[59]
    )
    for high in range(Scatter.outer):
        owner = high * inner + inner_low
        bring(("up", high), rows_of(up_in, own_rows)(owner), up_own.at[high])
        bring(("down", high), down_in.at[owner], down_own.at[high])
    bring("out", out_in.at[:, half_at], out_sum)
    bring("gate", gate_in.at[inner_high], gate_own)
    for step in range(1, chips):
        bring(("result", step), shard(result_in, far(step)), result_mine.at[step])
    bring("result", shard(result_in, seq), result_mine.at[0])
    bring("hidden", hidden_in, wide_ref)
    bring("weight", weight_in, weight_ref)
    bring("tokens", tokens_in, tokens_ref)
    fill_flags(retain_ref, lengths_ref)
    fill_taps(taps_ref, taps_in, seq, head_width)
    fill_column(column_ref, row_ref)
    small_ref[...] = jnp.zeros(small_ref.shape, full)
    taps_grad_ref[...] = jnp.zeros(taps_grad_ref.shape, full)
    greet_wait(n_seq, n_fsdp)
    gate_sum.leave()
    up_sum.start()
    for copy in result_sum.gives.values():
        copy.start()
    out_give.start()
    local["delta"].wait()
    local["big"].wait()

    def head_norm(step, total):
        base = pl.multiple_of(step * PB, PB)
        picked = permute_rows(column_ref[pl.ds(base, PB), :], grad_ref[...], tokens)
        for head in range(heads):
            at = slice(head * DK, head * DK + DK)
            grad = picked[:, at]
            delta = delta_ref[pl.ds(base, PB), at]
            inv = lax.rsqrt(jnp.mean(delta * delta, axis=1, keepdims=True) + EPS_NORM)
            unit = delta * inv
            total = total + jnp.sum(grad * unit, axis=0, keepdims=True)
            grad_unit = grad * gain_ref[...]
            shrunk = (
                inv * (grad_unit - unit * jnp.mean(grad_unit * unit, axis=1, keepdims=True))
            ).astype(low)
            grad_delta_ref[pl.ds(base, PB), at] = shrunk
            for sub in range(PB // BT):
                place = head * blocks + step * (PB // BT) + sub
                add_ref[place] = bdot(
                    big_ref[place, BT : 2 * BT, :], shrunk[sub * BT : sub * BT + BT], TN
                ).astype(low)
        return total

    gain_row = 3 * CONV
    small_ref[gain_row : gain_row + 1, 0:DK] = lax.fori_loop(
        0, tokens // PB, head_norm, jnp.zeros((1, DK), full)
    )
    for index in range(model // head_width):
        small_ref[gain_row + 1 + index : gain_row + 2 + index, :] = ffn_gain_ref[
            :, index * head_width : (index + 1) * head_width
        ]
    for step in range(1, chips):
        local["result", step].wait()
        result_sum.reduce(step)

    def retreat(step, grads):
        block = blocks - 1 - step
        through = retain_ref[2 * block] * retain_ref[2 * block + 1]
        lows = [grad.astype(low) for grad in grads]
        following = []
        for head in range(heads):
            place = head * blocks + block
            after_ref[place] = lows[head]
            following.append(
                grads[head] * through
                - bdot(big_ref[place, 0:BT, :], lows[head], TN)
                + add_ref[place].astype(full)
            )
        return tuple(following)

    zero = jnp.zeros((DK, DK), full)
    lax.fori_loop(0, blocks, retreat, (zero,) * heads)
    for name in ("packed", "inverse", "update", "state"):
        local[name].wait()

    conv_ref[BT : BT + HALO, :] = jnp.zeros((HALO, width), full)

    def first_stage():
        for high in range(Scatter.outer):
            local["up", high].wait()
        up_sum.combine()
        up_sum.leave()
        down_sum.start()
        local["gate"].wait()
        gate_total[...] = gate_sum.total()
        gate_share.start()

    def add_out():
        local["out"].wait()
        out_give.wait_recv()

        def add(number, carry):
            at = pl.ds(aligned(number * CHUNK, CHUNK), CHUNK)
            out_sum[at, :] = (out_sum[at, :].astype(full) + out_mate[at, :].astype(full)).astype(
                low
            )
            return carry

        lax.fori_loop(0, out_sum.shape[0] // CHUNK, add, 0)

    def second_stage():
        for high in range(Scatter.outer):
            local["down", high].wait()
        down_sum.combine()
        down_sum.leave()
        out_scatter.start()
        up_total[...] = up_sum.total()
        up_share.start()
        gate_share.relay()

    def result_stage():
        local["hidden"].wait()
        local["result"].wait()
        result_sum.arrive()

        def add(number, carry):
            at = pl.ds(aligned(number * CHUNK, CHUNK), CHUNK)
            result_ref[at, :] = (wide_ref[at, :] + result_sum.total(at)).astype(low)
            return carry

        lax.fori_loop(0, own // CHUNK, add, 0)

    def gradients(step, carry):
        for moment, stage in (
            (3, first_stage),
            (6, add_out),
            (10, second_stage),
            (13, result_stage),
        ):

            @pl.when(step == moment)
            def _():
                stage()

        block = blocks - 1 - step
        first, second, third = (
            retain_ref[2 * block],
            retain_ref[2 * block + 1],
            retain_ref[2 * block + 2],
        )
        base = pl.multiple_of(block * BT, BT)
        masks = tap_masks(first, second, third, BT + HALO)
        near_masks = [None] + [mask[:BT] for mask in masks[1:]]
        seen, kept = block_flags(first, second)
        rows, cols, cross = pair_mask(second)
        turned = jnp.where((rows < CH) & (cols >= CH), second, 1.0)
        lanes = iota((BT, BT), 1)
        strengths = sigmoid(
            packed_ref[pl.ds(HALO + base, BT), width : width + BT].astype(jnp.float32)
        )
        grad_strengths = jnp.zeros((BT, BT), jnp.float32)
        for head in range(heads):
            place = head * blocks + block
            convs, gates, acts = [], [], []
            for kind in range(3):
                at = (kind * heads + head) * DK
                window = packed_ref[pl.ds(base, HALO + BT), at : at + DK].astype(jnp.float32)
                taps = [
                    taps_ref[kind * CONV + back : kind * CONV + back + 1, head * DK : head * DK + DK]
                    for back in range(CONV)
                ]
                conv = conv_of(window, taps, near_masks)
                gate = sigmoid(conv)
                convs.append(conv)
                gates.append(gate)
                acts.append(conv * gate)
            inv_q = lax.rsqrt(jnp.sum(acts[0] * acts[0], axis=1, keepdims=True) + EPS_NORM)
            inv_k = lax.rsqrt(jnp.sum(acts[1] * acts[1], axis=1, keepdims=True) + EPS_NORM)
            query_low = (acts[0] * inv_q * DK ** (-0.5)).astype(jnp.bfloat16)
            key_low = (acts[1] * inv_k).astype(jnp.bfloat16)
            key = key_low.astype(jnp.float32)
            value = acts[2]
            beta = strengths[:, head : head + 1]
            grad_low = grad_delta_ref[pl.ds(base, BT), head * DK : head * DK + DK]
            after = after_ref[place]
            state = state_ref[place]
            update = update_ref[place]
            inner = bdot(key_low, jnp.concatenate([key_low, query_low], axis=0), NT)
            scores_t = jnp.where(rows <= cols, inner[:, BT:] * turned, 0.0)
            grad_update = bdot(scores_t, grad_low) + bdot(key * kept, after)
            solved = bdot(inverse_ref[place], grad_update, TN)
            solved_beta = solved * beta
            both = jnp.concatenate([grad_low, solved.astype(jnp.bfloat16)], axis=0)
            on_state = bdot(both, state, NT)
            on_update = bdot(both, update, NT)
            grad_scores = jnp.where(rows >= cols, on_update[:BT] * cross, 0.0)
            grad_strict = jnp.where(rows > cols, on_update[BT:] * cross, 0.0)
            grad_weighted = on_state[BT:] * seen
            turned_both = bdot(
                update,
                jnp.concatenate(
                    [grad_low, solved_beta.astype(jnp.bfloat16)], axis=0
                ),
                NT,
            )
            grad_scores_t = jnp.where(rows <= cols, turned_both[:, :BT] * turned, 0.0)
            strict_t = jnp.where(rows < cols, turned_both[:, BT:] * turned, 0.0)
            grad_query = on_state[:BT] * seen + bdot(grad_scores, key_low)
            grad_key = (
                bdot(grad_scores_t, query_low)
                + bdot(update, after, NT) * kept
                - beta * grad_weighted
                - bdot(grad_strict * beta + strict_t, key_low)
            )
            grad_value = solved_beta
            grad_beta = jnp.sum(
                solved * value - grad_strict * inner[:, :BT] - grad_weighted * key,
                axis=1,
                keepdims=True,
            )
            grad_strengths = jnp.where(lanes == head, grad_beta, grad_strengths)
            scaled = (
                inv_q
                * DK ** (-0.5)
                * (
                    grad_query
                    - acts[0]
                    * (inv_q * inv_q)
                    * jnp.sum(grad_query * acts[0], axis=1, keepdims=True)
                ),
                inv_k
                * (
                    grad_key
                    - acts[1] * (inv_k * inv_k) * jnp.sum(grad_key * acts[1], axis=1, keepdims=True)
                ),
                grad_value,
            )
            for kind in range(3):
                at = (kind * heads + head) * DK
                conv_ref[0:BT, at : at + DK] = (
                    scaled[kind] * gates[kind] * (1.0 + convs[kind] * (1.0 - gates[kind]))
                )
        grad_proj_ref[pl.ds(base, BT), width : width + BT] = (
            grad_strengths * strengths * (1.0 - strengths)
        ).astype(jnp.bfloat16)
        for kind in range(3):
            for head in range(heads):
                at = (kind * heads + head) * DK
                span = slice(head * DK, head * DK + DK)
                grads = conv_ref[:, at : at + DK]
                window = packed_ref[pl.ds(base, HALO + BT), at : at + DK].astype(jnp.float32)
                total = None
                for back in range(CONV):
                    row = kind * CONV + back
                    tap = taps_ref[row : row + 1, span]
                    masked = grads if back == 0 else grads * masks[back]
                    shifted = (
                        masked if back == 0 else pltpu.roll(masked, BT + HALO - back, 0)
                    )[:BT]
                    total = shifted * tap if total is None else total + shifted * tap
                    past = (window if back == 0 else pltpu.roll(window, back, 0))[HALO:]
                    taps_grad_ref[row : row + 1, span] += jnp.sum(
                        masked[:BT] * past, axis=0, keepdims=True
                    )
                grad_proj_ref[pl.ds(base, BT), at : at + DK] = total.astype(jnp.bfloat16)
        conv_ref[BT : BT + HALO, :] = conv_ref[0:HALO, :]
        return carry

    lax.fori_loop(0, blocks, gradients, 0)

    bring("keep_result", result_ref, result_out)
    bring("normed", normed_in, packed_ref.at[pl.ds(0, tokens)])
    bring("grad_hidden", grad_hidden_in, wide_ref)
    small_ref[0:gain_row, :] = taps_grad_ref[0:gain_row, :]
    small_gather.start()
    out_scatter.combine()
    out_scatter.leave()
    part = min(PB, own)

    def push_back(index, target, number):
        base = aligned(index * own + number * part, part)
        hot = jnp.where(row_ref[...] == iota((part, tokens), 0) + base, 1.0, 0.0).astype(low)
        arrived_ref[...] = lax.dot_general(
            hot, grad_proj_ref[...], NN, preferred_element_type=jnp.float32
        ).astype(low)
        target[number * part : (number + 1) * part, :] = bdot(
            arrived_ref[...], weight_ref[...], NT
        ).astype(low)

    local["weight"].wait()
    parts = own // part

    def push_far(number):
        for step in range(1, chips):
            push_back(far_mate(step), normed_give.at[step], number)
            normed_sum.gives[step, number].start()
            push_back(far(step), normed_mine.at[step], number)
            normed_sum.reduce(step, number)

    push_far(0)
    local["normed"].wait()

    def weight_grad(span):
        def step(number, carry):
            at = pl.ds(aligned(number * PB, PB), PB)
            weight_grad_ref[at, pl.ds(span[0], span[1])] = bdot(
                packed_ref[0:tokens, at], grad_proj_ref[:, pl.ds(span[0], span[1])], TN
            ).astype(low)
            return carry

        lax.fori_loop(0, model // PB, step, 0)

    weight_grad(spans[0])
    mixer_sums[0].start()
    for number in range(1, parts):
        push_far(number)
    weight_grad(spans[1])
    mixer_sums[0].combine()
    mixer_sums[0].leave()
    mixer_sums[1].start()
    down_total[...] = down_sum.total()
    down_share.start()
    up_share.relay()
    small_gather.relay()
    weight_grad(spans[2])
    weight_grad(spans[3])
    push_back(mate, normed_give.at[0], 0)
    normed_sum.gives[0, 0].start()
    mixer_sums[1].combine()
    mixer_sums[1].leave()
    mixer_sums[2].start()
    for number in range(1, parts):
        push_back(mate, normed_give.at[0], number)
        normed_sum.gives[0, number].start()
    push_back(seq, normed_mine.at[0], 0)
    mixer_sums[2].combine()
    mixer_sums[2].leave()
    mixer_sums[3].start()
    for number in range(1, parts):
        push_back(seq, normed_mine.at[0], number)
    out_far[chip] = out_scatter.total()
    for copy in out_across:
        copy.start()
    small_gather.finish()
    total = small_all[0]
    for owner in range(1, n_fsdp):
        total = total + small_all[owner]
    small_ref[...] = total
    small_spread.start()
    mixer_sums[3].combine()
    mixer_sums[3].leave()
    mixer_total[:, spans[0][0] : spans[0][0] + spans[0][1]] = mixer_sums[0].total()
    mixer_shares[0].start()
    gate_share.finish()
    spread_units(spread_ref.at[0], gate_all, n_seq, slab)
    bring("keep_gate", spread_ref.at[0], gate_out)
    mixer_total[:, spans[1][0] : spans[1][0] + spans[1][1]] = mixer_sums[1].total()
    mixer_shares[1].start()
    mixer_total[:, spans[2][0] : spans[2][0] + spans[2][1]] = mixer_sums[2].total()
    mixer_shares[2].start()
    down_share.relay()
    local["grad_hidden"].wait()
    local["tokens"].wait()

    def norm_back(number, total):
        at = pl.ds(aligned(number * CHUNK, CHUNK), CHUNK)
        values = tokens_ref[at, :].astype(full)
        inv = lax.rsqrt(jnp.mean(values * values, axis=1, keepdims=True) + EPS_NORM)
        unit = values * inv
        grad = normed_sum.total(at)
        grad_unit = grad * norm_gain_ref[...]
        wide_ref[at, :] += inv * (
            grad_unit - unit * jnp.mean(grad_unit * unit, axis=1, keepdims=True)
        )
        return total + jnp.sum(grad * unit, axis=0, keepdims=True)

    total = jnp.zeros((1, model), full)
    for number in range(parts):
        normed_sum.arrive(number)
        total = lax.fori_loop(
            number * part // CHUNK, (number + 1) * part // CHUNK, norm_back, total
        )
    for index in range(model // DK):
        norm_ref[index : index + 1, :] = total[:, index * DK : (index + 1) * DK]
    norm_first.start()
    bring("keep_tokens", wide_ref, tokens_out)
    mixer_total[:, spans[3][0] : spans[3][0] + spans[3][1]] = mixer_sums[3].total()
    mixer_shares[3].start()
    norm_half[...] = norm_first.total()
    norm_spread.start()
    total = small_spread.total()
    for owner in range(n_seq):
        small_sum[0:gain_row, owner * head_width : (owner + 1) * head_width] = small_seq[
            owner, 0:gain_row, :
        ]
    small_sum[gain_row : gain_row + 2, :] = jnp.zeros((2, model), full)
    small_sum[gain_row : gain_row + 1, 0:DK] = total[gain_row : gain_row + 1, 0:DK]
    for index in range(model // head_width):
        small_sum[
            gain_row + 1 : gain_row + 2, index * head_width : (index + 1) * head_width
        ] = total[gain_row + 1 + index : gain_row + 2 + index, :]
    bring("keep_small", small_sum, small_out)
    for copy in out_across:
        copy.wait_recv()
    total = out_far[0].astype(full)
    for index in range(1, chips):
        total = total + out_far[index].astype(full)
    out_total[...] = total.astype(low)
    out_swap.start()
    bring("keep_out", out_total, out_out.at[:, half_at])
    for each in mixer_shares:
        each.relay()
    up_share.finish()
    spread_units(spread_ref.at[1], up_all, n_seq, slab)
    bring("keep_up", spread_ref.at[1], up_out)
    norm_ref[...] = norm_spread.total()
    bring("keep_norm", norm_ref, norm_out)
    for each in [down_share] + mixer_shares:
        each.finish()
    for each in [gate_sum, up_sum, down_sum, out_scatter] + mixer_sums + [result_sum, normed_sum]:
        each.drain()
    for copy in out_across:
        copy.wait_send()
    out_give.wait_send()
    out_swap.wait()
    for name, copy in local.items():
        if str(name).startswith("keep_"):
            copy.wait()


def mixer_backward(n_seq, n_fsdp, small, saved, big):
    (lengths, row, grad_heads, taps, gain, norm_gain, ffn_gain) = small
    packed, delta, inverse, parts, update, state = saved
    normed, weight, own_tokens, hidden, grad_hidden, result, gate, up, down, out = big
    tokens = grad_heads.shape[0]
    width = packed.shape[1]
    head_width = grad_heads.shape[1]
    heads = head_width // DK
    count = heads * (tokens // BT)
    own, model = own_tokens.shape
    _, own_rows, units = gate.shape
    slab = down.shape[1]
    hidden_units = slab * n_fsdp * n_seq
    out_rows = out.shape[0] // n_fsdp
    half = out.shape[1] // 2
    chips = n_seq // 2
    outer = Scatter.outer
    near = outer * (n_fsdp // outer - 1)
    low, full = jnp.bfloat16, jnp.float32
    copies = (
        8 * Scatter.copies(n_fsdp)
        + SeqSum.copies(n_seq, 1 + own // min(PB, own))
        + 1
        + chips
        + 2 * (n_seq - 1)
        + n_fsdp
    )
    shares, gathers = 7 * Share.copies(n_seq), Gather.copies(n_fsdp)

    def shape(dims, kind=low):
        return jax.ShapeDtypeStruct(dims, kind)

    def held(*dims, kind=low):
        return pltpu.VMEM(dims, kind)

    def sum_buffers(rows, cols):
        return [held(near, rows, cols), held(outer - 1, rows, cols)]

    return pl.pallas_call(
        functools.partial(mixer_backward_kernel, heads, n_seq, n_fsdp),
        out_shape=(
            shape((own, model)),
            shape((own, model), full),
            shape((own_rows, hidden_units)),
            shape((own_rows, hidden_units)),
            shape((n_seq, slab, model)),
            shape((out_rows, 2 * half)),
            shape((own_rows, n_seq * head_width)),
            shape((own_rows, n_seq * head_width)),
            shape((own_rows, n_seq * head_width)),
            shape((n_seq, own_rows, DK)),
            shape((16, model), full),
            shape((model // DK, DK), full),
        ),
        in_specs=[spec(SMEM)] + [spec()] * 6 + [spec(ANY)] * 16,
        out_specs=(spec(ANY),) * 12,
        scratch_shapes=[
            pltpu.SMEM((tokens // CH + 2,), full),
            held(3 * CONV, head_width, kind=full),
            held(tokens, 1, kind=jnp.int32),
            held(tokens, head_width, kind=full),
            held(count, BT, BT),
            held(count, 2 * BT, BT),
            held(count, BT, BT),
            held(count, BT, BT),
            held(HALO + tokens, max(width, model)),
            held(tokens, head_width),
            held(count, BT, BT),
            held(count, BT, BT),
            held(BT + HALO, 3 * head_width, kind=full),
            held(tokens, width),
            held(min(PB, own), width),
            held(model, width),
            held(model, width),
            held(own, model, kind=full),
            held(own, model),
            held(own, model),
            held(chips, own, model),
            held(chips, own, model),
            held(chips - 1, own, model),
            held(chips, own, model),
            held(chips, own, model),
            held(chips, own, model),
            held(chips - 1, own, model),
            held(own_rows, units),
            held(outer - 1, own_rows, units),
            held(outer, own_rows, units),
            *sum_buffers(own_rows, units),
            held(outer, slab, model),
            *sum_buffers(slab, model),
            held(out.shape[0], half),
            held(out.shape[0], half),
            *sum_buffers(out_rows, half),
            held(chips, out_rows, half),
            *sum_buffers(own_rows, head_width),
            *sum_buffers(own_rows, head_width),
            *sum_buffers(own_rows, head_width),
            *sum_buffers(own_rows, DK),
            held(own_rows, units),
            held(own_rows, units),
            held(slab, model),
            held(out_rows, half),
            held(own_rows, width),
            held(n_seq, own_rows, units),
            held(n_seq, own_rows, units),
            held(2, own_rows, hidden_units),
            held(16, head_width, kind=full),
            held(SMALL_ROWS, head_width, kind=full),
            held(n_fsdp, SMALL_ROWS, head_width, kind=full),
            held(n_seq, SMALL_ROWS, head_width, kind=full),
            held(16, model, kind=full),
            held(model // DK, DK, kind=full),
            held(model // DK, DK, kind=full),
            held(n_fsdp, model // DK, DK, kind=full),
            held(n_seq, model // DK, DK, kind=full),
            pltpu.SemaphoreType.DMA((copies,)),
            pltpu.SemaphoreType.DMA((copies,)),
            pltpu.SemaphoreType.DMA((gathers,)),
            pltpu.SemaphoreType.DMA((gathers,)),
            pltpu.SemaphoreType.DMA((shares,)),
            pltpu.SemaphoreType.DMA((shares,)),
            pltpu.SemaphoreType.DMA((61,)),
        ],
        compiler_params=pltpu.CompilerParams(
            vmem_limit_bytes=63 << 20, collective_id=3, has_side_effects=True
        ),
        name="mixer_backward",
    )(
        lengths, row, grad_heads, taps, gain, norm_gain, ffn_gain, delta, inverse, parts,
        update, state, packed, normed, weight, own_tokens, hidden, grad_hidden, result,
        gate, up, down, out,
    )


def finish_kernel(
    heads,
    result_in,
    tokens_in,
    gate_in,
    up_in,
    down_in,
    out_in,
    query_in,
    key_in,
    value_in,
    beta_in,
    small_in,
    norm_in,
    result_ref,
    tokens_ref,
    norm_ref,
    query_ref,
    key_ref,
    value_ref,
    beta_ref,
    taps_ref,
    gain_ref,
    out_ref,
    ffn_ref,
    gate_ref,
    up_ref,
    down_ref,
):
    full = jnp.float32
    result_ref[...] = result_in[...]
    tokens_ref[...] = tokens_in[...]
    for source, target in (
        (gate_in, gate_ref),
        (up_in, up_ref),
        (out_in, out_ref),
        (query_in, query_ref),
        (key_in, key_ref),
        (value_in, value_ref),
        (down_in, down_ref),
    ):
        target[...] = source[...].astype(full)
    total = None
    row, col = iota((beta_ref.shape[0], DK), 0), iota((beta_ref.shape[0], DK), 1)
    for owner in range(beta_in.shape[0]):
        hot = jnp.where((col + owner * heads == row) & (col < heads), 1.0, 0.0)
        part = bdot(hot, beta_in[owner], NT)
        total = part if total is None else total + part
    beta_ref[...] = total
    for kind in range(3):
        for back in range(CONV):
            at = kind * CONV + back
            taps_ref[kind, back : back + 1, :] = small_in[at : at + 1, :]
    gain_ref[...] = small_in[3 * CONV : 3 * CONV + 1, 0:DK]
    ffn_ref[...] = small_in[3 * CONV + 1 : 3 * CONV + 2, :]
    for index in range(norm_in.shape[0]):
        norm_ref[:, index * DK : (index + 1) * DK] = norm_in[index : index + 1, :]


def finish(heads, arrays):
    result, tokens, gate, up, down, out, query, key, value, beta, small, norm = arrays
    full = jnp.float32
    model = small.shape[1]
    head_count = heads * beta.shape[0]

    def wide(array):
        return jax.ShapeDtypeStruct(array.shape, full)

    return pl.pallas_call(
        functools.partial(finish_kernel, heads),
        out_shape=(
            jax.ShapeDtypeStruct(result.shape, result.dtype),
            wide(tokens),
            jax.ShapeDtypeStruct((1, model), full),
            wide(query),
            wide(key),
            wide(value),
            jax.ShapeDtypeStruct((head_count, query.shape[0]), full),
            jax.ShapeDtypeStruct((3, CONV, model), full),
            jax.ShapeDtypeStruct((1, DK), full),
            wide(out),
            jax.ShapeDtypeStruct((1, model), full),
            wide(gate),
            wide(up),
            wide(down),
        ),
        in_specs=[spec()] * 12,
        out_specs=(spec(),) * 14,
        compiler_params=pltpu.CompilerParams(vmem_limit_bytes=63 << 20),
        name="finish",
    )(*arrays)


def own_slice(array, place, size, axis):
    return lax.dynamic_slice_in_dim(array, place * size, size, axis)


def local(
    n_seq,
    n_fsdp,
    tokens,
    norm_gain,
    w_query,
    w_key,
    w_value,
    w_beta,
    conv_taps,
    head_gain,
    w_out,
    ffn_gain,
    w_gate,
    w_up,
    w_down,
    cotangent,
    token_order,
    seq_lengths,
):
    place = lax.axis_index("seq")
    model = tokens.shape[1]
    head_count = w_beta.shape[1]
    heads = head_count // n_seq
    hidden_units = w_gate.shape[1]
    slab = hidden_units // (n_fsdp * n_seq)
    units = slab * n_fsdp

    row = token_order.reshape(1, -1)
    gain = head_gain.reshape(1, DK)
    mixed_tok, normed, w_mixer, full_gate, full_up, full_down, full_o, cot_all, *saved = (
        mixer_forward(
            n_seq,
            n_fsdp,
            seq_lengths,
            row,
            conv_taps,
            gain,
            norm_gain.reshape(1, model),
            (
                tokens,
                w_beta.T,
                cotangent,
                w_query,
                w_key,
                w_value,
                w_gate,
                w_up,
                w_down if slab % 8 == 0 else own_slice(w_down, place, slab, 0),
                w_out,
            ),
        )
    )
    full_down = full_down.reshape(units, model)
    (
        hidden,
        grad_hidden,
        grad_heads,
        result_part,
        wide_gate,
        wide_up,
        wide_down,
        wide_out,
        grad_ffn_gain,
    ) = ffn_block(
        n_seq,
        n_fsdp,
        tokens,
        mixed_tok,
        full_o,
        ffn_gain.reshape(1, model),
        full_gate,
        full_up,
        full_down,
        cot_all,
    )
    (
        result,
        grad_inputs,
        all_gate,
        all_up,
        part_down,
        all_out,
        all_query,
        all_key,
        all_value,
        part_beta,
        small,
        norm_sum,
    ) = mixer_backward(
        n_seq,
        n_fsdp,
        (
            seq_lengths,
            row,
            grad_heads,
            conv_taps,
            gain,
            norm_gain.reshape(1, model),
            grad_ffn_gain,
        ),
        saved,
        (
            normed,
            w_mixer,
            tokens,
            hidden,
            grad_hidden,
            result_part,
            wide_gate,
            wide_up,
            wide_down.reshape(n_fsdp, slab, model),
            wide_out,
        ),
    )
    outputs = finish(
        heads,
        (
            result,
            grad_inputs,
            all_gate,
            all_up,
            part_down.reshape(n_seq * slab, model),
            all_out,
            all_query,
            all_key,
            all_value,
            part_beta,
            small,
            norm_sum,
        ),
    )
    flat, turned = (2, 8, 10), (6,)
    return tuple(
        output.reshape(-1) if index in flat else output.T if index in turned else output
        for index, output in enumerate(outputs)
    )


def solution(mesh):
    tokens = P(("seq", "fsdp"), None)
    rows = P("fsdp", None)
    in_specs = (
        (tokens, P()) + (rows,) * 4 + (P(), P(), rows, P()) + (rows,) * 3 + (tokens, rows, rows)
    )
    out_specs = (
        (tokens, tokens, P()) + (rows,) * 4 + (P(), P(), rows, P()) + (rows,) * 3
    )
    return jax.shard_map(
        functools.partial(local, mesh.shape["seq"], mesh.shape["fsdp"]),
        mesh=mesh,
        in_specs=in_specs,
        out_specs=out_specs,
        check_vma=False,
    )
```

```python
import functools

import jax
import jax.numpy as jnp
from jax import lax
from jax.experimental import pallas as pl
from jax.experimental.pallas import tpu as pltpu
from jax.sharding import PartitionSpec as P

DK = 128
CONV = 4
CH = 64
BT = 128
HALO = 16
PB = 256
WIDE = 512
EPS_NORM = 1e-06

NN = (((1,), (0,)), ((), ()))
NT = (((1,), (1,)), ((), ()))
TN = (((0,), (0,)), ((), ()))


def bdot(first, second, dims=NN):
    return lax.dot_general(
        first.astype(jnp.bfloat16),
        second.astype(jnp.bfloat16),
        dims,
        preferred_element_type=jnp.float32,
    )


def iota(shape, axis):
    return lax.broadcasted_iota(jnp.int32, shape, axis)


def sigmoid(values):
    return 1.0 / (1.0 + jnp.exp(-values))


def fill_masks(mask_ref):
    rows, cols = iota((BT, BT), 0), iota((BT, BT), 1)
    size, level = 1, 0
    while size < BT:
        inside = (rows // (2 * size) == cols // (2 * size)) & (rows // size > cols // size)
        mask_ref[level] = jnp.where(inside, 1.0, 0.0)
        size, level = 2 * size, level + 1


def unit_lower_inverses(stricts, mask_ref):
    rows, cols = iota((BT, BT), 0), iota((BT, BT), 1)
    eye = jnp.where(rows == cols, 1.0, 0.0)
    inverses = [eye - strict * mask_ref[0] for strict in stricts]
    for level in range(1, 7):
        lows = [inverse.astype(jnp.bfloat16) for inverse in inverses]
        inner = [bdot(strict * mask_ref[level], low) for strict, low in zip(stricts, lows)]
        inverses = [
            inverse - bdot(low, mid) for inverse, low, mid in zip(inverses, lows, inner)
        ]
    return inverses


def tap_masks(first, second, third, count):
    rows = iota((count, 1), 0)
    flag = jnp.where(rows < CH, first, jnp.where(rows < BT, second, third))
    return [None] + [jnp.where(rows % CH < back, flag, 1.0) for back in range(1, CONV)]


def conv_of(halo_rows, taps, masks):
    total = halo_rows[HALO:] * taps[0]
    for back in range(1, CONV):
        total = total + pltpu.roll(halo_rows, back, 0)[HALO:] * (taps[back] * masks[back])
    return total


def block_flags(first, second):
    upper = iota((BT, 1), 0) < CH
    seen = jnp.where(upper, first, first * second)
    kept = jnp.where(upper, second, 1.0)
    return seen, kept


def pair_mask(second):
    rows, cols = iota((BT, BT), 0), iota((BT, BT), 1)
    cross = (rows >= CH) & (cols < CH)
    return rows, cols, jnp.where(cross, second, 1.0)


def permute_rows(column, source, width):
    hot = jnp.where(column == iota((column.shape[0], width), 1), 1.0, 0.0).astype(jnp.bfloat16)
    return lax.dot_general(hot, source, NN, preferred_element_type=jnp.float32)


def unpermute_rows(row, base, source, width):
    hot = jnp.where(row == iota((PB, width), 0) + base, 1.0, 0.0).astype(jnp.bfloat16)
    return lax.dot_general(hot, source, NN, preferred_element_type=jnp.float32)


MESH = pl.DeviceIdType.MESH
ANY = pl.ANY


class Gather:
    outer = 4

    @classmethod
    def copies(cls, n_fsdp):
        inner = n_fsdp // cls.outer
        return (cls.outer - 1) + cls.outer * (inner - 1)

    def __init__(self, n_fsdp, source, slot, sems, base, local_sem):
        self.inner = n_fsdp // self.outer
        self.me = lax.axis_index("fsdp")
        self.seq = lax.axis_index("seq")
        self.high, self.low = self.me // self.inner, self.me % self.inner
        self.source, self.slot = source, slot
        self.send, self.recv = sems
        self.base, self.local_sem = base, local_sem

    def at(self, high, low):
        return (high % self.outer) * self.inner + (low % self.inner)

    def copy(self, source, owner, target, index):
        return pltpu.make_async_remote_copy(
            src_ref=source,
            dst_ref=self.slot(owner),
            send_sem=self.send.at[self.base + index],
            recv_sem=self.recv.at[self.base + index],
            device_id=(self.seq, target),
            device_id_type=MESH,
        )

    def along_outer(self, step):
        return self.copy(self.source, self.me, self.at(self.high + step, self.low), step - 1)

    def along_inner(self, hop):
        return self.copy(
            self.source, self.me, self.at(self.high, self.low + hop), self.outer - 2 + hop
        )

    def passed_on(self, step, hop):
        owner = self.at(self.high - step, self.low)
        index = self.outer - 1 + (self.inner - 1) * step + hop - 1
        return self.copy(self.slot(owner), owner, self.at(self.high, self.low + hop), index)

    def own(self):
        return pltpu.make_async_copy(self.source, self.slot(self.me), self.local_sem)

    def start(self):
        for step in range(1, self.outer):
            self.along_outer(step).start()
        for hop in range(1, self.inner):
            self.along_inner(hop).start()
        self.own().start()

    def relay(self):
        for step in range(1, self.outer):
            self.along_outer(step).wait_recv()
            for hop in range(1, self.inner):
                self.passed_on(step, hop).start()

    def finish(self):
        self.own().wait()
        for hop in range(1, self.inner):
            self.along_inner(hop).wait_recv()
            for step in range(1, self.outer):
                self.passed_on(step, hop).wait_recv()
        for step in range(1, self.outer):
            self.along_outer(step).wait_send()
        for hop in range(1, self.inner):
            self.along_inner(hop).wait_send()
            for step in range(1, self.outer):
                self.passed_on(step, hop).wait_send()


class Share:
    @staticmethod
    def copies(n_seq):
        return 1 + 2 * (n_seq // 2 - 1)

    def __init__(self, n_seq, source, slot, sems, base, local_sem):
        self.n_seq, self.chips = n_seq, n_seq // 2
        self.me = lax.axis_index("seq")
        self.fsdp = lax.axis_index("fsdp")
        self.mate = self.me + 1 - 2 * (self.me % 2)
        self.source, self.slot = source, slot
        self.send, self.recv = sems
        self.base, self.local_sem = base, local_sem

    def copy(self, source, owner, target, index):
        return pltpu.make_async_remote_copy(
            src_ref=source,
            dst_ref=self.slot(owner),
            send_sem=self.send.at[self.base + index],
            recv_sem=self.recv.at[self.base + index],
            device_id=(target, self.fsdp),
            device_id_type=MESH,
        )

    def to_mate(self):
        return self.copy(self.source, self.me, self.mate, 0)

    def across(self, step):
        return self.copy(self.source, self.me, (self.me + 2 * step) % self.n_seq, step)

    def passed_on(self, step):
        owner = (self.me + self.n_seq - 2 * step) % self.n_seq
        return self.copy(self.slot(owner), owner, self.mate, self.chips - 1 + step)

    def own(self):
        return pltpu.make_async_copy(self.source, self.slot(self.me), self.local_sem)

    def start(self):
        for step in range(1, self.chips):
            self.across(step).start()
        self.to_mate().start()
        if self.local_sem is not None:
            self.own().start()

    def relay(self):
        for step in range(1, self.chips):
            self.across(step).wait_recv()
            self.passed_on(step).start()

    def waits(self):
        steps = range(1, self.chips)
        return [self.to_mate()] + [each(step) for step in steps for each in (self.across, self.passed_on)]

    def finish(self):
        if self.local_sem is not None:
            self.own().wait()
        self.to_mate().wait_recv()
        for step in range(1, self.chips):
            self.passed_on(step).wait_recv()
        self.to_mate().wait_send()
        for step in range(1, self.chips):
            self.across(step).wait_send()
            self.passed_on(step).wait_send()


def greet_signal(n_seq, n_fsdp):
    seq, fsdp = lax.axis_index("seq"), lax.axis_index("fsdp")
    barrier = pltpu.get_barrier_semaphore()
    for step in range(1, n_seq):
        pl.semaphore_signal(
            barrier, inc=1, device_id=((seq + step) % n_seq, fsdp), device_id_type=MESH
        )
    for step in range(1, n_fsdp):
        pl.semaphore_signal(
            barrier, inc=1, device_id=(seq, (fsdp + step) % n_fsdp), device_id_type=MESH
        )


def greet_wait(n_seq, n_fsdp):
    pl.semaphore_wait(pltpu.get_barrier_semaphore(), n_seq + n_fsdp - 2)


def greet(n_seq, n_fsdp):
    greet_signal(n_seq, n_fsdp)
    greet_wait(n_seq, n_fsdp)


def aligned(value, unit):
    return pl.multiple_of(value, unit)


def fill_flags(flags_ref, lengths_ref):
    def fill(span, carry):
        start, hit = 0, span == 0
        for index in range(lengths_ref.shape[1] - 1):
            start = start + lengths_ref[0, index]
            hit = hit | (span * CH == start)
        flags_ref[span] = jnp.where(hit, 0.0, 1.0)
        return carry

    lax.fori_loop(0, flags_ref.shape[0], fill, 0)


def fill_taps(taps_ref, taps_in, seq, width):
    for kind in range(3):
        for back in range(CONV):
            row = kind * CONV + back
            taps_ref[row : row + 1, :] = taps_in[
                kind, back : back + 1, pl.ds(aligned(seq * width, width), width)
            ]


def fill_column(column_ref, row_ref):
    for base in range(0, row_ref.shape[1], BT):
        rows = jnp.broadcast_to(row_ref[:, base : base + BT], (8, BT))
        column_ref[base : base + BT, :] = rows.T[:, 0:1]


def pick_units(target, source, seq, n_seq, slab):
    units, hidden = target.shape[1], source.shape[1]
    jump = slab * (n_seq - 1)
    for base in range(0, units, BT):
        size = min(BT, units - base)
        first, last = base // slab, (base + size - 1) // slab
        low = (base + jump * first) // BT * BT
        high = min(-(-(base + size + jump * (last + 1)) // BT) * BT, hidden)
        col = iota((high - low, size), 1) + base
        origin = col + jump * first + slab * seq - low
        for owner in range(first + 1, last + 1):
            origin = origin + jnp.where(col >= owner * slab, jump, 0)
        hot = jnp.where(iota((high - low, size), 0) == origin, 1.0, 0.0)
        target[:, base : base + size] = bdot(source[:, low:high], hot).astype(jnp.bfloat16)


def mixer_forward_kernel(
    heads,
    n_seq,
    n_fsdp,
    lengths_ref,
    row_ref,
    taps_in,
    gain_ref,
    norm_gain_ref,
    tokens_ref,
    beta_ref,
    cot_in,
    query_in,
    key_in,
    value_in,
    gate_in,
    up_in,
    down_in,
    out_in,
    tokens_mixed,
    normed_out,
    mixer_out,
    gate_all,
    up_all,
    down_all,
    out_all,
    cot_all,
    packed_out,
    delta_out,
    inverse_out,
    big_out,
    update_out,
    state_out,
    retain_ref,
    taps_ref,
    column_ref,
    packed_ref,
    delta_ref,
    inverse_ref,
    update_ref,
    state_ref,
    big_ref,
    mask_ref,
    fresh_ref,
    own_ref,
    add_ref,
    mixed_ref,
    ready_ref,
    chosen_ref,
    normed_ref,
    weight_ref,
    betas_ref,
    raw_ref,
    gate_mine,
    up_mine,
    down_mine,
    out_mine,
    gather_send,
    gather_recv,
    share_send,
    share_recv,
    local_sems,
):
    own_tokens = tokens_ref.shape[0]
    tokens = own_tokens * n_seq
    width = packed_ref.shape[1]
    head_width = heads * DK
    blocks = tokens // BT
    seq = lax.axis_index("seq")
    own_rows, _ = query_in.shape
    slab = down_mine.shape[0]
    out_rows, out_width = out_in.shape
    out_part = out_width // n_seq
    low = jnp.bfloat16

    local = {}

    def bring(name, source, target):
        copy = pltpu.make_async_copy(source, target, local_sems.at[len(local)])
        local[name] = copy
        copy.start()

    out_at = aligned(seq * out_part, out_part)
    bring("gate", gate_in, raw_ref.at[0])
    bring("up", up_in, raw_ref.at[1])
    bring("out", out_in.at[:, pl.ds(out_at, out_part)], out_mine)
    whole_shard = down_in.shape[0] > slab
    bring(
        "down",
        down_in.at[pl.ds(aligned(seq * slab, slab), slab)] if whole_shard else down_in,
        down_mine,
    )
    greet_signal(n_seq, n_fsdp)

    half_model = down_mine.shape[1] // 2
    part = min(PB, own_tokens)
    for base in range(0, own_tokens, part):
        values = tokens_ref[base : base + part, :].astype(jnp.float32)
        inv = lax.rsqrt(jnp.mean(values * values, axis=1, keepdims=True) + EPS_NORM)
        normed_ref[pl.ds(aligned(seq * own_tokens + base, part), part), :] = (
            values * inv * norm_gain_ref[...]
        ).astype(low)
    greet_wait(n_seq, n_fsdp)

    gather_sems = (gather_send, gather_recv)
    share_sems = (share_send, share_recv)
    per_gather = Gather.copies(n_fsdp)
    per_share = Share.copies(n_seq)

    def rows_slot(ref, size):
        return lambda owner: ref.at[pl.ds(aligned(owner * size, size), size)]

    def gather_piece(index, source, slot):
        return Gather(
            n_fsdp, source, slot, gather_sems, index * per_gather, local_sems.at[30 + index]
        )

    def head_columns(kind):
        return lambda owner: weight_ref.at[
            pl.ds(aligned(owner * own_rows, own_rows), own_rows),
            pl.ds(kind * head_width, head_width),
        ]

    pieces = [
        gather_piece(
            kind,
            source.at[:, pl.ds(aligned(seq * head_width, head_width), head_width)],
            head_columns(kind),
        )
        for kind, source in enumerate((query_in, key_in, value_in))
    ] + [
        gather_piece(
            3,
            out_mine,
            lambda owner: out_all.at[
                pl.ds(aligned(owner * out_rows, out_rows), out_rows), pl.ds(out_at, out_part)
            ],
        ),
        gather_piece(4, gate_mine, rows_slot(gate_all, own_rows)),
        gather_piece(5, up_mine, rows_slot(up_all, own_rows)),
    ] + [
        gather_piece(
            6 + index,
            down_mine.at[:, pl.ds(index * half_model, half_model)],
            (lambda place: lambda owner: down_all.at[owner, :, place])(
                pl.ds(index * half_model, half_model)
            ),
        )
        for index in range(2)
    ]
    betas = gather_piece(8, beta_ref, lambda owner: betas_ref.at[owner])
    share_normed = Share(
        n_seq,
        normed_ref.at[pl.ds(aligned(seq * own_tokens, own_tokens), own_tokens)],
        rows_slot(normed_ref, own_tokens),
        share_sems,
        0,
        None,
    )
    share_cot = Share(
        n_seq, cot_in, rows_slot(cot_all, own_tokens), share_sems, per_share, local_sems.at[39]
    )
    share_out = Share(
        n_seq,
        out_all.at[:, pl.ds(out_at, out_part)],
        lambda owner: out_all.at[:, pl.ds(aligned(owner * out_part, out_part), out_part)],
        share_sems,
        2 * per_share,
        None,
    )

    share_normed.start()
    pieces[0].start()
    betas.start()
    pieces[1].start()
    fill_flags(retain_ref, lengths_ref)
    fill_taps(taps_ref, taps_in, seq, head_width)
    fill_column(column_ref, row_ref)
    fill_masks(mask_ref)
    packed_ref[0:HALO, :] = jnp.zeros((HALO, width), low)
    local["gate"].wait()
    pick_units(gate_mine, raw_ref.at[0], seq, n_seq, slab)
    pieces[0].relay()
    pieces[2].start()
    betas.relay()
    pieces[1].relay()
    local["out"].wait()
    pieces[3].start()
    local["up"].wait()
    pick_units(up_mine, raw_ref.at[1], seq, n_seq, slab)
    share_normed.to_mate().wait_recv()

    def permute(step, carry, source, first):
        base = aligned(step * WIDE, WIDE)
        picked = permute_rows(
            column_ref[pl.ds(base, WIDE), :] - source * own_tokens,
            normed_ref[pl.ds(aligned(source * own_tokens, own_tokens), 2 * own_tokens), :],
            2 * own_tokens,
        )
        if not first:
            picked = picked + chosen_ref[pl.ds(base, WIDE), :].astype(jnp.float32)
        chosen_ref[pl.ds(base, WIDE), :] = picked.astype(low)
        return carry

    lax.fori_loop(
        0, tokens // WIDE, functools.partial(permute, source=seq // 2 * 2, first=True), 0
    )
    pieces[2].relay()
    pieces[4].start()
    betas.finish()
    mine = jnp.where(
        iota((beta_ref.shape[0], DK), 0) == iota((beta_ref.shape[0], DK), 1) + seq * heads, 1.0, 0.0
    )
    mine = jnp.where(iota(mine.shape, 1) < heads, mine, 0.0)
    for owner in range(n_fsdp):
        weight_ref[owner * own_rows : (owner + 1) * own_rows, 3 * head_width :] = bdot(
            betas_ref[owner], mine, TN
        ).astype(low)
    share_normed.relay()
    share_cot.start()
    for step in range(1, n_seq // 2):
        share_normed.passed_on(step).wait_recv()
        lax.fori_loop(
            0,
            tokens // WIDE,
            functools.partial(permute, source=(seq // 2 * 2 + n_seq - 2 * step) % n_seq, first=False),
            0,
        )
    pieces[3].relay()
    for piece in pieces[:3]:
        piece.finish()
    bring("keep_normed", chosen_ref, normed_out)
    bring("keep_mixer", weight_ref, mixer_out)

    def project(step, carry):
        base = aligned(step * WIDE, WIDE)
        packed_ref[pl.ds(HALO + base, WIDE), :] = bdot(
            chosen_ref[pl.ds(base, WIDE), :], weight_ref[...]
        ).astype(low)
        return carry

    lax.fori_loop(0, tokens // WIDE, project, 0)
    bring("keep_packed", packed_ref, packed_out)

    def middle(number):
        if number == 0:
            pieces[3].finish()
            share_out.start()
            pieces[4].relay()
            pieces[5].start()
        if number == 1:
            share_cot.relay()
        if number == 2:
            pieces[5].relay()
            local["down"].wait()
            pieces[6].start()
            share_out.relay()

    unroll = 2

    def prepare(step, carry):
        for number, moment in enumerate((1, 4, 7)):

            @pl.when(step == moment)
            def _():
                middle(number)

        places, stricts, kept_values = [], [], []
        for sub in range(unroll):
            block = step * unroll + sub
            first, second = retain_ref[2 * block], retain_ref[2 * block + 1]
            base = pl.multiple_of(block * BT, BT)
            masks = tap_masks(first, second, 1.0, BT)
            seen, kept = block_flags(first, second)
            rows, cols, cross = pair_mask(second)
            strengths = sigmoid(
                packed_ref[pl.ds(HALO + base, BT), 3 * heads * DK : 3 * heads * DK + BT].astype(
                    jnp.float32
                )
            )
            for head in range(heads):
                parts = []
                for kind in range(3):
                    at = (kind * heads + head) * DK
                    window = packed_ref[pl.ds(base, HALO + BT), at : at + DK].astype(jnp.float32)
                    taps = [
                        taps_ref[kind * CONV + back : kind * CONV + back + 1, head * DK : head * DK + DK]
                        for back in range(CONV)
                    ]
                    conv = conv_of(window, taps, masks)
                    parts.append(conv * sigmoid(conv))
                query, key, value = parts
                query = query * lax.rsqrt(
                    jnp.sum(query * query, axis=1, keepdims=True) + EPS_NORM
                ) * DK ** (-0.5)
                key = key * lax.rsqrt(jnp.sum(key * key, axis=1, keepdims=True) + EPS_NORM)
                query_low, key_low = query.astype(jnp.bfloat16), key.astype(jnp.bfloat16)
                query, key = query_low.astype(jnp.float32), key_low.astype(jnp.float32)
                beta = strengths[:, head : head + 1]
                inner = bdot(jnp.concatenate([key_low, query_low], axis=0), key_low, NT)
                stricts.append(jnp.where(rows > cols, inner[:BT] * cross * beta, 0.0))
                scores = jnp.where(rows >= cols, inner[BT:] * cross, 0.0)
                sides = jnp.concatenate([key * (beta * seen), value * beta], axis=1)
                kept_values.append((scores, sides, key * kept, query * seen))
                places.append(head * blocks + block)
        inverses = unit_lower_inverses(stricts, mask_ref)
        solved = [
            bdot(inverse, values[1]) for inverse, values in zip(inverses, kept_values)
        ]
        through = [bdot(values[0], both) for values, both in zip(kept_values, solved)]
        onward = [bdot(values[2], both, TN) for values, both in zip(kept_values, solved)]
        for index, place in enumerate(places):
            inverse_ref[place] = inverses[index].astype(jnp.bfloat16)
            big_ref[place, 0:BT, :] = onward[index][:, :DK].astype(jnp.bfloat16)
            big_ref[place, BT : 2 * BT, :] = (
                kept_values[index][3] - through[index][:, :DK]
            ).astype(jnp.bfloat16)
            big_ref[place, 2 * BT : 3 * BT, :] = solved[index][:, :DK].astype(jnp.bfloat16)
            add_ref[place] = onward[index][:, DK:]
            fresh_ref[place] = solved[index][:, DK:]
            own_ref[place] = through[index][:, DK:]
        return carry

    lax.fori_loop(0, blocks // unroll, prepare, 0)
    bring("keep_inverse", inverse_ref, inverse_out)
    bring("keep_big", big_ref.at[:, pl.ds(0, 2 * BT), :], big_out)

    def advance(block, states):
        through = retain_ref[2 * block] * retain_ref[2 * block + 1]
        base = pl.multiple_of(block * BT, BT)
        lows = [state.astype(jnp.bfloat16) for state in states]
        products = [bdot(big_ref[head * blocks + block], lows[head]) for head in range(heads)]
        following = []
        for head in range(heads):
            place = head * blocks + block
            product = products[head]
            state_ref[place] = lows[head]
            following.append(states[head] * through - product[:BT] + add_ref[place])
            update_ref[place] = (fresh_ref[place] - product[2 * BT :]).astype(jnp.bfloat16)
            delta = own_ref[place] + product[BT : 2 * BT]
            delta_ref[pl.ds(base, BT), head * DK : head * DK + DK] = delta
            inv = lax.rsqrt(jnp.mean(delta * delta, axis=1, keepdims=True) + EPS_NORM)
            ready_ref[pl.ds(base, BT), head * DK : head * DK + DK] = (
                delta * inv * gain_ref[...]
            ).astype(jnp.bfloat16)
        return tuple(following)

    zero = jnp.zeros((DK, DK), jnp.float32)
    lax.fori_loop(0, blocks, advance, (zero,) * heads)
    bring("keep_delta", delta_ref, delta_out)
    bring("keep_update", update_ref, update_out)
    bring("keep_state", state_ref, state_out)
    pieces[6].relay()
    pieces[7].start()

    def hand_over(shift):
        target = (seq + shift) % n_seq
        base = aligned(target * own_tokens, own_tokens)
        for at in range(0, own_tokens, part):
            first = aligned(base + at, part)
            hot = jnp.where(
                row_ref[...] == iota((part, tokens), 0) + first, 1.0, 0.0
            ).astype(low)
            mixed_ref[pl.ds(first, part), :] = lax.dot_general(
                hot, ready_ref[...], NN, preferred_element_type=jnp.float32
            ).astype(low)
        source = mixed_ref.at[pl.ds(base, own_tokens)]
        slot = tokens_mixed.at[:, pl.ds(aligned(seq * head_width, head_width), head_width)]
        if shift == 0:
            return pltpu.make_async_copy(source, slot, local_sems.at[40])
        return pltpu.make_async_remote_copy(
            src_ref=source,
            dst_ref=slot,
            send_sem=share_send.at[3 * per_share + shift],
            recv_sem=share_recv.at[3 * per_share + shift],
            device_id=(target, lax.axis_index("fsdp")),
            device_id_type=MESH,
        )

    handed = []
    for shift in sorted(range(n_seq), key=lambda shift: (shift in (0, 1), -shift)):
        copy = hand_over(shift)
        copy.start()
        handed.append(copy)
    pieces[7].relay()
    for copy in share_normed.waits():
        copy.wait_send()
    share_cot.finish()
    share_out.finish()
    for piece in pieces[4:]:
        piece.finish()
    for name, copy in local.items():
        if name.startswith("keep_"):
            copy.wait()
    for copy in handed:
        copy.wait()


VMEM = pltpu.MemorySpace.VMEM
SMEM = pltpu.MemorySpace.SMEM


def spec(space=VMEM):
    return pl.BlockSpec(memory_space=space)


def mixer_forward(n_seq, n_fsdp, lengths, row, taps, gain, norm_gain, shards):
    tokens_in, beta, cot, query, key, value, gate, up, down, out = shards
    own_tokens, model = tokens_in.shape
    tokens = own_tokens * n_seq
    heads = beta.shape[0] // n_seq
    width = (3 * heads + 1) * DK
    blocks = tokens // BT
    count = heads * blocks
    own_rows, hidden = gate.shape
    slab = hidden // (n_seq * n_fsdp)
    units = slab * n_fsdp
    low, full = jnp.bfloat16, jnp.float32
    gathers = 9 * Gather.copies(n_fsdp)
    shares = 3 * Share.copies(n_seq) + n_seq

    def shape(dims, kind=low):
        return jax.ShapeDtypeStruct(dims, kind)

    return pl.pallas_call(
        functools.partial(mixer_forward_kernel, heads, n_seq, n_fsdp),
        out_shape=(
            shape((own_tokens, n_seq * heads * DK)),
            shape((tokens, model)),
            shape((own_rows * n_fsdp, width)),
            shape((own_rows * n_fsdp, units)),
            shape((own_rows * n_fsdp, units)),
            shape((n_fsdp, slab, model)),
            shape((out.shape[0] * n_fsdp, out.shape[1])),
            shape((tokens, model)),
            shape((HALO + tokens, width)),
            shape((tokens, heads * DK), full),
            shape((count, BT, BT)),
            shape((count, 2 * BT, BT)),
            shape((count, BT, BT)),
            shape((count, BT, BT)),
        ),
        in_specs=[spec(SMEM)] + [spec()] * 7 + [spec(ANY)] * 7,
        out_specs=(spec(ANY),) * 14,
        scratch_shapes=[
            pltpu.SMEM((tokens // CH + 2,), full),
            pltpu.VMEM((3 * CONV, heads * DK), full),
            pltpu.VMEM((tokens, 1), jnp.int32),
            pltpu.VMEM((HALO + tokens, width), low),
            pltpu.VMEM((tokens, heads * DK), full),
            pltpu.VMEM((count, BT, BT), low),
            pltpu.VMEM((count, BT, BT), low),
            pltpu.VMEM((count, BT, BT), low),
            pltpu.VMEM((count, 3 * BT, BT), low),
            pltpu.VMEM((7, BT, BT), full),
            pltpu.VMEM((count, BT, BT), full),
            pltpu.VMEM((count, BT, BT), full),
            pltpu.VMEM((count, BT, BT), full),
            pltpu.VMEM((tokens, heads * DK), low),
            pltpu.VMEM((tokens, heads * DK), low),
            pltpu.VMEM((tokens, model), low),
            pltpu.VMEM((tokens, model), low),
            pltpu.VMEM((own_rows * n_fsdp, width), low),
            pltpu.VMEM((n_fsdp,) + beta.shape, low),
            pltpu.VMEM((2, own_rows, hidden), low),
            pltpu.VMEM((own_rows, units), low),
            pltpu.VMEM((own_rows, units), low),
            pltpu.VMEM((slab, model), low),
            pltpu.VMEM((out.shape[0], out.shape[1] // n_seq), low),
            pltpu.SemaphoreType.DMA((gathers,)),
            pltpu.SemaphoreType.DMA((gathers,)),
            pltpu.SemaphoreType.DMA((shares,)),
            pltpu.SemaphoreType.DMA((shares,)),
            pltpu.SemaphoreType.DMA((41,)),
        ],
        compiler_params=pltpu.CompilerParams(
            vmem_limit_bytes=60 << 20, collective_id=1, has_side_effects=True
        ),
        name="mixer_forward",
    )(
        lengths, row, taps, gain, norm_gain, tokens_in, beta, cot,
        query, key, value, gate, up, down, out,
    )


class Wire:
    def __init__(self, send, recv):
        self.send, self.recv, self.used = send, recv, 0

    def copy(self, source, target, seq, fsdp):
        index = self.used
        self.used += 1
        return pltpu.make_async_remote_copy(
            src_ref=source,
            dst_ref=target,
            send_sem=self.send.at[index],
            recv_sem=self.recv.at[index],
            device_id=(seq, fsdp),
            device_id_type=MESH,
        )


def ffn_copies(n_seq, parts):
    chips = n_seq // 2
    return parts * (2 + 4 * (chips - 1)) + parts * (n_seq - 1)


def ffn_kernel(
    n_seq,
    n_fsdp,
    tokens_ref,
    mixed_ref,
    out_ref,
    gain_ref,
    gate_in,
    up_in,
    down_in,
    cot_in,
    hidden_out,
    grad_hidden_out,
    heads_ref,
    result_ref,
    gate_parts,
    up_out,
    down_out,
    out_out,
    grad_gain_ref,
    hidden_ref,
    grad_hidden_ref,
    grad_up_ref,
    grad_down_ref,
    grad_out_ref,
    grad_gate_ref,
    gate_first,
    gate_ref,
    up_ref,
    down_ref,
    cot_ref,
    second_ref,
    second_t_ref,
    active_t_ref,
    lin_gate_ref,
    lin_up_ref,
    keep_ref,
    give_ref,
    from_mate_ref,
    reduce_ref,
    from_far_ref,
    attn_ref,
    mixed_grad_ref,
    stage_ref,
    outgo_ref,
    send_sems,
    recv_sems,
    local_sems,
):
    own, model = tokens_ref.shape
    group = own * n_seq
    part = min(PB, own)
    parts = own // part
    chips = n_seq // 2
    seq, fsdp = lax.axis_index("seq"), lax.axis_index("fsdp")
    mate = seq + 1 - 2 * (seq % 2)
    units = gate_ref.shape[1]
    low = jnp.bfloat16

    loads = [
        pltpu.make_async_copy(source, target, local_sems.at[index])
        for index, (source, target) in enumerate(
            ((gate_in, gate_ref), (up_in, up_ref), (down_in, down_ref), (cot_in, cot_ref))
        )
    ]
    for load in loads:
        load.start()
    kept = []

    def keep(source, target):
        copy = pltpu.make_async_copy(source, target, local_sems.at[6 + len(kept)])
        kept.append(copy)
        copy.start()


    wire = Wire(send_sems, recv_sems)

    def far(step):
        return (seq + n_seq - 2 * step) % n_seq

    def rows(ref, shard, index):
        return ref.at[pl.ds(aligned(shard * own + index * part, part), part)]

    def local_rows(ref, index):
        return ref.at[pl.ds(index * part, part)]

    to_mate, across, passed, give_mate, give_far, reduced = {}, {}, {}, {}, {}, {}
    for index in range(parts):
        mine = rows(second_ref, seq, index)
        to_mate[index] = wire.copy(mine, mine, mate, fsdp)
        give_mate[index] = wire.copy(
            local_rows(give_ref.at[0], index), local_rows(from_mate_ref.at[0], index), mate, fsdp
        )
        for step in range(1, chips):
            across[step, index] = wire.copy(mine, mine, (seq + 2 * step) % n_seq, fsdp)
            there = rows(second_ref, far(step), index)
            passed[step, index] = wire.copy(there, there, mate, fsdp)
            give_far[step, index] = wire.copy(
                local_rows(give_ref.at[step], index),
                local_rows(from_mate_ref.at[step], index),
                mate,
                fsdp,
            )
            reduced[step, index] = wire.copy(
                local_rows(reduce_ref.at[step - 1], index),
                local_rows(from_far_ref.at[step - 1], index),
                far(step),
                fsdp,
            )

    own_rows = model // n_fsdp
    inner = n_fsdp // 4
    high_at, low_at = fsdp // inner, fsdp % inner

    def wide_copies(source, target):
        copies = []
        for hop in range(1, inner):
            lower = (low_at + hop) % inner
            for high in range(4):
                block = aligned((high * inner + lower) * own_rows, own_rows)
                copies.append(
                    wire.copy(
                        source.at[pl.ds(block, own_rows)],
                        target.at[(hop - 1) * 4 + high],
                        seq,
                        high_at * inner + lower,
                    )
                )
        return copies

    gate_copies = wide_copies(grad_gate_ref, gate_first)

    greet(n_seq, n_fsdp)

    for index in range(parts):
        at = slice(index * part, index * part + part)
        hidden = tokens_ref[at, :].astype(jnp.float32) + bdot(mixed_ref[at, :], out_ref[...])
        hidden_ref[at, :] = hidden
        inv = lax.rsqrt(jnp.mean(hidden * hidden, axis=1, keepdims=True) + EPS_NORM)
        second_ref[pl.ds(aligned(seq * own + index * part, part), part), :] = (
            hidden * inv * gain_ref[...]
        ).astype(low)
        for step in range(1, chips if index == 0 else 1):
            across[step, index].start()
        to_mate[index].start()
    keep(hidden_ref, hidden_out)
    for load in loads:
        load.wait()

    count = n_seq * parts

    def block(number, carry):
        near = number < 2 * parts
        late = number - 2 * parts
        step_at = late // (2 * parts) + 1
        rest = late % (2 * parts)
        far_at = (seq + 2 * n_seq - 2 * step_at) % n_seq
        far_mate = far_at + 1 - 2 * (far_at % 2)
        shard = jnp.where(
            near,
            jnp.where(number < parts, seq, mate),
            jnp.where(rest % 2 == 0, far_mate, far_at),
        )
        index_at = jnp.where(near, number % parts, rest // 2)
        base = aligned(shard * own + index_at * part, part)

        for index in range(1, parts):

            @pl.when(number == 2 * parts - parts + index)
            def _():
                for step in range(1, chips):
                    across[step, index - 1].wait_send()
                    across[step, index].start()

        for index in range(parts):

            @pl.when(number == parts + index)
            def _():
                to_mate[index].wait_recv()

            for step in range(1, chips):

                @pl.when(number == 2 * parts * step + 2 * index)
                def _():
                    across[step, index].wait_recv()
                    passed[step, index].start()
                    passed[step, index].wait_recv()

        second = second_ref[pl.ds(base, part), :]
        second_t_ref[:, pl.ds(base, part)] = second.T
        gate_lin = bdot(second, gate_ref[...])
        up_lin = bdot(second, up_ref[...])
        cot = cot_ref[pl.ds(base, part), :]
        grad_active = bdot(cot, down_ref[...], NT)
        gate_sig = sigmoid(gate_lin)
        silu = gate_lin * gate_sig
        active = (silu * up_lin).astype(low)
        active_t_ref[:, pl.ds(base, part)] = active.T
        grad_gate = (grad_active * up_lin * (gate_sig + silu * (1.0 - gate_sig))).astype(low)
        grad_up = (grad_active * silu).astype(low)
        lin_gate_ref[pl.ds(base, part), :] = grad_gate
        lin_up_ref[pl.ds(base, part), :] = grad_up
        grad_second = bdot(grad_gate, gate_ref[...], NT) + bdot(grad_up, up_ref[...], NT)
        stage_ref[...] = grad_second
        slot = number % 2

        def leaving(where):
            return pltpu.make_async_copy(
                outgo_ref.at[slot],
                result_ref.at[pl.ds(where, part)],
                local_sems.at[4 + slot],
            )

        @pl.when(number >= 2)
        def _():
            leaving(base).wait()

        outgo_ref[slot] = bdot(active, down_ref[...]).astype(low)
        leaving(base).start()

        for index in range(parts):
            at = slice(index * part, index * part + part)

            @pl.when(number == index)
            def _():
                keep_ref[at, :] = stage_ref[...]

            @pl.when(number == parts + index)
            def _():
                give_ref[0, at, :] = stage_ref[...].astype(low)
                give_mate[index].start()

            for step in range(1, chips):

                @pl.when(number == 2 * parts * step + 2 * index)
                def _():
                    give_ref[step, at, :] = stage_ref[...].astype(low)
                    give_far[step, index].start()

                @pl.when(number == 2 * parts * step + 2 * index + 1)
                def _():
                    give_far[step, index].wait_recv()
                    reduce_ref[step - 1, at, :] = (
                        stage_ref[...] + from_mate_ref[step, at, :].astype(jnp.float32)
                    ).astype(low)
                    reduced[step, index].start()

        return carry

    lax.fori_loop(0, count, block, 0)

    for slot in range(2):
        pltpu.make_async_copy(
            outgo_ref.at[slot], result_ref.at[pl.ds(0, part)], local_sems.at[4 + slot]
        ).wait()

    tile = 256

    def wide_tile(target, lines):
        def step(number, carry):
            base = aligned(number * tile, tile)
            target[pl.ds(base, tile), :] = bdot(
                second_t_ref[pl.ds(base, tile), :], lines[...]
            ).astype(low)
            return carry

        lax.fori_loop(0, model // tile, step, 0)

    wide_tile(grad_gate_ref, lin_gate_ref)
    for copy in gate_copies:
        copy.start()
    wide_tile(grad_up_ref, lin_up_ref)
    keep(grad_up_ref, up_out)

    grad_gain_ref[...] = jnp.zeros(grad_gain_ref.shape, jnp.float32)
    width = model // n_seq
    handed = []
    for index in range(parts):
        at = slice(index * part, index * part + part)
        give_mate[index].wait_recv()
        total = keep_ref[at, :] + from_mate_ref[0, at, :].astype(jnp.float32)
        for step in range(1, chips):
            reduced[step, index].wait_recv()
            total = total + from_far_ref[step - 1, at, :].astype(jnp.float32)
        hidden = hidden_ref[at, :]
        inv = lax.rsqrt(jnp.mean(hidden * hidden, axis=1, keepdims=True) + EPS_NORM)
        unit = hidden * inv
        grad_gain_ref[...] += jnp.sum(total * unit, axis=0, keepdims=True)
        grad_unit = total * gain_ref[...]
        grad_hidden = inv * (
            grad_unit - unit * jnp.mean(grad_unit * unit, axis=1, keepdims=True)
        ) + cot_ref[pl.ds(aligned(seq * own + index * part, part), part), :].astype(jnp.float32)
        grad_hidden_ref[at, :] = grad_hidden
        attn = grad_hidden.astype(low)
        attn_ref[at, :] = attn
        mixed_grad_ref[at, :] = bdot(attn, out_ref[...], NT).astype(low)
        for shift in range(1, n_seq):
            target = (seq + shift) % n_seq
            copy = wire.copy(
                mixed_grad_ref.at[at, pl.ds(aligned(target * width, width), width)],
                rows(heads_ref, seq, index),
                target,
                fsdp,
            )
            copy.start()
            handed.append(copy)
        heads_ref[pl.ds(aligned(seq * own + index * part, part), part), :] = mixed_grad_ref[
            at, pl.ds(aligned(seq * width, width), width)
        ]

    keep(grad_hidden_ref, grad_hidden_out)

    def down_tile(number, carry):
        base = aligned(number * tile, tile)
        grad_down_ref[:, pl.ds(base, tile)] = bdot(
            active_t_ref[...], cot_ref[:, pl.ds(base, tile)]
        ).astype(low)
        return carry

    lax.fori_loop(0, model // tile, down_tile, 0)
    keep(grad_down_ref, down_out)

    for base in range(0, model, tile):
        grad_out_ref[base : base + tile, :] = bdot(
            mixed_ref[:, base : base + tile], attn_ref[...], TN
        ).astype(low)
    keep(grad_out_ref, out_out)

    for index in range(parts):
        to_mate[index].wait_send()
        give_mate[index].wait_send()
        for step in range(1, chips):
            if index == parts - 1:
                across[step, index].wait_send()
            passed[step, index].wait_send()
            give_far[step, index].wait_send()
            reduced[step, index].wait_send()
    for copy in handed:
        copy.wait()
    for copy in gate_copies:
        copy.wait_recv()
    for high in range(4):
        block = aligned((high * inner + low_at) * own_rows, own_rows)
        total = grad_gate_ref[pl.ds(block, own_rows), :].astype(jnp.float32)
        for hop in range(1, inner):
            total = total + gate_first[(hop - 1) * 4 + high].astype(jnp.float32)
        gate_parts[high] = total.astype(low)
    for copy in gate_copies:
        copy.wait_send()
    for copy in kept:
        copy.wait()


def ffn_block(n_seq, n_fsdp, tokens, mixed, out, gain, gate, up, down, cot):
    own, model = tokens.shape
    group = own * n_seq
    units = gate.shape[1]
    chips = n_seq // 2
    low, full = jnp.bfloat16, jnp.float32
    part = min(PB, own)
    near = 4 * (n_fsdp // 4 - 1)
    own_rows = model // n_fsdp
    copies = ffn_copies(n_seq, own // part) + near

    def shape(dims, kind=low):
        return jax.ShapeDtypeStruct(dims, kind)

    return pl.pallas_call(
        functools.partial(ffn_kernel, n_seq, n_fsdp),
        out_shape=(
            shape((own, model), full),
            shape((own, model), full),
            shape((group, model // n_seq)),
            shape((group, model)),
            shape((4, own_rows, units)),
            shape((model, units)),
            shape((units, model)),
            shape((model, model)),
            shape((1, model), full),
        ),
        in_specs=[spec()] * 4 + [spec(ANY)] * 4,
        out_specs=(spec(ANY),) * 2 + (spec(), spec(ANY), spec()) + (spec(ANY),) * 3 + (spec(),),
        scratch_shapes=[
            pltpu.VMEM((own, model), full),
            pltpu.VMEM((own, model), full),
            pltpu.VMEM((model, units), low),
            pltpu.VMEM((units, model), low),
            pltpu.VMEM((model, model), low),
            pltpu.VMEM((model, units), low),
            pltpu.VMEM((near, own_rows, units), low),
            pltpu.VMEM((model, units), low),
            pltpu.VMEM((model, units), low),
            pltpu.VMEM((units, model), low),
            pltpu.VMEM((group, model), low),
            pltpu.VMEM((group, model), low),
            pltpu.VMEM((model, group), low),
            pltpu.VMEM((units, group), low),
            pltpu.VMEM((group, units), low),
            pltpu.VMEM((group, units), low),
            pltpu.VMEM((own, model), full),
            pltpu.VMEM((chips, own, model), low),
            pltpu.VMEM((chips, own, model), low),
            pltpu.VMEM((chips - 1, own, model), low),
            pltpu.VMEM((chips - 1, own, model), low),
            pltpu.VMEM((own, model), low),
            pltpu.VMEM((own, model), low),
            pltpu.VMEM((part, model), full),
            pltpu.VMEM((2, part, model), low),
            pltpu.SemaphoreType.DMA((copies,)),
            pltpu.SemaphoreType.DMA((copies,)),
            pltpu.SemaphoreType.DMA((11,)),
        ],
        compiler_params=pltpu.CompilerParams(
            vmem_limit_bytes=63 << 20, collective_id=2, has_side_effects=True
        ),
        name="ffn",
    )(tokens, mixed, out, gain, gate, up, down, cot)


class Scatter:
    outer = 4

    @classmethod
    def copies(cls, n_fsdp):
        return cls.outer * (n_fsdp // cls.outer - 1) + cls.outer - 1

    def __init__(self, n_fsdp, wire, block, parts, mine, first, second):
        self.inner = n_fsdp // self.outer
        me = lax.axis_index("fsdp")
        seq = lax.axis_index("seq")
        self.high, self.low = me // self.inner, me % self.inner
        self.parts, self.mine, self.first, self.second = parts, mine, first, second
        self.near, self.away = [], []
        for hop in range(1, self.inner if first is not None else 1):
            lower = (self.low + hop) % self.inner
            for high in range(self.outer):
                self.near.append(
                    wire.copy(
                        block(high * self.inner + lower),
                        first.at[(hop - 1) * self.outer + high],
                        seq,
                        self.high * self.inner + lower,
                    )
                )
        for step in range(1, self.outer):
            higher = (self.high + step) % self.outer
            self.away.append(
                wire.copy(parts(higher), second.at[step - 1], seq, higher * self.inner + self.low)
            )

    def start(self):
        for copy in self.near:
            copy.start()

    def combine(self):
        for copy in self.near:
            copy.wait_recv()
        for high in range(self.outer):
            block = self.parts(high)
            total = block[...].astype(jnp.float32)
            for hop in range(1, self.inner):
                total = total + self.first[(hop - 1) * self.outer + high].astype(jnp.float32)
            block[...] = total.astype(jnp.bfloat16)

    def leave(self):
        for copy in self.away:
            copy.start()

    def total(self):
        for copy in self.away:
            copy.wait_recv()
        total = self.mine()[...].astype(jnp.float32)
        for step in range(1, self.outer):
            total = total + self.second[step - 1].astype(jnp.float32)
        return total.astype(jnp.bfloat16)

    def drain(self):
        for copy in self.near + self.away:
            copy.wait_send()


CHUNK = 64


class SeqSum:
    @staticmethod
    def copies(n_seq, parts):
        return (n_seq - 1) * parts

    def __init__(self, n_seq, wire, give, mine, from_mate, from_far, parts=1):
        self.chips = n_seq // 2
        self.size = from_mate.shape[1] // parts
        seq, fsdp = lax.axis_index("seq"), lax.axis_index("fsdp")
        mate = seq + 1 - 2 * (seq % 2)
        self.mine, self.from_mate, self.from_far = mine, from_mate, from_far
        self.gives, self.across = {}, {}
        for part in range(parts):
            rows = pl.ds(part * self.size, self.size)
            for step in range(self.chips):
                self.gives[step, part] = wire.copy(
                    give(step).at[rows], from_mate.at[step, rows], mate, fsdp
                )
            for step in range(1, self.chips):
                self.across[step, part] = wire.copy(
                    mine(step).at[rows],
                    from_far.at[step - 1, rows],
                    (seq + n_seq - 2 * step) % n_seq,
                    fsdp,
                )

    def reduce(self, step, part=0):
        self.gives[step, part].wait_recv()
        mine = self.mine(step)

        def add(number, carry):
            at = pl.ds(aligned(part * self.size + number * CHUNK, CHUNK), CHUNK)
            mine[at, :] = (
                mine[at, :].astype(jnp.float32) + self.from_mate[step, at, :].astype(jnp.float32)
            ).astype(jnp.bfloat16)
            return carry

        lax.fori_loop(0, self.size // CHUNK, add, 0)
        self.across[step, part].start()

    def arrive(self, part=0):
        self.gives[0, part].wait_recv()
        for step in range(1, self.chips):
            self.across[step, part].wait_recv()

    def total(self, at):
        total = self.mine(0)[at, :].astype(jnp.float32) + self.from_mate[0, at, :].astype(
            jnp.float32
        )
        for step in range(1, self.chips):
            total = total + self.from_far[step - 1, at, :].astype(jnp.float32)
        return total

    def drain(self):
        for copy in [*self.gives.values(), *self.across.values()]:
            copy.wait_send()


class Direct:
    def __init__(self, size, axis, wire, source, slots):
        seq, fsdp = lax.axis_index("seq"), lax.axis_index("fsdp")
        self.me, self.source, self.slots = lax.axis_index(axis), source, slots
        self.sent = [
            wire.copy(
                source,
                slots.at[self.me],
                (seq + step) % size if axis == "seq" else seq,
                (fsdp + step) % size if axis == "fsdp" else fsdp,
            )
            for step in range(1, size)
        ]

    def start(self):
        for copy in self.sent:
            copy.start()
        self.slots[self.me] = self.source[...]

    def total(self):
        for copy in self.sent:
            copy.wait()
        total = self.slots[0]
        for index in range(1, self.slots.shape[0]):
            total = total + self.slots[index]
        return total


def spread_units(target, pieces, n_seq, slab):
    units, hidden = pieces.shape[2], target.shape[1]
    whole = slab * n_seq
    for base in range(0, hidden, BT):
        total = None
        for owner in range(n_seq):
            first, last = base // whole, (base + BT - 1) // whole
            low = first * slab // BT * BT
            high = min(-(-((last + 1) * slab) // BT) * BT, units)
            col = iota((high - low, BT), 1) + base
            origin = col - first * whole - owner * slab
            inside = (origin >= 0) & (origin < slab)
            origin = origin + first * slab
            for shard in range(first + 1, last + 1):
                there = col - shard * whole - owner * slab
                ours = (there >= 0) & (there < slab)
                origin = jnp.where(ours, there + shard * slab, origin)
                inside = inside | ours
            hot = jnp.where((iota((high - low, BT), 0) + low == origin) & inside, 1.0, 0.0)
            part = bdot(pieces[owner, :, low:high], hot)
            total = part if total is None else total + part
        target[:, base : base + BT] = total.astype(jnp.bfloat16)


SMALL_ROWS = 24


def mixer_backward_kernel(
    heads,
    n_seq,
    n_fsdp,
    lengths_ref,
    row_ref,
    grad_ref,
    taps_in,
    gain_ref,
    norm_gain_ref,
    ffn_gain_ref,
    delta_in,
    inverse_in,
    big_in,
    update_in,
    state_in,
    packed_in,
    normed_in,
    weight_in,
    tokens_in,
    hidden_in,
    grad_hidden_in,
    result_in,
    gate_in,
    up_in,
    down_in,
    out_in,
    result_out,
    tokens_out,
    gate_out,
    up_out,
    down_out,
    out_out,
    query_out,
    key_out,
    value_out,
    beta_out,
    small_out,
    norm_out,
    retain_ref,
    taps_ref,
    column_ref,
    delta_ref,
    inverse_ref,
    big_ref,
    update_ref,
    state_ref,
    packed_ref,
    grad_delta_ref,
    add_ref,
    after_ref,
    conv_ref,
    grad_proj_ref,
    arrived_ref,
    weight_ref,
    weight_grad_ref,
    wide_ref,
    tokens_ref,
    result_ref,
    result_mine,
    result_mate,
    result_far,
    normed_mine,
    normed_give,
    normed_mate,
    normed_far,
    gate_own,
    gate_second,
    up_own,
    up_first,
    up_second,
    down_own,
    down_first,
    down_second,
    out_sum,
    out_mate,
    out_first,
    out_second,
    out_far,
    query_first,
    query_second,
    key_first,
    key_second,
    value_first,
    value_second,
    beta_first,
    beta_second,
    gate_total,
    up_total,
    down_total,
    out_total,
    mixer_total,
    gate_all,
    up_all,
    spread_ref,
    taps_grad_ref,
    small_ref,
    small_all,
    small_seq,
    small_sum,
    norm_ref,
    norm_half,
    norm_all,
    norm_seq,
    send_sems,
    recv_sems,
    gather_send,
    gather_recv,
    share_send,
    share_recv,
    local_sems,
):
    tokens = grad_ref.shape[0]
    blocks = tokens // BT
    head_width = heads * DK
    width = 3 * head_width
    own = tokens // n_seq
    model = tokens_ref.shape[1]
    own_rows, units = gate_own.shape
    slab = down_own.shape[1]
    seq, fsdp = lax.axis_index("seq"), lax.axis_index("fsdp")
    mate = seq + 1 - 2 * (seq % 2)
    core = seq % 2
    chip = seq // 2
    chips = n_seq // 2
    inner = n_fsdp // Scatter.outer
    inner_high, inner_low = fsdp // inner, fsdp % inner
    low, full = jnp.bfloat16, jnp.float32

    local = {}

    def bring(name, source, target):
        copy = pltpu.make_async_copy(source, target, local_sems.at[len(local)])
        local[name] = copy
        copy.start()

    def far(step):
        return (seq + n_seq - 2 * step) % n_seq

    def far_mate(step):
        there = far(step)
        return there + 1 - 2 * (there % 2)

    def shard(ref, index):
        return ref.at[pl.ds(aligned(index * own, own), own)]

    for name, source, target in (
        ("delta", delta_in, delta_ref),
        ("big", big_in, big_ref),
        ("packed", packed_in, packed_ref.at[:, pl.ds(0, packed_in.shape[1])]),
        ("inverse", inverse_in, inverse_ref),
        ("update", update_in, update_ref),
        ("state", state_in, state_ref),
    ):
        bring(name, source, target)
    greet_signal(n_seq, n_fsdp)
    wire = Wire(send_sems, recv_sems)
    result_sum = SeqSum(
        n_seq,
        wire,
        lambda step: shard(result_in, mate if step == 0 else far_mate(step)),
        lambda step: result_mine.at[step],
        result_mate,
        result_far,
    )
    normed_sum = SeqSum(
        n_seq,
        wire,
        lambda step: normed_give.at[step],
        lambda step: normed_mine.at[step],
        normed_mate,
        normed_far,
        own // min(PB, own),
    )
    half = out_sum.shape[1]
    out_rows = out_sum.shape[0] // n_fsdp
    half_at = pl.ds(aligned(core * half, half), half)
    out_give = wire.copy(
        out_in.at[:, pl.ds(aligned((1 - core) * half, half), half)], out_mate, mate, fsdp
    )

    def rows_of(ref, size):
        return lambda owner: ref.at[pl.ds(aligned(owner * size, size), size)]

    def scatter(block, first, second):
        def parts(high):
            return block(high * inner + inner_low)

        return Scatter(n_fsdp, wire, block, parts, lambda: parts(inner_high), first, second)

    gate_sum = Scatter(
        n_fsdp, wire, None, lambda high: gate_in.at[high], lambda: gate_own, None, gate_second
    )
    up_sum = Scatter(
        n_fsdp,
        wire,
        rows_of(up_in, own_rows),
        lambda high: up_own.at[high],
        lambda: up_own.at[inner_high],
        up_first,
        up_second,
    )
    down_sum = Scatter(
        n_fsdp,
        wire,
        lambda owner: down_in.at[owner],
        lambda high: down_own.at[high],
        lambda: down_own.at[inner_high],
        down_first,
        down_second,
    )
    out_scatter = scatter(rows_of(out_sum, out_rows), out_first, out_second)
    spans = [(kind * head_width, head_width) for kind in range(3)] + [(width, DK)]

    def mixer_block(span):
        return lambda owner: weight_grad_ref.at[
            pl.ds(aligned(owner * own_rows, own_rows), own_rows), pl.ds(span[0], span[1])
        ]

    mixer_sums = [
        scatter(mixer_block(span), first, second)
        for span, first, second in zip(
            spans,
            (query_first, key_first, value_first, beta_first),
            (query_second, key_second, value_second, beta_second),
        )
    ]
    out_across = [
        wire.copy(out_far.at[chip], out_far.at[chip], (seq + 2 * step) % n_seq, fsdp)
        for step in range(1, chips)
    ]
    out_swap = wire.copy(out_total, out_out.at[:, half_at], mate, fsdp)

    share_sems = (share_send, share_recv)
    gather_sems = (gather_send, gather_recv)
    per_share, per_gather = Share.copies(n_seq), Gather.copies(n_fsdp)

    def share(index, source, slot):
        return Share(
            n_seq, source, slot, share_sems, index * per_share, local_sems.at[50 + index]
        )

    def stacked(ref):
        return lambda owner: ref.at[owner]

    def head_columns(ref):
        return lambda owner: ref.at[:, pl.ds(aligned(owner * head_width, head_width), head_width)]

    gate_share = share(0, gate_total, stacked(gate_all))
    up_share = share(1, up_total, stacked(up_all))
    down_share = share(2, down_total, stacked(down_out))
    mixer_shares = [
        share(3 + index, mixer_total.at[:, pl.ds(span[0], span[1])], slot)
        for index, (span, slot) in enumerate(
            zip(
                spans,
                (
                    head_columns(query_out),
                    head_columns(key_out),
                    head_columns(value_out),
                    stacked(beta_out),
                ),
            )
        )
    ]
    small_spread = Direct(n_seq, "seq", wire, small_ref, small_seq)
    norm_first = Direct(n_fsdp, "fsdp", wire, norm_ref, norm_all)
    norm_spread = Direct(n_seq, "seq", wire, norm_half, norm_seq)
    small_gather = Gather(
        n_fsdp, small_ref, stacked(small_all), gather_sems, 0, local_sems.at[59]
    )
    for high in range(Scatter.outer):
        owner = high * inner + inner_low
        bring(("up", high), rows_of(up_in, own_rows)(owner), up_own.at[high])
        bring(("down", high), down_in.at[owner], down_own.at[high])
    bring("out", out_in.at[:, half_at], out_sum)
    bring("gate", gate_in.at[inner_high], gate_own)
    for step in range(1, chips):
        bring(("result", step), shard(result_in, far(step)), result_mine.at[step])
    bring("result", shard(result_in, seq), result_mine.at[0])
    bring("hidden", hidden_in, wide_ref)
    bring("weight", weight_in, weight_ref)
    bring("tokens", tokens_in, tokens_ref)
    fill_flags(retain_ref, lengths_ref)
    fill_taps(taps_ref, taps_in, seq, head_width)
    fill_column(column_ref, row_ref)
    small_ref[...] = jnp.zeros(small_ref.shape, full)
    taps_grad_ref[...] = jnp.zeros(taps_grad_ref.shape, full)
    greet_wait(n_seq, n_fsdp)
    gate_sum.leave()
    up_sum.start()
    for copy in result_sum.gives.values():
        copy.start()
    out_give.start()
    local["delta"].wait()
    local["big"].wait()

    def head_norm(step, total):
        base = pl.multiple_of(step * PB, PB)
        picked = permute_rows(column_ref[pl.ds(base, PB), :], grad_ref[...], tokens)
        for head in range(heads):
            at = slice(head * DK, head * DK + DK)
            grad = picked[:, at]
            delta = delta_ref[pl.ds(base, PB), at]
            inv = lax.rsqrt(jnp.mean(delta * delta, axis=1, keepdims=True) + EPS_NORM)
            unit = delta * inv
            total = total + jnp.sum(grad * unit, axis=0, keepdims=True)
            grad_unit = grad * gain_ref[...]
            shrunk = (
                inv * (grad_unit - unit * jnp.mean(grad_unit * unit, axis=1, keepdims=True))
            ).astype(low)
            grad_delta_ref[pl.ds(base, PB), at] = shrunk
            for sub in range(PB // BT):
                place = head * blocks + step * (PB // BT) + sub
                add_ref[place] = bdot(
                    big_ref[place, BT : 2 * BT, :], shrunk[sub * BT : sub * BT + BT], TN
                ).astype(low)
        return total

    gain_row = 3 * CONV
    small_ref[gain_row : gain_row + 1, 0:DK] = lax.fori_loop(
        0, tokens // PB, head_norm, jnp.zeros((1, DK), full)
    )
    for index in range(model // head_width):
        small_ref[gain_row + 1 + index : gain_row + 2 + index, :] = ffn_gain_ref[
            :, index * head_width : (index + 1) * head_width
        ]
    for step in range(1, chips):
        local["result", step].wait()
        result_sum.reduce(step)

    def retreat(step, grads):
        block = blocks - 1 - step
        through = retain_ref[2 * block] * retain_ref[2 * block + 1]
        lows = [grad.astype(low) for grad in grads]
        following = []
        for head in range(heads):
            place = head * blocks + block
            after_ref[place] = lows[head]
            following.append(
                grads[head] * through
                - bdot(big_ref[place, 0:BT, :], lows[head], TN)
                + add_ref[place].astype(full)
            )
        return tuple(following)

    zero = jnp.zeros((DK, DK), full)
    lax.fori_loop(0, blocks, retreat, (zero,) * heads)
    for name in ("packed", "inverse", "update", "state"):
        local[name].wait()

    conv_ref[BT : BT + HALO, :] = jnp.zeros((HALO, width), full)

    def first_stage():
        for high in range(Scatter.outer):
            local["up", high].wait()
        up_sum.combine()
        up_sum.leave()
        down_sum.start()
        local["gate"].wait()
        gate_total[...] = gate_sum.total()
        gate_share.start()

    def add_out():
        local["out"].wait()
        out_give.wait_recv()

        def add(number, carry):
            at = pl.ds(aligned(number * CHUNK, CHUNK), CHUNK)
            out_sum[at, :] = (out_sum[at, :].astype(full) + out_mate[at, :].astype(full)).astype(
                low
            )
            return carry

        lax.fori_loop(0, out_sum.shape[0] // CHUNK, add, 0)

    def second_stage():
        for high in range(Scatter.outer):
            local["down", high].wait()
        down_sum.combine()
        down_sum.leave()
        out_scatter.start()
        up_total[...] = up_sum.total()
        up_share.start()
        gate_share.relay()

    def result_stage():
        local["hidden"].wait()
        local["result"].wait()
        result_sum.arrive()

        def add(number, carry):
            at = pl.ds(aligned(number * CHUNK, CHUNK), CHUNK)
            result_ref[at, :] = (wide_ref[at, :] + result_sum.total(at)).astype(low)
            return carry

        lax.fori_loop(0, own // CHUNK, add, 0)

    def gradients(step, carry):
        for moment, stage in (
            (3, first_stage),
            (6, add_out),
            (10, second_stage),
            (13, result_stage),
        ):

            @pl.when(step == moment)
            def _():
                stage()

        block = blocks - 1 - step
        first, second, third = (
            retain_ref[2 * block],
            retain_ref[2 * block + 1],
            retain_ref[2 * block + 2],
        )
        base = pl.multiple_of(block * BT, BT)
        masks = tap_masks(first, second, third, BT + HALO)
        near_masks = [None] + [mask[:BT] for mask in masks[1:]]
        seen, kept = block_flags(first, second)
        rows, cols, cross = pair_mask(second)
        turned = jnp.where((rows < CH) & (cols >= CH), second, 1.0)
        lanes = iota((BT, BT), 1)
        strengths = sigmoid(
            packed_ref[pl.ds(HALO + base, BT), width : width + BT].astype(jnp.float32)
        )
        grad_strengths = jnp.zeros((BT, BT), jnp.float32)
        for head in range(heads):
            place = head * blocks + block
            convs, gates, acts = [], [], []
            for kind in range(3):
                at = (kind * heads + head) * DK
                window = packed_ref[pl.ds(base, HALO + BT), at : at + DK].astype(jnp.float32)
                taps = [
                    taps_ref[kind * CONV + back : kind * CONV + back + 1, head * DK : head * DK + DK]
                    for back in range(CONV)
                ]
                conv = conv_of(window, taps, near_masks)
                gate = sigmoid(conv)
                convs.append(conv)
                gates.append(gate)
                acts.append(conv * gate)
            inv_q = lax.rsqrt(jnp.sum(acts[0] * acts[0], axis=1, keepdims=True) + EPS_NORM)
            inv_k = lax.rsqrt(jnp.sum(acts[1] * acts[1], axis=1, keepdims=True) + EPS_NORM)
            query_low = (acts[0] * inv_q * DK ** (-0.5)).astype(jnp.bfloat16)
            key_low = (acts[1] * inv_k).astype(jnp.bfloat16)
            key = key_low.astype(jnp.float32)
            value = acts[2]
            beta = strengths[:, head : head + 1]
            grad_low = grad_delta_ref[pl.ds(base, BT), head * DK : head * DK + DK]
            after = after_ref[place]
            state = state_ref[place]
            update = update_ref[place]
            inner = bdot(key_low, jnp.concatenate([key_low, query_low], axis=0), NT)
            scores_t = jnp.where(rows <= cols, inner[:, BT:] * turned, 0.0)
            grad_update = bdot(scores_t, grad_low) + bdot(key * kept, after)
            solved = bdot(inverse_ref[place], grad_update, TN)
            solved_beta = solved * beta
            both = jnp.concatenate([grad_low, solved.astype(jnp.bfloat16)], axis=0)
            on_state = bdot(both, state, NT)
            on_update = bdot(both, update, NT)
            grad_scores = jnp.where(rows >= cols, on_update[:BT] * cross, 0.0)
            grad_strict = jnp.where(rows > cols, on_update[BT:] * cross, 0.0)
            grad_weighted = on_state[BT:] * seen
            turned_both = bdot(
                update,
                jnp.concatenate(
                    [grad_low, solved_beta.astype(jnp.bfloat16)], axis=0
                ),
                NT,
            )
            grad_scores_t = jnp.where(rows <= cols, turned_both[:, :BT] * turned, 0.0)
            strict_t = jnp.where(rows < cols, turned_both[:, BT:] * turned, 0.0)
            grad_query = on_state[:BT] * seen + bdot(grad_scores, key_low)
            grad_key = (
                bdot(grad_scores_t, query_low)
                + bdot(update, after, NT) * kept
                - beta * grad_weighted
                - bdot(grad_strict * beta + strict_t, key_low)
            )
            grad_value = solved_beta
            grad_beta = jnp.sum(
                solved * value - grad_strict * inner[:, :BT] - grad_weighted * key,
                axis=1,
                keepdims=True,
            )
            grad_strengths = jnp.where(lanes == head, grad_beta, grad_strengths)
            scaled = (
                inv_q
                * DK ** (-0.5)
                * (
                    grad_query
                    - acts[0]
                    * (inv_q * inv_q)
                    * jnp.sum(grad_query * acts[0], axis=1, keepdims=True)
                ),
                inv_k
                * (
                    grad_key
                    - acts[1] * (inv_k * inv_k) * jnp.sum(grad_key * acts[1], axis=1, keepdims=True)
                ),
                grad_value,
            )
            for kind in range(3):
                at = (kind * heads + head) * DK
                conv_ref[0:BT, at : at + DK] = (
                    scaled[kind] * gates[kind] * (1.0 + convs[kind] * (1.0 - gates[kind]))
                )
        grad_proj_ref[pl.ds(base, BT), width : width + BT] = (
            grad_strengths * strengths * (1.0 - strengths)
        ).astype(jnp.bfloat16)
        for kind in range(3):
            for head in range(heads):
                at = (kind * heads + head) * DK
                span = slice(head * DK, head * DK + DK)
                grads = conv_ref[:, at : at + DK]
                window = packed_ref[pl.ds(base, HALO + BT), at : at + DK].astype(jnp.float32)
                total = None
                for back in range(CONV):
                    row = kind * CONV + back
                    tap = taps_ref[row : row + 1, span]
                    masked = grads if back == 0 else grads * masks[back]
                    shifted = (
                        masked if back == 0 else pltpu.roll(masked, BT + HALO - back, 0)
                    )[:BT]
                    total = shifted * tap if total is None else total + shifted * tap
                    past = (window if back == 0 else pltpu.roll(window, back, 0))[HALO:]
                    taps_grad_ref[row : row + 1, span] += jnp.sum(
                        masked[:BT] * past, axis=0, keepdims=True
                    )
                grad_proj_ref[pl.ds(base, BT), at : at + DK] = total.astype(jnp.bfloat16)
        conv_ref[BT : BT + HALO, :] = conv_ref[0:HALO, :]
        return carry

    lax.fori_loop(0, blocks, gradients, 0)

    bring("keep_result", result_ref, result_out)
    bring("normed", normed_in, packed_ref.at[pl.ds(0, tokens)])
    bring("grad_hidden", grad_hidden_in, wide_ref)
    small_ref[0:gain_row, :] = taps_grad_ref[0:gain_row, :]
    small_gather.start()
    out_scatter.combine()
    out_scatter.leave()
    part = min(PB, own)

    def push_back(index, target, number):
        base = aligned(index * own + number * part, part)
        hot = jnp.where(row_ref[...] == iota((part, tokens), 0) + base, 1.0, 0.0).astype(low)
        arrived_ref[...] = lax.dot_general(
            hot, grad_proj_ref[...], NN, preferred_element_type=jnp.float32
        ).astype(low)
        target[number * part : (number + 1) * part, :] = bdot(
            arrived_ref[...], weight_ref[...], NT
        ).astype(low)

    local["weight"].wait()
    parts = own // part

    def push_far(number):
        for step in range(1, chips):
            push_back(far_mate(step), normed_give.at[step], number)
            normed_sum.gives[step, number].start()
            push_back(far(step), normed_mine.at[step], number)
            normed_sum.reduce(step, number)

    push_far(0)
    local["normed"].wait()

    def weight_grad(span):
        def step(number, carry):
            at = pl.ds(aligned(number * PB, PB), PB)
            weight_grad_ref[at, pl.ds(span[0], span[1])] = bdot(
                packed_ref[0:tokens, at], grad_proj_ref[:, pl.ds(span[0], span[1])], TN
            ).astype(low)
            return carry

        lax.fori_loop(0, model // PB, step, 0)

    weight_grad(spans[0])
    mixer_sums[0].start()
    for number in range(1, parts):
        push_far(number)
    weight_grad(spans[1])
    mixer_sums[0].combine()
    mixer_sums[0].leave()
    mixer_sums[1].start()
    down_total[...] = down_sum.total()
    down_share.start()
    up_share.relay()
    small_gather.relay()
    weight_grad(spans[2])
    weight_grad(spans[3])
    push_back(mate, normed_give.at[0], 0)
    normed_sum.gives[0, 0].start()
    mixer_sums[1].combine()
    mixer_sums[1].leave()
    mixer_sums[2].start()
    for number in range(1, parts):
        push_back(mate, normed_give.at[0], number)
        normed_sum.gives[0, number].start()
    push_back(seq, normed_mine.at[0], 0)
    mixer_sums[2].combine()
    mixer_sums[2].leave()
    mixer_sums[3].start()
    for number in range(1, parts):
        push_back(seq, normed_mine.at[0], number)
    out_far[chip] = out_scatter.total()
    for copy in out_across:
        copy.start()
    small_gather.finish()
    total = small_all[0]
    for owner in range(1, n_fsdp):
        total = total + small_all[owner]
    small_ref[...] = total
    small_spread.start()
    mixer_sums[3].combine()
    mixer_sums[3].leave()
    mixer_total[:, spans[0][0] : spans[0][0] + spans[0][1]] = mixer_sums[0].total()
    mixer_shares[0].start()
    gate_share.finish()
    spread_units(spread_ref.at[0], gate_all, n_seq, slab)
    bring("keep_gate", spread_ref.at[0], gate_out)
    mixer_total[:, spans[1][0] : spans[1][0] + spans[1][1]] = mixer_sums[1].total()
    mixer_shares[1].start()
    mixer_total[:, spans[2][0] : spans[2][0] + spans[2][1]] = mixer_sums[2].total()
    mixer_shares[2].start()
    down_share.relay()
    local["grad_hidden"].wait()
    local["tokens"].wait()

    def norm_back(number, total):
        at = pl.ds(aligned(number * CHUNK, CHUNK), CHUNK)
        values = tokens_ref[at, :].astype(full)
        inv = lax.rsqrt(jnp.mean(values * values, axis=1, keepdims=True) + EPS_NORM)
        unit = values * inv
        grad = normed_sum.total(at)
        grad_unit = grad * norm_gain_ref[...]
        wide_ref[at, :] += inv * (
            grad_unit - unit * jnp.mean(grad_unit * unit, axis=1, keepdims=True)
        )
        return total + jnp.sum(grad * unit, axis=0, keepdims=True)

    total = jnp.zeros((1, model), full)
    for number in range(parts):
        normed_sum.arrive(number)
        total = lax.fori_loop(
            number * part // CHUNK, (number + 1) * part // CHUNK, norm_back, total
        )
    for index in range(model // DK):
        norm_ref[index : index + 1, :] = total[:, index * DK : (index + 1) * DK]
    norm_first.start()
    bring("keep_tokens", wide_ref, tokens_out)
    mixer_total[:, spans[3][0] : spans[3][0] + spans[3][1]] = mixer_sums[3].total()
    mixer_shares[3].start()
    norm_half[...] = norm_first.total()
    norm_spread.start()
    total = small_spread.total()
    for owner in range(n_seq):
        small_sum[0:gain_row, owner * head_width : (owner + 1) * head_width] = small_seq[
            owner, 0:gain_row, :
        ]
    small_sum[gain_row : gain_row + 2, :] = jnp.zeros((2, model), full)
    small_sum[gain_row : gain_row + 1, 0:DK] = total[gain_row : gain_row + 1, 0:DK]
    for index in range(model // head_width):
        small_sum[
            gain_row + 1 : gain_row + 2, index * head_width : (index + 1) * head_width
        ] = total[gain_row + 1 + index : gain_row + 2 + index, :]
    bring("keep_small", small_sum, small_out)
    for copy in out_across:
        copy.wait_recv()
    total = out_far[0].astype(full)
    for index in range(1, chips):
        total = total + out_far[index].astype(full)
    out_total[...] = total.astype(low)
    out_swap.start()
    bring("keep_out", out_total, out_out.at[:, half_at])
    for each in mixer_shares:
        each.relay()
    up_share.finish()
    spread_units(spread_ref.at[1], up_all, n_seq, slab)
    bring("keep_up", spread_ref.at[1], up_out)
    norm_ref[...] = norm_spread.total()
    bring("keep_norm", norm_ref, norm_out)
    for each in [down_share] + mixer_shares:
        each.finish()
    for each in [gate_sum, up_sum, down_sum, out_scatter] + mixer_sums + [result_sum, normed_sum]:
        each.drain()
    for copy in out_across:
        copy.wait_send()
    out_give.wait_send()
    out_swap.wait()
    for name, copy in local.items():
        if str(name).startswith("keep_"):
            copy.wait()


def mixer_backward(n_seq, n_fsdp, small, saved, big):
    (lengths, row, grad_heads, taps, gain, norm_gain, ffn_gain) = small
    packed, delta, inverse, parts, update, state = saved
    normed, weight, own_tokens, hidden, grad_hidden, result, gate, up, down, out = big
    tokens = grad_heads.shape[0]
    width = packed.shape[1]
    head_width = grad_heads.shape[1]
    heads = head_width // DK
    count = heads * (tokens // BT)
    own, model = own_tokens.shape
    _, own_rows, units = gate.shape
    slab = down.shape[1]
    hidden_units = slab * n_fsdp * n_seq
    out_rows = out.shape[0] // n_fsdp
    half = out.shape[1] // 2
    chips = n_seq // 2
    outer = Scatter.outer
    near = outer * (n_fsdp // outer - 1)
    low, full = jnp.bfloat16, jnp.float32
    copies = (
        8 * Scatter.copies(n_fsdp)
        + SeqSum.copies(n_seq, 1 + own // min(PB, own))
        + 1
        + chips
        + 2 * (n_seq - 1)
        + n_fsdp
    )
    shares, gathers = 7 * Share.copies(n_seq), Gather.copies(n_fsdp)

    def shape(dims, kind=low):
        return jax.ShapeDtypeStruct(dims, kind)

    def held(*dims, kind=low):
        return pltpu.VMEM(dims, kind)

    def sum_buffers(rows, cols):
        return [held(near, rows, cols), held(outer - 1, rows, cols)]

    return pl.pallas_call(
        functools.partial(mixer_backward_kernel, heads, n_seq, n_fsdp),
        out_shape=(
            shape((own, model)),
            shape((own, model), full),
            shape((own_rows, hidden_units)),
            shape((own_rows, hidden_units)),
            shape((n_seq, slab, model)),
            shape((out_rows, 2 * half)),
            shape((own_rows, n_seq * head_width)),
            shape((own_rows, n_seq * head_width)),
            shape((own_rows, n_seq * head_width)),
            shape((n_seq, own_rows, DK)),
            shape((16, model), full),
            shape((model // DK, DK), full),
        ),
        in_specs=[spec(SMEM)] + [spec()] * 6 + [spec(ANY)] * 16,
        out_specs=(spec(ANY),) * 12,
        scratch_shapes=[
            pltpu.SMEM((tokens // CH + 2,), full),
            held(3 * CONV, head_width, kind=full),
            held(tokens, 1, kind=jnp.int32),
            held(tokens, head_width, kind=full),
            held(count, BT, BT),
            held(count, 2 * BT, BT),
            held(count, BT, BT),
            held(count, BT, BT),
            held(HALO + tokens, max(width, model)),
            held(tokens, head_width),
            held(count, BT, BT),
            held(count, BT, BT),
            held(BT + HALO, 3 * head_width, kind=full),
            held(tokens, width),
            held(min(PB, own), width),
            held(model, width),
            held(model, width),
            held(own, model, kind=full),
            held(own, model),
            held(own, model),
            held(chips, own, model),
            held(chips, own, model),
            held(chips - 1, own, model),
            held(chips, own, model),
            held(chips, own, model),
            held(chips, own, model),
            held(chips - 1, own, model),
            held(own_rows, units),
            held(outer - 1, own_rows, units),
            held(outer, own_rows, units),
            *sum_buffers(own_rows, units),
            held(outer, slab, model),
            *sum_buffers(slab, model),
            held(out.shape[0], half),
            held(out.shape[0], half),
            *sum_buffers(out_rows, half),
            held(chips, out_rows, half),
            *sum_buffers(own_rows, head_width),
            *sum_buffers(own_rows, head_width),
            *sum_buffers(own_rows, head_width),
            *sum_buffers(own_rows, DK),
            held(own_rows, units),
            held(own_rows, units),
            held(slab, model),
            held(out_rows, half),
            held(own_rows, width),
            held(n_seq, own_rows, units),
            held(n_seq, own_rows, units),
            held(2, own_rows, hidden_units),
            held(16, head_width, kind=full),
            held(SMALL_ROWS, head_width, kind=full),
            held(n_fsdp, SMALL_ROWS, head_width, kind=full),
            held(n_seq, SMALL_ROWS, head_width, kind=full),
            held(16, model, kind=full),
            held(model // DK, DK, kind=full),
            held(model // DK, DK, kind=full),
            held(n_fsdp, model // DK, DK, kind=full),
            held(n_seq, model // DK, DK, kind=full),
            pltpu.SemaphoreType.DMA((copies,)),
            pltpu.SemaphoreType.DMA((copies,)),
            pltpu.SemaphoreType.DMA((gathers,)),
            pltpu.SemaphoreType.DMA((gathers,)),
            pltpu.SemaphoreType.DMA((shares,)),
            pltpu.SemaphoreType.DMA((shares,)),
            pltpu.SemaphoreType.DMA((61,)),
        ],
        compiler_params=pltpu.CompilerParams(
            vmem_limit_bytes=63 << 20, collective_id=3, has_side_effects=True
        ),
        name="mixer_backward",
    )(
        lengths, row, grad_heads, taps, gain, norm_gain, ffn_gain, delta, inverse, parts,
        update, state, packed, normed, weight, own_tokens, hidden, grad_hidden, result,
        gate, up, down, out,
    )


def finish_kernel(
    heads,
    result_in,
    tokens_in,
    gate_in,
    up_in,
    down_in,
    out_in,
    query_in,
    key_in,
    value_in,
    beta_in,
    small_in,
    norm_in,
    result_ref,
    tokens_ref,
    norm_ref,
    query_ref,
    key_ref,
    value_ref,
    beta_ref,
    taps_ref,
    gain_ref,
    out_ref,
    ffn_ref,
    gate_ref,
    up_ref,
    down_ref,
):
    full = jnp.float32
    result_ref[...] = result_in[...]
    tokens_ref[...] = tokens_in[...]
    for source, target in (
        (gate_in, gate_ref),
        (up_in, up_ref),
        (out_in, out_ref),
        (query_in, query_ref),
        (key_in, key_ref),
        (value_in, value_ref),
        (down_in, down_ref),
    ):
        target[...] = source[...].astype(full)
    total = None
    row, col = iota((beta_ref.shape[0], DK), 0), iota((beta_ref.shape[0], DK), 1)
    for owner in range(beta_in.shape[0]):
        hot = jnp.where((col + owner * heads == row) & (col < heads), 1.0, 0.0)
        part = bdot(hot, beta_in[owner], NT)
        total = part if total is None else total + part
    beta_ref[...] = total
    for kind in range(3):
        for back in range(CONV):
            at = kind * CONV + back
            taps_ref[kind, back : back + 1, :] = small_in[at : at + 1, :]
    gain_ref[...] = small_in[3 * CONV : 3 * CONV + 1, 0:DK]
    ffn_ref[...] = small_in[3 * CONV + 1 : 3 * CONV + 2, :]
    for index in range(norm_in.shape[0]):
        norm_ref[:, index * DK : (index + 1) * DK] = norm_in[index : index + 1, :]


def finish(heads, arrays):
    result, tokens, gate, up, down, out, query, key, value, beta, small, norm = arrays
    full = jnp.float32
    model = small.shape[1]
    head_count = heads * beta.shape[0]

    def wide(array):
        return jax.ShapeDtypeStruct(array.shape, full)

    return pl.pallas_call(
        functools.partial(finish_kernel, heads),
        out_shape=(
            jax.ShapeDtypeStruct(result.shape, result.dtype),
            wide(tokens),
            jax.ShapeDtypeStruct((1, model), full),
            wide(query),
            wide(key),
            wide(value),
            jax.ShapeDtypeStruct((head_count, query.shape[0]), full),
            jax.ShapeDtypeStruct((3, CONV, model), full),
            jax.ShapeDtypeStruct((1, DK), full),
            wide(out),
            jax.ShapeDtypeStruct((1, model), full),
            wide(gate),
            wide(up),
            wide(down),
        ),
        in_specs=[spec()] * 12,
        out_specs=(spec(),) * 14,
        compiler_params=pltpu.CompilerParams(vmem_limit_bytes=63 << 20),
        name="finish",
    )(*arrays)


def own_slice(array, place, size, axis):
    return lax.dynamic_slice_in_dim(array, place * size, size, axis)


def local(
    n_seq,
    n_fsdp,
    tokens,
    norm_gain,
    w_query,
    w_key,
    w_value,
    w_beta,
    conv_taps,
    head_gain,
    w_out,
    ffn_gain,
    w_gate,
    w_up,
    w_down,
    cotangent,
    token_order,
    seq_lengths,
):
    place = lax.axis_index("seq")
    model = tokens.shape[1]
    head_count = w_beta.shape[1]
    heads = head_count // n_seq
    hidden_units = w_gate.shape[1]
    slab = hidden_units // (n_fsdp * n_seq)
    units = slab * n_fsdp

    row = token_order.reshape(1, -1)
    gain = head_gain.reshape(1, DK)
    mixed_tok, normed, w_mixer, full_gate, full_up, full_down, full_o, cot_all, *saved = (
        mixer_forward(
            n_seq,
            n_fsdp,
            seq_lengths,
            row,
            conv_taps,
            gain,
            norm_gain.reshape(1, model),
            (
                tokens,
                w_beta.T,
                cotangent,
                w_query,
                w_key,
                w_value,
                w_gate,
                w_up,
                w_down if slab % 8 == 0 else own_slice(w_down, place, slab, 0),
                w_out,
            ),
        )
    )
    full_down = full_down.reshape(units, model)
    (
        hidden,
        grad_hidden,
        grad_heads,
        result_part,
        wide_gate,
        wide_up,
        wide_down,
        wide_out,
        grad_ffn_gain,
    ) = ffn_block(
        n_seq,
        n_fsdp,
        tokens,
        mixed_tok,
        full_o,
        ffn_gain.reshape(1, model),
        full_gate,
        full_up,
        full_down,
        cot_all,
    )
    (
        result,
        grad_inputs,
        all_gate,
        all_up,
        part_down,
        all_out,
        all_query,
        all_key,
        all_value,
        part_beta,
        small,
        norm_sum,
    ) = mixer_backward(
        n_seq,
        n_fsdp,
        (
            seq_lengths,
            row,
            grad_heads,
            conv_taps,
            gain,
            norm_gain.reshape(1, model),
            grad_ffn_gain,
        ),
        saved,
        (
            normed,
            w_mixer,
            tokens,
            hidden,
            grad_hidden,
            result_part,
            wide_gate,
            wide_up,
            wide_down.reshape(n_fsdp, slab, model),
            wide_out,
        ),
    )
    outputs = finish(
        heads,
        (
            result,
            grad_inputs,
            all_gate,
            all_up,
            part_down.reshape(n_seq * slab, model),
            all_out,
            all_query,
            all_key,
            all_value,
            part_beta,
            small,
            norm_sum,
        ),
    )
    flat, turned = (2, 8, 10), (6,)
    return tuple(
        output.reshape(-1) if index in flat else output.T if index in turned else output
        for index, output in enumerate(outputs)
    )


def solution(mesh):
    tokens = P(("seq", "fsdp"), None)
    rows = P("fsdp", None)
    in_specs = (
        (tokens, P()) + (rows,) * 4 + (P(), P(), rows, P()) + (rows,) * 3 + (tokens, rows, rows)
    )
    out_specs = (
        (tokens, tokens, P()) + (rows,) * 4 + (P(), P(), rows, P()) + (rows,) * 3
    )
    return jax.shard_map(
        functools.partial(local, mesh.shape["seq"], mesh.shape["fsdp"]),
        mesh=mesh,
        in_specs=in_specs,
        out_specs=out_specs,
        check_vma=False,
    )
```
